32 devices in a mesh: dp: 8 (over z, x), row: 2 (over core), col: 2 (over y).
Axes of the slice: x: 2, y: 2, z: 4, core: 2. Of those that a mesh axis runs over, the one named last changes fastest.
Arguments:
- latents: bfloat16 [8, 2, 4, 64, 64], P('dp', None, None, 'row', 'col'), may hold values from -6 to 6
- levels: int32 [8], P('dp'), may hold values from 1 to 2, as said below
- timesteps: int32 [8, 2], P('dp'), may hold values from 0 to 999
- patch_weight: bfloat16 [2, 1152, 16], P(None, ('row', 'col')), may hold values from -1.5 to 1.5
- patch_bias: bfloat16 [2, 1152], P(None, ('row', 'col')), may hold values from -3 to 3
- ada_weight: bfloat16 [2, 1152, 6912], P(None, ('row', 'col')), may hold values from -0.1875 to 0.1875
- ada_bias: bfloat16 [2, 6912], P(None, ('row', 'col')), may hold values from -2 to 2
- qkv_weight: bfloat16 [2, 1152, 3456], P(None, ('row', 'col')), may hold values from -0.1875 to 0.1875
- qk_gains: bfloat16 [2, 2, 72], replicated, may hold values from 0.25 to 1.75
- out_weight: bfloat16 [2, 1152, 1152], P(None, ('row', 'col')), may hold values from -1.5 to 1.5
- gate_weight: bfloat16 [2, 1152, 3072], P(None, ('row', 'col')), may hold values from -0.1875 to 0.1875
- up_weight: bfloat16 [2, 1152, 3072], P(None, ('row', 'col')), may hold values from -0.1875 to 0.1875
- down_weight: bfloat16 [2, 3072, 1152], P(None, ('row', 'col')), may hold values from -0.109375 to 0.109375
- cotangent: bfloat16 [8, 2, 32, 32, 1152], P('dp', None, 'row', 'col'), may hold values from -6 to 6
Outputs:
- hidden_out: bfloat16 [8, 2, 32, 32, 1152], P('dp', None, 'row', 'col')
- latent_grad: float32 [8, 2, 4, 64, 64], P('dp', None, None, 'row', 'col')
- patch_weight_grad: float32 [2, 1152, 16], P(None, ('dp', 'row', 'col'))
- patch_bias_grad: float32 [2, 1152], P(None, ('dp', 'row', 'col'))
- ada_weight_grad: float32 [2, 1152, 6912], P(None, ('dp', 'row', 'col'))
- ada_bias_grad: float32 [2, 6912], P(None, ('dp', 'row', 'col'))
- qkv_weight_grad: float32 [2, 1152, 3456], P(None, ('dp', 'row', 'col'))
- qk_gains_grad: float32 [2, 2, 72], replicated
- out_weight_grad: float32 [2, 1152, 1152], P(None, ('dp', 'row', 'col'))
- gate_weight_grad: float32 [2, 1152, 3072], P(None, ('dp', 'row', 'col'))
- up_weight_grad: float32 [2, 1152, 3072], P(None, ('dp', 'row', 'col'))
- down_weight_grad: float32 [2, 3072, 1152], P(None, ('dp', 'row', 'col'))
The draws below stay inside these ranges and needn't reach their ends.
Inputs may be any that keep to these rules, and one draw needn't show every extreme that they name: Every image has 1 to 2 live noise levels, and some image has 2.
All inputs are finite; a program needn't handle non-finite values.
Results may differ from the reference program's by a relative error of at most 0.025.
Values may be sent and summed in bfloat16 or wider, within the bound.
No kernel may reach another device: no remote copies, remote signals or barrier semaphores. Data moves between devices by JAX's collectives and lax.ppermute only.
A program may use at most 576 MiB of HBM per device.

```python
import math
import jax
import jax.numpy as jnp
from jax import lax

D = 1152
HEADS = 16
HD = 72
FF = 3072
CH = 4
LAT = 64
LEV = 2
NT = 1000
IMAGES = 8
PV = 16


def draw_levels(key, part):
    first_key, second_key = jax.random.split(jax.random.fold_in(key, 11))
    counts = jax.random.randint(first_key, (IMAGES,), 1, LEV + 1)
    chosen = jax.random.randint(second_key, (), 0, IMAGES)
    return jnp.where(jnp.arange(IMAGES) == chosen, LEV, counts).astype(jnp.int32)


def plant(array, own_key, least, top_value):
    index_at = [jax.random.randint(jax.random.fold_in(own_key, axis), (), 0, length) for axis, length in enumerate(array.shape)]
    main_axis = array.shape.index(max(array.shape))
    beside = index_at[:main_axis] + [(index_at[main_axis] + 1) % array.shape[main_axis]] + index_at[main_axis + 1:]
    return array.at[tuple(index_at)].set(least).at[tuple(beside)].set(top_value)


def block_levels(rng, extent, pieces, smallest, largest):
    def one(axis_at, shards_of):
        draws = jax.random.uniform(jax.random.fold_in(jax.random.fold_in(rng, 6), axis_at), (shards_of,), jnp.float32, smallest / len(pieces), largest / len(pieces))
        return jnp.repeat(jnp.exp(draws), extent[axis_at] // shards_of).reshape((-1,) + (1,) * (len(extent) - axis_at - 1))

    gain = one(*pieces[0])
    for cut in pieces[1:]:
        gain = gain * one(*cut)
    return gain


def scatter_about(rng, shape, spread, limit, cuts=(), held_as=jnp.bfloat16):
    values = spread * jax.random.normal(rng, shape, jnp.float32)
    if cuts:
        values = values * block_levels(rng, shape, cuts, -0.22, 0.18)
    return jnp.clip(values, -limit, limit).astype(held_as)


def setup_inputs(seed: int = 0) -> dict:
    splits = jax.random.split(jax.random.key(seed), 15)
    return {
        "latents": scatter_about(splits[0], (IMAGES, LEV, CH, LAT, LAT), 1.0, 6.0, ((0, 8), (3, 2), (4, 2))),
        "levels": draw_levels(jax.random.fold_in(splits[14], 71), 0),
        "timesteps": plant(jax.random.randint(splits[2], (IMAGES, LEV), 0, NT), jax.random.fold_in(splits[2], 1), 0, NT - 1).astype(jnp.int32),
        "patch_weight": scatter_about(splits[3], (2, D, PV), PV ** -0.5, 1.5, ((1, 4),)),
        "patch_bias": scatter_about(splits[4], (2, D), 0.5, 3.0, ((1, 4),)),
        "ada_weight": scatter_about(splits[5], (2, D, 6 * D), D ** -0.5, 0.1875, ((1, 4),)),
        "ada_bias": scatter_about(splits[6], (2, 6 * D), 0.3, 2.0, ((1, 4),)),
        "qkv_weight": scatter_about(splits[7], (2, D, 3 * D), D ** -0.5, 0.1875, ((1, 4),)),
        "qk_gains": jnp.clip(1.0 + 0.15 * jax.random.normal(splits[8], (2, 2, HD), jnp.float32), 0.25, 1.75).astype(jnp.bfloat16),
        "out_weight": scatter_about(splits[9], (2, D, D), (D // 64) ** -0.5, 1.5, ((1, 4),)),
        "gate_weight": scatter_about(splits[10], (2, D, FF), D ** -0.5, 0.1875, ((1, 4),)),
        "up_weight": scatter_about(splits[11], (2, D, FF), D ** -0.5, 0.1875, ((1, 4),)),
        "down_weight": scatter_about(splits[12], (2, FF, D), FF ** -0.5, 0.109375, ((1, 4),)),
        "cotangent": scatter_about(splits[13], (IMAGES, LEV, LAT // 2, LAT // 2, D), 1.0, 6.0, ((0, 8), (2, 2), (3, 2))),
    }


@jax.custom_vjp
def low(v):
    return lax.optimization_barrier(v.astype(jnp.bfloat16)).astype(jnp.float32)

@jax.custom_vjp
def low_back(v):
    return v

def low_keep(v):
    return (low(v), None)

def low_pass(kept, grad):
    return (grad,)

def back_keep(v):
    return (v, None)

def back_low(kept, grad):
    return (low(grad),)
low.defvjp(low_keep, low_pass)
low_back.defvjp(back_keep, back_low)
epsilon = 1e-06
highest = lax.Precision.HIGHEST

def matmul(left, right):
    return jnp.dot(left, right, precision=highest, preferred_element_type=jnp.float32)

def rms_norm(value):
    return value * lax.rsqrt(lax.optimization_barrier(jnp.mean(value * value, axis=-1, keepdims=True)) + epsilon)

def rotate(value, cos_row, sin_row, cos_col, sin_col):
    quarter = value.shape[-1] // 4
    first = value[..., :quarter]
    second = value[..., quarter:2 * quarter]
    third = value[..., 2 * quarter:3 * quarter]
    fourth = value[..., 3 * quarter:]
    return jnp.concatenate([first * cos_row - second * sin_row, first * sin_row + second * cos_row, third * cos_col - fourth * sin_col, third * sin_col + fourth * cos_col], axis=-1)

def time_features(steps, width):
    half = width // 2
    freqs = jnp.exp(-math.log(10000.0) * jnp.arange(half).astype(jnp.float32) / half)
    angles = steps.astype(jnp.float32)[:, None] * freqs[None, :]
    return jnp.concatenate([jnp.cos(angles), jnp.sin(angles)], axis=-1)

def rope_tables(grid):
    tokens = jnp.arange(grid * grid)
    quarter = HD // 4
    freqs = jnp.exp(-math.log(10000.0) * jnp.arange(quarter).astype(jnp.float32) / quarter)
    angle_row = (tokens // grid).astype(jnp.float32)[:, None] * freqs
    angle_col = (tokens % grid).astype(jnp.float32)[:, None] * freqs
    return (jnp.cos(angle_row)[:, None, :], jnp.sin(angle_row)[:, None, :], jnp.cos(angle_col)[:, None, :], jnp.sin(angle_col)[:, None, :])

def attend(items):
    query, key_rot, value = items
    temper = query.shape[-1] ** (-0.5)
    scores = low_back(jnp.einsum('qhd,khd->hqk', query, key_rot, precision=highest) * temper)
    top = lax.optimization_barrier(jnp.max(scores, axis=-1, keepdims=True))
    expo = jnp.exp(scores - top)
    probs = low(expo / lax.optimization_barrier(jnp.sum(expo, axis=-1, keepdims=True)))
    return jnp.einsum('hqk,khd->qhd', probs, value, precision=highest)

def block(hidden0, mods, qkv_w, gains, out_w, gate_w, up_w, down_w, tables):
    shift1, scale1, gate1, shift2, scale2, gate2 = mods
    count, seq, width = hidden0.shape
    attn_in = low(rms_norm(hidden0) * (1.0 + scale1) + shift1)
    qkv = low_back(matmul(attn_in.reshape(count * seq, width), qkv_w)).reshape(count, seq, 3, HEADS, HD)
    query = rms_norm(qkv[:, :, 0]) * gains[0]
    keys = rms_norm(qkv[:, :, 1]) * gains[1]
    query_r = low(rotate(query, tables[0], tables[1], tables[2], tables[3]))
    key_r = low(rotate(keys, tables[0], tables[1], tables[2], tables[3]))
    value_b = low(qkv[:, :, 2])
    outputs = lax.map(jax.checkpoint(attend), (query_r, key_r, value_b))
    out_b = low(low_back(outputs)).reshape(count * seq, width)
    att = low_back(matmul(out_b, out_w)).reshape(count, seq, width)
    hidden1 = hidden0 + gate1 * att
    mlp_in = low(rms_norm(hidden1) * (1.0 + scale2) + shift2).reshape(count * seq, width)
    gate_pre = low_back(matmul(mlp_in, gate_w))
    up_pre = low_back(matmul(mlp_in, up_w))
    inner = low(jax.nn.silu(gate_pre) * up_pre)
    mlp_out = low_back(matmul(inner, down_w)).reshape(count, seq, width)
    return hidden1 + gate2 * mlp_out

def image_layer(latent, count, steps, weights):
    patch_w, patch_b, ada_w, ada_b, qkv_w, gains, out_w, gate_w, up_w, down_w = weights
    grid = LAT // 2
    seq = grid * grid
    width = patch_w.shape[1]
    tables = rope_tables(grid)
    moved = jnp.roll(jnp.roll(latent, 1, axis=2), 1, axis=3)
    patches = moved.reshape(LEV, CH, grid, 2, grid, 2).transpose(0, 2, 4, 1, 3, 5).reshape(LEV, seq, CH * 4)
    enc_h0 = low_back(matmul(patches[0], patch_w[0].T) + patch_b[0]).reshape(1, seq, width)
    enc_sil = low(jax.nn.silu(time_features(steps[:1], width)))
    enc_mod = (matmul(enc_sil, ada_w[0]) + ada_b[0]).reshape(1, 6, 1, width)
    encoded = block(enc_h0, [enc_mod[:, k] for k in range(6)], qkv_w[0], gains[0], out_w[0], gate_w[0], up_w[0], down_w[0], tables)
    dec_h0 = low_back(matmul(patches.reshape(LEV * seq, CH * 4), patch_w[1].T) + patch_b[1]).reshape(LEV, seq, width)
    cond = encoded + time_features(steps, width)[:, None, :]
    dec_sil = low(jax.nn.silu(cond)).reshape(LEV * seq, width)
    dec_mod = low_back(matmul(dec_sil, ada_w[1]) + ada_b[1]).reshape(LEV, seq, 6, width)
    decoded = block(dec_h0, [dec_mod[:, :, k] for k in range(6)], qkv_w[1], gains[1], out_w[1], gate_w[1], up_w[1], down_w[1], tables)
    live = (jnp.arange(LEV) < count).astype(jnp.float32)[:, None, None]
    return (decoded * live).reshape(LEV, grid, grid, width)

def reference(latents, levels, timesteps, patch_weight, patch_bias, ada_weight, ada_bias, qkv_weight, qk_gains, out_weight, gate_weight, up_weight, down_weight, cotangent):

    def forward(latent_all, patch_w, patch_b, ada_w, ada_b, qkv_w, gains, out_w, gate_w, up_w, down_w):
        weights = (patch_w, patch_b, ada_w, ada_b, qkv_w, gains, out_w, gate_w, up_w, down_w)

        def one_image(items):
            return image_layer(items[0], items[1], items[2], weights)
        return lax.map(jax.checkpoint(one_image), (latent_all, levels, timesteps))
    result, pullback = jax.vjp(forward, latents.astype(jnp.float32), patch_weight.astype(jnp.float32), patch_bias.astype(jnp.float32), ada_weight.astype(jnp.float32), ada_bias.astype(jnp.float32), qkv_weight.astype(jnp.float32), qk_gains.astype(jnp.float32), out_weight.astype(jnp.float32), gate_weight.astype(jnp.float32), up_weight.astype(jnp.float32), down_weight.astype(jnp.float32))
    grads = pullback(cotangent.astype(jnp.float32))
    return (result.astype(jnp.bfloat16), grads[0], grads[1], grads[2], grads[3], grads[4], grads[5], grads[6], grads[7], grads[8], grads[9], grads[10])
```

```python
import functools
import math

import jax
import jax.numpy as jnp
from jax import lax
from jax.experimental import pallas as pl
from jax.experimental.pallas import tpu as pltpu
from jax.sharding import PartitionSpec as P

epsilon = 1e-06
highest = lax.Precision.HIGHEST
low = jnp.bfloat16
full = jnp.float32
WINDOW = 256
MIB = 1 << 20


def matmul(left, right):
    return jnp.dot(left, right, preferred_element_type=full)


def matmul_t(left, right):
    return lax.dot_general(left, right, (((1,), (1,)), ((), ())), preferred_element_type=full)


def outer_sum(left, right):
    return lax.dot_general(left, right, (((0,), (0,)), ((), ())), preferred_element_type=full)


def rms_scale(value):
    return lax.rsqrt(jnp.mean(value * value, axis=-1, keepdims=True) + epsilon)


def rms_back(value, inverse, grad):
    return inverse * grad - value * inverse**3 * jnp.mean(value * grad, axis=-1, keepdims=True)


def swap(value, item):
    if isinstance(item, str):
        return lax.ppermute(value, item, [(0, 1), (1, 0)])
    size = lax.axis_size("dp")
    return lax.ppermute(value, "dp", [(i, i ^ (1 << item)) for i in range(size)])


def time_features(steps, width):
    half = width // 2
    freqs = jnp.exp(-math.log(10000.0) * jnp.arange(half).astype(full) / half)
    angles = steps.astype(full)[:, None] * freqs[None, :]
    return jnp.concatenate([jnp.cos(angles), jnp.sin(angles)], axis=-1)


def whole(shape):
    return pl.BlockSpec(shape, lambda *_: (0,) * len(shape))


def params(mib):
    return pltpu.CompilerParams(vmem_limit_bytes=mib * MIB)


def split_dot(value, onehot):
    top = value.astype(low)
    rest = (value - top.astype(full)).astype(low)
    return matmul(top, onehot) + matmul(rest, onehot)


def turned(value, cosine, sine, even, quarter):
    width = value.shape[-1]
    ahead = pltpu.roll(value, width - quarter, axis=1)
    behind = pltpu.roll(value, quarter, axis=1)
    return value * cosine + jnp.where(even, ahead, behind) * sine


def even_lanes(shape, head):
    lane = lax.broadcasted_iota(jnp.int32, shape, 1)
    return lax.rem(lax.div(lax.rem(lane, head), head // 4), 2) == 0


def qk_back_body(
    head, dq_ref, dk_ref, dkx_ref, dv_ref, dvx_ref, qkv_ref, cos_ref, sin_ref, gain_ref, mem_ref, memt_ref, out_ref, gg_ref
):
    width = dq_ref.shape[-1]

    @pl.when(pl.program_id(0) == 0)
    def _():
        gg_ref[...] = jnp.zeros_like(gg_ref)

    cosine = cos_ref[...]
    sine = -sin_ref[...]
    even = even_lanes(cosine.shape, head)
    member = mem_ref[...]
    member_t = memt_ref[...]
    grads = (dq_ref[...], dk_ref[...] + dkx_ref[...].astype(full))
    for part in (0, 1):
        value = qkv_ref[:, part * width : (part + 1) * width]
        mean = split_dot(value * value, member) * (1.0 / head)
        inverse_h = lax.rsqrt(mean + epsilon)
        inverse = split_dot(inverse_h, member_t)
        grad_n = turned(grads[part], cosine, sine, even, head // 4)
        normed = value * inverse
        gg_ref[part : part + 1, :] += jnp.sum(grad_n * normed, axis=0, keepdims=True)
        weighted = grad_n * gain_ref[part : part + 1, :]
        dots = split_dot(value * weighted, member) * (1.0 / head) * inverse_h * inverse_h
        back = inverse * weighted - normed * split_dot(dots, member_t)
        out_ref[:, part * width : (part + 1) * width] = back.astype(low)
    out_ref[:, 2 * width :] = (dv_ref[...] + dvx_ref[...].astype(full)).astype(low)


def qk_back(dq, dk, dkx, dv, dvx, qkv, cosine, sine, gains, member, member_t, head):
    tokens, width = dq.shape
    step = 128
    rows = lambda n: pl.BlockSpec((step, n), lambda i: (i, 0))
    return pl.pallas_call(
        functools.partial(qk_back_body, head),
        grid=(tokens // step,),
        in_specs=[rows(width)] * 5
        + [rows(2 * width), rows(width), rows(width), whole(gains.shape), whole(member.shape), whole(member_t.shape)],
        out_specs=[rows(3 * width), whole((8, width))],
        out_shape=[jax.ShapeDtypeStruct((tokens, 3 * width), low), jax.ShapeDtypeStruct((8, width), full)],
        compiler_params=params(48),
        cost_estimate=pl.CostEstimate(flops=30 * qkv.size, bytes_accessed=12 * qkv.size, transcendentals=0),
        name="qk_back",
    )(dq, dk, dkx, dv, dvx, qkv, cosine, sine, gains, member, member_t)


def head_window(head, width):
    index = pl.program_id(0)
    start = index * head
    base = jnp.minimum(lax.div(start, 128) * 128, width - WINDOW)
    return index, pl.multiple_of(base, 128), start - base


def window_mask(shape, offset, head):
    lane = lax.broadcasted_iota(jnp.int32, shape, 1)
    return jnp.logical_and(lane >= offset, lane < offset + head)


def attend_body(head, q_ref, kl_ref, kr_ref, vl_ref, vr_ref, o_ref, lse_ref, acc_ref):
    tokens, width = q_ref.shape
    index, base, offset = head_window(head, width)
    cols = pl.ds(base, WINDOW)
    factor = head ** (-0.5) * math.log2(math.e)

    @pl.when(index == 0)
    def _():
        acc_ref[...] = jnp.zeros_like(acc_ref)
        lse_ref[...] = jnp.zeros_like(lse_ref)

    step = 256
    mask = window_mask((step, WINDOW), offset, head)
    lane = lax.broadcasted_iota(jnp.int32, (step, lse_ref.shape[1]), 1)
    for first in range(0, tokens, step):
        rows = slice(first, first + step)
        query = jnp.where(mask, q_ref[rows, cols], jnp.zeros((), low))
        left = matmul_t(query, kl_ref[:, cols])
        right = matmul_t(query, kr_ref[:, cols])
        top = jnp.maximum(jnp.max(left, axis=1, keepdims=True), jnp.max(right, axis=1, keepdims=True)) * factor
        left = jnp.exp2(left * factor - top)
        right = jnp.exp2(right * factor - top)
        total = jnp.sum(left, axis=1, keepdims=True) + jnp.sum(right, axis=1, keepdims=True)
        out = matmul(left.astype(low), vl_ref[:, cols]) + matmul(right.astype(low), vr_ref[:, cols])
        acc_ref[rows, cols] += jnp.where(mask, out * (1.0 / total), 0.0)
        lse_ref[rows, :] += jnp.where(lane == index, top + jnp.log2(total), 0.0)

    @pl.when(index == pl.num_programs(0) - 1)
    def _():
        o_ref[...] = acc_ref[...].astype(low)


def attend(query, key_l, key_r, value_l, value_r, head):
    tokens, width = query.shape
    heads = width // head
    return pl.pallas_call(
        functools.partial(attend_body, head),
        grid=(heads,),
        in_specs=[whole((tokens, width))] * 5,
        out_specs=[whole((tokens, width)), whole((tokens, 128))],
        out_shape=[jax.ShapeDtypeStruct((tokens, width), low), jax.ShapeDtypeStruct((tokens, 128), full)],
        scratch_shapes=[pltpu.VMEM((tokens, width), full)],
        compiler_params=params(56),
        cost_estimate=pl.CostEstimate(
            flops=8 * tokens * tokens * WINDOW * heads, bytes_accessed=14 * tokens * width, transcendentals=2 * tokens * tokens * heads
        ),
        name="attend",
    )(query, key_l, key_r, value_l, value_r)


def attend_back_body(
    head,
    q_ref,
    kl_ref,
    kr_ref,
    vl_ref,
    vr_ref,
    do_ref,
    lse_ref,
    dq_ref,
    dkl_ref,
    dkr_ref,
    dvl_ref,
    dvr_ref,
    dkr_acc,
    dvr_acc,
):
    tokens, width = q_ref.shape
    index, base, offset = head_window(head, width)
    cols = pl.ds(base, WINDOW)
    temper = head ** (-0.5)
    factor = temper * math.log2(math.e)

    @pl.when(index == 0)
    def _():
        for ref in (dq_ref, dkl_ref, dvl_ref, dkr_acc, dvr_acc):
            ref[...] = jnp.zeros_like(ref)

    step = 256
    mask = window_mask((step, WINDOW), offset, head)
    for first in range(0, tokens, step):
        rows = slice(first, first + step)
        query = jnp.where(mask, q_ref[rows, cols], jnp.zeros((), low))
        grad = jnp.where(mask, do_ref[rows, cols], jnp.zeros((), low))
        level = lse_ref[pl.ds(index, 1), rows]
        probs = []
        grads = []
        for k_ref, v_ref in ((kl_ref, vl_ref), (kr_ref, vr_ref)):
            scores = matmul_t(k_ref[:, cols], query)
            prob = jnp.exp2(scores * factor - level)
            probs.append(prob)
            grads.append(prob * matmul_t(v_ref[:, cols], grad))
        delta = jnp.sum(grads[0], axis=0, keepdims=True) + jnp.sum(grads[1], axis=0, keepdims=True)
        grad_q = 0.0
        for part, (k_ref, dk, dv) in enumerate(((kl_ref, dkl_ref, dvl_ref), (kr_ref, dkr_acc, dvr_acc))):
            dv[:, cols] += matmul(probs[part].astype(low), grad)
            grad_s = (grads[part] - probs[part] * delta).astype(low)
            dk[:, cols] += matmul(grad_s, query)
            grad_q = grad_q + outer_sum(grad_s, k_ref[:, cols])
        dq_ref[rows, cols] += jnp.where(mask, grad_q * temper, 0.0)

    @pl.when(index == pl.num_programs(0) - 1)
    def _():
        dkl_ref[...] = dkl_ref[...] * temper
        dkr_ref[...] = (dkr_acc[...] * temper).astype(low)
        dvr_ref[...] = dvr_acc[...].astype(low)


def attend_back(query, key_l, key_r, value_l, value_r, grad, levels, head):
    tokens, width = query.shape
    heads = width // head
    wide = jax.ShapeDtypeStruct((tokens, width), full)
    thin = jax.ShapeDtypeStruct((tokens, width), low)
    return pl.pallas_call(
        functools.partial(attend_back_body, head),
        grid=(heads,),
        in_specs=[whole((tokens, width))] * 6 + [whole(levels.shape)],
        out_specs=[whole((tokens, width))] * 5,
        out_shape=[wide, wide, thin, wide, thin],
        scratch_shapes=[pltpu.VMEM((tokens, width), full)] * 2,
        compiler_params=params(60),
        cost_estimate=pl.CostEstimate(
            flops=20 * tokens * tokens * WINDOW * heads, bytes_accessed=28 * tokens * width, transcendentals=2 * tokens * tokens * heads
        ),
        name="attend_back",
    )(query, key_l, key_r, value_l, value_r, grad, levels)


class Weight:
    def __init__(self, offsets, pieces, columns):
        self.offsets = offsets
        self.arrays = [piece[0] for piece in pieces]
        self.plan = [piece[1:] for piece in pieces]
        self.height = sum(piece[3] for piece in pieces)
        self.columns = columns


def piece_source(ref, lead, first, count):
    source = ref if lead is None else ref.at[lead]
    return source.at[:, pl.ds(first, count)]


def anywhere(count):
    return [pl.BlockSpec(memory_space=pl.ANY)] * count


class Stream:
    def __init__(self, weights, tile, late):
        self.weights = weights
        self.tile = tile
        self.late = late
        self.steps = weights[0].columns // tile

    def specs(self):
        return [pl.BlockSpec(memory_space=pltpu.SMEM)] + anywhere(sum(len(w.arrays) for w in self.weights) + len(self.late))

    def operands(self):
        arrays = [self.weights[0].offsets]
        for w in self.weights:
            arrays += w.arrays
        return arrays + list(self.late)

    def scratch(self):
        shapes = []
        for w in self.weights:
            shapes += [pltpu.VMEM((2, w.height, self.tile), low), pltpu.SemaphoreType.DMA((2, len(w.arrays)))]
        for value in self.late:
            shapes += [pltpu.VMEM(value.shape, value.dtype), pltpu.SemaphoreType.DMA((1,))]
        return shapes

    def bind(self, operand_refs, scratch_refs):
        self.offs = operand_refs[0]
        at = 1
        self.pieces = []
        for w in self.weights:
            self.pieces.append(operand_refs[at : at + len(w.arrays)])
            at += len(w.arrays)
        late_refs = operand_refs[at:]
        self.buffers = scratch_refs[0 : 2 * len(self.weights) : 2]
        self.sems = scratch_refs[1 : 2 * len(self.weights) : 2]
        rest = scratch_refs[2 * len(self.weights) :]
        self.late_bufs = rest[0::2]
        self.late_copies = [
            pltpu.make_async_copy(ref, buf, sem.at[0]) for ref, buf, sem in zip(late_refs, rest[0::2], rest[1::2])
        ]

    def copies(self, step, slot):
        out = []
        for w, refs, buf, sem in zip(self.weights, self.pieces, self.buffers, self.sems):
            for at, (ref, (lead, first, rows)) in enumerate(zip(refs, w.plan)):
                source = piece_source(ref, lead, pl.multiple_of(first + step * self.tile, 128), self.tile)
                start = pl.multiple_of(self.offs[at], 16)
                out.append(pltpu.make_async_copy(source, buf.at[slot, pl.ds(start, rows), :], sem.at[slot, at]))
        return out

    def advance(self):
        step = pl.program_id(0)
        slot = lax.rem(step, 2)

        @pl.when(step == 0)
        def _():
            for copy in self.copies(0, 0):
                copy.start()
            for copy in self.late_copies:
                copy.start()

        @pl.when(step + 1 < self.steps)
        def _():
            for copy in self.copies(step + 1, 1 - slot):
                copy.start()

        for copy in self.copies(step, slot):
            copy.wait()
        return step, [buf.at[slot] for buf in self.buffers]

    def wait_late(self):
        for copy in self.late_copies:
            copy.wait()
        return self.late_bufs


def stream_call(name, stream, body, ins, in_specs, outs, out_specs, scratch, flops, mib=58):
    operands = stream.operands()
    frame = stream.scratch()

    def kernel(*refs):
        count = len(operands)
        ops, refs = refs[:count], refs[count:]
        inputs, refs = refs[: len(ins)], refs[len(ins) :]
        outputs, refs = refs[: len(outs)], refs[len(outs) :]
        stream.bind(ops, refs[: len(frame)])
        body(stream, inputs, outputs, refs[len(frame) :])

    moved = sum(v.size * v.dtype.itemsize for v in list(ins) + list(stream.late) + list(outs))
    moved += sum(2 * w.height * w.columns for w in stream.weights)
    return pl.pallas_call(
        kernel,
        grid=(stream.steps,),
        in_specs=stream.specs() + in_specs,
        out_specs=out_specs,
        out_shape=outs,
        scratch_shapes=frame + scratch,
        compiler_params=params(mib),
        cost_estimate=pl.CostEstimate(flops=flops, bytes_accessed=moved, transcendentals=0),
        name=name,
    )(*operands, *ins)


def by_rows(tokens, fun, step=128):
    @pl.loop(0, tokens // step)
    def _(i):
        fun(pl.ds(pl.multiple_of(i * step, step), step))


def take(ref, rows):
    return ref[rows, :] if ref.shape[0] > 1 else ref[...]


def give(ref, rows, value):
    if ref.shape[0] > 1:
        ref[rows, :] = value.astype(ref.dtype)
    else:
        ref[...] += jnp.sum(value, axis=0, keepdims=True)


def like(shape, dtype):
    return jax.ShapeDtypeStruct(shape, dtype)


def ada_matmul(value, weight, bias):
    tokens = value.shape[0]
    tile = weight.height
    stream = Stream([weight], tile, [])

    def body(stream, ins, outs, scratch):
        _, (w,) = stream.advance()
        outs[0][...] = matmul(ins[0][...], w[...]) + ins[1][...]

    return stream_call(
        "ada",
        stream,
        body,
        [value, bias],
        [whole(value.shape), pl.BlockSpec((1, tile), lambda j: (0, j))],
        [like((tokens, weight.columns), full)],
        [pl.BlockSpec((tokens, tile), lambda j: (0, j))],
        [],
        2 * tokens * weight.height * weight.columns,
    )[0]


def qkv_matmul(value, weight, cosine, sine, gains, member, member_t, head):
    tokens, width = value.shape
    stream = Stream([weight], width, [cosine, sine])

    def body(stream, ins, outs, scratch):
        x_ref, gain_ref, mem_ref, memt_ref = ins
        q_ref, k_ref, v_ref, raw_ref = outs
        (acc_ref,) = scratch
        step, (w,) = stream.advance()
        cos_ref, sin_ref = stream.late_bufs
        acc_ref[...] = matmul(x_ref[...], w[...])

        @pl.when(step == 0)
        def _():
            stream.wait_late()

        def head_norm(part, out):
            def rows_of(rows):
                raw = acc_ref[rows, :]
                raw_ref[rows, :] = raw
                mean = split_dot(raw * raw, mem_ref[...]) * (1.0 / head)
                inverse = split_dot(lax.rsqrt(mean + epsilon), memt_ref[...])
                normed = raw * inverse * gain_ref[part : part + 1, :]
                even = even_lanes(raw.shape, head)
                out[rows, :] = turned(normed, cos_ref[rows, :], sin_ref[rows, :], even, head // 4).astype(low)

            by_rows(tokens, rows_of)

        @pl.when(step == 0)
        def _():
            head_norm(0, q_ref)

        @pl.when(step == 1)
        def _():
            head_norm(1, k_ref)

        @pl.when(step == 2)
        def _():
            v_ref[...] = acc_ref[...].astype(low)

    flat = like((tokens, width), low)
    return stream_call(
        "qkv",
        stream,
        body,
        [value, gains, member, member_t],
        [whole(v.shape) for v in (value, gains, member, member_t)],
        [flat, flat, flat, like((tokens, 2 * width), full)],
        [whole((tokens, width))] * 3 + [pl.BlockSpec((tokens, width), lambda j: (0, jnp.minimum(j, 1)))],
        [pltpu.VMEM((tokens, width), full)],
        2 * tokens * weight.height * weight.columns,
    )


def out_matmul(value, weight, hidden0, mods):
    tokens, width = value.shape
    stream = Stream([weight], 384, [hidden0] + mods)

    def body(stream, ins, outs, scratch):
        att_ref, h1_ref, b_ref = outs
        (acc_ref,) = scratch
        step, (w,) = stream.advance()
        acc_ref[step] = matmul(ins[0][...], w[...])

        @pl.when(step == stream.steps - 1)
        def _():
            h0_ref, gate_ref, shift_ref, scale_ref = stream.wait_late()

            def rows_of(rows):
                att = jnp.concatenate([acc_ref[k, rows, :] for k in range(stream.steps)], axis=1)
                hidden1 = h0_ref[rows, :] + take(gate_ref, rows) * att
                normed = hidden1 * rms_scale(hidden1)
                att_ref[rows, :] = att.astype(low)
                h1_ref[rows, :] = hidden1
                b_ref[rows, :] = (normed * (1.0 + take(scale_ref, rows)) + take(shift_ref, rows)).astype(low)

            by_rows(tokens, rows_of)

    return stream_call(
        "attout",
        stream,
        body,
        [value],
        [whole(value.shape)],
        [like((tokens, width), low), like((tokens, width), full), like((tokens, width), low)],
        [whole((tokens, width))] * 3,
        [pltpu.VMEM((stream.steps, tokens, 384), full)],
        2 * tokens * weight.height * weight.columns,
    )


def gate_up_matmul(value, gate, up):
    tokens, width = value.shape
    tile = 512
    stream = Stream([gate, up], tile, [])

    def body(stream, ins, outs, scratch):
        hid_ref, g_ref, u_ref = outs
        _, (wg, wu) = stream.advance()
        g = matmul(ins[0][...], wg[...])
        u = matmul(ins[0][...], wu[...])
        g_ref[...] = g.astype(low)
        u_ref[...] = u.astype(low)
        hid_ref[...] = (g * jax.nn.sigmoid(g) * u).astype(low)

    flat = like((tokens, gate.columns), low)
    return stream_call(
        "gateup",
        stream,
        body,
        [value],
        [whole(value.shape)],
        [flat] * 3,
        [pl.BlockSpec((tokens, tile), lambda j: (0, j))] * 3,
        [],
        4 * tokens * gate.height * gate.columns,
    )


def down_matmul(value, weight, hidden1, gate):
    tokens, depth = value.shape
    width = weight.columns
    stream = Stream([weight], width, [hidden1, gate])

    def body(stream, ins, outs, scratch):
        mlp_ref, h2_ref = outs
        (acc_ref,) = scratch
        hid_ref = ins[0]
        at = 0
        copies = stream.copies(0, 0)
        for copy in copies + stream.late_copies:
            copy.start()
        for k, (_, _, rows) in enumerate(weight.plan):
            copies[k].wait()
            first = stream.offs[k]
            left = hid_ref[:, pl.ds(pl.multiple_of(first, 128), rows)]
            part = matmul(left, stream.buffers[0][0, pl.ds(pl.multiple_of(first, 128), rows), :])
            if k == 0:
                acc_ref[...] = part
            else:
                acc_ref[...] += part
        h1_ref, gate_ref = stream.wait_late()

        def rows_of(rows):
            mlp = acc_ref[rows, :]
            mlp_ref[rows, :] = mlp.astype(low)
            h2_ref[rows, :] = h1_ref[rows, :] + take(gate_ref, rows) * mlp

        by_rows(tokens, rows_of)

    return stream_call(
        "down",
        stream,
        body,
        [value],
        [whole(value.shape)],
        [like((tokens, width), low), like((tokens, width), full)],
        [whole((tokens, width))] * 2,
        [pltpu.VMEM((tokens, width), full)],
        2 * tokens * depth * width,
    )


def down_back(grad, weight, gate_pre, up_pre):
    tokens, width = grad.shape
    depth = weight.height
    stream = Stream([weight], width, [gate_pre, up_pre])

    def body(stream, ins, outs, scratch):
        dg_ref, du_ref = outs
        copies = stream.copies(0, 0)
        for copy in copies + stream.late_copies:
            copy.start()
        for k, (_, _, count) in enumerate(weight.plan):
            copies[k].wait()
            if k == 0:
                g_ref, u_ref = stream.wait_late()
            first = pl.multiple_of(stream.offs[k], 128)
            for at in range(0, count, 384):
                cols = pl.ds(pl.multiple_of(first + at, 128), 384)

                def rows_of(rows):
                    inner = matmul_t(ins[0][rows, :], stream.buffers[0][0, cols, :])
                    g = g_ref[rows, cols].astype(full)
                    u = u_ref[rows, cols].astype(full)
                    sigma = jax.nn.sigmoid(g)
                    active = g * sigma
                    dg_ref[rows, cols] = (inner * u * (sigma + active * (1.0 - sigma))).astype(low)
                    du_ref[rows, cols] = (inner * active).astype(low)

                by_rows(tokens, rows_of, 256)

    flat = like((tokens, depth), low)
    return stream_call(
        "downback",
        stream,
        body,
        [grad],
        [whole(grad.shape)],
        [flat, flat],
        [whole((tokens, depth))] * 2,
        [],
        2 * tokens * depth * width,
    )


def back_matmul(name, grads, weights, tile, late, outs, finish):
    tokens = grads[0].shape[0]
    width = weights[0].height
    stream = Stream(weights, tile, late)

    def body(stream, ins, outs, scratch):
        (acc_ref,) = scratch
        step, tiles = stream.advance()
        part = matmul_t(ins[0][...], tiles[0][...])
        for value, w in zip(ins[1:], tiles[1:]):
            part = part + matmul_t(value[...], w[...])

        @pl.when(step == 0)
        def _():
            acc_ref[...] = part

        @pl.when(step > 0)
        def _():
            acc_ref[...] += part

        @pl.when(step == stream.steps - 1)
        def _():
            refs = stream.wait_late()
            for ref in outs:
                if ref.shape[0] == 1:
                    ref[...] = jnp.zeros_like(ref)
            by_rows(tokens, lambda rows: finish(rows, acc_ref[rows, :], refs, outs))

    return stream_call(
        name,
        stream,
        body,
        list(grads),
        [pl.BlockSpec((tokens, tile), lambda j: (0, j))] * len(grads),
        outs,
        [whole(value.shape) for value in outs],
        [pltpu.VMEM((tokens, width), full)],
        2 * tokens * width * weights[0].columns * len(weights),
    )


def mlp_back(grads, weights, grad2, hidden1, att, mods):
    tokens, width = grad2.shape
    lead = mods[0].shape[0]

    def finish(rows, db, refs, outs):
        dh2_ref, h1_ref, att_ref, scale_ref, gate_ref = refs
        hidden1 = h1_ref[rows, :]
        inverse = rms_scale(hidden1)
        normed = hidden1 * inverse
        weighted = db * (1.0 + take(scale_ref, rows))
        back = inverse * (weighted - normed * jnp.mean(normed * weighted, axis=-1, keepdims=True))
        grad1 = dh2_ref[rows, :] + back
        outs[0][rows, :] = grad1
        outs[1][rows, :] = (grad1 * take(gate_ref, rows)).astype(low)
        give(outs[2], rows, db)
        give(outs[3], rows, db * normed)
        give(outs[4], rows, grad1 * att_ref[rows, :].astype(full))

    outs = [like((tokens, width), full), like((tokens, width), low)]
    outs += [like((lead, width), low if lead > 1 else full)] * 3
    return back_matmul("mlpback", grads, weights, 512, [grad2, hidden1, att] + mods, outs, finish)


def qkv_back(grad, weight, grad1, hidden0, scale):
    tokens, width = grad1.shape
    lead = scale.shape[0]

    def finish(rows, da, refs, outs):
        dh1_ref, h0_ref, scale_ref = refs
        hidden0 = h0_ref[rows, :]
        inverse = rms_scale(hidden0)
        normed = hidden0 * inverse
        weighted = da * (1.0 + take(scale_ref, rows))
        back = inverse * (weighted - normed * jnp.mean(normed * weighted, axis=-1, keepdims=True))
        outs[0][rows, :] = (dh1_ref[rows, :] + back).astype(low)
        give(outs[1], rows, da)
        give(outs[2], rows, da * normed)

    outs = [like((tokens, width), low)] + [like((lead, width), low if lead > 1 else full)] * 2
    return back_matmul("qkvback", [grad], [weight], width, [grad1, hidden0, scale], outs, finish)


def out_back(grad, weight):
    def finish(rows, value, refs, outs):
        outs[0][rows, :] = value.astype(low)

    return back_matmul("outback", [grad], [weight], 384, [], [like(grad.shape, low)], finish)[0]


def ada_back(grad, weight, cond):
    def finish(rows, value, refs, outs):
        cond = refs[0][rows, :]
        sigma = jax.nn.sigmoid(cond)
        outs[0][rows, :] = value * sigma * (1.0 + cond * (1.0 - sigma))

    return back_matmul("adaback", [grad], [weight], weight.height, [cond], [like(cond.shape, full)], finish)[0]


def tie(value, *others):
    others = [v for v in others if v is not None]
    if not others:
        return value
    return lax.optimization_barrier((value, *others))[0]


class Gather:
    def __init__(self, place, depth):
        self.place = place
        self.depth = depth
        self.over_col = []
        self.over_dp = []

    def pull(self, shards, which):
        row, col, bit = self.place
        rows = shards[0].shape[1]
        half = rows // 2
        mine = jnp.concatenate(
            [lax.dynamic_slice(s, (which, bit * half, 0), (1, half, s.shape[2]))[0] for s in shards], axis=1
        )
        if len(self.over_col) >= self.depth:
            mine = tie(mine, self.over_col[-self.depth])
        first = swap(mine, "col")
        self.over_col.append(first)
        relay = first
        if len(self.over_dp) >= self.depth:
            relay = tie(first, self.over_dp[-self.depth])
        second = swap(relay, 0)
        self.over_dp.append(second)
        first_s = swap(first, "row")
        second_s = swap(second, "row")
        own = (2 * row + col) * rows
        other = (2 * row + 1 - col) * rows
        own_s = (2 * (1 - row) + col) * rows
        other_s = (2 * (1 - row) + 1 - col) * rows
        offsets = [own, own_s, other + bit * half, other + (1 - bit) * half, other_s + bit * half, other_s + (1 - bit) * half]
        offsets = jnp.stack(offsets).astype(jnp.int32)
        out = []
        at = 0
        for s in shards:
            n = s.shape[2]
            far = swap(tie(s[which], first), "row")
            pieces = [
                (s, which, 0, rows),
                (far, None, 0, rows),
                (first, None, at, half),
                (second, None, at, half),
                (first_s, None, at, half),
                (second_s, None, at, half),
            ]
            out.append(Weight(offsets, pieces, n))
            at += n
        return out


def item_weight(item):
    return {"row": 2, "col": 1}.get(item) or 4 << item


def halving_order(path, width, block, me):
    at = jnp.arange(width)
    position = at // block
    owner = me
    for k, item in enumerate(path):
        owner = owner ^ (((position >> (len(path) - 1 - k)) & 1) * item_weight(item))
    return owner * block + at % block


class Share:
    def __init__(self, value, order, path):
        self.value = value
        self.order = list(order)
        self.path = list(path)
        self.got = None

    def parts(self, item):
        rows, columns = self.value.shape
        if self.order[0] == item:
            self.order = self.order[1:]
            return self.value[: rows // 2], self.value[rows // 2 :]
        self.order.remove(item)
        value = self.value.reshape(2, 2, rows // 4, columns)
        return value[:, 0].reshape(rows // 2, columns), value[:, 1].reshape(rows // 2, columns)

    def start(self):
        if self.path:
            item = self.path.pop(0)
            self.kept, away = self.parts(item)
            self.got = swap(away, item)
        return self

    def finish(self):
        if self.got is not None:
            self.value = (self.kept.astype(full) + self.got.astype(full)).astype(low)
            self.got = None
        return self.value


class BlockShare(Share):
    def __init__(self, value, coords, path, block):
        names = sorted((item for item in path if not isinstance(item, str)), reverse=True) + ["row", "col"]
        super().__init__(value.reshape((2,) * len(names) + (block, value.shape[-1])), names, path)
        self.coords = coords

    def parts(self, item):
        axis = self.order.index(item)
        self.order.remove(item)
        mine = self.coords[item]
        return (
            lax.dynamic_index_in_dim(self.value, mine, axis, keepdims=False),
            lax.dynamic_index_in_dim(self.value, 1 - mine, axis, keepdims=False),
        )


class Ordered:
    def __init__(self, left, right):
        self.left = left
        self.right = right
        self.half = left.shape[1] // 2
        self.got = swap(outer_sum(left[:, self.half :], right).astype(low), "row")

    def keep(self):
        return (outer_sum(self.left[:, : self.half], self.right) + self.got.astype(full)).astype(low)


class Agenda:
    def __init__(self):
        self.tasks = {}

    def add(self, name, task):
        self.tasks[name] = task.start()

    def step(self, value, *names):
        done = []
        for name in names:
            if name in self.tasks:
                task = self.tasks[name]
                done.append(task.finish())
                task.start()
        return tie(value, *done)

    def result(self, name):
        task = self.tasks[name]
        while True:
            value = task.finish()
            if not task.path:
                return value
            task.start()


def block_forward(hidden0, mods, mats, gains, tabs, ties):
    shift1, scale1, gate1, shift2, scale2, gate2 = mods
    qkv_w, out_w, gate_w, up_w, down_w = mats
    cosine, sine, member, member_t, head = tabs
    attn_in = (hidden0 * rms_scale(hidden0) * (1.0 + scale1) + shift1).astype(low)
    query, key, value, raw = qkv_matmul(attn_in, qkv_w, cosine, sine, gains, member, member_t, head)
    key_r = swap(key, "row")
    value_r = swap(value, "row")
    out_b, lse = attend(tie(query, *ties.get("attend", ())), key, key_r, value, value_r, head)
    att, hidden1, mlp_in = out_matmul(tie(out_b, *ties.get("out", ())), out_w, hidden0, [gate1, shift2, scale2])
    inner, gate_pre, up_pre = gate_up_matmul(tie(mlp_in, *ties.get("gate", ())), gate_w, up_w)
    mlp_out, hidden2 = down_matmul(tie(inner, *ties.get("down", ())), down_w, hidden1, gate2)
    cache = (hidden0, attn_in, raw, query, key, key_r, value, value_r, out_b, lse, att)
    cache += (hidden1, mlp_in, gate_pre, up_pre, inner, mlp_out)
    return hidden2, cache


def block_backward(grad2, cache, mods, mats, gains, tabs, comm, tag, plan):
    (hidden0, attn_in, raw, query, key, key_r, value, value_r, out_b, lse, att) = cache[:11]
    (hidden1, mlp_in, gate_pre, up_pre, inner, mlp_out) = cache[11:]
    shift1, scale1, gate1, shift2, scale2, gate2 = mods
    qkv_w, out_w, gate_w, up_w, down_w = mats
    cosine, sine, member, member_t, head = tabs
    agenda, orders, paths, coords = comm
    block = down_w.height // (4 * lax.axis_size("dp"))

    def reached(value, point, *more):
        return tie(agenda.step(value, *plan.get(point, ())), *more)

    def ordered(left, name):
        return matmul(left, orders[name]).astype(low)

    grad_mlp = (grad2 * gate2).astype(low)
    dgate2 = grad2 * mlp_out.astype(full)
    if gate2.shape[0] == 1:
        dgate2 = jnp.sum(dgate2, axis=0, keepdims=True)
    grad_mlp = reached(grad_mlp, "down")
    g_down = outer_sum(inner, grad_mlp).astype(low)
    agenda.add("down" + tag, BlockShare(g_down, coords, paths["down"], block))
    grad_gate, grad_up = down_back(reached(grad_mlp, "downback", g_down), down_w, gate_pre, up_pre)
    grad_gate = reached(grad_gate, "gate", agenda.tasks["down" + tag].got)
    w_gate = Ordered(ordered(mlp_in, "gate"), grad_gate)
    w_up = Ordered(ordered(mlp_in, "up"), grad_up)
    grad_gate = reached(grad_gate, "mlpback", w_gate.got, w_up.got)
    grad1, grad_att, dshift2, dscale2, dgate1 = mlp_back(
        [grad_gate, grad_up], [gate_w, up_w], grad2, hidden1, att, [scale2, gate1]
    )
    k_gate = w_gate.keep()
    k_up = w_up.keep()
    agenda.add("gate" + tag, Share(k_gate, paths["gate"][1:], paths["gate"][1:]))
    agenda.add("up" + tag, Share(k_up, paths["up"][1:], paths["up"][1:]))
    grad_att = reached(grad_att, "out", k_gate, k_up)
    w_out = Ordered(ordered(out_b, "out"), grad_att)
    grad_ob = out_back(tie(grad_att, w_out.got), out_w)
    k_out = w_out.keep()
    agenda.add("out" + tag, Share(k_out, paths["out"][1:], paths["out"][1:]))
    grad_ob = reached(grad_ob, "attend", k_out)
    dq, dkl, dkr, dvl, dvr = attend_back(query, key, key_r, value, value_r, grad_ob, lse.T, head)
    dkx = swap(dkr, "row")
    dvx = swap(dvr, "row")
    dq = reached(dq, "qk", dkx, dvx)
    grad_qkv, gain_rows = qk_back(dq, dkl, dkx, dvl, dvx, raw, cosine, sine, gains, member, member_t, head)
    grad_qkv = reached(grad_qkv, "qkv")
    w_qkv = Ordered(ordered(attn_in, "qkv"), grad_qkv)
    grad0, dshift1, dscale1 = qkv_back(reached(grad_qkv, "qkvback", w_qkv.got), qkv_w, grad1, hidden0, scale1)
    k_qkv = w_qkv.keep()
    wide = k_qkv.shape[1]
    cut = wide // 256 * 128
    order = paths["qkv"][1:]
    swapped = [order[1], order[0]] + order[2:]
    agenda.add("qkva" + tag, Share(k_qkv[:, :cut], order, order))
    agenda.add("qkvb" + tag, Share(k_qkv[:, cut:], order, swapped))
    dmods = [dshift1, dscale1, dgate1, dshift2, dscale2, dgate2]
    return grad0, dmods, gain_rows[:2], k_qkv


def per_device(
    latents,
    levels,
    timesteps,
    patch_weight,
    patch_bias,
    ada_weight,
    ada_bias,
    qkv_weight,
    qk_gains,
    out_weight,
    gate_weight,
    up_weight,
    down_weight,
    cotangent,
):
    images, slots, chans, rows_loc, cols_loc = latents.shape
    n_data = lax.axis_size("dp")
    assert images == 1 and slots == 2
    assert lax.axis_size("row") == 2 and lax.axis_size("col") == 2
    row = lax.axis_index("row")
    col = lax.axis_index("col")
    data = lax.axis_index("dp")
    bits = (n_data - 1).bit_length()
    bit = data & 1
    place = (row, col, bit)
    left = col == 0
    coords = {"row": row, "col": col}
    for k in range(bits):
        coords[k] = (data >> k) & 1
    grid_rows = rows_loc // 2
    grid_cols = cols_loc
    half_cols = grid_cols // 2
    tokens = grid_rows * grid_cols
    width = cotangent.shape[-1]
    head = qk_gains.shape[2]
    heads = width // head
    pvals = chans * 4
    shard = width // 4
    me = data * 4 + row * 2 + col
    own_rows = width // (4 * n_data)

    def pair(own, other, axis):
        return jnp.concatenate([jnp.where(left, own, other), jnp.where(left, other, own)], axis=axis)

    small = jnp.concatenate(
        [jnp.swapaxes(patch_weight, 1, 2).reshape(2 * pvals, shard), patch_bias, ada_bias.reshape(12, shard)], axis=0
    )
    small = pair(small[None], swap(small, "col")[None], 0)
    other = swap(small, "row")
    small = jnp.where(row == 0, jnp.stack([small, other]), jnp.stack([other, small])).reshape(4, 2 * pvals + 14, shard)
    patch_w = small[:, : 2 * pvals].transpose(1, 0, 2).reshape(2, pvals, width)
    patch_b = small[:, 2 * pvals : 2 * pvals + 2].transpose(1, 0, 2).reshape(2, width).astype(full)
    ada_b = small[:, 2 * pvals + 2 :].reshape(4, 2, 6 * shard).transpose(1, 0, 2).reshape(2, 6, width).astype(full)

    blk = latents[0]
    wide = pair(blk, swap(blk, "col"), 3)
    top_row = swap(wide[:, :, rows_loc - 1 :], "row")
    framed = jnp.concatenate([top_row, wide[:, :, : rows_loc - 1]], axis=2)
    framed = jnp.concatenate([framed[..., -1:], framed[..., :-1]], axis=3)
    patches = (
        framed.reshape(slots, chans, grid_rows, 2, grid_cols, 2).transpose(0, 2, 4, 1, 3, 5).reshape(slots, tokens, pvals)
    )
    enc_patches = patches[0]
    dec_patches = jnp.where(left, patches[0], patches[1])

    temb = time_features(timesteps[0], width)
    sil0 = jax.nn.silu(temb[:1]).astype(low)
    temb_own = jnp.where(left, temb[:1], temb[1:])
    part = matmul(lax.dynamic_slice(sil0, (0, (2 * row + col) * shard), (1, shard)), ada_weight[0])
    part = part.reshape(6, width)
    part = part + swap(part, "col")
    part = part + swap(part, "row")
    enc_mod = part + ada_b[0]
    enc_mods = [enc_mod[k : k + 1] for k in range(6)]
    sil_all = sil0
    for k in range(bits):
        sil_all = jnp.concatenate([sil_all, swap(sil_all, k)], axis=0)

    gather = Gather(place, 3)
    enc_qkv, enc_out = gather.pull([qkv_weight, out_weight], 0)
    enc_gate, enc_up = gather.pull([gate_weight, up_weight], 0)
    (enc_down,) = gather.pull([down_weight], 0)
    (dec_ada,) = gather.pull([ada_weight], 1)
    dec_qkv, dec_out = gather.pull([qkv_weight, out_weight], 1)
    dec_gate, dec_up = gather.pull([gate_weight, up_weight], 1)
    (dec_down,) = gather.pull([down_weight], 1)
    enc_mats = (enc_qkv, enc_out, enc_gate, enc_up, enc_down)
    dec_mats = (dec_qkv, dec_out, dec_gate, dec_up, dec_down)
    over_col, over_dp = gather.over_col, gather.over_dp

    own = jnp.where(left, cotangent[0, 0], cotangent[0, 1])
    got = swap(jnp.where(left, cotangent[0, 1], cotangent[0, 0]), "col")
    cot = pair(own, got, 1).reshape(tokens, width)

    quarter = head // 4
    lanes = jnp.arange(width)
    within = lanes % head
    section = within // quarter
    lane_freq = jnp.exp(-math.log(10000.0) * (within % quarter).astype(full) / quarter)
    row_pos = (row * grid_rows + jnp.arange(grid_rows)).astype(full)
    col_pos = jnp.arange(grid_cols).astype(full)
    row_angle = row_pos[:, None] * lane_freq[None, :]
    col_angle = col_pos[:, None] * lane_freq[None, :]
    by_row = section < 2
    sign = jnp.where(section % 2 == 0, -1.0, 1.0).astype(full)

    def table(fun):
        return jnp.where(by_row, fun(row_angle)[:, None, :], fun(col_angle)[None, :, :]).reshape(tokens, width)

    cosine = table(jnp.cos)
    sine = table(jnp.sin) * sign
    member = (lanes[:, None] // head == jnp.arange(128)[None, :]).astype(low)
    tabs = (cosine, sine, member, member.T, head)
    gain_rows = jnp.tile(qk_gains.astype(full), (1, 1, heads))

    rest = list(range(2, bits))
    path_y = ["row", "col", 0, 1] + rest
    path_x = ["row", 0, "col", 1] + rest
    path_z = ["row", 1, "col", 0] + rest
    path_w = ["row", 1, 0, "col"] + rest
    paths = {"down": path_z, "gate": path_y, "up": path_x, "out": path_w, "qkv": path_y, "ada": path_y}
    perm = {}
    orders = {}
    for name in ("gate", "up", "out", "qkv", "ada"):
        key = tuple(paths[name])
        if key not in perm:
            source = halving_order(paths[name], width, own_rows, me)
            perm[key] = (lanes[:, None] == source[None, :]).astype(low)
        orders[name] = perm[key]

    enc_h0 = matmul(enc_patches, patch_w[0]) + patch_b[0]
    ties = {"attend": over_col[1:2], "out": over_col[2:3]}
    encoded, enc_cache = block_forward(enc_h0, enc_mods, enc_mats, gain_rows[0], tabs, ties)
    dec_h0 = matmul(dec_patches, patch_w[1]) + patch_b[1]
    cond = encoded + temb_own
    dec_sil = jax.nn.silu(cond).astype(low)
    dec_mod = ada_matmul(dec_sil, dec_ada, ada_b[1].reshape(1, 6 * width))
    dec_mods = [dec_mod[:, k * width : (k + 1) * width] for k in range(6)]
    ties = {"attend": over_col[5:6], "out": over_col[6:7]}
    decoded, dec_cache = block_forward(dec_h0, dec_mods, dec_mats, gain_rows[1], tabs, ties)
    live = (col < levels[0]).astype(full)
    result = (decoded * live).astype(low).reshape(grid_rows, grid_cols, width)
    near = jnp.where(left, result[:, :half_cols], result[:, half_cols:])
    away = swap(jnp.where(left, result[:, half_cols:], result[:, :half_cols]), "col")
    result = jnp.stack([jnp.where(left, near, away), jnp.where(left, away, near)])[None]

    agenda = Agenda()
    comm = (agenda, orders, paths, coords)
    dec_grad2 = cot.astype(full) * live
    plan = {
        "mlpback": ["down1"],
        "attend": ["down1"],
        "qk": ["gate1", "up1", "out1"],
        "qkvback": ["down1"],
    }
    dec_grad0, dec_dmods, dec_gains, k_qkv = block_backward(
        dec_grad2, dec_cache, dec_mods, dec_mats, gain_rows[1], tabs, comm, "1", plan
    )
    dmod_low = jnp.concatenate([piece.astype(low) for piece in dec_dmods], axis=1)
    dmod_low = tie(agenda.step(dmod_low, "gate1", "up1", "out1"), k_qkv)
    w_ada = Ordered(matmul(dec_sil, orders["ada"]).astype(low), dmod_low)
    dec_bada = jnp.sum(dmod_low.astype(full), axis=0).reshape(6, width)
    enc_grad2 = ada_back(tie(dmod_low, w_ada.got), dec_ada, cond)
    k_ada = w_ada.keep()
    order = paths["ada"][1:]
    agenda.add("adaa1", Share(k_ada[:, : 3 * width], order, order))
    agenda.add("adab1", Share(k_ada[:, 3 * width :], order, [order[1], order[0]] + order[2:]))
    enc_grad2 = tie(agenda.step(enc_grad2, "qkva1", "qkvb1", "down1", "gate1", "up1", "out1"), k_ada)

    def patch_rows(patch, grad):
        ones = jnp.ones((tokens, 1), low)
        return outer_sum(jnp.concatenate([patch, ones], axis=1), grad)

    total = jnp.concatenate([patch_rows(dec_patches, dec_grad0), dec_bada, dec_gains], axis=0)
    for item in ["row", "col"] + list(range(bits)):
        total = total + swap(total, item)
    dec_small = total

    plan = {
        "gate": ["qkva1", "qkvb1"],
        "mlpback": ["down0", "adaa1", "adab1"],
        "attend": ["down0", "adaa1", "adab1", "qkva1", "qkvb1"],
        "qk": ["gate0", "up0", "out0", "adaa1", "adab1"],
        "qkvback": ["down0"],
    }
    enc_grad0, enc_dmods, enc_gains, _ = block_backward(
        enc_grad2, enc_cache, enc_mods, enc_mats, gain_rows[0], tabs, comm, "0", plan
    )
    dec_small = tie(dec_small, enc_grad0)
    dmod_enc = jnp.concatenate(enc_dmods, axis=0)
    total = jnp.concatenate([patch_rows(enc_patches, enc_grad0), enc_gains, dmod_enc], axis=0)
    for item in ["row", "col"]:
        total = total + swap(total, item)
    dmod_all = total[None, pvals + 3 :]
    total = total[: pvals + 3]
    for k in range(bits):
        total = total + swap(total, k)
        dmod_all = jnp.concatenate([dmod_all, swap(dmod_all, k)], axis=0)
    enc_small = total
    enc_ada = jnp.dot(
        lax.dynamic_slice(sil_all, (0, me * own_rows), (n_data, own_rows)).astype(full).T,
        dmod_all.reshape(n_data, 6 * width),
        precision=highest,
        preferred_element_type=full,
    )
    enc_bada = jnp.sum(dmod_all, axis=0)

    def image(dpatch):
        return (
            dpatch.reshape(grid_rows, grid_cols, chans, 2, 2).transpose(2, 0, 3, 1, 4).reshape(chans, rows_loc, 2 * cols_loc)
        )

    enc_image = image(matmul_t(enc_grad0, patch_w[0]))
    dec_image = image(matmul_t(dec_grad0, patch_w[1]))
    zero = jnp.zeros_like(dec_image)
    grads = jnp.stack([enc_image + jnp.where(left, dec_image, zero), jnp.where(left, zero, dec_image)])
    grads = jnp.concatenate([grads[..., 1:], grads[..., :1]], axis=3)
    below = swap(grads[:, :, :1], "row")
    grads = jnp.concatenate([grads[:, :, 1:], below], axis=2)
    one = grads[..., :cols_loc]
    two = grads[..., cols_loc:]
    latent_grad = (jnp.where(left, one, two) + swap(jnp.where(left, two, one), "col"))[None]

    def own_lanes(value):
        return lax.dynamic_slice(value, (0, me * own_rows), (value.shape[0], own_rows))

    enc_patch = own_lanes(enc_small[: pvals + 1])
    dec_patch = own_lanes(dec_small[: pvals + 1])
    g_patch = jnp.stack([enc_patch[:pvals].T, dec_patch[:pvals].T])
    g_patch_b = jnp.stack([enc_patch[pvals], dec_patch[pvals]])
    bada = jnp.stack([enc_bada.reshape(-1), dec_small[pvals + 1 : pvals + 7].reshape(-1)])
    own_bada = 6 * own_rows
    g_bada = lax.dynamic_slice(bada, (0, me * own_bada), (2, own_bada))
    gains = jnp.stack([enc_small[pvals + 1 :], dec_small[pvals + 7 :]])
    gains = gains.reshape(2, 2, heads, head).sum(axis=2)
    def both(name):
        return jnp.stack([agenda.result(name + "0").astype(full), agenda.result(name + "1").astype(full)])

    g_ada = jnp.concatenate([agenda.result("adaa1"), agenda.result("adab1")], axis=1)
    g_ada_all = jnp.stack([enc_ada, g_ada.astype(full)])
    g_qkv = jnp.concatenate([both("qkva"), both("qkvb")], axis=2)
    stacked = [g_qkv, both("out"), both("gate"), both("up"), both("down")]
    return (
        result,
        latent_grad,
        g_patch,
        g_patch_b,
        g_ada_all,
        g_bada,
        stacked[0],
        gains,
        stacked[1],
        stacked[2],
        stacked[3],
        stacked[4],
    )


def solution(mesh):
    tile = ("row", "col")
    every = ("dp", "row", "col")
    return jax.shard_map(
        per_device,
        mesh=mesh,
        in_specs=(
            P("dp", None, None, "row", "col"),
            P("dp"),
            P("dp", None),
            P(None, tile, None),
            P(None, tile),
            P(None, tile, None),
            P(None, tile),
            P(None, tile, None),
            P(),
            P(None, tile, None),
            P(None, tile, None),
            P(None, tile, None),
            P(None, tile, None),
            P("dp", None, "row", "col", None),
        ),
        out_specs=(
            P("dp", None, "row", "col", None),
            P("dp", None, None, "row", "col"),
            P(None, every, None),
            P(None, every),
            P(None, every, None),
            P(None, every),
            P(None, every, None),
            P(),
            P(None, every, None),
            P(None, every, None),
            P(None, every, None),
            P(None, every, None),
        ),
        check_vma=False,
    )
```

```python
import functools
import math

import jax
import jax.numpy as jnp
from jax import lax
from jax.experimental import pallas as pl
from jax.experimental.pallas import tpu as pltpu
from jax.sharding import PartitionSpec as P

epsilon = 1e-06
highest = lax.Precision.HIGHEST
low = jnp.bfloat16
full = jnp.float32
WINDOW = 256
MIB = 1 << 20


def matmul(left, right):
    return jnp.dot(left, right, preferred_element_type=full)


def matmul_t(left, right):
    return lax.dot_general(left, right, (((1,), (1,)), ((), ())), preferred_element_type=full)


def outer_sum(left, right):
    return lax.dot_general(left, right, (((0,), (0,)), ((), ())), preferred_element_type=full)


def rms_scale(value):
    return lax.rsqrt(jnp.mean(value * value, axis=-1, keepdims=True) + epsilon)


def rms_back(value, inverse, grad):
    return inverse * grad - value * inverse**3 * jnp.mean(value * grad, axis=-1, keepdims=True)


def swap(value, item):
    if isinstance(item, str):
        return lax.ppermute(value, item, [(0, 1), (1, 0)])
    size = lax.axis_size("dp")
    return lax.ppermute(value, "dp", [(i, i ^ (1 << item)) for i in range(size)])


def time_features(steps, width):
    half = width // 2
    freqs = jnp.exp(-math.log(10000.0) * jnp.arange(half).astype(full) / half)
    angles = steps.astype(full)[:, None] * freqs[None, :]
    return jnp.concatenate([jnp.cos(angles), jnp.sin(angles)], axis=-1)


def whole(shape):
    return pl.BlockSpec(shape, lambda *_: (0,) * len(shape))


def params(mib):
    return pltpu.CompilerParams(vmem_limit_bytes=mib * MIB)


def split_dot(value, onehot):
    top = value.astype(low)
    rest = (value - top.astype(full)).astype(low)
    return matmul(top, onehot) + matmul(rest, onehot)


def turned(value, cosine, sine, even, quarter):
    width = value.shape[-1]
    ahead = pltpu.roll(value, width - quarter, axis=1)
    behind = pltpu.roll(value, quarter, axis=1)
    return value * cosine + jnp.where(even, ahead, behind) * sine


def even_lanes(shape, head):
    lane = lax.broadcasted_iota(jnp.int32, shape, 1)
    return lax.rem(lax.div(lax.rem(lane, head), head // 4), 2) == 0


def qk_back_body(head, dq_ref, dkv_ref, dkvx_ref, qkv_ref, cos_ref, sin_ref, gain_ref, mem_ref, memt_ref, out_ref, gg_ref):
    width = dq_ref.shape[-1]

    @pl.when(pl.program_id(0) == 0)
    def _():
        gg_ref[...] = jnp.zeros_like(gg_ref)

    cosine = cos_ref[...]
    sine = -sin_ref[...]
    even = even_lanes(cosine.shape, head)
    member = mem_ref[...]
    member_t = memt_ref[...]
    grads = (dq_ref[...], dkv_ref[:, :width] + dkvx_ref[:, :width].astype(full))
    for part in (0, 1):
        value = qkv_ref[:, part * width : (part + 1) * width]
        mean = split_dot(value * value, member) * (1.0 / head)
        inverse_h = lax.rsqrt(mean + epsilon)
        inverse = split_dot(inverse_h, member_t)
        grad_n = turned(grads[part], cosine, sine, even, head // 4)
        normed = value * inverse
        gg_ref[part : part + 1, :] += jnp.sum(grad_n * normed, axis=0, keepdims=True)
        weighted = grad_n * gain_ref[part : part + 1, :]
        dots = split_dot(value * weighted, member) * (1.0 / head) * inverse_h * inverse_h
        back = inverse * weighted - normed * split_dot(dots, member_t)
        out_ref[:, part * width : (part + 1) * width] = back.astype(low)
    out_ref[:, 2 * width :] = (dkv_ref[:, width:] + dkvx_ref[:, width:].astype(full)).astype(low)


def qk_back(dq, dkv, dkvx, raw, cosine, sine, gains, member, member_t, head):
    tokens, width = dq.shape
    step = 128
    rows = lambda n: pl.BlockSpec((step, n), lambda i: (i, 0))
    return pl.pallas_call(
        functools.partial(qk_back_body, head),
        grid=(tokens // step,),
        in_specs=[rows(width)]
        + [rows(2 * width)] * 3
        + [rows(width), rows(width), whole(gains.shape), whole(member.shape), whole(member_t.shape)],
        out_specs=[rows(3 * width), whole((8, width))],
        out_shape=[jax.ShapeDtypeStruct((tokens, 3 * width), low), jax.ShapeDtypeStruct((8, width), full)],
        compiler_params=params(48),
        cost_estimate=pl.CostEstimate(flops=60 * raw.size, bytes_accessed=18 * raw.size, transcendentals=0),
        name="qk_back",
    )(dq, dkv, dkvx, raw, cosine, sine, gains, member, member_t)


def head_window(head, width):
    index = pl.program_id(0)
    start = index * head
    base = jnp.minimum(lax.div(start, 128) * 128, width - WINDOW)
    return index, pl.multiple_of(base, 128), start - base


def window_mask(shape, offset, head):
    lane = lax.broadcasted_iota(jnp.int32, shape, 1)
    return jnp.logical_and(lane >= offset, lane < offset + head)


def attend_body(head, q_ref, kvl_ref, kvr_ref, o_ref, lse_ref, acc_ref):
    tokens, width = q_ref.shape
    index, base, offset = head_window(head, width)
    cols = pl.ds(base, WINDOW)
    vals = pl.ds(pl.multiple_of(width + base, 128), WINDOW)
    factor = head ** (-0.5) * math.log2(math.e)

    @pl.when(index == 0)
    def _():
        acc_ref[...] = jnp.zeros_like(acc_ref)
        lse_ref[...] = jnp.zeros_like(lse_ref)

    step = 256
    mask = window_mask((step, WINDOW), offset, head)
    lane = lax.broadcasted_iota(jnp.int32, (step, lse_ref.shape[1]), 1)
    for first in range(0, tokens, step):
        rows = slice(first, first + step)
        query = jnp.where(mask, q_ref[rows, cols], jnp.zeros((), low))
        left = matmul_t(query, kvl_ref[:, cols])
        right = matmul_t(query, kvr_ref[:, cols])
        top = jnp.maximum(jnp.max(left, axis=1, keepdims=True), jnp.max(right, axis=1, keepdims=True)) * factor
        left = jnp.exp2(left * factor - top)
        right = jnp.exp2(right * factor - top)
        total = jnp.sum(left, axis=1, keepdims=True) + jnp.sum(right, axis=1, keepdims=True)
        out = matmul(left.astype(low), kvl_ref[:, vals]) + matmul(right.astype(low), kvr_ref[:, vals])
        acc_ref[rows, cols] += jnp.where(mask, out * (1.0 / total), 0.0)
        lse_ref[rows, :] += jnp.where(lane == index, top + jnp.log2(total), 0.0)

    @pl.when(index == pl.num_programs(0) - 1)
    def _():
        o_ref[...] = acc_ref[...].astype(low)


def attend(query, kv_l, kv_r, head):
    tokens, width = query.shape
    heads = width // head
    return pl.pallas_call(
        functools.partial(attend_body, head),
        grid=(heads,),
        in_specs=[whole((tokens, width))] + [whole((tokens, 2 * width))] * 2,
        out_specs=[whole((tokens, width)), whole((tokens, 128))],
        out_shape=[jax.ShapeDtypeStruct((tokens, width), low), jax.ShapeDtypeStruct((tokens, 128), full)],
        scratch_shapes=[pltpu.VMEM((tokens, width), full)],
        compiler_params=params(56),
        cost_estimate=pl.CostEstimate(
            flops=8 * tokens * tokens * WINDOW * heads, bytes_accessed=14 * tokens * width, transcendentals=2 * tokens * tokens * heads
        ),
        name="attend",
    )(query, kv_l, kv_r)


def attend_back_body(head, q_ref, kvl_ref, kvr_ref, do_ref, lse_ref, dq_ref, dl_ref, dr_ref, dr_acc):
    tokens, width = q_ref.shape
    index, base, offset = head_window(head, width)
    cols = pl.ds(base, WINDOW)
    vals = pl.ds(pl.multiple_of(width + base, 128), WINDOW)
    temper = head ** (-0.5)
    factor = temper * math.log2(math.e)

    @pl.when(index == 0)
    def _():
        for ref in (dq_ref, dl_ref, dr_acc):
            ref[...] = jnp.zeros_like(ref)

    step = 256
    mask = window_mask((step, WINDOW), offset, head)
    for first in range(0, tokens, step):
        rows = slice(first, first + step)
        query = jnp.where(mask, q_ref[rows, cols], jnp.zeros((), low))
        grad = jnp.where(mask, do_ref[rows, cols], jnp.zeros((), low))
        level = lse_ref[pl.ds(index, 1), rows]
        probs = []
        grads = []
        for ref in (kvl_ref, kvr_ref):
            scores = matmul_t(ref[:, cols], query)
            prob = jnp.exp2(scores * factor - level)
            probs.append(prob)
            grads.append(prob * matmul_t(ref[:, vals], grad))
        delta = jnp.sum(grads[0], axis=0, keepdims=True) + jnp.sum(grads[1], axis=0, keepdims=True)
        grad_q = 0.0
        for part, (ref, acc) in enumerate(((kvl_ref, dl_ref), (kvr_ref, dr_acc))):
            acc[:, vals] += matmul(probs[part].astype(low), grad)
            grad_s = (grads[part] - probs[part] * delta).astype(low)
            acc[:, cols] += matmul(grad_s, query)
            grad_q = grad_q + outer_sum(grad_s, ref[:, cols])
        dq_ref[rows, cols] += jnp.where(mask, grad_q * temper, 0.0)

    @pl.when(index == pl.num_programs(0) - 1)
    def _():
        dl_ref[:, :width] = dl_ref[:, :width] * temper
        dr_ref[:, :width] = (dr_acc[:, :width] * temper).astype(low)
        dr_ref[:, width:] = dr_acc[:, width:].astype(low)


def attend_back(query, kv_l, kv_r, grad, levels, head):
    tokens, width = query.shape
    heads = width // head
    both = (tokens, 2 * width)
    one = (tokens, width)
    return pl.pallas_call(
        functools.partial(attend_back_body, head),
        grid=(heads,),
        in_specs=[whole(one), whole(both), whole(both), whole(one), whole(levels.shape)],
        out_specs=[whole(one), whole(both), whole(both)],
        out_shape=[like(one, full), like(both, full), like(both, low)],
        scratch_shapes=[pltpu.VMEM(both, full)],
        compiler_params=params(60),
        cost_estimate=pl.CostEstimate(
            flops=20 * tokens * tokens * WINDOW * heads, bytes_accessed=28 * tokens * width, transcendentals=2 * tokens * tokens * heads
        ),
        name="attend_back",
    )(query, kv_l, kv_r, grad, levels)


class Weight:
    def __init__(self, segments):
        self.segments = segments
        self.columns = sum(columns for _, _, columns in segments)
        self.plan = [piece[1:] for piece in segments[0][1]]
        self.height = sum(rows for _, _, rows in self.plan)
        for _, pieces, _ in segments:
            assert [piece[3] for piece in pieces] == [rows for _, _, rows in self.plan]


def piece_source(ref, lead, first, count):
    for index in lead:
        ref = ref.at[index]
    return ref.at[:, pl.ds(first, count)]


class Cols:
    def __init__(self, array, first, count):
        self.array = array
        self.first = first
        self.shape = (array.shape[0], count)
        self.dtype = array.dtype
        self.size = array.shape[0] * count

    def value(self):
        return self.array[:, self.first : self.first + self.shape[1]]


def plain(value):
    return value.value() if isinstance(value, Cols) else value


def anywhere(count):
    return [pl.BlockSpec(memory_space=pl.ANY)] * count


class Stream:
    def __init__(self, weights, tile, late):
        self.weights = weights
        self.tile = tile
        self.late = late
        self.steps = weights[0].columns // tile

    def pieces_of(self):
        return [pieces for w in self.weights for _, pieces, _ in w.segments]

    def specs(self):
        return [pl.BlockSpec(memory_space=pltpu.SMEM)] + anywhere(sum(len(p) for p in self.pieces_of()) + len(self.late))

    def operands(self):
        offsets = jnp.concatenate([offs for w in self.weights for offs, _, _ in w.segments])
        arrays = [piece[0] for pieces in self.pieces_of() for piece in pieces]
        return [offsets] + arrays + [v.array if isinstance(v, Cols) else v for v in self.late]

    def scratch(self):
        shapes = []
        for w in self.weights:
            shapes += [pltpu.VMEM((2, w.height, self.tile), low), pltpu.SemaphoreType.DMA((2, len(w.plan)))]
        for value in self.late:
            shapes += [pltpu.VMEM(value.shape, value.dtype), pltpu.SemaphoreType.DMA((1,))]
        return shapes

    def bind(self, operand_refs, scratch_refs):
        self.offs = operand_refs[0]
        refs = list(operand_refs[1:])
        self.refs = []
        for w in self.weights:
            mine = []
            for _, pieces, _ in w.segments:
                mine.append(refs[: len(pieces)])
                refs = refs[len(pieces) :]
            self.refs.append(mine)
        self.buffers = scratch_refs[0 : 2 * len(self.weights) : 2]
        self.sems = scratch_refs[1 : 2 * len(self.weights) : 2]
        rest = scratch_refs[2 * len(self.weights) :]
        self.late_bufs = rest[0::2]
        self.late_copies = []
        for value, ref, buf, sem in zip(self.late, refs, rest[0::2], rest[1::2]):
            if isinstance(value, Cols):
                ref = ref.at[:, pl.ds(value.first, value.shape[1])]
            self.late_copies.append(pltpu.make_async_copy(ref, buf, sem.at[0]))

    def segment_copies(self, index, number, column, slot):
        w = self.weights[index]
        base = sum(len(x.plan) * len(x.segments) for x in self.weights[:index]) + number * len(w.plan)
        out = []
        for at, (_, lead, first, rows) in enumerate(w.segments[number][1]):
            source = piece_source(self.refs[index][number][at], lead, pl.multiple_of(first + column, 128), self.tile)
            start = pl.multiple_of(self.offs[base + at], 16)
            target = self.buffers[index].at[slot, pl.ds(start, rows), :]
            out.append(pltpu.make_async_copy(source, target, self.sems[index].at[slot, at]))
        return out

    def copies(self, step, slot):
        return [copy for index in range(len(self.weights)) for copy in self.segment_copies(index, 0, step * self.tile, slot)]

    def start_tile(self, step, slot):
        for index, w in enumerate(self.weights):
            first = 0
            for number, (_, _, columns) in enumerate(w.segments):
                count = columns // self.tile

                def start():
                    for copy in self.segment_copies(index, number, (step - first) * self.tile, slot):
                        copy.start()

                if len(w.segments) == 1:
                    start()
                else:
                    pl.when(jnp.logical_and(step >= first, step < first + count))(start)
                first += count

    def wait_tile(self, slot):
        for index in range(len(self.weights)):
            for copy in self.segment_copies(index, 0, 0, slot):
                copy.wait()

    def advance(self):
        step = pl.program_id(0)
        slot = lax.rem(step, 2)

        @pl.when(step == 0)
        def _():
            self.start_tile(jnp.int32(0), 0)
            for copy in self.late_copies:
                copy.start()

        @pl.when(step + 1 < self.steps)
        def _():
            self.start_tile(step + 1, 1 - slot)

        self.wait_tile(slot)
        return step, [buf.at[slot] for buf in self.buffers]

    def wait_late(self):
        for copy in self.late_copies:
            copy.wait()
        return self.late_bufs


def stream_call(name, stream, body, ins, in_specs, outs, out_specs, scratch, flops, mib=58):
    operands = stream.operands()
    frame = stream.scratch()

    def kernel(*refs):
        count = len(operands)
        ops, refs = refs[:count], refs[count:]
        inputs, refs = refs[: len(ins)], refs[len(ins) :]
        outputs, refs = refs[: len(outs)], refs[len(outs) :]
        stream.bind(ops, refs[: len(frame)])
        body(stream, inputs, outputs, refs[len(frame) :])

    moved = sum(v.size * v.dtype.itemsize for v in list(ins) + list(stream.late) + list(outs))
    moved += sum(2 * w.height * w.columns for w in stream.weights)
    return pl.pallas_call(
        kernel,
        grid=(stream.steps,),
        in_specs=stream.specs() + in_specs,
        out_specs=out_specs,
        out_shape=outs,
        scratch_shapes=frame + scratch,
        compiler_params=params(mib),
        cost_estimate=pl.CostEstimate(flops=flops, bytes_accessed=moved, transcendentals=0),
        name=name,
    )(*operands, *ins)


def by_rows(tokens, fun, step=128):
    @pl.loop(0, tokens // step)
    def _(i):
        fun(pl.ds(pl.multiple_of(i * step, step), step))


def take(ref, rows):
    return ref[rows, :] if ref.shape[0] > 1 else ref[...]


def give(ref, rows, value):
    if ref.shape[0] > 1:
        ref[rows, :] = value.astype(ref.dtype)
    else:
        ref[...] += jnp.sum(value, axis=0, keepdims=True)


def like(shape, dtype):
    return jax.ShapeDtypeStruct(shape, dtype)


def ada_matmul(value, weight, bias):
    tokens = value.shape[0]
    tile = weight.height
    stream = Stream([weight], tile, [])

    def body(stream, ins, outs, scratch):
        _, (w,) = stream.advance()
        outs[0][...] = matmul(ins[0][...], w[...]) + ins[1][...]

    return stream_call(
        "ada",
        stream,
        body,
        [value, bias],
        [whole(value.shape), pl.BlockSpec((1, tile), lambda j: (0, j))],
        [like((tokens, weight.columns), full)],
        [pl.BlockSpec((tokens, tile), lambda j: (0, j))],
        [],
        2 * tokens * weight.height * weight.columns,
    )[0]


def mod_partial(row, weight, width):
    shard = weight.shape[1]
    tall = jnp.broadcast_to(row, (16, shard))

    def body(x_ref, w_ref, out_ref):
        out_ref[0] = matmul(x_ref[...], w_ref[...])[:8]

    out = pl.pallas_call(
        body,
        grid=(6,),
        in_specs=[whole(tall.shape), pl.BlockSpec((None, shard, width), lambda j: (0, 0, j))],
        out_specs=pl.BlockSpec((1, 8, width), lambda j: (j, 0, 0)),
        out_shape=like((6, 8, width), full),
        compiler_params=params(16),
        cost_estimate=pl.CostEstimate(flops=0, bytes_accessed=12 * shard * width, transcendentals=0),
        name="modpart",
    )(tall, weight)
    return out[:, 0]


def qkv_matmul(value, weight, cosine, sine, gains, member, member_t, head):
    tokens, width = value.shape
    stream = Stream([weight], width, [cosine, sine])

    def body(stream, ins, outs, scratch):
        x_ref, gain_ref, mem_ref, memt_ref = ins
        q_ref, kv_ref, raw_ref = outs
        (acc_ref,) = scratch
        step, (w,) = stream.advance()
        cos_ref, sin_ref = stream.late_bufs
        acc_ref[...] = matmul(x_ref[...], w[...])

        @pl.when(step == 0)
        def _():
            stream.wait_late()

        def head_norm(part, out, cols):
            def rows_of(rows):
                raw = acc_ref[rows, :]
                raw_ref[rows, :] = raw
                mean = split_dot(raw * raw, mem_ref[...]) * (1.0 / head)
                inverse = split_dot(lax.rsqrt(mean + epsilon), memt_ref[...])
                normed = raw * inverse * gain_ref[part : part + 1, :]
                even = even_lanes(raw.shape, head)
                out[rows, cols] = turned(normed, cos_ref[rows, :], sin_ref[rows, :], even, head // 4).astype(low)

            by_rows(tokens, rows_of)

        @pl.when(step == 0)
        def _():
            head_norm(0, q_ref, slice(0, width))

        @pl.when(step == 1)
        def _():
            head_norm(1, kv_ref, slice(0, width))

        @pl.when(step == 2)
        def _():
            kv_ref[:, width:] = acc_ref[...].astype(low)

    flat = like((tokens, width), low)
    return stream_call(
        "qkv",
        stream,
        body,
        [value, gains, member, member_t],
        [whole(v.shape) for v in (value, gains, member, member_t)],
        [flat, like((tokens, 2 * width), low), like((tokens, 2 * width), full)],
        [whole((tokens, width)), whole((tokens, 2 * width)), pl.BlockSpec((tokens, width), lambda j: (0, jnp.minimum(j, 1)))],
        [pltpu.VMEM((tokens, width), full)],
        2 * tokens * weight.height * weight.columns,
    )


def out_matmul(value, weight, hidden0, mods):
    tokens, width = value.shape
    stream = Stream([weight], 384, [hidden0] + mods)

    def body(stream, ins, outs, scratch):
        att_ref, h1_ref, b_ref = outs
        (acc_ref,) = scratch
        step, (w,) = stream.advance()
        acc_ref[step] = matmul(ins[0][...], w[...])

        @pl.when(step == stream.steps - 1)
        def _():
            h0_ref, gate_ref, shift_ref, scale_ref = stream.wait_late()

            def rows_of(rows):
                att = jnp.concatenate([acc_ref[k, rows, :] for k in range(stream.steps)], axis=1)
                hidden1 = h0_ref[rows, :] + take(gate_ref, rows) * att
                normed = hidden1 * rms_scale(hidden1)
                att_ref[rows, :] = att.astype(low)
                h1_ref[rows, :] = hidden1
                b_ref[rows, :] = (normed * (1.0 + take(scale_ref, rows)) + take(shift_ref, rows)).astype(low)

            by_rows(tokens, rows_of)

    return stream_call(
        "attout",
        stream,
        body,
        [value],
        [whole(value.shape)],
        [like((tokens, width), low), like((tokens, width), full), like((tokens, width), low)],
        [whole((tokens, width))] * 3,
        [pltpu.VMEM((stream.steps, tokens, 384), full)],
        2 * tokens * weight.height * weight.columns,
    )


def gate_up_matmul(value, gate, up):
    tokens, width = value.shape
    tile = 512
    stream = Stream([gate, up], tile, [])

    def body(stream, ins, outs, scratch):
        hid_ref, g_ref, u_ref = outs
        _, (wg, wu) = stream.advance()
        g = matmul(ins[0][...], wg[...])
        u = matmul(ins[0][...], wu[...])
        g_ref[...] = g.astype(low)
        u_ref[...] = u.astype(low)
        hid_ref[...] = (g * jax.nn.sigmoid(g) * u).astype(low)

    flat = like((tokens, gate.columns), low)
    return stream_call(
        "gateup",
        stream,
        body,
        [value],
        [whole(value.shape)],
        [flat] * 3,
        [pl.BlockSpec((tokens, tile), lambda j: (0, j))] * 3,
        [],
        4 * tokens * gate.height * gate.columns,
    )


def down_matmul(value, weight, hidden1, gate):
    tokens, depth = value.shape
    width = weight.columns
    stream = Stream([weight], width, [hidden1, gate])

    def body(stream, ins, outs, scratch):
        mlp_ref, h2_ref = outs
        (acc_ref,) = scratch
        hid_ref = ins[0]
        at = 0
        copies = stream.copies(0, 0)
        for copy in copies + stream.late_copies:
            copy.start()
        for k, (_, _, rows) in enumerate(weight.plan):
            copies[k].wait()
            first = stream.offs[k]
            left = hid_ref[:, pl.ds(pl.multiple_of(first, 128), rows)]
            part = matmul(left, stream.buffers[0][0, pl.ds(pl.multiple_of(first, 128), rows), :])
            if k == 0:
                acc_ref[...] = part
            else:
                acc_ref[...] += part
        h1_ref, gate_ref = stream.wait_late()

        def rows_of(rows):
            mlp = acc_ref[rows, :]
            mlp_ref[rows, :] = mlp.astype(low)
            h2_ref[rows, :] = h1_ref[rows, :] + take(gate_ref, rows) * mlp

        by_rows(tokens, rows_of)

    return stream_call(
        "down",
        stream,
        body,
        [value],
        [whole(value.shape)],
        [like((tokens, width), low), like((tokens, width), full)],
        [whole((tokens, width))] * 2,
        [pltpu.VMEM((tokens, width), full)],
        2 * tokens * depth * width,
    )


def down_back(grad, weight, gate_pre, up_pre):
    tokens, width = grad.shape
    depth = weight.height
    stream = Stream([weight], width, [gate_pre, up_pre])

    def body(stream, ins, outs, scratch):
        dg_ref, du_ref = outs
        copies = stream.copies(0, 0)
        for copy in copies + stream.late_copies:
            copy.start()
        for k, (_, _, count) in enumerate(weight.plan):
            copies[k].wait()
            if k == 0:
                g_ref, u_ref = stream.wait_late()
            first = pl.multiple_of(stream.offs[k], 128)
            for at in range(0, count, 384):
                cols = pl.ds(pl.multiple_of(first + at, 128), 384)

                def rows_of(rows):
                    inner = matmul_t(ins[0][rows, :], stream.buffers[0][0, cols, :])
                    g = g_ref[rows, cols].astype(full)
                    u = u_ref[rows, cols].astype(full)
                    sigma = jax.nn.sigmoid(g)
                    active = g * sigma
                    dg_ref[rows, cols] = (inner * u * (sigma + active * (1.0 - sigma))).astype(low)
                    du_ref[rows, cols] = (inner * active).astype(low)

                by_rows(tokens, rows_of, 256)

    flat = like((tokens, depth), low)
    return stream_call(
        "downback",
        stream,
        body,
        [grad],
        [whole(grad.shape)],
        [flat, flat],
        [whole((tokens, depth))] * 2,
        [],
        2 * tokens * depth * width,
    )


def back_matmul(name, grads, weights, tile, late, outs, finish):
    tokens = grads[0].shape[0]
    width = weights[0].height
    stream = Stream(weights, tile, late)

    def body(stream, ins, outs, scratch):
        (acc_ref,) = scratch
        step, tiles = stream.advance()
        part = matmul_t(ins[0][...], tiles[0][...])
        for value, w in zip(ins[1:], tiles[1:]):
            part = part + matmul_t(value[...], w[...])

        @pl.when(step == 0)
        def _():
            acc_ref[...] = part

        @pl.when(step > 0)
        def _():
            acc_ref[...] += part

        @pl.when(step == stream.steps - 1)
        def _():
            refs = stream.wait_late()
            for ref in outs:
                if ref.shape[0] == 1:
                    ref[...] = jnp.zeros_like(ref)
            by_rows(tokens, lambda rows: finish(rows, acc_ref[rows, :], refs, outs))

    return stream_call(
        name,
        stream,
        body,
        list(grads),
        [pl.BlockSpec((tokens, tile), lambda j: (0, j))] * len(grads),
        outs,
        [whole(value.shape) for value in outs],
        [pltpu.VMEM((tokens, width), full)],
        2 * tokens * width * weights[0].columns * len(weights),
    )


def mlp_back(grads, weights, grad2, hidden1, att, mods):
    tokens, width = grad2.shape
    lead = mods[0].shape[0]

    def finish(rows, db, refs, outs):
        dh2_ref, h1_ref, att_ref, scale_ref, gate_ref = refs
        hidden1 = h1_ref[rows, :]
        inverse = rms_scale(hidden1)
        normed = hidden1 * inverse
        weighted = db * (1.0 + take(scale_ref, rows))
        back = inverse * (weighted - normed * jnp.mean(normed * weighted, axis=-1, keepdims=True))
        grad1 = dh2_ref[rows, :] + back
        outs[0][rows, :] = grad1
        outs[1][rows, :] = (grad1 * take(gate_ref, rows)).astype(low)
        give(outs[2], rows, db)
        give(outs[3], rows, db * normed)
        give(outs[4], rows, grad1 * att_ref[rows, :].astype(full))

    outs = [like((tokens, width), full), like((tokens, width), low)]
    outs += [like((lead, width), low if lead > 1 else full)] * 3
    return back_matmul("mlpback", grads, weights, 512, [grad2, hidden1, att] + mods, outs, finish)


def qkv_back(grad, weight, grad1, hidden0, scale):
    tokens, width = grad1.shape
    lead = scale.shape[0]

    def finish(rows, da, refs, outs):
        dh1_ref, h0_ref, scale_ref = refs
        hidden0 = h0_ref[rows, :]
        inverse = rms_scale(hidden0)
        normed = hidden0 * inverse
        weighted = da * (1.0 + take(scale_ref, rows))
        back = inverse * (weighted - normed * jnp.mean(normed * weighted, axis=-1, keepdims=True))
        outs[0][rows, :] = (dh1_ref[rows, :] + back).astype(low)
        give(outs[1], rows, da)
        give(outs[2], rows, da * normed)

    outs = [like((tokens, width), low)] + [like((lead, width), low if lead > 1 else full)] * 2
    return back_matmul("qkvback", [grad], [weight], width, [grad1, hidden0, scale], outs, finish)


def out_back(grad, weight):
    def finish(rows, value, refs, outs):
        outs[0][rows, :] = value.astype(low)

    return back_matmul("outback", [grad], [weight], 384, [], [like(grad.shape, low)], finish)[0]


def ada_back(grads, weight, cond):
    tokens, width = cond.shape
    tile = weight.height
    stream = Stream([weight], tile, [cond])

    def body(stream, ins, outs, scratch):
        (acc_ref,) = scratch
        step, (w,) = stream.advance()
        for k, grad in enumerate(ins):

            @pl.when(step == k)
            def _():
                part = matmul_t(grad[...], w[...])
                acc_ref[...] = part if k == 0 else acc_ref[...] + part

        @pl.when(step == stream.steps - 1)
        def _():
            (cond_ref,) = stream.wait_late()

            def rows_of(rows):
                cond = cond_ref[rows, :]
                sigma = jax.nn.sigmoid(cond)
                outs[0][rows, :] = acc_ref[rows, :] * sigma * (1.0 + cond * (1.0 - sigma))

            by_rows(tokens, rows_of)

    return stream_call(
        "adaback",
        stream,
        body,
        list(grads),
        [whole(grad.shape) for grad in grads],
        [like((tokens, width), full)],
        [whole((tokens, width))],
        [pltpu.VMEM((tokens, width), full)],
        2 * tokens * width * weight.columns,
    )[0]


def ordered_grad(left, order, rights, tile):
    tokens, width = left.shape
    many = len(rights) > 1
    columns = sum(right.shape[1] for right in rights)
    steps = columns // tile

    def body(order_ref, left_ref, *refs):
        ys, out_ref, turned_ref = refs[: len(rights)], refs[-2], refs[-1]
        step = pl.program_id(0)

        @pl.when(step == 0)
        def _():
            turned_ref[...] = matmul_t(order_ref[...], left_ref[...]).astype(low)

        if not many:
            out_ref[...] = matmul(turned_ref[...], ys[0][...]).astype(low)
            return
        for k, y in enumerate(ys):

            @pl.when(step == k)
            def _():
                out_ref[...] = matmul(turned_ref[...], y[...]).astype(low)

    tiles = [whole(right.shape) for right in rights] if many else [pl.BlockSpec((tokens, tile), lambda j: (0, j))]
    return pl.pallas_call(
        body,
        grid=(steps,),
        in_specs=[whole(order.shape), whole(left.shape)] + tiles,
        out_specs=pl.BlockSpec((width, tile), lambda j: (0, j)),
        out_shape=like((width, columns), low),
        scratch_shapes=[pltpu.VMEM((width, tokens), low)],
        compiler_params=params(56),
        cost_estimate=pl.CostEstimate(
            flops=2 * tokens * width * (columns + width), bytes_accessed=2 * width * (columns + 2 * width), transcendentals=0
        ),
        name="wgrad",
    )(order, left, *rights)


def down_grad(left, right, groups):
    tokens, depth = left.shape
    columns = right.shape[1]
    tile = depth // groups

    def body(left_ref, right_ref, out_ref):
        value = outer_sum(left_ref[...], right_ref[...]).astype(low)
        out_ref[0, 0] = value[: tile // 2]
        out_ref[1, 0] = value[tile // 2 :]

    return pl.pallas_call(
        body,
        grid=(groups,),
        in_specs=[pl.BlockSpec((tokens, tile), lambda j: (0, j)), whole(right.shape)],
        out_specs=pl.BlockSpec((2, 1, tile // 2, columns), lambda j: (0, j, 0, 0)),
        out_shape=like((2, groups, tile // 2, columns), low),
        compiler_params=params(40),
        cost_estimate=pl.CostEstimate(
            flops=2 * tokens * depth * columns, bytes_accessed=2 * depth * (columns + tokens), transcendentals=0
        ),
        name="wdown",
    )(left, right)


def tie(value, *others):
    others = [v for v in others if v is not None]
    if not others:
        return value
    return lax.optimization_barrier((value, *others))[0]


class Flight:
    def __init__(self, token):
        self.token = token
        self.held = []
        self.todo = []

    def send(self, value, item, holder, name):
        setattr(holder, name, swap(tie(value, self.token), item))
        self.held.append((holder, name))

    def watch(self, holder, name):
        self.held.append((holder, name))

    def then(self, action):
        self.todo.append(action)

    def fence(self, values, starts=()):
        values = list(values)
        held, todo = self.held, self.todo
        self.held, self.todo = [], []
        arrays = values + [getattr(holder, name) for holder, name in held]
        arrays = lax.optimization_barrier(tuple(arrays))
        self.token = arrays[0]
        for (holder, name), value in zip(held, arrays[len(values) :]):
            setattr(holder, name, value)
        for action in todo:
            action()
        for start in starts:
            start(self)
        return arrays[: len(values)]


class Bundle:
    def __init__(self, place, own, shards, parts, which, relay_bit):
        self.row, self.col, coords = place
        self.own = own
        self.shards = shards
        self.parts = parts
        self.which = which
        self.relay_bit = relay_bit
        self.rows = shards[parts[0][0]].shape[1]
        self.half = self.rows // 2
        self.at = coords[relay_bit] * self.half

    def over_col(self, flight):
        mine = [
            lax.dynamic_slice(self.shards[name], (self.which, self.at, first), (1, self.half, n))[0]
            for name, first, n in self.parts
        ]
        flight.send(jnp.concatenate(mine, axis=1), "col", self, "first")

    def relay(self, flight):
        flight.send(self.first, self.relay_bit, self, "second")

    def first_row(self, flight):
        flight.send(self.first, "row", self, "first_s")

    def second_row(self, flight):
        flight.send(self.second, "row", self, "second_s")

    def rows_both(self, flight):
        self.first_row(flight)
        self.second_row(flight)

    def segment(self, wanted):
        row, col, rows, half, at = self.row, self.col, self.rows, self.half, self.at
        other = (2 * row + 1 - col) * rows
        other_s = (2 * (1 - row) + 1 - col) * rows
        offsets = [col * rows, (col + 2) * rows, other + at, other_s + at]
        offsets += [other + (half - at), other_s + (half - at)]
        offsets = jnp.stack(offsets).astype(jnp.int32)
        begin = 0
        for name, first, n in self.parts:
            if name == wanted:
                own_all = self.own[name]
                lead = () if own_all.ndim == 3 else (self.which,)
                pieces = [(own_all, (0,) + lead, first, rows), (own_all, (1,) + lead, first, rows)]
                got = [self.first, self.first_s, self.second, self.second_s]
                pieces += [(value, (), begin, half) for value in got]
                return (offsets, pieces, n)
            begin += n
        raise KeyError(wanted)


def weight_of(name, *bundles):
    return Weight([bundle.segment(name) for bundle in bundles])


def item_weight(item):
    return {"row": 2, "col": 1}.get(item) or 4 << item


def halving_order(path, width, block, me):
    at = jnp.arange(width)
    position = at // block
    owner = me
    for k, item in enumerate(path):
        bit = (position >> (len(path) - 1 - k)) & 1
        if item == "row":
            owner = (owner & ~2) | (2 * bit)
        else:
            owner = owner ^ (bit * item_weight(item))
    return owner * block + at % block


class Share:
    def __init__(self, value, order, path):
        self.value = value
        self.order = list(order)
        self.path = list(path)

    def parts(self, item):
        rows, columns = self.value.shape
        if self.order[0] == item:
            self.order = self.order[1:]
            return self.value[: rows // 2], self.value[rows // 2 :]
        self.order.remove(item)
        value = self.value.reshape(2, 2, rows // 4, columns)
        return value[:, 0].reshape(rows // 2, columns), value[:, 1].reshape(rows // 2, columns)


    def joined(self, kept, got):
        return (kept.astype(full) + got.astype(full)).astype(kept.dtype)


class BlockShare(Share):
    def __init__(self, value, order, path, coords):
        super().__init__(value, order, path)
        self.coords = coords

    def parts(self, item):
        axis = self.order.index(item)
        self.order.remove(item)
        mine = self.coords[item]
        return (
            lax.dynamic_index_in_dim(self.value, mine, axis, keepdims=False),
            lax.dynamic_index_in_dim(self.value, 1 - mine, axis, keepdims=False),
        )


class Total:
    def __init__(self, value, path):
        self.value = value
        self.path = list(path)

    def parts(self, item):
        return self.value, self.value

    def joined(self, kept, got):
        return kept + got


class TotalAndRows(Total):
    def __init__(self, value, count, path):
        super().__init__(value, path)
        self.count = count

    def joined(self, kept, got):
        n = self.count
        return jnp.concatenate([kept[:n] + got[:n], kept[n:], got[n:]], axis=0)


class Parcel:
    got = None


class Agenda:
    def __init__(self):
        self.tasks = {}

    def go(self, *names):
        def action(flight):
            tasks = [self.tasks[name] for name in names]
            items = [task.path.pop(0) for task in tasks]
            assert len(set(items)) == 1
            pairs = [task.parts(items[0]) for task in tasks]
            parcel = Parcel()
            away = pairs[0][1] if len(pairs) == 1 else jnp.concatenate([pair[1] for pair in pairs], axis=-1)
            flight.send(away, items[0], parcel, "got")

            def arrive():
                at = 0
                for task, (kept, _) in zip(tasks, pairs):
                    if len(tasks) == 1:
                        task.value = task.joined(kept, parcel.got)
                    else:
                        n = kept.shape[-1]
                        task.value = task.joined(kept, parcel.got[..., at : at + n])
                        at += n

            flight.then(arrive)

        return action


def row_sum(value):
    return lax.psum_scatter(value, "row", scatter_dimension=0, tiled=True)


def row_sum_blocks(left, right, bits, block):
    if (4 * block) % 128 == 0:
        value = down_grad(left, right, 2**bits)
        value = lax.psum_scatter(value, "row", scatter_dimension=0, tiled=False)
    else:
        value = outer_sum(left, right).astype(low)
        value = value.reshape(2**bits, 2, 2 * block, value.shape[1])
        value = lax.psum_scatter(value, "row", scatter_dimension=1, tiled=False)
    return value.reshape((2,) * (bits + 1) + (block, value.shape[-1]))


def block_forward(hidden0, mods, mats, gains, tabs, flight, points):
    shift1, scale1, gate1, shift2, scale2, gate2 = mods
    cosine, sine, member, member_t, head = tabs
    used = {}

    def mat(name):
        used[name] = mats[name]()
        return used[name]

    def fence(point, *values):
        if point not in points:
            return values if len(values) > 1 else values[0]
        values = flight.fence(values, points[point])
        return values if len(values) > 1 else values[0]

    attn_in = (hidden0 * rms_scale(hidden0) * (1.0 + plain(scale1)) + plain(shift1)).astype(low)
    attn_in = fence("qkv", attn_in)
    query, kv, raw = qkv_matmul(attn_in, mat("qkv"), cosine, sine, gains, member, member_t, head)
    query, kv = fence("attend", query, kv)
    kv_r = swap(kv, "row")
    out_b, lse = attend(query, kv, kv_r, head)
    out_b = fence("out", out_b)
    att, hidden1, mlp_in = out_matmul(out_b, mat("out"), hidden0, [gate1, shift2, scale2])
    mlp_in = fence("gate", mlp_in)
    inner, gate_pre, up_pre = gate_up_matmul(mlp_in, mat("gate"), mat("up"))
    inner = fence("down", inner)
    mlp_out, hidden2 = down_matmul(inner, mat("down"), hidden1, gate2)
    cache = (hidden0, attn_in, raw, query, kv, kv_r, out_b, lse, att)
    cache += (hidden1, mlp_in, gate_pre, up_pre, inner, mlp_out)
    used = tuple(used[name] for name in ("qkv", "out", "gate", "up", "down"))
    return hidden2, cache, used


class Sum:
    value = None


def block_backward(grad2, cache, mods, mats, gains, tabs, comm, tag, plan):
    (hidden0, attn_in, raw, query, kv, kv_r, out_b, lse, att) = cache[:9]
    (hidden1, mlp_in, gate_pre, up_pre, inner, mlp_out) = cache[9:]
    shift1, scale1, gate1, shift2, scale2, gate2 = mods
    qkv_w, out_w, gate_w, up_w, down_w = mats
    cosine, sine, member, member_t, head = tabs
    flight, agenda, orders, paths, coords = comm
    n_data = lax.axis_size("dp")
    bits = (n_data - 1).bit_length()
    block = down_w.height // (4 * n_data)

    def fence(point, *values):
        values = flight.fence(values, plan.get(point, ()))
        return values if len(values) > 1 else values[0]

    def summed(left, name, right, tile):
        return row_sum(ordered_grad(left, orders[name], [right], tile))

    def watch(name, task):
        agenda.tasks[name + tag] = task
        flight.watch(task, "value")

    def begin(name, value):
        path = paths[name][1:]
        watch(name, Share(value, path, path))

    def begin_halves(name, value, cut):
        path = paths[name][1:]
        other = [path[1], path[0]] + path[2:]
        watch(name + "a", Share(value[:, :cut], path, path))
        watch(name + "b", Share(value[:, cut:], path, other))

    def begin_down(value):
        order = list(reversed(range(bits))) + ["col"]
        if tag == "0":
            watch("down", BlockShare(value, order, paths["down"][1:], coords))
            return
        path = paths["qkv"][1:]
        other = [path[1], path[0]] + path[2:]
        cut = value.shape[-1] // 256 * 128
        watch("downa", BlockShare(value[..., :cut], order, path, coords))
        watch("downb", BlockShare(value[..., cut:], order, other, coords))

    grad2 = fence("start", grad2)
    grad_mlp = (grad2 * plain(gate2)).astype(low)
    dgate2 = grad2 * mlp_out.astype(full)
    if gate2.shape[0] == 1:
        dgate2 = jnp.sum(dgate2, axis=0, keepdims=True)
    r_down = row_sum_blocks(inner, grad_mlp, bits, block)
    grad_gate, grad_up = down_back(grad_mlp, down_w, gate_pre, up_pre)
    begin_down(r_down)
    grad_gate, grad_up = fence("gate", grad_gate, grad_up)
    r_gate = summed(mlp_in, "gate", grad_gate, 512)
    r_up = summed(mlp_in, "up", grad_up, 512)
    grad1, grad_att, dshift2, dscale2, dgate1 = mlp_back(
        [grad_gate, grad_up], [gate_w, up_w], grad2, hidden1, att, [scale2, gate1]
    )
    grad_att = fence("out", grad_att)
    r_out = summed(out_b, "out", grad_att, 384)
    grad_ob = out_back(grad_att, out_w)
    begin("gate", r_gate)
    begin("up", r_up)
    grad_ob = fence("attend", grad_ob)
    dq, dkv, dkv_r = attend_back(query, kv, kv_r, grad_ob, lse.T, head)
    begin("out", r_out)
    dq, dkv_r = fence("qk", dq, dkv_r)
    grad_qkv, gain_rows = qk_back(dq, dkv, swap(dkv_r, "row"), raw, cosine, sine, gains, member, member_t, head)
    grad_qkv = fence("qkv", grad_qkv)
    r_qkv = summed(attn_in, "qkv", grad_qkv, 384)
    grad0, dshift1, dscale1 = qkv_back(grad_qkv, qkv_w, grad1, hidden0, scale1)
    dmods = [dshift1, dscale1, dgate1, dshift2, dscale2, dgate2]
    begin_halves("qkv", r_qkv, r_qkv.shape[1] // 256 * 128)
    return grad0, dmods, gain_rows[:2], begin_halves


def per_device(
    latents,
    levels,
    timesteps,
    patch_weight,
    patch_bias,
    ada_weight,
    ada_bias,
    qkv_weight,
    qk_gains,
    out_weight,
    gate_weight,
    up_weight,
    down_weight,
    cotangent,
):
    images, slots, chans, rows_loc, cols_loc = latents.shape
    n_data = lax.axis_size("dp")
    assert images == 1 and slots == 2
    assert lax.axis_size("row") == 2 and lax.axis_size("col") == 2
    row = lax.axis_index("row")
    col = lax.axis_index("col")
    data = lax.axis_index("dp")
    bits = (n_data - 1).bit_length()
    left = col == 0
    coords = {"row": row, "col": col}
    place = (row, col, coords)
    for k in range(bits):
        coords[k] = (data >> k) & 1
    grid_rows = rows_loc // 2
    grid_cols = cols_loc
    half_cols = grid_cols // 2
    tokens = grid_rows * grid_cols
    width = cotangent.shape[-1]
    head = qk_gains.shape[2]
    heads = width // head
    pvals = chans * 4
    shard = width // 4
    me = data * 4 + row * 2 + col
    own_rows = width // (4 * n_data)

    def pair(own, other, axis):
        return jnp.concatenate([jnp.where(left, own, other), jnp.where(left, other, own)], axis=axis)

    own = {}
    for name, s in (
        ("qkv", qkv_weight),
        ("out", out_weight),
        ("gate", gate_weight),
        ("up", up_weight),
        ("down", down_weight),
        ("ada", ada_weight[1]),
    ):
        own[name] = lax.all_gather(s, "row", axis=0)
    shards = {"qkv": qkv_weight, "out": out_weight, "gate": gate_weight, "up": up_weight, "down": down_weight}
    shards["ada"] = ada_weight

    def bundle(which, relay_bit, *parts):
        return Bundle(place, own, shards, parts, which, relay_bit)

    ff = gate_weight.shape[2]
    b_q0 = bundle(0, 0, ("qkv", 0, width))
    b_kv0 = bundle(0, 1, ("qkv", width, 2 * width))
    b_og0 = bundle(0, 0, ("out", 0, width), ("gate", 0, ff))
    b_up0 = bundle(0, 1, ("up", 0, ff))
    b_down0 = bundle(0, 0, ("down", 0, width))
    b_ada_a = bundle(1, 1, ("ada", 0, 3 * width))
    b_ada_b = bundle(1, 0, ("ada", 3 * width, 3 * width))
    b_qkv1 = bundle(1, 1, ("qkv", 0, 3 * width))
    b_og1 = bundle(1, 0, ("out", 0, width), ("gate", 0, ff))
    b_up1 = bundle(1, 1, ("up", 0, ff))
    b_down1 = bundle(1, 0, ("down", 0, width))
    enc_mats = {
        "qkv": lambda: weight_of("qkv", b_q0, b_kv0),
        "out": lambda: weight_of("out", b_og0),
        "gate": lambda: weight_of("gate", b_og0),
        "up": lambda: weight_of("up", b_up0),
        "down": lambda: weight_of("down", b_down0),
    }
    dec_mats = {
        "qkv": lambda: weight_of("qkv", b_qkv1),
        "out": lambda: weight_of("out", b_og1),
        "gate": lambda: weight_of("gate", b_og1),
        "up": lambda: weight_of("up", b_up1),
        "down": lambda: weight_of("down", b_down1),
    }

    small = jnp.concatenate(
        [jnp.swapaxes(patch_weight, 1, 2).reshape(2 * pvals, shard), patch_bias, ada_bias.reshape(12, shard)], axis=0
    )
    small_other = swap(small, "col")
    blk = latents[0]
    blk_other = swap(blk, "col")
    flight = Flight(small)

    class Start:
        pass

    Start.small, Start.blk = small_other, blk_other
    flight.watch(Start, "small")
    flight.watch(Start, "blk")
    temb = time_features(timesteps[0], width)
    (temb,) = flight.fence([temb], [b_q0.over_col, b_kv0.over_col])
    small = pair(small[None], Start.small[None], 0)
    small_row = swap(small, "row")
    small = jnp.where(row == 0, jnp.stack([small, small_row]), jnp.stack([small_row, small]))
    small = small.reshape(4, 2 * pvals + 14, shard)
    patch_w = small[:, : 2 * pvals].transpose(1, 0, 2).reshape(2, pvals, width)
    patch_b = small[:, 2 * pvals : 2 * pvals + 2].transpose(1, 0, 2).reshape(2, width).astype(full)
    ada_b = small[:, 2 * pvals + 2 :].reshape(4, 2, 6 * shard).transpose(1, 0, 2).reshape(2, 6, width).astype(full)

    wide = pair(blk, Start.blk, 3)
    top_row = swap(wide[:, :, rows_loc - 1 :], "row")
    framed = jnp.concatenate([top_row, wide[:, :, : rows_loc - 1]], axis=2)
    framed = jnp.concatenate([framed[..., -1:], framed[..., :-1]], axis=3)
    patches = (
        framed.reshape(slots, chans, grid_rows, 2, grid_cols, 2).transpose(0, 2, 4, 1, 3, 5).reshape(slots, tokens, pvals)
    )
    enc_patches = patches[0]
    dec_patches = jnp.where(left, patches[0], patches[1])

    sil0 = jax.nn.silu(temb[:1]).astype(low)
    temb_own = jnp.where(left, temb[:1], temb[1:])
    part = mod_partial(lax.dynamic_slice(sil0, (0, (2 * row + col) * shard), (1, shard)), ada_weight, width)

    cot_own = jnp.where(left, cotangent[0, 0], cotangent[0, 1])

    class Cotangent:
        got = None

    def send_cotangent(flight):
        flight.send(jnp.where(left, cotangent[0, 1], cotangent[0, 0]), "col", Cotangent, "got")

    quarter = head // 4
    lanes = jnp.arange(width)
    within = lanes % head
    section = within // quarter
    lane_freq = jnp.exp(-math.log(10000.0) * (within % quarter).astype(full) / quarter)
    row_pos = (row * grid_rows + jnp.arange(grid_rows)).astype(full)
    col_pos = jnp.arange(grid_cols).astype(full)
    row_angle = row_pos[:, None] * lane_freq[None, :]
    col_angle = col_pos[:, None] * lane_freq[None, :]
    by_row = section < 2
    sign = jnp.where(section % 2 == 0, -1.0, 1.0).astype(full)

    def table(fun):
        return jnp.where(by_row, fun(row_angle)[:, None, :], fun(col_angle)[None, :, :]).reshape(tokens, width)

    cosine = table(jnp.cos)
    sine = table(jnp.sin) * sign
    member = (lanes[:, None] // head == jnp.arange(128)[None, :]).astype(low)
    tabs = (cosine, sine, member, member.T, head)
    gain_rows = jnp.tile(qk_gains.astype(full), (1, 1, heads))

    rest = list(range(2, bits))
    path_y = ["row", "col", 0, 1] + rest
    path_x = ["row", 0, "col", 1] + rest
    path_z = ["row", 1, "col", 0] + rest
    path_w = ["row", 1, 0, "col"] + rest
    paths = {"down": path_z, "gate": path_y, "up": path_x, "out": path_x, "qkv": path_y, "ada": path_y}
    perm = {}
    orders = {}
    for name in ("gate", "up", "out", "qkv", "ada"):
        key = tuple(paths[name])
        if key not in perm:
            source = halving_order(paths[name], width, own_rows, me)
            perm[key] = lax.optimization_barrier((source[:, None] == lanes[None, :]).astype(low))
        orders[name] = perm[key]

    enc_h0 = matmul(enc_patches, patch_w[0]) + patch_b[0]
    starts = [b_q0.relay, b_kv0.relay, b_og0.over_col, b_q0.first_row, b_kv0.first_row]
    enc_h0, part, cosine, sine = flight.fence([enc_h0, part, cosine, sine], starts)
    part = part + swap(part, "row")
    part = part + swap(part, "col")
    enc_mod = part + ada_b[0]
    enc_mods = [enc_mod[k : k + 1] for k in range(6)]
    tabs = (cosine, sine) + tabs[2:]
    points = {
        "qkv": [b_q0.second_row, b_kv0.second_row, b_up0.over_col, b_og0.relay],
        "attend": [b_down0.over_col, b_ada_a.over_col, b_up0.relay, b_og0.first_row],
        "out": [b_og0.second_row, b_up0.rows_both, b_ada_b.over_col, b_down0.relay, b_ada_a.relay],
        "down": [b_down0.rows_both, b_qkv1.over_col, b_ada_b.relay, b_ada_a.rows_both],
    }
    encoded, enc_cache, enc_mats = block_forward(enc_h0, enc_mods, enc_mats, gain_rows[0], tabs, flight, points)
    dec_h0 = matmul(dec_patches, patch_w[1]) + patch_b[1]
    cond = encoded + temb_own
    dec_sil = jax.nn.silu(cond).astype(low)
    (dec_sil,) = flight.fence([dec_sil], [b_ada_b.rows_both, b_og1.over_col, b_qkv1.relay])
    dec_ada = weight_of("ada", b_ada_a, b_ada_b)
    dec_mod = ada_matmul(dec_sil, dec_ada, ada_b[1].reshape(1, 6 * width))
    dec_mods = [Cols(dec_mod, k * width, width) for k in range(6)]
    points = {
        "qkv": [b_qkv1.rows_both, b_up1.over_col, b_og1.relay],
        "attend": [b_down1.over_col, b_up1.relay, b_og1.rows_both],
        "out": [b_up1.rows_both, b_down1.relay, send_cotangent],
        "down": [b_down1.rows_both],
    }
    decoded, dec_cache, dec_mats = block_forward(dec_h0, dec_mods, dec_mats, gain_rows[1], tabs, flight, points)
    live = (col < levels[0]).astype(full)
    result = (decoded * live).astype(low).reshape(grid_rows, grid_cols, width)
    near = jnp.where(left, result[:, :half_cols], result[:, half_cols:])
    far = jnp.where(left, result[:, half_cols:], result[:, :half_cols])

    class Away:
        got = None

    def send_result(flight):
        flight.send(far, "col", Away, "got")


    agenda = Agenda()
    go = agenda.go
    comm = (flight, agenda, orders, paths, coords)
    cot = pair(cot_own, Cotangent.got, 1).reshape(tokens, width)
    dec_grad2 = cot.astype(full) * live
    plan = {
        "start": [send_result],
        "gate": [go("downa1"), go("downb1")],
        "out": [go("downa1"), go("downb1")],
        "attend": [go("gate1"), go("up1")],
        "qk": [go("gate1"), go("up1"), go("downa1", "downb1")],
        "qkv": [go("out1"), go("downa1", "downb1"), go("gate1", "up1")],
    }
    dec_grad0, dec_dmods, dec_gains, begin_halves = block_backward(
        dec_grad2, dec_cache, dec_mods, dec_mats, gain_rows[1], tabs, comm, "1", plan
    )
    away = Away.got
    result = jnp.stack([jnp.where(left, near, away), jnp.where(left, away, near)])[None]
    dec_dmods = [piece.astype(low) for piece in dec_dmods]
    dec_dmods = flight.fence(dec_dmods, [go("qkva1"), go("qkvb1"), go("out1"), go("gate1", "up1")])
    r_ada = row_sum(ordered_grad(dec_sil, orders["ada"], dec_dmods, width))
    dec_bada = jnp.stack([jnp.sum(piece.astype(full), axis=0) for piece in dec_dmods])
    enc_grad2 = ada_back(dec_dmods, dec_ada, cond)

    def patch_rows(patch, grad):
        ones = jnp.ones((tokens, 1), low)
        return outer_sum(jnp.concatenate([patch, ones], axis=1), grad)

    total = jnp.concatenate([patch_rows(dec_patches, dec_grad0), dec_bada, dec_gains], axis=0)
    agenda.tasks["small"] = Total(total, ["row", "col"] + list(range(bits)))

    def begin_ada(flight):
        begin_halves("ada", r_ada, r_ada.shape[1] // 2)

    plan = {
        "start": [go("qkva1"), go("qkvb1"), go("small"), begin_ada],
        "gate": [go("adaa1"), go("adab1"), go("down0")],
        "out": [go("small"), go("adaa1"), go("adab1"), go("qkva1", "qkvb1", "out1")],
        "attend": [go("small"), go("gate0"), go("up0"), go("adaa1", "adab1")],
        "qk": [go("small"), go("gate0"), go("up0"), go("qkva1", "qkvb1", "out1")],
        "qkv": [go("small"), go("down0"), go("out0"), go("adaa1", "adab1")],
    }
    enc_grad0, enc_dmods, enc_gains, _ = block_backward(
        enc_grad2, enc_cache, enc_mods, enc_mats, gain_rows[0], tabs, comm, "0", plan
    )
    dmod_enc = jnp.concatenate(enc_dmods, axis=0)
    total = jnp.concatenate([patch_rows(enc_patches, enc_grad0), enc_gains, dmod_enc], axis=0)
    total, enc_grad0 = flight.fence([total, enc_grad0], [go("qkva0"), go("qkvb0"), go("out0"), go("gate0", "up0")])
    total = total + swap(total, "row")
    total = total + swap(total, "col")
    count = pvals + 3
    tiny = TotalAndRows(jnp.concatenate([total, sil0.astype(full)], axis=0), count, list(range(bits)))
    agenda.tasks["tiny"] = tiny
    flight.watch(tiny, "value")
    flight.fence([total], [go("tiny"), go("qkva0"), go("qkvb0"), go("down0"), go("gate0", "up0")])
    flight.fence([total], [go("tiny"), go("qkva0", "qkvb0", "out0"), go("down0")])
    flight.fence([total], [go("tiny"), go("qkva0", "qkvb0", "out0")])
    flight.fence([total])
    while any(task.path for task in agenda.tasks.values()):
        flight.fence([total], [go(name) for name, task in agenda.tasks.items() if task.path])
        flight.fence([total])
    dec_small = agenda.tasks["small"].value
    total = tiny.value[:count]
    dmod_all = tiny.value[count:]
    dmod_all = dmod_all.reshape(n_data, 7, width)
    enc_small = total
    enc_ada = jnp.dot(
        lax.dynamic_slice(dmod_all, (0, 6, me * own_rows), (n_data, 1, own_rows))[:, 0].T,
        dmod_all[:, :6].reshape(n_data, 6 * width),
        precision=highest,
        preferred_element_type=full,
    )
    enc_bada = jnp.sum(dmod_all[:, :6], axis=0)

    def image(dpatch):
        return (
            dpatch.reshape(grid_rows, grid_cols, chans, 2, 2).transpose(2, 0, 3, 1, 4).reshape(chans, rows_loc, 2 * cols_loc)
        )

    enc_image = image(matmul_t(enc_grad0, patch_w[0]))
    dec_image = image(matmul_t(dec_grad0, patch_w[1]))
    zero = jnp.zeros_like(dec_image)
    grads = jnp.stack([enc_image + jnp.where(left, dec_image, zero), jnp.where(left, zero, dec_image)])
    grads = jnp.concatenate([grads[..., 1:], grads[..., :1]], axis=3)
    below = swap(grads[:, :, :1], "row")
    grads = jnp.concatenate([grads[:, :, 1:], below], axis=2)
    one = grads[..., :cols_loc]
    two = grads[..., cols_loc:]
    latent_grad = (jnp.where(left, one, two) + swap(jnp.where(left, two, one), "col"))[None]

    def own_lanes(value):
        return lax.dynamic_slice(value, (0, me * own_rows), (value.shape[0], own_rows))

    enc_patch = own_lanes(enc_small[: pvals + 1])
    dec_patch = own_lanes(dec_small[: pvals + 1])
    g_patch = jnp.stack([enc_patch[:pvals].T, dec_patch[:pvals].T])
    g_patch_b = jnp.stack([enc_patch[pvals], dec_patch[pvals]])
    bada = jnp.stack([enc_bada.reshape(-1), dec_small[pvals + 1 : pvals + 7].reshape(-1)])
    own_bada = 6 * own_rows
    g_bada = lax.dynamic_slice(bada, (0, me * own_bada), (2, own_bada))
    gains = jnp.stack([enc_small[pvals + 1 :], dec_small[pvals + 7 :]])
    gains = gains.reshape(2, 2, heads, head).sum(axis=2)
    def both(name):
        parts = [agenda.tasks[name + tag].value.astype(full) for tag in "01"]
        return jnp.stack(parts)

    for task in agenda.tasks.values():
        assert not task.path
    g_ada = jnp.concatenate([agenda.tasks["adaa1"].value, agenda.tasks["adab1"].value], axis=1)
    g_ada_all = jnp.stack([enc_ada, g_ada.astype(full)])
    g_qkv = jnp.concatenate([both("qkva"), both("qkvb")], axis=2)
    down1 = jnp.concatenate([agenda.tasks["downa1"].value, agenda.tasks["downb1"].value], axis=1)
    g_down = jnp.stack([agenda.tasks["down0"].value.astype(full), down1.astype(full)])
    stacked = [g_qkv, both("out"), both("gate"), both("up"), g_down]
    return (
        result,
        latent_grad,
        g_patch,
        g_patch_b,
        g_ada_all,
        g_bada,
        stacked[0],
        gains,
        stacked[1],
        stacked[2],
        stacked[3],
        stacked[4],
    )


def solution(mesh):
    tile = ("row", "col")
    every = ("dp", "row", "col")
    return jax.shard_map(
        per_device,
        mesh=mesh,
        in_specs=(
            P("dp", None, None, "row", "col"),
            P("dp"),
            P("dp", None),
            P(None, tile, None),
            P(None, tile),
            P(None, tile, None),
            P(None, tile),
            P(None, tile, None),
            P(),
            P(None, tile, None),
            P(None, tile, None),
            P(None, tile, None),
            P(None, tile, None),
            P("dp", None, "row", "col", None),
        ),
        out_specs=(
            P("dp", None, "row", "col", None),
            P("dp", None, None, "row", "col"),
            P(None, every, None),
            P(None, every),
            P(None, every, None),
            P(None, every),
            P(None, every, None),
            P(),
            P(None, every, None),
            P(None, every, None),
            P(None, every, None),
            P(None, every, None),
        ),
        check_vma=False,
    )
```

```python
import functools
import math

import jax
import jax.numpy as jnp
from jax import lax
from jax.experimental import pallas as pl
from jax.experimental.pallas import tpu as pltpu
from jax.sharding import PartitionSpec as P

epsilon = 1e-06
highest = lax.Precision.HIGHEST
low = jnp.bfloat16
full = jnp.float32
WINDOW = 256
MIB = 1 << 20


def matmul(left, right):
    return jnp.dot(left, right, preferred_element_type=full)


def matmul_t(left, right):
    return lax.dot_general(left, right, (((1,), (1,)), ((), ())), preferred_element_type=full)


def outer_sum(left, right):
    return lax.dot_general(left, right, (((0,), (0,)), ((), ())), preferred_element_type=full)


def rms_scale(value):
    return lax.rsqrt(jnp.mean(value * value, axis=-1, keepdims=True) + epsilon)


def rms_back(value, inverse, grad):
    return inverse * grad - value * inverse**3 * jnp.mean(value * grad, axis=-1, keepdims=True)


def swap(value, item):
    if isinstance(item, str):
        return lax.ppermute(value, item, [(0, 1), (1, 0)])
    size = lax.axis_size("dp")
    return lax.ppermute(value, "dp", [(i, i ^ (1 << item)) for i in range(size)])


def time_features(steps, width):
    half = width // 2
    freqs = jnp.exp(-math.log(10000.0) * jnp.arange(half).astype(full) / half)
    angles = steps.astype(full)[:, None] * freqs[None, :]
    return jnp.concatenate([jnp.cos(angles), jnp.sin(angles)], axis=-1)


def whole(shape):
    return pl.BlockSpec(shape, lambda *_: (0,) * len(shape))


def params(mib):
    return pltpu.CompilerParams(vmem_limit_bytes=mib * MIB)


def split_dot(value, onehot):
    top = value.astype(low)
    rest = (value - top.astype(full)).astype(low)
    return matmul(top, onehot) + matmul(rest, onehot)


def turned(value, cosine, sine, even, quarter):
    width = value.shape[-1]
    ahead = pltpu.roll(value, width - quarter, axis=1)
    behind = pltpu.roll(value, quarter, axis=1)
    return value * cosine + jnp.where(even, ahead, behind) * sine


def even_lanes(gain_ref, shape):
    return jnp.broadcast_to(gain_ref[2:3, :] > 0.5, shape)


def qk_back_body(head, dq_ref, dkv_ref, dkvx_ref, qkv_ref, cos_ref, sin_ref, gain_ref, mem_ref, memt_ref, out_ref, gg_ref):
    width = dq_ref.shape[-1]

    @pl.when(pl.program_id(0) == 0)
    def _():
        gg_ref[...] = jnp.zeros_like(gg_ref)

    cosine = cos_ref[...]
    sine = -sin_ref[...]
    even = even_lanes(gain_ref, cosine.shape)
    member = mem_ref[...]
    member_t = memt_ref[...]
    grads = (dq_ref[...], dkv_ref[:, :width] + dkvx_ref[:, :width].astype(full))
    for part in (0, 1):
        value = qkv_ref[:, part * width : (part + 1) * width]
        mean = split_dot(value * value, member) * (1.0 / head)
        inverse_h = lax.rsqrt(mean + epsilon)
        inverse = split_dot(inverse_h, member_t)
        grad_n = turned(grads[part], cosine, sine, even, head // 4)
        normed = value * inverse
        gg_ref[part : part + 1, :] += jnp.sum(grad_n * normed, axis=0, keepdims=True)
        weighted = grad_n * gain_ref[part : part + 1, :]
        dots = split_dot(value * weighted, member) * (1.0 / head) * inverse_h * inverse_h
        back = inverse * weighted - normed * split_dot(dots, member_t)
        out_ref[:, part * width : (part + 1) * width] = back.astype(low)
    out_ref[:, 2 * width :] = (dkv_ref[:, width:] + dkvx_ref[:, width:].astype(full)).astype(low)


def qk_back(dq, dkv, dkvx, raw, cosine, sine, gains, member, member_t, head):
    tokens, width = dq.shape
    step = 128
    rows = lambda n: pl.BlockSpec((step, n), lambda i: (i, 0))
    return pl.pallas_call(
        functools.partial(qk_back_body, head),
        grid=(tokens // step,),
        in_specs=[rows(width)]
        + [rows(2 * width)] * 3
        + [rows(width), rows(width), whole(gains.shape), whole(member.shape), whole(member_t.shape)],
        out_specs=[rows(3 * width), whole((8, width))],
        out_shape=[jax.ShapeDtypeStruct((tokens, 3 * width), low), jax.ShapeDtypeStruct((8, width), full)],
        compiler_params=params(48),
        cost_estimate=pl.CostEstimate(flops=60 * raw.size, bytes_accessed=18 * raw.size, transcendentals=0),
        name="qk_back",
    )(dq, dkv, dkvx, raw, cosine, sine, gains, member, member_t)


def head_window(head, width):
    index = pl.program_id(0)
    start = index * head
    base = jnp.minimum(lax.div(start, 128) * 128, width - WINDOW)
    return index, pl.multiple_of(base, 128), start - base


def window_mask(shape, offset, head):
    lane = lax.broadcasted_iota(jnp.int32, shape, 1)
    return jnp.logical_and(lane >= offset, lane < offset + head)


def attend_body(head, q_ref, kvl_ref, kvr_ref, o_ref, lse_ref, acc_ref):
    tokens, width = q_ref.shape
    index, base, offset = head_window(head, width)
    cols = pl.ds(base, WINDOW)
    vals = pl.ds(pl.multiple_of(width + base, 128), WINDOW)

    @pl.when(index == 0)
    def _():
        acc_ref[...] = jnp.zeros_like(acc_ref)
        lse_ref[...] = jnp.zeros_like(lse_ref)

    step = 256
    mask_k = window_mask((tokens, WINDOW), offset, head)
    one = jnp.ones((), low)
    value_l = jnp.where(mask_k, kvl_ref[:, vals], one)
    value_r = jnp.where(mask_k, kvr_ref[:, vals], one)
    mask = window_mask((step, WINDOW), offset, head)
    lane = lax.broadcasted_iota(jnp.int32, (step, lse_ref.shape[1]), 1)
    for first in range(0, tokens, step):
        rows = slice(first, first + step)
        query = jnp.where(mask, q_ref[rows, cols], jnp.zeros((), low))
        left = jnp.exp2(matmul_t(query, kvl_ref[:, cols])).astype(low)
        right = jnp.exp2(matmul_t(query, kvr_ref[:, cols])).astype(low)
        out = matmul(left, value_l) + matmul(right, value_r)
        total = jnp.max(jnp.where(mask, 0.0, out), axis=1, keepdims=True)
        acc_ref[rows, cols] += jnp.where(mask, out * (1.0 / total), 0.0)
        lse_ref[rows, :] += jnp.where(lane == index, jnp.log2(total), 0.0)

    @pl.when(index == pl.num_programs(0) - 1)
    def _():
        o_ref[...] = acc_ref[...].astype(low)


def attend(query, kv_l, kv_r, head):
    tokens, width = query.shape
    heads = width // head
    return pl.pallas_call(
        functools.partial(attend_body, head),
        grid=(heads,),
        in_specs=[whole((tokens, width))] + [whole((tokens, 2 * width))] * 2,
        out_specs=[whole((tokens, width)), whole((tokens, 128))],
        out_shape=[jax.ShapeDtypeStruct((tokens, width), low), jax.ShapeDtypeStruct((tokens, 128), full)],
        scratch_shapes=[pltpu.VMEM((tokens, width), full)],
        compiler_params=params(56),
        cost_estimate=pl.CostEstimate(
            flops=8 * tokens * tokens * WINDOW * heads, bytes_accessed=14 * tokens * width, transcendentals=2 * tokens * tokens * heads
        ),
        name="attend",
    )(query, kv_l, kv_r)


def in_three(column):
    top = column.astype(low)
    rest = column - top.astype(full)
    middle = rest.astype(low)
    return top, middle, (rest - middle.astype(full)).astype(low)


def attend_back_body(head, q_ref, kvl_ref, kvr_ref, do_ref, o_ref, lse_ref, dq_ref, dl_ref, dr_ref, dr_acc):
    tokens, width = q_ref.shape
    index, base, offset = head_window(head, width)
    cols = pl.ds(base, WINDOW)
    vals = pl.ds(pl.multiple_of(width + base, 128), WINDOW)
    temper = head ** (-0.5)

    @pl.when(index == 0)
    def _():
        for ref in (dq_ref, dl_ref, dr_acc):
            ref[...] = jnp.zeros_like(ref)

    shape = (tokens, WINDOW)
    mask = window_mask(shape, offset, head)
    lane = lax.broadcasted_iota(jnp.int32, shape, 1)
    spare = jnp.where(offset >= 3, 0, WINDOW - 3)
    zero = jnp.zeros((), low)
    minus = jnp.where(jnp.logical_and(lane >= spare, lane < spare + 3), -jnp.ones((), low), zero)
    query = jnp.where(mask, q_ref[:, cols], zero)
    grad = jnp.where(mask, do_ref[:, cols], zero)
    delta = jnp.sum(grad.astype(full) * o_ref[:, cols].astype(full), axis=1, keepdims=True)
    small = lax.broadcasted_iota(jnp.int32, lse_ref.shape, 1)
    level = jnp.sum(jnp.where(small == index, lse_ref[...], 0.0), axis=1, keepdims=True)
    query_x = query
    grad_x = grad
    for k, (a, b) in enumerate(zip(in_three(level), in_three(delta))):
        at = lane == spare + k
        query_x = jnp.where(at, a, query_x)
        grad_x = jnp.where(at, b, grad_x)
    grad_q = 0.0
    for ref, acc in ((kvl_ref, dl_ref), (kvr_ref, dr_acc)):
        key = jnp.where(mask, ref[:, cols], minus)
        value = jnp.where(mask, ref[:, vals], minus)
        prob = jnp.exp2(matmul_t(key, query_x))
        grad_s = (prob * matmul_t(value, grad_x)).astype(low)
        acc[:, vals] += matmul(prob.astype(low), grad)
        acc[:, cols] += matmul(grad_s, query)
        grad_q = grad_q + outer_sum(grad_s, key)
    dq_ref[:, cols] += jnp.where(mask, grad_q * temper, 0.0)

    @pl.when(index == pl.num_programs(0) - 1)
    def _():
        back = math.log(2.0)
        dl_ref[:, :width] = dl_ref[:, :width] * back
        dr_ref[:, :width] = (dr_acc[:, :width] * back).astype(low)
        dr_ref[:, width:] = dr_acc[:, width:].astype(low)


def attend_back(query, kv_l, kv_r, grad, out, levels, head):
    tokens, width = query.shape
    heads = width // head
    both = (tokens, 2 * width)
    one = (tokens, width)
    return pl.pallas_call(
        functools.partial(attend_back_body, head),
        grid=(heads,),
        in_specs=[whole(one), whole(both), whole(both), whole(one), whole(one), whole(levels.shape)],
        out_specs=[whole(one), whole(both), whole(both)],
        out_shape=[like(one, full), like(both, full), like(both, low)],
        scratch_shapes=[pltpu.VMEM(both, full)],
        compiler_params=params(62),
        cost_estimate=pl.CostEstimate(
            flops=20 * tokens * tokens * WINDOW * heads, bytes_accessed=28 * tokens * width, transcendentals=2 * tokens * tokens * heads
        ),
        name="attend_back",
    )(query, kv_l, kv_r, grad, out, levels)


class Weight:
    def __init__(self, segments):
        self.segments = segments
        self.columns = sum(columns for _, _, columns in segments)
        self.plan = [piece[1:] for piece in segments[0][1]]
        self.height = sum(rows for _, _, rows in self.plan)
        for _, pieces, _ in segments:
            assert [piece[3] for piece in pieces] == [rows for _, _, rows in self.plan]


def piece_source(ref, lead, first, count):
    for index in lead:
        ref = ref.at[index]
    return ref.at[:, pl.ds(first, count)]


class Cols:
    def __init__(self, array, first, count):
        self.source = array
        self.first = first
        self.count = count

    @property
    def array(self):
        return self.source if isinstance(self.source, jax.Array) else self.source.value

    @property
    def shape(self):
        return (self.array.shape[0], self.count)

    @property
    def dtype(self):
        return self.array.dtype

    @property
    def size(self):
        return self.array.shape[0] * self.count

    def value(self):
        return self.array[:, self.first : self.first + self.shape[1]]


def plain(value):
    return value.value() if isinstance(value, Cols) else value


def anywhere(count):
    return [pl.BlockSpec(memory_space=pl.ANY)] * count


class Stream:
    def __init__(self, weights, tile, late):
        self.weights = weights
        self.tile = tile
        self.late = late
        self.steps = weights[0].columns // tile

    def pieces_of(self):
        return [pieces for w in self.weights for _, pieces, _ in w.segments]

    def specs(self):
        return [pl.BlockSpec(memory_space=pltpu.SMEM)] + anywhere(sum(len(p) for p in self.pieces_of()) + len(self.late))

    def operands(self):
        offsets = jnp.concatenate([offs for w in self.weights for offs, _, _ in w.segments])
        arrays = [piece[0] for pieces in self.pieces_of() for piece in pieces]
        return [offsets] + arrays + [v.array if isinstance(v, Cols) else v for v in self.late]

    def scratch(self):
        shapes = []
        for w in self.weights:
            shapes += [pltpu.VMEM((2, w.height, self.tile), low), pltpu.SemaphoreType.DMA((2, len(w.plan)))]
        for value in self.late:
            shapes += [pltpu.VMEM(value.shape, value.dtype), pltpu.SemaphoreType.DMA((1,))]
        return shapes

    def bind(self, operand_refs, scratch_refs):
        self.offs = operand_refs[0]
        refs = list(operand_refs[1:])
        self.refs = []
        for w in self.weights:
            mine = []
            for _, pieces, _ in w.segments:
                mine.append(refs[: len(pieces)])
                refs = refs[len(pieces) :]
            self.refs.append(mine)
        self.buffers = scratch_refs[0 : 2 * len(self.weights) : 2]
        self.sems = scratch_refs[1 : 2 * len(self.weights) : 2]
        rest = scratch_refs[2 * len(self.weights) :]
        self.late_bufs = rest[0::2]
        self.late_copies = []
        for value, ref, buf, sem in zip(self.late, refs, rest[0::2], rest[1::2]):
            if isinstance(value, Cols):
                ref = ref.at[:, pl.ds(value.first, value.shape[1])]
            self.late_copies.append(pltpu.make_async_copy(ref, buf, sem.at[0]))

    def segment_copies(self, index, number, column, slot):
        w = self.weights[index]
        base = sum(len(x.plan) * len(x.segments) for x in self.weights[:index]) + number * len(w.plan)
        out = []
        for at, (_, lead, first, rows) in enumerate(w.segments[number][1]):
            source = piece_source(self.refs[index][number][at], lead, pl.multiple_of(first + column, 128), self.tile)
            start = pl.multiple_of(self.offs[base + at], 16)
            target = self.buffers[index].at[slot, pl.ds(start, rows), :]
            out.append(pltpu.make_async_copy(source, target, self.sems[index].at[slot, at]))
        return out

    def copies(self, step, slot):
        return [copy for index in range(len(self.weights)) for copy in self.segment_copies(index, 0, step * self.tile, slot)]

    def start_tile(self, step, slot):
        for index, w in enumerate(self.weights):
            first = 0
            for number, (_, _, columns) in enumerate(w.segments):
                count = columns // self.tile

                def start():
                    for copy in self.segment_copies(index, number, (step - first) * self.tile, slot):
                        copy.start()

                if len(w.segments) == 1:
                    start()
                else:
                    pl.when(jnp.logical_and(step >= first, step < first + count))(start)
                first += count

    def wait_tile(self, slot):
        for index in range(len(self.weights)):
            for copy in self.segment_copies(index, 0, 0, slot):
                copy.wait()

    def advance(self):
        step = pl.program_id(0)
        slot = lax.rem(step, 2)

        @pl.when(step == 0)
        def _():
            self.start_tile(jnp.int32(0), 0)
            for copy in self.late_copies:
                copy.start()

        @pl.when(step + 1 < self.steps)
        def _():
            self.start_tile(step + 1, 1 - slot)

        self.wait_tile(slot)
        return step, [buf.at[slot] for buf in self.buffers]

    def wait_late(self):
        for copy in self.late_copies:
            copy.wait()
        return self.late_bufs


def stream_call(name, stream, body, ins, in_specs, outs, out_specs, scratch, flops, mib=58):
    operands = stream.operands()
    frame = stream.scratch()

    def kernel(*refs):
        count = len(operands)
        ops, refs = refs[:count], refs[count:]
        inputs, refs = refs[: len(ins)], refs[len(ins) :]
        outputs, refs = refs[: len(outs)], refs[len(outs) :]
        stream.bind(ops, refs[: len(frame)])
        body(stream, inputs, outputs, refs[len(frame) :])

    moved = sum(v.size * v.dtype.itemsize for v in list(ins) + list(stream.late) + list(outs))
    moved += sum(2 * w.height * w.columns for w in stream.weights)
    return pl.pallas_call(
        kernel,
        grid=(stream.steps,),
        in_specs=stream.specs() + in_specs,
        out_specs=out_specs,
        out_shape=outs,
        scratch_shapes=frame + scratch,
        compiler_params=params(mib),
        cost_estimate=pl.CostEstimate(flops=flops, bytes_accessed=moved, transcendentals=0),
        name=name,
    )(*operands, *ins)


def by_rows(tokens, fun, step=128):
    @pl.loop(0, tokens // step)
    def _(i):
        fun(pl.ds(pl.multiple_of(i * step, step), step))


def take(ref, rows):
    return ref[rows, :] if ref.shape[0] > 1 else ref[...]


def give(ref, rows, value):
    if ref.shape[0] > 1:
        ref[rows, :] = value.astype(ref.dtype)
    else:
        ref[...] += jnp.sum(value, axis=0, keepdims=True)


def like(shape, dtype):
    return jax.ShapeDtypeStruct(shape, dtype)


def ada_matmul(value, weight, bias):
    tokens = value.shape[0]
    tile = weight.height
    stream = Stream([weight], tile, [])

    def body(stream, ins, outs, scratch):
        _, (w,) = stream.advance()
        outs[0][...] = matmul(ins[0][...], w[...]) + ins[1][...]

    return stream_call(
        "ada",
        stream,
        body,
        [value, bias],
        [whole(value.shape), pl.BlockSpec((1, tile), lambda j: (0, j))],
        [like((tokens, weight.columns), full)],
        [pl.BlockSpec((tokens, tile), lambda j: (0, j))],
        [],
        2 * tokens * weight.height * weight.columns,
    )[0]


def mod_partial(row, weight, width):
    shard = weight.shape[1]
    tall = jnp.broadcast_to(row, (16, shard))

    def body(x_ref, w_ref, out_ref):
        out_ref[0] = matmul(x_ref[...], w_ref[...])[:8]

    out = pl.pallas_call(
        body,
        grid=(6,),
        in_specs=[whole(tall.shape), pl.BlockSpec((None, shard, width), lambda j: (0, 0, j))],
        out_specs=pl.BlockSpec((1, 8, width), lambda j: (j, 0, 0)),
        out_shape=like((6, 8, width), full),
        compiler_params=params(60),
        cost_estimate=pl.CostEstimate(flops=0, bytes_accessed=12 * shard * width, transcendentals=0),
        name="modpart",
    )(tall, weight)
    return out[:, 0]


def qkv_matmul(value, weight, cosine, sine, gains, member, member_t, head):
    tokens, width = value.shape
    stream = Stream([weight], width, [cosine, sine])

    def body(stream, ins, outs, scratch):
        x_ref, gain_ref, mem_ref, memt_ref = ins
        q_ref, kv_ref, raw_ref = outs
        (acc_ref,) = scratch
        step, (w,) = stream.advance()
        cos_ref, sin_ref = stream.late_bufs
        acc_ref[...] = matmul(x_ref[...], w[...])

        @pl.when(step == 0)
        def _():
            stream.wait_late()

        def head_norm(part, out, cols):
            def rows_of(rows):
                raw = acc_ref[rows, :]
                raw_ref[rows, :] = raw
                mean = split_dot(raw * raw, mem_ref[...]) * (1.0 / head)
                inverse = split_dot(lax.rsqrt(mean + epsilon), memt_ref[...])
                normed = raw * inverse * gain_ref[part : part + 1, :]
                even = even_lanes(gain_ref, raw.shape)
                out[rows, cols] = turned(normed, cos_ref[rows, :], sin_ref[rows, :], even, head // 4).astype(low)

            by_rows(tokens, rows_of)

        @pl.when(step == 0)
        def _():
            head_norm(0, q_ref, slice(0, width))

        @pl.when(step == 1)
        def _():
            head_norm(1, kv_ref, slice(0, width))

        @pl.when(step == 2)
        def _():
            kv_ref[:, width:] = acc_ref[...].astype(low)

    flat = like((tokens, width), low)
    return stream_call(
        "qkv",
        stream,
        body,
        [value, gains, member, member_t],
        [whole(v.shape) for v in (value, gains, member, member_t)],
        [flat, like((tokens, 2 * width), low), like((tokens, 2 * width), full)],
        [whole((tokens, width)), whole((tokens, 2 * width)), pl.BlockSpec((tokens, width), lambda j: (0, jnp.minimum(j, 1)))],
        [pltpu.VMEM((tokens, width), full)],
        2 * tokens * weight.height * weight.columns,
    )


def out_matmul(value, weight, hidden0, mods):
    tokens, width = value.shape
    stream = Stream([weight], 384, [hidden0] + mods)

    def body(stream, ins, outs, scratch):
        att_ref, h1_ref, b_ref = outs
        (acc_ref,) = scratch
        step, (w,) = stream.advance()
        acc_ref[step] = matmul(ins[0][...], w[...])

        @pl.when(step == stream.steps - 1)
        def _():
            h0_ref, gate_ref, shift_ref, scale_ref = stream.wait_late()

            def rows_of(rows):
                att = jnp.concatenate([acc_ref[k, rows, :] for k in range(stream.steps)], axis=1)
                hidden1 = h0_ref[rows, :] + take(gate_ref, rows) * att
                normed = hidden1 * rms_scale(hidden1)
                att_ref[rows, :] = att.astype(low)
                h1_ref[rows, :] = hidden1
                b_ref[rows, :] = (normed * (1.0 + take(scale_ref, rows)) + take(shift_ref, rows)).astype(low)

            by_rows(tokens, rows_of)

    return stream_call(
        "attout",
        stream,
        body,
        [value],
        [whole(value.shape)],
        [like((tokens, width), low), like((tokens, width), full), like((tokens, width), low)],
        [whole((tokens, width))] * 3,
        [pltpu.VMEM((stream.steps, tokens, 384), full)],
        2 * tokens * weight.height * weight.columns,
    )


def gate_up_matmul(value, gate, up):
    tokens, width = value.shape
    tile = 512
    stream = Stream([gate, up], tile, [])

    def body(stream, ins, outs, scratch):
        hid_ref, g_ref, u_ref = outs
        _, (wg, wu) = stream.advance()
        g = matmul(ins[0][...], wg[...])
        u = matmul(ins[0][...], wu[...])
        g_ref[...] = g.astype(low)
        u_ref[...] = u.astype(low)
        hid_ref[...] = (g * jax.nn.sigmoid(g) * u).astype(low)

    flat = like((tokens, gate.columns), low)
    return stream_call(
        "gateup",
        stream,
        body,
        [value],
        [whole(value.shape)],
        [flat] * 3,
        [pl.BlockSpec((tokens, tile), lambda j: (0, j))] * 3,
        [],
        4 * tokens * gate.height * gate.columns,
    )


def down_matmul(value, weight, hidden1, gate):
    tokens, depth = value.shape
    width = weight.columns
    stream = Stream([weight], width, [hidden1, gate])

    def body(stream, ins, outs, scratch):
        mlp_ref, h2_ref = outs
        (acc_ref,) = scratch
        hid_ref = ins[0]
        at = 0
        copies = stream.copies(0, 0)
        for copy in copies + stream.late_copies:
            copy.start()
        for k, (_, _, rows) in enumerate(weight.plan):
            copies[k].wait()
            first = stream.offs[k]
            left = hid_ref[:, pl.ds(pl.multiple_of(first, 128), rows)]
            part = matmul(left, stream.buffers[0][0, pl.ds(pl.multiple_of(first, 128), rows), :])
            if k == 0:
                acc_ref[...] = part
            else:
                acc_ref[...] += part
        h1_ref, gate_ref = stream.wait_late()

        def rows_of(rows):
            mlp = acc_ref[rows, :]
            mlp_ref[rows, :] = mlp.astype(low)
            h2_ref[rows, :] = h1_ref[rows, :] + take(gate_ref, rows) * mlp

        by_rows(tokens, rows_of)

    return stream_call(
        "down",
        stream,
        body,
        [value],
        [whole(value.shape)],
        [like((tokens, width), low), like((tokens, width), full)],
        [whole((tokens, width))] * 2,
        [pltpu.VMEM((tokens, width), full)],
        2 * tokens * depth * width,
    )


def down_back(grad, weight, gate_pre, up_pre):
    tokens, width = grad.shape
    depth = weight.height
    stream = Stream([weight], width, [gate_pre, up_pre])

    def body(stream, ins, outs, scratch):
        dg_ref, du_ref = outs
        copies = stream.copies(0, 0)
        for copy in copies + stream.late_copies:
            copy.start()
        for k, (_, _, count) in enumerate(weight.plan):
            copies[k].wait()
            if k == 0:
                g_ref, u_ref = stream.wait_late()
            first = pl.multiple_of(stream.offs[k], 128)
            for at in range(0, count, 384):
                cols = pl.ds(pl.multiple_of(first + at, 128), 384)

                def rows_of(rows):
                    inner = matmul_t(ins[0][rows, :], stream.buffers[0][0, cols, :])
                    g = g_ref[rows, cols].astype(full)
                    u = u_ref[rows, cols].astype(full)
                    sigma = jax.nn.sigmoid(g)
                    active = g * sigma
                    dg_ref[rows, cols] = (inner * u * (sigma + active * (1.0 - sigma))).astype(low)
                    du_ref[rows, cols] = (inner * active).astype(low)

                by_rows(tokens, rows_of, 256)

    flat = like((tokens, depth), low)
    return stream_call(
        "downback",
        stream,
        body,
        [grad],
        [whole(grad.shape)],
        [flat, flat],
        [whole((tokens, depth))] * 2,
        [],
        2 * tokens * depth * width,
    )


def back_matmul(name, grads, weights, tile, late, outs, finish):
    tokens = grads[0].shape[0]
    width = weights[0].height
    stream = Stream(weights, tile, late)

    def body(stream, ins, outs, scratch):
        (acc_ref,) = scratch
        step, tiles = stream.advance()
        part = matmul_t(ins[0][...], tiles[0][...])
        for value, w in zip(ins[1:], tiles[1:]):
            part = part + matmul_t(value[...], w[...])

        @pl.when(step == 0)
        def _():
            acc_ref[...] = part

        @pl.when(step > 0)
        def _():
            acc_ref[...] += part

        @pl.when(step == stream.steps - 1)
        def _():
            refs = stream.wait_late()
            for ref in outs:
                if ref.shape[0] == 1:
                    ref[...] = jnp.zeros_like(ref)
            by_rows(tokens, lambda rows: finish(rows, acc_ref[rows, :], refs, outs))

    return stream_call(
        name,
        stream,
        body,
        list(grads),
        [pl.BlockSpec((tokens, tile), lambda j: (0, j))] * len(grads),
        outs,
        [whole(value.shape) for value in outs],
        [pltpu.VMEM((tokens, width), full)],
        2 * tokens * width * weights[0].columns * len(weights),
    )


def mlp_back(grads, weights, grad2, hidden1, att, mods):
    tokens, width = grad2.shape
    lead = mods[0].shape[0]

    def finish(rows, db, refs, outs):
        dh2_ref, h1_ref, att_ref, scale_ref, gate_ref = refs
        hidden1 = h1_ref[rows, :]
        inverse = rms_scale(hidden1)
        normed = hidden1 * inverse
        weighted = db * (1.0 + take(scale_ref, rows))
        back = inverse * (weighted - normed * jnp.mean(normed * weighted, axis=-1, keepdims=True))
        grad1 = dh2_ref[rows, :] + back
        outs[0][rows, :] = grad1
        outs[1][rows, :] = (grad1 * take(gate_ref, rows)).astype(low)
        give(outs[2], rows, db)
        give(outs[3], rows, db * normed)
        give(outs[4], rows, grad1 * att_ref[rows, :].astype(full))

    outs = [like((tokens, width), full), like((tokens, width), low)]
    outs += [like((lead, width), low if lead > 1 else full)] * 3
    return back_matmul("mlpback", grads, weights, 512, [grad2, hidden1, att] + mods, outs, finish)


def qkv_back(grad, weight, grad1, hidden0, scale):
    tokens, width = grad1.shape
    lead = scale.shape[0]

    def finish(rows, da, refs, outs):
        dh1_ref, h0_ref, scale_ref = refs
        hidden0 = h0_ref[rows, :]
        inverse = rms_scale(hidden0)
        normed = hidden0 * inverse
        weighted = da * (1.0 + take(scale_ref, rows))
        back = inverse * (weighted - normed * jnp.mean(normed * weighted, axis=-1, keepdims=True))
        outs[0][rows, :] = (dh1_ref[rows, :] + back).astype(low)
        give(outs[1], rows, da)
        give(outs[2], rows, da * normed)

    outs = [like((tokens, width), low)] + [like((lead, width), low if lead > 1 else full)] * 2
    return back_matmul("qkvback", [grad], [weight], width, [grad1, hidden0, scale], outs, finish)


def out_back(grad, weight):
    def finish(rows, value, refs, outs):
        outs[0][rows, :] = value.astype(low)

    return back_matmul("outback", [grad], [weight], 384, [], [like(grad.shape, low)], finish)[0]


def ada_back(grads, weight, cond):
    tokens, width = cond.shape
    tile = weight.height
    stream = Stream([weight], tile, [cond])

    def body(stream, ins, outs, scratch):
        (acc_ref,) = scratch
        step, (w,) = stream.advance()
        for k, grad in enumerate(ins):

            @pl.when(step == k)
            def _():
                part = matmul_t(grad[...], w[...])
                acc_ref[...] = part if k == 0 else acc_ref[...] + part

        @pl.when(step == stream.steps - 1)
        def _():
            (cond_ref,) = stream.wait_late()

            def rows_of(rows):
                cond = cond_ref[rows, :]
                sigma = jax.nn.sigmoid(cond)
                outs[0][rows, :] = acc_ref[rows, :] * sigma * (1.0 + cond * (1.0 - sigma))

            by_rows(tokens, rows_of)

    return stream_call(
        "adaback",
        stream,
        body,
        list(grads),
        [whole(grad.shape) for grad in grads],
        [like((tokens, width), full)],
        [whole((tokens, width))],
        [pltpu.VMEM((tokens, width), full)],
        2 * tokens * width * weight.columns,
    )[0]


def ordered_grad(left, order, rights, tile):
    tokens, width = left.shape
    many = len(rights) > 1
    columns = sum(right.shape[1] for right in rights)
    steps = columns // tile

    def body(order_ref, left_ref, *refs):
        ys, out_ref, turned_ref = refs[: len(rights)], refs[-2], refs[-1]
        step = pl.program_id(0)

        @pl.when(step == 0)
        def _():
            turned_ref[...] = matmul_t(order_ref[...], left_ref[...]).astype(low)

        if not many:
            out_ref[...] = matmul(turned_ref[...], ys[0][...]).astype(low)
            return
        for k, y in enumerate(ys):

            @pl.when(step == k)
            def _():
                out_ref[...] = matmul(turned_ref[...], y[...]).astype(low)

    tiles = [whole(right.shape) for right in rights] if many else [pl.BlockSpec((tokens, tile), lambda j: (0, j))]
    return pl.pallas_call(
        body,
        grid=(steps,),
        in_specs=[whole(order.shape), whole(left.shape)] + tiles,
        out_specs=pl.BlockSpec((width, tile), lambda j: (0, j)),
        out_shape=like((width, columns), low),
        scratch_shapes=[pltpu.VMEM((width, tokens), low)],
        compiler_params=params(56),
        cost_estimate=pl.CostEstimate(
            flops=2 * tokens * width * (columns + width), bytes_accessed=2 * width * (columns + 2 * width), transcendentals=0
        ),
        name="wgrad",
    )(order, left, *rights)


def down_grad(left, right, groups):
    tokens, depth = left.shape
    columns = right.shape[1]
    tile = depth // groups

    def body(left_ref, right_ref, out_ref):
        value = outer_sum(left_ref[...], right_ref[...]).astype(low)
        out_ref[0, 0] = value[: tile // 2]
        out_ref[1, 0] = value[tile // 2 :]

    return pl.pallas_call(
        body,
        grid=(groups,),
        in_specs=[pl.BlockSpec((tokens, tile), lambda j: (0, j)), whole(right.shape)],
        out_specs=pl.BlockSpec((2, 1, tile // 2, columns), lambda j: (0, j, 0, 0)),
        out_shape=like((2, groups, tile // 2, columns), low),
        compiler_params=params(40),
        cost_estimate=pl.CostEstimate(
            flops=2 * tokens * depth * columns, bytes_accessed=2 * depth * (columns + tokens), transcendentals=0
        ),
        name="wdown",
    )(left, right)


def tie(value, *others):
    others = [v for v in others if v is not None]
    if not others:
        return value
    return lax.optimization_barrier((value, *others))[0]


class Flight:
    def __init__(self, token):
        self.token = token
        self.held = []
        self.todo = []

    def send(self, value, item, holder, name):
        setattr(holder, name, swap(tie(value, self.token), item))
        self.held.append((holder, name))

    def watch(self, holder, name):
        self.held.append((holder, name))

    def then(self, action):
        self.todo.append(action)

    def fence(self, values, starts=()):
        values = list(values)
        held, todo = self.held, self.todo
        self.held, self.todo = [], []
        arrays = values + [getattr(holder, name) for holder, name in held]
        arrays = lax.optimization_barrier(tuple(arrays))
        self.token = arrays[0]
        for (holder, name), value in zip(held, arrays[len(values) :]):
            setattr(holder, name, value)
        for action in todo:
            action()
        for start in starts:
            start(self)
        return arrays[: len(values)]


class Bundle:
    def __init__(self, place, own, shards, parts, which, relay_bit):
        self.row, self.col, coords = place
        self.own = own
        self.shards = shards
        self.parts = parts
        self.which = which
        self.relay_bit = relay_bit
        self.rows = shards[parts[0][0]].shape[1]
        self.half = self.rows // 2
        self.at = coords[relay_bit] * self.half

    def over_col(self, flight):
        at = tie(self.at, flight.token)
        mine = [
            lax.dynamic_slice(self.shards[name], (self.which, at, first), (1, self.half, n))[0]
            for name, first, n in self.parts
        ]
        flight.send(jnp.concatenate(mine, axis=1), "col", self, "first")

    def relay(self, flight):
        flight.send(self.first, self.relay_bit, self, "second")

    def first_row(self, flight):
        flight.send(self.first, "row", self, "first_s")

    def second_row(self, flight):
        flight.send(self.second, "row", self, "second_s")

    def rows_both(self, flight):
        self.first_row(flight)
        self.second_row(flight)

    def segment(self, wanted):
        row, col, rows, half, at = self.row, self.col, self.rows, self.half, self.at
        other = (2 * row + 1 - col) * rows
        other_s = (2 * (1 - row) + 1 - col) * rows
        offsets = [col * rows, (col + 2) * rows, other + at, other_s + at]
        offsets += [other + (half - at), other_s + (half - at)]
        offsets = jnp.stack(offsets).astype(jnp.int32)
        begin = 0
        for name, first, n in self.parts:
            if name == wanted:
                own_all = self.own[name]
                lead = () if own_all.ndim == 3 else (self.which,)
                pieces = [(own_all, (0,) + lead, first, rows), (own_all, (1,) + lead, first, rows)]
                got = [self.first, self.first_s, self.second, self.second_s]
                pieces += [(value, (), begin, half) for value in got]
                return (offsets, pieces, n)
            begin += n
        raise KeyError(wanted)


def weight_of(name, *bundles):
    return Weight([bundle.segment(name) for bundle in bundles])


def item_weight(item):
    return {"row": 2, "col": 1}.get(item) or 4 << item


def halving_order(path, width, block, me):
    at = jnp.arange(width)
    position = at // block
    owner = me
    for k, item in enumerate(path):
        bit = (position >> (len(path) - 1 - k)) & 1
        if item == "row":
            owner = (owner & ~2) | (2 * bit)
        else:
            owner = owner ^ (bit * item_weight(item))
    return owner * block + at % block


class Slice:
    def __init__(self, held, columns):
        self.held = held
        self.columns = columns

    def get(self):
        return self.held.value[..., self.columns]


class Share:
    def __init__(self, value, order, path):
        self.value = value
        self.order = list(order)
        self.path = list(path)

    def cut(self):
        if isinstance(self.value, Slice):
            self.value = self.value.get()

    def parts(self, item):
        self.cut()
        rows, columns = self.value.shape
        if self.order[0] == item:
            self.order = self.order[1:]
            return self.value[: rows // 2], self.value[rows // 2 :]
        self.order.remove(item)
        value = self.value.reshape(2, 2, rows // 4, columns)
        return value[:, 0].reshape(rows // 2, columns), value[:, 1].reshape(rows // 2, columns)


    def joined(self, kept, got):
        return (kept.astype(full) + got.astype(full)).astype(kept.dtype)


class BlockShare(Share):
    def __init__(self, value, order, path, coords):
        super().__init__(value, order, path)
        self.coords = coords

    def parts(self, item):
        self.cut()
        axis = self.order.index(item)
        self.order.remove(item)
        mine = self.coords[item]
        return (
            lax.dynamic_index_in_dim(self.value, mine, axis, keepdims=False),
            lax.dynamic_index_in_dim(self.value, 1 - mine, axis, keepdims=False),
        )


class Total:
    def __init__(self, value, path):
        self.value = value
        self.path = list(path)

    def parts(self, item):
        return self.value, self.value

    def joined(self, kept, got):
        return kept + got


class TotalAndRows(Total):
    def __init__(self, value, count, path):
        super().__init__(value, path)
        self.count = count

    def joined(self, kept, got):
        n = self.count
        return jnp.concatenate([kept[:n] + got[:n], kept[n:], got[n:]], axis=0)


class Parcel:
    got = None


class Agenda:
    def __init__(self):
        self.tasks = {}

    def go(self, *names):
        def action(flight):
            tasks = [self.tasks[name] for name in names]
            items = [task.path.pop(0) for task in tasks]
            assert len(set(items)) == 1
            pairs = [task.parts(items[0]) for task in tasks]
            parcel = Parcel()
            away = pairs[0][1] if len(pairs) == 1 else jnp.concatenate([pair[1] for pair in pairs], axis=-1)
            flight.send(away, items[0], parcel, "got")

            def arrive():
                at = 0
                for task, (kept, _) in zip(tasks, pairs):
                    if len(tasks) == 1:
                        task.value = task.joined(kept, parcel.got)
                    else:
                        n = kept.shape[-1]
                        task.value = task.joined(kept, parcel.got[..., at : at + n])
                        at += n

            flight.then(arrive)

        return action


def row_sum(value):
    return lax.psum_scatter(value, "row", scatter_dimension=0, tiled=True)


def row_sum_blocks(left, right, bits, block):
    if (4 * block) % 128 == 0:
        value = down_grad(left, right, 2**bits)
        value = lax.psum_scatter(value, "row", scatter_dimension=0, tiled=False)
    else:
        value = outer_sum(left, right).astype(low)
        value = value.reshape(2**bits, 2, 2 * block, value.shape[1])
        value = lax.psum_scatter(value, "row", scatter_dimension=1, tiled=False)
    return value.reshape((2,) * (bits + 1) + (block, value.shape[-1]))


def block_forward(hidden0, mods, mats, gains, tabs, flight, points):
    shift1, scale1, gate1, shift2, scale2, gate2 = mods
    cosine, sine, member, member_t, head = tabs
    used = {}

    def mat(name):
        used[name] = mats[name]()
        return used[name]

    def fence(point, *values):
        if point not in points:
            return values if len(values) > 1 else values[0]
        values = flight.fence(values, points[point])
        return values if len(values) > 1 else values[0]

    attn_in = (hidden0 * rms_scale(hidden0) * (1.0 + plain(scale1)) + plain(shift1)).astype(low)
    attn_in = fence("qkv", attn_in)
    query, kv, raw = qkv_matmul(attn_in, mat("qkv"), cosine, sine, gains[0], member, member_t, head)
    query, kv = fence("attend", query, kv)
    kv_r = swap(kv, "row")
    out_b, lse = attend(query, kv, kv_r, head)
    out_b = fence("out", out_b)
    att, hidden1, mlp_in = out_matmul(out_b, mat("out"), hidden0, [gate1, shift2, scale2])
    mlp_in = fence("gate", mlp_in)
    inner, gate_pre, up_pre = gate_up_matmul(mlp_in, mat("gate"), mat("up"))
    inner = fence("down", inner)
    mlp_out, hidden2 = down_matmul(inner, mat("down"), hidden1, gate2)
    cache = (hidden0, attn_in, raw, query, kv, kv_r, out_b, lse, att)
    cache += (hidden1, mlp_in, gate_pre, up_pre, inner, mlp_out)
    used = tuple(used[name] for name in ("qkv", "out", "gate", "up", "down"))
    return hidden2, cache, used


class Sum:
    value = None


def block_backward(grad2, cache, mods, mats, gains, tabs, comm, tag, plan):
    (hidden0, attn_in, raw, query, kv, kv_r, out_b, lse, att) = cache[:9]
    (hidden1, mlp_in, gate_pre, up_pre, inner, mlp_out) = cache[9:]
    shift1, scale1, gate1, shift2, scale2, gate2 = mods
    qkv_w, out_w, gate_w, up_w, down_w = mats
    cosine, sine, member, member_t, head = tabs
    flight, agenda, orders, paths, coords = comm
    n_data = lax.axis_size("dp")
    bits = (n_data - 1).bit_length()
    block = down_w.height // (4 * n_data)

    def fence(point, *values):
        values = flight.fence(values, plan.get(point, ()))
        return values if len(values) > 1 else values[0]

    def summed(left, name, right, tile):
        return row_sum(ordered_grad(left, orders[name], [right], tile))

    def watch(name, task):
        agenda.tasks[name + tag] = task
        flight.watch(task, "value")

    def begin(name, value):
        path = paths[name][1:]
        watch(name[0], Share(value, path, path))

    def begin_halves(name, value, cut):
        path = paths[name][1:]
        other = [path[1], path[0]] + path[2:]
        held = Sum()
        held.value = value
        flight.watch(held, "value")
        agenda.tasks[name[0] + "a" + tag] = Share(Slice(held, slice(0, cut)), path, path)
        agenda.tasks[name[0] + "b" + tag] = Share(Slice(held, slice(cut, None)), path, other)

    def begin_down(value):
        order = list(reversed(range(bits))) + ["col"]
        if tag == "0":
            watch("d", BlockShare(value, order, paths["down"][1:], coords))
            return
        path = paths["qkv"][1:]
        other = [path[1], path[0]] + path[2:]
        cut = value.shape[-1] // 256 * 128
        held = Sum()
        held.value = value
        flight.watch(held, "value")
        agenda.tasks["da" + tag] = BlockShare(Slice(held, slice(0, cut)), order, path, coords)
        agenda.tasks["db" + tag] = BlockShare(Slice(held, slice(cut, None)), order, other, coords)

    grad2 = fence("start", grad2)
    grad_mlp = (grad2 * plain(gate2)).astype(low)
    dgate2 = grad2 * mlp_out.astype(full)
    if gate2.shape[0] == 1:
        dgate2 = jnp.sum(dgate2, axis=0, keepdims=True)
    r_down = row_sum_blocks(inner, grad_mlp, bits, block)
    grad_gate, grad_up = down_back(grad_mlp, down_w, gate_pre, up_pre)
    begin_down(r_down)
    grad_gate, grad_up = fence("gate", grad_gate, grad_up)
    r_gate = summed(mlp_in, "gate", grad_gate, 512)
    r_up = summed(mlp_in, "up", grad_up, 512)
    grad1, grad_att, dshift2, dscale2, dgate1 = mlp_back(
        [grad_gate, grad_up], [gate_w, up_w], grad2, hidden1, att, [scale2, gate1]
    )
    grad_att = fence("out", grad_att)
    r_out = summed(out_b, "out", grad_att, 384)
    grad_ob = out_back(grad_att, out_w)
    begin("gate", r_gate)
    begin("up", r_up)
    grad_ob = fence("attend", grad_ob)
    dq, dkv, dkv_r = attend_back(query, kv, kv_r, grad_ob, out_b, lse, head)
    begin("out", r_out)
    dq, dkv_r = fence("qk", dq, dkv_r)
    grad_qkv, gain_rows = qk_back(dq, dkv, swap(dkv_r, "row"), raw, cosine, sine, gains[1], member, member_t, head)
    grad_qkv = fence("qkv", grad_qkv)
    r_qkv = summed(attn_in, "qkv", grad_qkv, 384)
    grad0, dshift1, dscale1 = qkv_back(grad_qkv, qkv_w, grad1, hidden0, scale1)
    dmods = [dshift1, dscale1, dgate1, dshift2, dscale2, dgate2]
    begin_halves("qkv", r_qkv, r_qkv.shape[1] // 256 * 128)
    return grad0, dmods, gain_rows[:2], begin_halves


def per_device(
    latents,
    levels,
    timesteps,
    patch_weight,
    patch_bias,
    ada_weight,
    ada_bias,
    qkv_weight,
    qk_gains,
    out_weight,
    gate_weight,
    up_weight,
    down_weight,
    cotangent,
):
    images, slots, chans, rows_loc, cols_loc = latents.shape
    n_data = lax.axis_size("dp")
    assert images == 1 and slots == 2
    assert lax.axis_size("row") == 2 and lax.axis_size("col") == 2
    row = lax.axis_index("row")
    col = lax.axis_index("col")
    data = lax.axis_index("dp")
    bits = (n_data - 1).bit_length()
    left = col == 0
    coords = {"row": row, "col": col}
    place = (row, col, coords)
    for k in range(bits):
        coords[k] = (data >> k) & 1
    grid_rows = rows_loc // 2
    grid_cols = cols_loc
    half_cols = grid_cols // 2
    tokens = grid_rows * grid_cols
    width = cotangent.shape[-1]
    head = qk_gains.shape[2]
    heads = width // head
    pvals = chans * 4
    shard = width // 4
    me = data * 4 + row * 2 + col
    own_rows = width // (4 * n_data)

    def pair(own, other, axis):
        return jnp.concatenate([jnp.where(left, own, other), jnp.where(left, other, own)], axis=axis)

    own = {}
    for name, s in (
        ("qkv", qkv_weight),
        ("out", out_weight),
        ("gate", gate_weight),
        ("up", up_weight),
        ("down", down_weight),
        ("ada", ada_weight),
    ):
        own[name] = lax.all_gather(s, "row", axis=0)
    shards = {"qkv": qkv_weight, "out": out_weight, "gate": gate_weight, "up": up_weight, "down": down_weight}
    shards["ada"] = ada_weight

    def bundle(which, relay_bit, *parts):
        return Bundle(place, own, shards, parts, which, relay_bit)

    ff = gate_weight.shape[2]
    b_q0 = bundle(0, 0, ("qkv", 0, width))
    b_kv0 = bundle(0, 1, ("qkv", width, 2 * width))
    b_out0 = bundle(0, 0, ("out", 0, width))
    b_gate0 = bundle(0, 0, ("gate", 0, ff))
    b_up0 = bundle(0, 1, ("up", 0, ff))
    b_down0 = bundle(0, 0, ("down", 0, width))
    b_ada_a = bundle(1, 1, ("ada", 0, 3 * width))
    b_ada_b = bundle(1, 0, ("ada", 3 * width, 3 * width))
    b_qkv1 = bundle(1, 1, ("qkv", 0, 3 * width))
    b_og1 = bundle(1, 0, ("out", 0, width), ("gate", 0, ff))
    b_up1 = bundle(1, 1, ("up", 0, ff))
    b_down1 = bundle(1, 0, ("down", 0, width))
    enc_mats = {
        "qkv": lambda: weight_of("qkv", b_q0, b_kv0),
        "out": lambda: weight_of("out", b_out0),
        "gate": lambda: weight_of("gate", b_gate0),
        "up": lambda: weight_of("up", b_up0),
        "down": lambda: weight_of("down", b_down0),
    }
    dec_mats = {
        "qkv": lambda: weight_of("qkv", b_qkv1),
        "out": lambda: weight_of("out", b_og1),
        "gate": lambda: weight_of("gate", b_og1),
        "up": lambda: weight_of("up", b_up1),
        "down": lambda: weight_of("down", b_down1),
    }

    small = jnp.concatenate(
        [jnp.swapaxes(patch_weight, 1, 2).reshape(2 * pvals, shard), patch_bias, ada_bias.reshape(12, shard)], axis=0
    )
    small_other = swap(small, "col")
    blk = latents[0]
    blk_other = swap(blk, "col")
    flight = Flight(small)

    class Start:
        pass

    Start.small, Start.blk = small_other, blk_other
    flight.watch(Start, "small")
    flight.watch(Start, "blk")
    (blk,) = flight.fence([blk])
    small = pair(small[None], Start.small[None], 0)
    wide = pair(blk, Start.blk, 3)
    flight.send(small, "row", Start, "small")
    flight.send(wide[:, :, rows_loc - 1 :], "row", Start, "top")
    small, wide = flight.fence([small, wide], [b_q0.over_col, b_kv0.over_col])
    temb = time_features(tie(timesteps, wide)[0], width)
    small = jnp.where(row == 0, jnp.stack([small, Start.small]), jnp.stack([Start.small, small]))
    small = small.reshape(4, 2 * pvals + 14, shard)
    patch_w = small[:, : 2 * pvals].transpose(1, 0, 2).reshape(2, pvals, width)
    patch_b = small[:, 2 * pvals : 2 * pvals + 2].transpose(1, 0, 2).reshape(2, width).astype(full)
    ada_b = small[:, 2 * pvals + 2 :].reshape(4, 2, 6 * shard).transpose(1, 0, 2).reshape(2, 6, width).astype(full)

    framed = jnp.concatenate([Start.top, wide[:, :, : rows_loc - 1]], axis=2)
    framed = jnp.concatenate([framed[..., -1:], framed[..., :-1]], axis=3)
    patches = (
        framed.reshape(slots, chans, grid_rows, 2, grid_cols, 2).transpose(0, 2, 4, 1, 3, 5).reshape(slots, tokens, pvals)
    )
    enc_patches = patches[0]
    dec_patches = jnp.where(left, patches[0], patches[1])

    sil0 = jax.nn.silu(temb[:1]).astype(low)
    temb_own = jnp.where(left, temb[:1], temb[1:])
    part = mod_partial(lax.dynamic_slice(sil0, (0, (2 * row + col) * shard), (1, shard)), ada_weight, width)

    cot_own = jnp.where(left, cotangent[0, 0], cotangent[0, 1])

    class Cotangent:
        got = None

    def send_cotangent(flight):
        flight.send(jnp.where(left, cotangent[0, 1], cotangent[0, 0]), "col", Cotangent, "got")

    quarter = head // 4
    lanes = tie(jnp.arange(width), flight.token)
    within = lanes % head
    section = within // quarter
    lane_freq = jnp.exp(-math.log(10000.0) * (within % quarter).astype(full) / quarter)
    row_pos = (row * grid_rows + jnp.arange(grid_rows)).astype(full)
    col_pos = jnp.arange(grid_cols).astype(full)
    row_angle = row_pos[:, None] * lane_freq[None, :]
    col_angle = col_pos[:, None] * lane_freq[None, :]
    by_row = section < 2
    sign = jnp.where(section % 2 == 0, -1.0, 1.0).astype(full)

    def table(fun):
        return jnp.where(by_row, fun(row_angle)[:, None, :], fun(col_angle)[None, :, :]).reshape(tokens, width)

    cosine = table(jnp.cos)
    sine = table(jnp.sin) * sign
    member = (lanes[:, None] // head == jnp.arange(128)[None, :]).astype(low)
    tabs = (cosine, sine, member, member.T, head)
    gain_rows = jnp.tile(qk_gains.astype(full), (1, 1, heads))
    even = jnp.broadcast_to((section % 2 == 0).astype(full), (2, 1, width))
    temper = head ** (-0.5) * math.log2(math.e)
    scaled = jnp.concatenate([gain_rows[:, :1] * temper, gain_rows[:, 1:], even], axis=1)
    gain_rows = jnp.concatenate([gain_rows, even], axis=1)
    gain_rows = [(scaled[k], gain_rows[k]) for k in range(2)]

    rest = list(range(2, bits))
    path_y = ["row", "col", 0, 1] + rest
    path_x = ["row", 0, "col", 1] + rest
    path_z = ["row", 1, "col", 0] + rest
    path_w = ["row", 1, 0, "col"] + rest
    paths = {"down": path_z, "gate": path_y, "up": path_x, "out": path_x, "qkv": path_y, "ada": path_y}
    perm = {}
    orders = {}
    for name in ("gate", "up", "out", "qkv", "ada"):
        key = tuple(paths[name])
        if key not in perm:
            source = halving_order(paths[name], width, own_rows, me)
            perm[key] = lax.optimization_barrier((source[:, None] == lanes[None, :]).astype(low))
        orders[name] = perm[key]

    enc_h0 = matmul(enc_patches, patch_w[0]) + patch_b[0]
    starts = [b_q0.relay, b_kv0.relay, b_out0.over_col, b_q0.first_row, b_kv0.first_row]
    enc_h0, part, cosine, sine = flight.fence([enc_h0, part, cosine, sine], starts)
    part = part + swap(part, "row")
    part = part + swap(part, "col")
    enc_mod = part + ada_b[0]
    enc_mods = [enc_mod[k : k + 1] for k in range(6)]
    tabs = (cosine, sine) + tabs[2:]
    points = {
        "qkv": [b_q0.second_row, b_kv0.second_row, b_gate0.over_col, b_out0.relay],
        "attend": [b_up0.over_col, b_gate0.relay, b_out0.first_row],
        "out": [b_out0.second_row, b_up0.relay, b_down0.over_col, b_gate0.rows_both],
        "gate": [b_up0.rows_both, b_ada_a.over_col, b_down0.relay],
        "down": [b_down0.rows_both, b_qkv1.over_col, b_ada_a.relay],
    }
    encoded, enc_cache, enc_mats = block_forward(enc_h0, enc_mods, enc_mats, gain_rows[0], tabs, flight, points)
    dec_h0 = matmul(dec_patches, patch_w[1]) + patch_b[1]
    cond = encoded + temb_own
    dec_sil = jax.nn.silu(cond).astype(low)
    (dec_sil,) = flight.fence([dec_sil], [b_ada_a.rows_both, b_ada_b.over_col, b_qkv1.relay])
    ada_bias1 = ada_b[1].reshape(1, 6 * width)
    mod_a = ada_matmul(dec_sil, weight_of("ada", b_ada_a), ada_bias1[:, : 3 * width])
    dec_mods = [Cols(mod_a, k * width, width) for k in range(3)]
    held = Sum()

    def second_mods(flight):
        held.value = ada_matmul(tie(dec_sil, flight.token), weight_of("ada", b_ada_b), ada_bias1[:, 3 * width :])
        flight.watch(held, "value")

    dec_mods += [Cols(held, k * width, width) for k in range(3)]
    points = {
        "qkv": [b_qkv1.rows_both, b_og1.over_col, b_ada_b.relay],
        "attend": [b_ada_b.rows_both, second_mods, b_up1.over_col, b_og1.relay],
        "out": [b_og1.rows_both, b_down1.over_col, b_up1.relay],
        "gate": [b_up1.rows_both, b_down1.relay, send_cotangent],
        "down": [b_down1.rows_both],
    }
    decoded, dec_cache, dec_mats = block_forward(dec_h0, dec_mods, dec_mats, gain_rows[1], tabs, flight, points)
    live = (col < levels[0]).astype(full)
    result = (decoded * live).astype(low).reshape(grid_rows, grid_cols, width)
    near = jnp.where(left, result[:, :half_cols], result[:, half_cols:])
    far = jnp.where(left, result[:, half_cols:], result[:, :half_cols])

    class Away:
        got = None

    def send_result(flight):
        flight.send(far, "col", Away, "got")


    agenda = Agenda()
    go = agenda.go
    comm = (flight, agenda, orders, paths, coords)
    cot = pair(cot_own, Cotangent.got, 1).reshape(tokens, width)
    dec_grad2 = cot.astype(full) * live
    plan = {
        "start": [send_result],
        "gate": [go("da1"), go("db1")],
        "out": [go("da1"), go("db1")],
        "attend": [go("g1"), go("u1")],
        "qk": [go("g1"), go("u1"), go("da1", "db1")],
        "qkv": [go("o1"), go("da1", "db1"), go("g1", "u1")],
    }
    dec_grad0, dec_dmods, dec_gains, begin_halves = block_backward(
        dec_grad2, dec_cache, dec_mods, dec_mats, gain_rows[1], tabs, comm, "1", plan
    )
    away = Away.got
    result = jnp.stack([jnp.where(left, near, away), jnp.where(left, away, near)])[None]
    dec_dmods = [piece.astype(low) for piece in dec_dmods]
    dec_dmods = flight.fence(dec_dmods, [go("qa1"), go("qb1"), go("o1"), go("g1", "u1")])
    r_ada = row_sum(ordered_grad(dec_sil, orders["ada"], dec_dmods, width))
    dec_bada = jnp.stack([jnp.sum(piece.astype(full), axis=0) for piece in dec_dmods])
    enc_grad2 = ada_back(dec_dmods, weight_of("ada", b_ada_a, b_ada_b), cond)

    def patch_rows(patch, grad):
        ones = jnp.ones((tokens, 1), low)
        return outer_sum(jnp.concatenate([patch, ones], axis=1), grad)

    total = jnp.concatenate([patch_rows(dec_patches, dec_grad0), dec_bada, dec_gains], axis=0)
    agenda.tasks["s"] = Total(total, ["row", "col"] + list(range(bits)))

    def begin_ada(flight):
        begin_halves("ada", r_ada, r_ada.shape[1] // 2)

    plan = {
        "start": [go("qa1"), go("qb1"), go("s"), begin_ada],
        "gate": [go("aa1"), go("ab1"), go("d0")],
        "out": [go("s"), go("aa1"), go("ab1"), go("qa1", "qb1", "o1")],
        "attend": [go("s"), go("g0"), go("u0"), go("aa1", "ab1")],
        "qk": [go("s"), go("g0"), go("u0"), go("qa1", "qb1", "o1")],
        "qkv": [go("s"), go("d0"), go("o0"), go("aa1", "ab1")],
    }
    enc_grad0, enc_dmods, enc_gains, _ = block_backward(
        enc_grad2, enc_cache, enc_mods, enc_mats, gain_rows[0], tabs, comm, "0", plan
    )
    dmod_enc = jnp.concatenate(enc_dmods, axis=0)
    total = jnp.concatenate([patch_rows(enc_patches, enc_grad0), enc_gains, dmod_enc], axis=0)
    total, enc_grad0 = flight.fence([total, enc_grad0], [go("qa0"), go("qb0"), go("o0"), go("g0", "u0")])
    total = total + swap(total, "row")
    total = total + swap(total, "col")
    count = pvals + 3
    tiny = TotalAndRows(jnp.concatenate([total, sil0.astype(full)], axis=0), count, list(range(bits)))
    agenda.tasks["t"] = tiny
    flight.watch(tiny, "value")
    flight.fence([total], [go("t"), go("qa0"), go("qb0"), go("d0"), go("g0", "u0")])
    flight.fence([total], [go("t"), go("qa0", "qb0", "o0"), go("d0")])
    flight.fence([total], [go("t"), go("qa0", "qb0", "o0")])
    flight.fence([total])
    while any(task.path for task in agenda.tasks.values()):
        flight.fence([total], [go(name) for name, task in agenda.tasks.items() if task.path])
        flight.fence([total])
    dec_small = agenda.tasks["s"].value
    total = tiny.value[:count]
    dmod_all = tiny.value[count:]
    dmod_all = dmod_all.reshape(n_data, 7, width)
    enc_small = total
    enc_ada = jnp.dot(
        lax.dynamic_slice(dmod_all, (0, 6, me * own_rows), (n_data, 1, own_rows))[:, 0].T,
        dmod_all[:, :6].reshape(n_data, 6 * width),
        precision=highest,
        preferred_element_type=full,
    )
    enc_bada = jnp.sum(dmod_all[:, :6], axis=0)

    def image(dpatch):
        return (
            dpatch.reshape(grid_rows, grid_cols, chans, 2, 2).transpose(2, 0, 3, 1, 4).reshape(chans, rows_loc, 2 * cols_loc)
        )

    enc_image = image(matmul_t(enc_grad0, patch_w[0]))
    dec_image = image(matmul_t(dec_grad0, patch_w[1]))
    zero = jnp.zeros_like(dec_image)
    grads = jnp.stack([enc_image + jnp.where(left, dec_image, zero), jnp.where(left, zero, dec_image)])
    grads = jnp.concatenate([grads[..., 1:], grads[..., :1]], axis=3)
    below = swap(grads[:, :, :1], "row")
    grads = jnp.concatenate([grads[:, :, 1:], below], axis=2)
    one = grads[..., :cols_loc]
    two = grads[..., cols_loc:]
    latent_grad = (jnp.where(left, one, two) + swap(jnp.where(left, two, one), "col"))[None]

    def own_lanes(value):
        return lax.dynamic_slice(value, (0, me * own_rows), (value.shape[0], own_rows))

    enc_patch = own_lanes(enc_small[: pvals + 1])
    dec_patch = own_lanes(dec_small[: pvals + 1])
    g_patch = jnp.stack([enc_patch[:pvals].T, dec_patch[:pvals].T])
    g_patch_b = jnp.stack([enc_patch[pvals], dec_patch[pvals]])
    bada = jnp.stack([enc_bada.reshape(-1), dec_small[pvals + 1 : pvals + 7].reshape(-1)])
    own_bada = 6 * own_rows
    g_bada = lax.dynamic_slice(bada, (0, me * own_bada), (2, own_bada))
    gains = jnp.stack([enc_small[pvals + 1 :], dec_small[pvals + 7 :]])
    gains = gains.reshape(2, 2, heads, head).sum(axis=2)
    def both(name):
        parts = [agenda.tasks[name + tag].value.astype(full) for tag in "01"]
        return jnp.stack(parts)

    for task in agenda.tasks.values():
        assert not task.path
    g_ada = jnp.concatenate([agenda.tasks["aa1"].value, agenda.tasks["ab1"].value], axis=1)
    g_ada_all = jnp.stack([enc_ada, g_ada.astype(full)])
    g_qkv = jnp.concatenate([both("qa"), both("qb")], axis=2)
    down1 = jnp.concatenate([agenda.tasks["da1"].value, agenda.tasks["db1"].value], axis=1)
    g_down = jnp.stack([agenda.tasks["d0"].value.astype(full), down1.astype(full)])
    stacked = [g_qkv, both("o"), both("g"), both("u"), g_down]
    return (
        result,
        latent_grad,
        g_patch,
        g_patch_b,
        g_ada_all,
        g_bada,
        stacked[0],
        gains,
        stacked[1],
        stacked[2],
        stacked[3],
        stacked[4],
    )


def solution(mesh):
    tile = ("row", "col")
    every = ("dp", "row", "col")
    return jax.shard_map(
        per_device,
        mesh=mesh,
        in_specs=(
            P("dp", None, None, "row", "col"),
            P("dp"),
            P("dp", None),
            P(None, tile, None),
            P(None, tile),
            P(None, tile, None),
            P(None, tile),
            P(None, tile, None),
            P(),
            P(None, tile, None),
            P(None, tile, None),
            P(None, tile, None),
            P(None, tile, None),
            P("dp", None, "row", "col", None),
        ),
        out_specs=(
            P("dp", None, "row", "col", None),
            P("dp", None, None, "row", "col"),
            P(None, every, None),
            P(None, every),
            P(None, every, None),
            P(None, every),
            P(None, every, None),
            P(),
            P(None, every, None),
            P(None, every, None),
            P(None, every, None),
            P(None, every, None),
        ),
        check_vma=False,
    )
```

```python
import functools
import math

import jax
import jax.numpy as jnp
from jax import lax
from jax.experimental import pallas as pl
from jax.experimental.pallas import tpu as pltpu
from jax.sharding import PartitionSpec as P

epsilon = 1e-06
highest = lax.Precision.HIGHEST
low = jnp.bfloat16
full = jnp.float32
WINDOW = 256
MIB = 1 << 20


def matmul(left, right):
    return jnp.dot(left, right, preferred_element_type=full)


def matmul_t(left, right):
    return lax.dot_general(left, right, (((1,), (1,)), ((), ())), preferred_element_type=full)


def outer_sum(left, right):
    return lax.dot_general(left, right, (((0,), (0,)), ((), ())), preferred_element_type=full)


def rms_scale(value):
    return lax.rsqrt(jnp.mean(value * value, axis=-1, keepdims=True) + epsilon)


def rms_back(value, inverse, grad):
    return inverse * grad - value * inverse**3 * jnp.mean(value * grad, axis=-1, keepdims=True)


def swap(value, item):
    if isinstance(item, str):
        return lax.ppermute(value, item, [(0, 1), (1, 0)])
    size = lax.axis_size("dp")
    return lax.ppermute(value, "dp", [(i, i ^ (1 << item)) for i in range(size)])


def time_features(steps, width):
    half = width // 2
    freqs = jnp.exp(-math.log(10000.0) * jnp.arange(half).astype(full) / half)
    angles = steps.astype(full)[:, None] * freqs[None, :]
    return jnp.concatenate([jnp.cos(angles), jnp.sin(angles)], axis=-1)


def whole(shape):
    return pl.BlockSpec(shape, lambda *_: (0,) * len(shape))


def params(mib):
    return pltpu.CompilerParams(vmem_limit_bytes=mib * MIB)


def head_mean(value, member, head):
    return matmul(value.astype(low), member) * (1.0 / head)


def split_dot(value, onehot):
    top = value.astype(low)
    rest = (value - top.astype(full)).astype(low)
    return matmul(top, onehot) + matmul(rest, onehot)


def turned(value, cosine, sine, even, quarter):
    width = value.shape[-1]
    ahead = pltpu.roll(value, width - quarter, axis=1)
    behind = pltpu.roll(value, quarter, axis=1)
    return value * cosine + jnp.where(even, ahead, behind) * sine


def even_lanes(gain_ref, shape):
    return jnp.broadcast_to(gain_ref[2:3, :] > 0.5, shape)


def qk_back_body(head, dq_ref, dkv_ref, dkvx_ref, qkv_ref, cos_ref, sin_ref, gain_ref, mem_ref, memt_ref, out_ref, gg_ref):
    width = dq_ref.shape[-1]

    @pl.when(pl.program_id(0) == 0)
    def _():
        gg_ref[...] = jnp.zeros_like(gg_ref)

    cosine = cos_ref[...]
    sine = -sin_ref[...]
    even = even_lanes(gain_ref, cosine.shape)
    member = mem_ref[...]
    member_t = memt_ref[...]
    grads = (dq_ref[...], dkv_ref[:, :width] + dkvx_ref[:, :width].astype(full))
    for part in (0, 1):
        value = qkv_ref[:, part * width : (part + 1) * width]
        mean = head_mean(value * value, member, head)
        inverse_h = lax.rsqrt(mean + epsilon)
        inverse = split_dot(inverse_h, member_t)
        grad_n = turned(grads[part], cosine, sine, even, head // 4)
        normed = value * inverse
        gg_ref[part : part + 1, :] += jnp.sum(grad_n * normed, axis=0, keepdims=True)
        weighted = grad_n * gain_ref[part : part + 1, :]
        dots = head_mean(value * weighted, member, head) * inverse_h * inverse_h
        back = inverse * weighted - normed * split_dot(dots, member_t)
        out_ref[:, part * width : (part + 1) * width] = back.astype(low)
    out_ref[:, 2 * width :] = (dkv_ref[:, width:] + dkvx_ref[:, width:].astype(full)).astype(low)


def qk_back(dq, dkv, dkvx, raw, cosine, sine, gains, member, member_t, head):
    tokens, width = dq.shape
    step = 256
    rows = lambda n: pl.BlockSpec((step, n), lambda i: (i, 0))
    return pl.pallas_call(
        functools.partial(qk_back_body, head),
        grid=(tokens // step,),
        in_specs=[rows(width)]
        + [rows(2 * width)] * 3
        + [rows(width), rows(width), whole(gains.shape), whole(member.shape), whole(member_t.shape)],
        out_specs=[rows(3 * width), whole((8, width))],
        out_shape=[jax.ShapeDtypeStruct((tokens, 3 * width), low), jax.ShapeDtypeStruct((8, width), full)],
        compiler_params=params(60),
        cost_estimate=pl.CostEstimate(flops=60 * raw.size, bytes_accessed=18 * raw.size, transcendentals=0),
        name="qk_back",
    )(dq, dkv, dkvx, raw, cosine, sine, gains, member, member_t)


def head_window(head, width):
    index = pl.program_id(0)
    start = index * head
    base = jnp.minimum(lax.div(start, 128) * 128, width - WINDOW)
    return index, pl.multiple_of(base, 128), start - base


def window_mask(shape, offset, head):
    lane = lax.broadcasted_iota(jnp.int32, shape, 1)
    return jnp.logical_and(lane >= offset, lane < offset + head)


def attend_body(head, q_ref, kvl_ref, kvr_ref, o_ref, lse_ref, acc_ref):
    tokens, width = q_ref.shape
    index, base, offset = head_window(head, width)
    cols = pl.ds(base, WINDOW)
    vals = pl.ds(pl.multiple_of(width + base, 128), WINDOW)

    @pl.when(index == 0)
    def _():
        acc_ref[...] = jnp.zeros_like(acc_ref)
        lse_ref[...] = jnp.zeros_like(lse_ref)

    step = 256
    mask_k = window_mask((tokens, WINDOW), offset, head)
    one = jnp.ones((), low)
    value_l = jnp.where(mask_k, kvl_ref[:, vals], one)
    value_r = jnp.where(mask_k, kvr_ref[:, vals], one)
    mask = window_mask((step, WINDOW), offset, head)
    lane = lax.broadcasted_iota(jnp.int32, (step, lse_ref.shape[1]), 1)
    for first in range(0, tokens, step):
        rows = slice(first, first + step)
        query = jnp.where(mask, q_ref[rows, cols], jnp.zeros((), low))
        left = jnp.exp2(matmul_t(query, kvl_ref[:, cols])).astype(low)
        right = jnp.exp2(matmul_t(query, kvr_ref[:, cols])).astype(low)
        out = matmul(left, value_l) + matmul(right, value_r)
        total = jnp.max(jnp.where(mask, 0.0, out), axis=1, keepdims=True)
        acc_ref[rows, cols] += jnp.where(mask, out * (1.0 / total), 0.0)
        lse_ref[rows, :] += jnp.where(lane == index, jnp.log2(total), 0.0)

    @pl.when(index == pl.num_programs(0) - 1)
    def _():
        o_ref[...] = acc_ref[...].astype(low)


def attend(query, kv_l, kv_r, head):
    tokens, width = query.shape
    heads = width // head
    return pl.pallas_call(
        functools.partial(attend_body, head),
        grid=(heads,),
        in_specs=[whole((tokens, width))] + [whole((tokens, 2 * width))] * 2,
        out_specs=[whole((tokens, width)), whole((tokens, 128))],
        out_shape=[jax.ShapeDtypeStruct((tokens, width), low), jax.ShapeDtypeStruct((tokens, 128), full)],
        scratch_shapes=[pltpu.VMEM((tokens, width), full)],
        compiler_params=params(56),
        cost_estimate=pl.CostEstimate(
            flops=8 * tokens * tokens * WINDOW * heads, bytes_accessed=14 * tokens * width, transcendentals=2 * tokens * tokens * heads
        ),
        name="attend",
    )(query, kv_l, kv_r)


def in_three(column):
    top = column.astype(low)
    rest = column - top.astype(full)
    middle = rest.astype(low)
    return top, middle, (rest - middle.astype(full)).astype(low)


def attend_back_body(head, q_ref, kvl_ref, kvr_ref, do_ref, o_ref, lse_ref, dq_ref, dl_ref, dr_ref, dr_acc):
    tokens, width = q_ref.shape
    index, base, offset = head_window(head, width)
    cols = pl.ds(base, WINDOW)
    vals = pl.ds(pl.multiple_of(width + base, 128), WINDOW)
    temper = head ** (-0.5)

    @pl.when(index == 0)
    def _():
        for ref in (dq_ref, dl_ref, dr_acc):
            ref[...] = jnp.zeros_like(ref)

    shape = (tokens, WINDOW)
    mask = window_mask(shape, offset, head)
    lane = lax.broadcasted_iota(jnp.int32, shape, 1)
    spare = jnp.where(offset >= 3, 0, WINDOW - 3)
    zero = jnp.zeros((), low)
    minus = jnp.where(jnp.logical_and(lane >= spare, lane < spare + 3), -jnp.ones((), low), zero)
    query = jnp.where(mask, q_ref[:, cols], zero)
    grad = jnp.where(mask, do_ref[:, cols], zero)
    delta = jnp.sum(grad.astype(full) * o_ref[:, cols].astype(full), axis=1, keepdims=True)
    small = lax.broadcasted_iota(jnp.int32, lse_ref.shape, 1)
    level = jnp.sum(jnp.where(small == index, lse_ref[...], 0.0), axis=1, keepdims=True)
    query_x = query
    grad_x = grad
    for k, (a, b) in enumerate(zip(in_three(level), in_three(delta))):
        at = lane == spare + k
        query_x = jnp.where(at, a, query_x)
        grad_x = jnp.where(at, b, grad_x)
    grad_q = 0.0
    for ref, acc in ((kvl_ref, dl_ref), (kvr_ref, dr_acc)):
        key = jnp.where(mask, ref[:, cols], minus)
        value = jnp.where(mask, ref[:, vals], minus)
        prob = jnp.exp2(matmul_t(key, query_x))
        grad_s = (prob * matmul_t(value, grad_x)).astype(low)
        acc[:, vals] += matmul(prob.astype(low), grad)
        acc[:, cols] += matmul(grad_s, query)
        grad_q = grad_q + outer_sum(grad_s, key)
    dq_ref[:, cols] += jnp.where(mask, grad_q * temper, 0.0)

    @pl.when(index == pl.num_programs(0) - 1)
    def _():
        back = math.log(2.0)
        dl_ref[:, :width] = dl_ref[:, :width] * back
        dr_ref[:, :width] = (dr_acc[:, :width] * back).astype(low)
        dr_ref[:, width:] = dr_acc[:, width:].astype(low)


def attend_back(query, kv_l, kv_r, grad, out, levels, head):
    tokens, width = query.shape
    heads = width // head
    both = (tokens, 2 * width)
    one = (tokens, width)
    return pl.pallas_call(
        functools.partial(attend_back_body, head),
        grid=(heads,),
        in_specs=[whole(one), whole(both), whole(both), whole(one), whole(one), whole(levels.shape)],
        out_specs=[whole(one), whole(both), whole(both)],
        out_shape=[like(one, full), like(both, full), like(both, low)],
        scratch_shapes=[pltpu.VMEM(both, full)],
        compiler_params=params(62),
        cost_estimate=pl.CostEstimate(
            flops=20 * tokens * tokens * WINDOW * heads, bytes_accessed=28 * tokens * width, transcendentals=2 * tokens * tokens * heads
        ),
        name="attend_back",
    )(query, kv_l, kv_r, grad, out, levels)


class Weight:
    def __init__(self, segments):
        self.segments = segments
        self.columns = sum(columns for _, _, columns in segments)
        self.plan = [piece[1:] for piece in segments[0][1]]
        self.height = sum(rows for _, _, rows in self.plan)
        for _, pieces, _ in segments:
            assert [piece[3] for piece in pieces] == [rows for _, _, rows in self.plan]


def piece_source(ref, lead, first, count):
    for index in lead:
        ref = ref.at[index]
    return ref.at[:, pl.ds(first, count)]


class Cols:
    def __init__(self, array, first, count):
        self.source = array
        self.first = first
        self.count = count

    @property
    def array(self):
        return self.source if isinstance(self.source, jax.Array) else self.source.value

    @property
    def shape(self):
        return (self.array.shape[0], self.count)

    @property
    def dtype(self):
        return self.array.dtype

    @property
    def size(self):
        return self.array.shape[0] * self.count

    def value(self):
        return self.array[:, self.first : self.first + self.shape[1]]


def plain(value):
    return value.value() if isinstance(value, Cols) else value


def anywhere(count):
    return [pl.BlockSpec(memory_space=pl.ANY)] * count


class Stream:
    def __init__(self, weights, tile, late):
        self.weights = weights
        self.tile = tile
        self.late = late
        self.steps = weights[0].columns // tile

    def pieces_of(self):
        return [pieces for w in self.weights for _, pieces, _ in w.segments]

    def specs(self):
        return [pl.BlockSpec(memory_space=pltpu.SMEM)] + anywhere(sum(len(p) for p in self.pieces_of()) + len(self.late))

    def operands(self):
        offsets = jnp.concatenate([offs for w in self.weights for offs, _, _ in w.segments])
        arrays = [piece[0] for pieces in self.pieces_of() for piece in pieces]
        return [offsets] + arrays + [v.array if isinstance(v, Cols) else v for v in self.late]

    def scratch(self):
        shapes = []
        for w in self.weights:
            shapes += [pltpu.VMEM((2, w.height, self.tile), low), pltpu.SemaphoreType.DMA((2, len(w.plan)))]
        for value in self.late:
            shapes += [pltpu.VMEM(value.shape, value.dtype), pltpu.SemaphoreType.DMA((1,))]
        return shapes

    def bind(self, operand_refs, scratch_refs):
        self.offs = operand_refs[0]
        refs = list(operand_refs[1:])
        self.refs = []
        for w in self.weights:
            mine = []
            for _, pieces, _ in w.segments:
                mine.append(refs[: len(pieces)])
                refs = refs[len(pieces) :]
            self.refs.append(mine)
        self.buffers = scratch_refs[0 : 2 * len(self.weights) : 2]
        self.sems = scratch_refs[1 : 2 * len(self.weights) : 2]
        rest = scratch_refs[2 * len(self.weights) :]
        self.late_bufs = rest[0::2]
        self.late_copies = []
        for value, ref, buf, sem in zip(self.late, refs, rest[0::2], rest[1::2]):
            if isinstance(value, Cols):
                ref = ref.at[:, pl.ds(value.first, value.shape[1])]
            self.late_copies.append(pltpu.make_async_copy(ref, buf, sem.at[0]))

    def segment_copies(self, index, number, column, slot):
        w = self.weights[index]
        base = sum(len(x.plan) * len(x.segments) for x in self.weights[:index]) + number * len(w.plan)
        out = []
        for at, (_, lead, first, rows) in enumerate(w.segments[number][1]):
            source = piece_source(self.refs[index][number][at], lead, pl.multiple_of(first + column, 128), self.tile)
            start = pl.multiple_of(self.offs[base + at], 16)
            target = self.buffers[index].at[slot, pl.ds(start, rows), :]
            out.append(pltpu.make_async_copy(source, target, self.sems[index].at[slot, at]))
        return out

    def copies(self, step, slot):
        return [copy for index in range(len(self.weights)) for copy in self.segment_copies(index, 0, step * self.tile, slot)]

    def start_tile(self, step, slot):
        for index, w in enumerate(self.weights):
            first = 0
            for number, (_, _, columns) in enumerate(w.segments):
                count = columns // self.tile

                def start():
                    for copy in self.segment_copies(index, number, (step - first) * self.tile, slot):
                        copy.start()

                if len(w.segments) == 1:
                    start()
                else:
                    pl.when(jnp.logical_and(step >= first, step < first + count))(start)
                first += count

    def wait_tile(self, slot):
        for index in range(len(self.weights)):
            for copy in self.segment_copies(index, 0, 0, slot):
                copy.wait()

    def advance(self):
        step = pl.program_id(0)
        slot = lax.rem(step, 2)

        @pl.when(step == 0)
        def _():
            self.start_tile(jnp.int32(0), 0)
            for copy in self.late_copies:
                copy.start()

        @pl.when(step + 1 < self.steps)
        def _():
            self.start_tile(step + 1, 1 - slot)

        self.wait_tile(slot)
        return step, [buf.at[slot] for buf in self.buffers]

    def wait_late(self):
        for copy in self.late_copies:
            copy.wait()
        return self.late_bufs


def stream_call(name, stream, body, ins, in_specs, outs, out_specs, scratch, flops, mib=58):
    operands = stream.operands()
    frame = stream.scratch()

    def kernel(*refs):
        count = len(operands)
        ops, refs = refs[:count], refs[count:]
        inputs, refs = refs[: len(ins)], refs[len(ins) :]
        outputs, refs = refs[: len(outs)], refs[len(outs) :]
        stream.bind(ops, refs[: len(frame)])
        body(stream, inputs, outputs, refs[len(frame) :])

    moved = sum(v.size * v.dtype.itemsize for v in list(ins) + list(stream.late) + list(outs))
    moved += sum(2 * w.height * w.columns for w in stream.weights)
    return pl.pallas_call(
        kernel,
        grid=(stream.steps,),
        in_specs=stream.specs() + in_specs,
        out_specs=out_specs,
        out_shape=outs,
        scratch_shapes=frame + scratch,
        compiler_params=params(mib),
        cost_estimate=pl.CostEstimate(flops=flops, bytes_accessed=moved, transcendentals=0),
        name=name,
    )(*operands, *ins)


def by_rows(tokens, fun, step=128):
    @pl.loop(0, tokens // step)
    def _(i):
        fun(pl.ds(pl.multiple_of(i * step, step), step))


def take(ref, rows):
    return ref[rows, :] if ref.shape[0] > 1 else ref[...]


def give(ref, rows, value):
    if ref.shape[0] > 1:
        ref[rows, :] = value.astype(ref.dtype)
    else:
        ref[...] += jnp.sum(value, axis=0, keepdims=True)


def like(shape, dtype):
    return jax.ShapeDtypeStruct(shape, dtype)


def ada_matmul(value, weight, bias):
    tokens = value.shape[0]
    tile = weight.height
    stream = Stream([weight], tile, [])

    def body(stream, ins, outs, scratch):
        _, (w,) = stream.advance()
        outs[0][...] = matmul(ins[0][...], w[...]) + ins[1][...]

    return stream_call(
        "ada",
        stream,
        body,
        [value, bias],
        [whole(value.shape), pl.BlockSpec((1, tile), lambda j: (0, j))],
        [like((tokens, weight.columns), full)],
        [pl.BlockSpec((tokens, tile), lambda j: (0, j))],
        [],
        2 * tokens * weight.height * weight.columns,
    )[0]


def mod_partial(row, weight, width):
    shard = weight.shape[1]
    tall = jnp.broadcast_to(row, (16, shard))

    def body(x_ref, w_ref, out_ref):
        out_ref[0] = matmul(x_ref[...], w_ref[...])[:8]

    out = pl.pallas_call(
        body,
        grid=(6,),
        in_specs=[whole(tall.shape), pl.BlockSpec((None, shard, width), lambda j: (0, 0, j))],
        out_specs=pl.BlockSpec((1, 8, width), lambda j: (j, 0, 0)),
        out_shape=like((6, 8, width), full),
        compiler_params=params(60),
        cost_estimate=pl.CostEstimate(flops=0, bytes_accessed=12 * shard * width, transcendentals=0),
        name="modpart",
    )(tall, weight)
    return out[:, 0]


def qkv_matmul(value, weight, cosine, sine, gains, member, member_t, head):
    tokens, width = value.shape
    stream = Stream([weight], width, [cosine, sine])

    def body(stream, ins, outs, scratch):
        x_ref, gain_ref, mem_ref, memt_ref = ins
        q_ref, kv_ref, raw_ref = outs
        (acc_ref,) = scratch
        step, (w,) = stream.advance()
        cos_ref, sin_ref = stream.late_bufs
        acc_ref[...] = matmul(x_ref[...], w[...])

        @pl.when(step == 0)
        def _():
            stream.wait_late()

        def head_norm(part, out, cols):
            def rows_of(rows):
                raw = acc_ref[rows, :]
                raw_ref[rows, :] = raw
                mean = head_mean(raw * raw, mem_ref[...], head)
                inverse = split_dot(lax.rsqrt(mean + epsilon), memt_ref[...])
                normed = raw * inverse * gain_ref[part : part + 1, :]
                even = even_lanes(gain_ref, raw.shape)
                out[rows, cols] = turned(normed, cos_ref[rows, :], sin_ref[rows, :], even, head // 4).astype(low)

            by_rows(tokens, rows_of, 256)

        @pl.when(step == 0)
        def _():
            head_norm(0, q_ref, slice(0, width))

        @pl.when(step == 1)
        def _():
            head_norm(1, kv_ref, slice(0, width))

        @pl.when(step == 2)
        def _():
            kv_ref[:, width:] = acc_ref[...].astype(low)

    flat = like((tokens, width), low)
    return stream_call(
        "qkv",
        stream,
        body,
        [value, gains, member, member_t],
        [whole(v.shape) for v in (value, gains, member, member_t)],
        [flat, like((tokens, 2 * width), low), like((tokens, 2 * width), full)],
        [whole((tokens, width)), whole((tokens, 2 * width)), pl.BlockSpec((tokens, width), lambda j: (0, jnp.minimum(j, 1)))],
        [pltpu.VMEM((tokens, width), full)],
        2 * tokens * weight.height * weight.columns,
    )


def out_matmul(value, weight, hidden0, mods):
    tokens, width = value.shape
    stream = Stream([weight], 384, [hidden0] + mods)

    def body(stream, ins, outs, scratch):
        att_ref, h1_ref, b_ref = outs
        (acc_ref,) = scratch
        step, (w,) = stream.advance()
        acc_ref[step] = matmul(ins[0][...], w[...])

        @pl.when(step == stream.steps - 1)
        def _():
            h0_ref, gate_ref, shift_ref, scale_ref = stream.wait_late()

            def rows_of(rows):
                att = jnp.concatenate([acc_ref[k, rows, :] for k in range(stream.steps)], axis=1)
                hidden1 = h0_ref[rows, :] + take(gate_ref, rows) * att
                normed = hidden1 * rms_scale(hidden1)
                att_ref[rows, :] = att.astype(low)
                h1_ref[rows, :] = hidden1
                b_ref[rows, :] = (normed * (1.0 + take(scale_ref, rows)) + take(shift_ref, rows)).astype(low)

            by_rows(tokens, rows_of)

    return stream_call(
        "attout",
        stream,
        body,
        [value],
        [whole(value.shape)],
        [like((tokens, width), low), like((tokens, width), full), like((tokens, width), low)],
        [whole((tokens, width))] * 3,
        [pltpu.VMEM((stream.steps, tokens, 384), full)],
        2 * tokens * weight.height * weight.columns,
    )


def gate_up_matmul(value, gate, up):
    tokens, width = value.shape
    tile = 1024
    stream = Stream([gate, up], tile, [])

    def body(stream, ins, outs, scratch):
        hid_ref, g_ref, u_ref = outs
        _, (wg, wu) = stream.advance()
        g = matmul(ins[0][...], wg[...])
        u = matmul(ins[0][...], wu[...])
        g_ref[...] = g.astype(low)
        u_ref[...] = u.astype(low)
        hid_ref[...] = (g * jax.nn.sigmoid(g) * u).astype(low)

    flat = like((tokens, gate.columns), low)
    return stream_call(
        "gateup",
        stream,
        body,
        [value],
        [whole(value.shape)],
        [flat] * 3,
        [pl.BlockSpec((tokens, tile), lambda j: (0, j))] * 3,
        [],
        4 * tokens * gate.height * gate.columns,
    )


def down_matmul(value, weight, hidden1, gate):
    tokens, depth = value.shape
    width = weight.columns
    stream = Stream([weight], width, [hidden1, gate])

    def body(stream, ins, outs, scratch):
        mlp_ref, h2_ref = outs
        (acc_ref,) = scratch
        hid_ref = ins[0]
        at = 0
        copies = stream.copies(0, 0)
        for copy in copies + stream.late_copies:
            copy.start()
        for k, (_, _, rows) in enumerate(weight.plan):
            copies[k].wait()
            first = stream.offs[k]
            left = hid_ref[:, pl.ds(pl.multiple_of(first, 128), rows)]
            part = matmul(left, stream.buffers[0][0, pl.ds(pl.multiple_of(first, 128), rows), :])
            if k == 0:
                acc_ref[...] = part
            else:
                acc_ref[...] += part
        h1_ref, gate_ref = stream.wait_late()

        def rows_of(rows):
            mlp = acc_ref[rows, :]
            mlp_ref[rows, :] = mlp.astype(low)
            h2_ref[rows, :] = h1_ref[rows, :] + take(gate_ref, rows) * mlp

        by_rows(tokens, rows_of)

    return stream_call(
        "down",
        stream,
        body,
        [value],
        [whole(value.shape)],
        [like((tokens, width), low), like((tokens, width), full)],
        [whole((tokens, width))] * 2,
        [pltpu.VMEM((tokens, width), full)],
        2 * tokens * depth * width,
    )


def down_back(grad, weight, gate_pre, up_pre):
    tokens, width = grad.shape
    depth = weight.height
    stream = Stream([weight], width, [gate_pre, up_pre])

    def body(stream, ins, outs, scratch):
        dg_ref, du_ref = outs
        copies = stream.copies(0, 0)
        for copy in copies + stream.late_copies:
            copy.start()
        for k, (_, _, count) in enumerate(weight.plan):
            copies[k].wait()
            if k == 0:
                g_ref, u_ref = stream.wait_late()
            first = pl.multiple_of(stream.offs[k], 128)
            for at in range(0, count, 384):
                cols = pl.ds(pl.multiple_of(first + at, 128), 384)
                inner = matmul_t(ins[0][...], stream.buffers[0][0, cols, :])
                g = g_ref[:, cols].astype(full)
                u = u_ref[:, cols].astype(full)
                sigma = jax.nn.sigmoid(g)
                active = g * sigma
                dg_ref[:, cols] = (inner * u * (sigma + active * (1.0 - sigma))).astype(low)
                du_ref[:, cols] = (inner * active).astype(low)

    flat = like((tokens, depth), low)
    return stream_call(
        "downback",
        stream,
        body,
        [grad],
        [whole(grad.shape)],
        [flat, flat],
        [whole((tokens, depth))] * 2,
        [],
        2 * tokens * depth * width,
    )


def back_matmul(name, grads, weights, tile, late, outs, finish):
    tokens = grads[0].shape[0]
    width = weights[0].height
    stream = Stream(weights, tile, late)

    def body(stream, ins, outs, scratch):
        (acc_ref,) = scratch
        step, tiles = stream.advance()
        part = matmul_t(ins[0][...], tiles[0][...])
        for value, w in zip(ins[1:], tiles[1:]):
            part = part + matmul_t(value[...], w[...])

        @pl.when(step == 0)
        def _():
            acc_ref[...] = part

        @pl.when(step > 0)
        def _():
            acc_ref[...] += part

        @pl.when(step == stream.steps - 1)
        def _():
            refs = stream.wait_late()
            for ref in outs:
                if ref.shape[0] == 1:
                    ref[...] = jnp.zeros_like(ref)
            by_rows(tokens, lambda rows: finish(rows, acc_ref[rows, :], refs, outs))

    return stream_call(
        name,
        stream,
        body,
        list(grads),
        [pl.BlockSpec((tokens, tile), lambda j: (0, j))] * len(grads),
        outs,
        [whole(value.shape) for value in outs],
        [pltpu.VMEM((tokens, width), full)],
        2 * tokens * width * weights[0].columns * len(weights),
    )


def mlp_back(grads, weights, grad2, hidden1, att, mods):
    tokens, width = grad2.shape
    lead = mods[0].shape[0]

    def finish(rows, db, refs, outs):
        dh2_ref, h1_ref, att_ref, scale_ref, gate_ref = refs
        hidden1 = h1_ref[rows, :]
        inverse = rms_scale(hidden1)
        normed = hidden1 * inverse
        weighted = db * (1.0 + take(scale_ref, rows))
        back = inverse * (weighted - normed * jnp.mean(normed * weighted, axis=-1, keepdims=True))
        grad1 = dh2_ref[rows, :] + back
        outs[0][rows, :] = grad1
        outs[1][rows, :] = (grad1 * take(gate_ref, rows)).astype(low)
        give(outs[2], rows, db)
        give(outs[3], rows, db * normed)
        give(outs[4], rows, grad1 * att_ref[rows, :].astype(full))

    outs = [like((tokens, width), full), like((tokens, width), low)]
    outs += [like((lead, width), low if lead > 1 else full)] * 3
    return back_matmul("mlpback", grads, weights, 1024, [grad2, hidden1, att] + mods, outs, finish)


def qkv_back(grad, weight, grad1, hidden0, scale):
    tokens, width = grad1.shape
    lead = scale.shape[0]

    def finish(rows, da, refs, outs):
        dh1_ref, h0_ref, scale_ref = refs
        hidden0 = h0_ref[rows, :]
        inverse = rms_scale(hidden0)
        normed = hidden0 * inverse
        weighted = da * (1.0 + take(scale_ref, rows))
        back = inverse * (weighted - normed * jnp.mean(normed * weighted, axis=-1, keepdims=True))
        outs[0][rows, :] = (dh1_ref[rows, :] + back).astype(low)
        give(outs[1], rows, da)
        give(outs[2], rows, da * normed)

    outs = [like((tokens, width), low)] + [like((lead, width), low if lead > 1 else full)] * 2
    return back_matmul("qkvback", [grad], [weight], width, [grad1, hidden0, scale], outs, finish)


def out_back(grad, weight):
    def finish(rows, value, refs, outs):
        outs[0][rows, :] = value.astype(low)

    return back_matmul("outback", [grad], [weight], 1152, [], [like(grad.shape, low)], finish)[0]


def ada_back(grads, weight, cond):
    tokens, width = cond.shape
    tile = weight.height
    stream = Stream([weight], tile, [cond])

    def body(stream, ins, outs, scratch):
        (acc_ref,) = scratch
        step, (w,) = stream.advance()
        for k, grad in enumerate(ins):

            @pl.when(step == k)
            def _():
                part = matmul_t(grad[...], w[...])
                acc_ref[...] = part if k == 0 else acc_ref[...] + part

        @pl.when(step == stream.steps - 1)
        def _():
            (cond_ref,) = stream.wait_late()

            def rows_of(rows):
                cond = cond_ref[rows, :]
                sigma = jax.nn.sigmoid(cond)
                outs[0][rows, :] = acc_ref[rows, :] * sigma * (1.0 + cond * (1.0 - sigma))

            by_rows(tokens, rows_of)

    return stream_call(
        "adaback",
        stream,
        body,
        list(grads),
        [whole(grad.shape) for grad in grads],
        [like((tokens, width), full)],
        [whole((tokens, width))],
        [pltpu.VMEM((tokens, width), full)],
        2 * tokens * width * weight.columns,
    )[0]


def ordered_grad(left, order, rights, tile):
    tokens, width = left.shape
    many = len(rights) > 1
    columns = sum(right.shape[1] for right in rights)
    steps = columns // tile

    def body(order_ref, left_ref, *refs):
        ys, out_ref, turned_ref = refs[: len(rights)], refs[-2], refs[-1]
        step = pl.program_id(0)

        @pl.when(step == 0)
        def _():
            turned_ref[...] = matmul_t(order_ref[...], left_ref[...]).astype(low)

        if not many:
            out_ref[...] = matmul(turned_ref[...], ys[0][...]).astype(low)
            return
        for k, y in enumerate(ys):

            @pl.when(step == k)
            def _():
                out_ref[...] = matmul(turned_ref[...], y[...]).astype(low)

    tiles = [whole(right.shape) for right in rights] if many else [pl.BlockSpec((tokens, tile), lambda j: (0, j))]
    return pl.pallas_call(
        body,
        grid=(steps,),
        in_specs=[whole(order.shape), whole(left.shape)] + tiles,
        out_specs=pl.BlockSpec((width, tile), lambda j: (0, j)),
        out_shape=like((width, columns), low),
        scratch_shapes=[pltpu.VMEM((width, tokens), low)],
        compiler_params=params(56),
        cost_estimate=pl.CostEstimate(
            flops=2 * tokens * width * (columns + width), bytes_accessed=2 * width * (columns + 2 * width), transcendentals=0
        ),
        name="wgrad",
    )(order, left, *rights)


def down_grad(left, right, groups):
    tokens, depth = left.shape
    columns = right.shape[1]
    tile = depth // groups

    def body(left_ref, right_ref, out_ref):
        value = outer_sum(left_ref[...], right_ref[...]).astype(low)
        out_ref[0, 0] = value[: tile // 2]
        out_ref[1, 0] = value[tile // 2 :]

    return pl.pallas_call(
        body,
        grid=(groups,),
        in_specs=[pl.BlockSpec((tokens, tile), lambda j: (0, j)), whole(right.shape)],
        out_specs=pl.BlockSpec((2, 1, tile // 2, columns), lambda j: (0, j, 0, 0)),
        out_shape=like((2, groups, tile // 2, columns), low),
        compiler_params=params(40),
        cost_estimate=pl.CostEstimate(
            flops=2 * tokens * depth * columns, bytes_accessed=2 * depth * (columns + tokens), transcendentals=0
        ),
        name="wdown",
    )(left, right)


def tie(value, *others):
    others = [v for v in others if v is not None]
    if not others:
        return value
    return lax.optimization_barrier((value, *others))[0]


class Flight:
    def __init__(self, token):
        self.token = token
        self.held = []
        self.todo = []

    def send(self, value, item, holder, name):
        setattr(holder, name, swap(tie(value, self.token), item))
        self.held.append((holder, name))

    def watch(self, holder, name):
        self.held.append((holder, name))

    def then(self, action):
        self.todo.append(action)

    def fence(self, values, starts=()):
        values = list(values)
        held, todo = self.held, self.todo
        self.held, self.todo = [], []
        arrays = values + [getattr(holder, name) for holder, name in held]
        arrays = lax.optimization_barrier(tuple(arrays))
        self.token = arrays[0]
        for (holder, name), value in zip(held, arrays[len(values) :]):
            setattr(holder, name, value)
        for action in todo:
            action()
        for start in starts:
            start(self)
        return arrays[: len(values)]


class Bundle:
    def __init__(self, place, own, shards, parts, which, relay_bit):
        self.row, self.col, coords = place
        self.own = own
        self.shards = shards
        self.parts = parts
        self.which = which
        self.relay_bit = relay_bit
        self.rows = shards[parts[0][0]].shape[1]
        self.half = self.rows // 2
        self.at = coords[relay_bit] * self.half

    def over_col(self, flight):
        at = tie(self.at, flight.token)
        mine = [
            lax.dynamic_slice(self.shards[name], (self.which, at, first), (1, self.half, n))[0]
            for name, first, n in self.parts
        ]
        flight.send(jnp.concatenate(mine, axis=1), "col", self, "first")

    def relay(self, flight):
        flight.send(self.first, self.relay_bit, self, "second")

    def first_row(self, flight):
        flight.send(self.first, "row", self, "first_s")

    def second_row(self, flight):
        flight.send(self.second, "row", self, "second_s")

    def rows_both(self, flight):
        self.first_row(flight)
        self.second_row(flight)

    def segment(self, wanted):
        row, col, rows, half, at = self.row, self.col, self.rows, self.half, self.at
        other = (2 * row + 1 - col) * rows
        other_s = (2 * (1 - row) + 1 - col) * rows
        offsets = [col * rows, (col + 2) * rows, other + at, other_s + at]
        offsets += [other + (half - at), other_s + (half - at)]
        offsets = jnp.stack(offsets).astype(jnp.int32)
        begin = 0
        for name, first, n in self.parts:
            if name == wanted:
                own_all = self.own[name]
                lead = () if own_all.ndim == 3 else (self.which,)
                pieces = [(own_all, (0,) + lead, first, rows), (own_all, (1,) + lead, first, rows)]
                got = [self.first, self.first_s, self.second, self.second_s]
                pieces += [(value, (), begin, half) for value in got]
                return (offsets, pieces, n)
            begin += n
        raise KeyError(wanted)


def weight_of(name, *bundles):
    return Weight([bundle.segment(name) for bundle in bundles])


def item_weight(item):
    return {"row": 2, "col": 1}.get(item) or 4 << item


def halving_order(path, width, block, me):
    at = jnp.arange(width)
    position = at // block
    owner = me
    for k, item in enumerate(path):
        bit = (position >> (len(path) - 1 - k)) & 1
        if item == "row":
            owner = (owner & ~2) | (2 * bit)
        else:
            owner = owner ^ (bit * item_weight(item))
    return owner * block + at % block


class Slice:
    def __init__(self, held, columns):
        self.held = held
        self.columns = columns

    def get(self):
        return self.held.value[..., self.columns]


class Share:
    def __init__(self, value, order, path):
        self.value = value
        self.order = list(order)
        self.path = list(path)

    def cut(self):
        if isinstance(self.value, Slice):
            self.value = self.value.get()

    def parts(self, item):
        self.cut()
        rows, columns = self.value.shape
        if self.order[0] == item:
            self.order = self.order[1:]
            return self.value[: rows // 2], self.value[rows // 2 :]
        self.order.remove(item)
        value = self.value.reshape(2, 2, rows // 4, columns)
        return value[:, 0].reshape(rows // 2, columns), value[:, 1].reshape(rows // 2, columns)


    def joined(self, kept, got):
        return (kept.astype(full) + got.astype(full)).astype(kept.dtype)


class BlockShare(Share):
    def __init__(self, value, order, path, coords):
        super().__init__(value, order, path)
        self.coords = coords

    def parts(self, item):
        self.cut()
        axis = self.order.index(item)
        self.order.remove(item)
        mine = self.coords[item]
        return (
            lax.dynamic_index_in_dim(self.value, mine, axis, keepdims=False),
            lax.dynamic_index_in_dim(self.value, 1 - mine, axis, keepdims=False),
        )


class Total:
    def __init__(self, value, path):
        self.value = value
        self.path = list(path)

    def parts(self, item):
        return self.value, self.value.astype(low)

    def joined(self, kept, got):
        return kept + got.astype(full)


class TotalAndRows(Total):
    def __init__(self, value, count, path):
        super().__init__(value, path)
        self.count = count

    def joined(self, kept, got):
        n = self.count
        got = got.astype(full)
        return jnp.concatenate([kept[:n] + got[:n], kept[n:], got[n:]], axis=0)


class Parcel:
    got = None


class Agenda:
    def __init__(self):
        self.tasks = {}

    def go(self, *names):
        def action(flight):
            tasks = [self.tasks[name] for name in names]
            items = [task.path.pop(0) for task in tasks]
            assert len(set(items)) == 1
            pairs = [task.parts(items[0]) for task in tasks]
            parcel = Parcel()
            away = pairs[0][1] if len(pairs) == 1 else jnp.concatenate([pair[1] for pair in pairs], axis=-1)
            flight.send(away, items[0], parcel, "got")

            def arrive():
                at = 0
                for task, (kept, _) in zip(tasks, pairs):
                    if len(tasks) == 1:
                        task.value = task.joined(kept, parcel.got)
                    else:
                        n = kept.shape[-1]
                        task.value = task.joined(kept, parcel.got[..., at : at + n])
                        at += n

            flight.then(arrive)

        return action


def row_sum(value):
    return lax.psum_scatter(value, "row", scatter_dimension=0, tiled=True)


def grad_blocks(left, right, bits, block):
    if (4 * block) % 128 == 0:
        value = down_grad(left, right, 2**bits)
    else:
        value = outer_sum(left, right).astype(low).reshape(2**bits, 2, 2 * block, right.shape[1])
        value = jnp.swapaxes(value, 0, 1)
    return value.reshape((2,) * (bits + 2) + (block, right.shape[1]))


def block_forward(hidden0, mods, mats, gains, tabs, flight, points):
    shift1, scale1, gate1, shift2, scale2, gate2 = mods
    cosine, sine, member, member_t, head = tabs
    used = {}

    def mat(name):
        used[name] = mats[name]()
        return used[name]

    def fence(point, *values):
        if point not in points:
            return values if len(values) > 1 else values[0]
        values = flight.fence(values, points[point])
        return values if len(values) > 1 else values[0]

    attn_in = (hidden0 * rms_scale(hidden0) * (1.0 + plain(scale1)) + plain(shift1)).astype(low)
    attn_in = fence("qkv", attn_in)
    query, kv, raw = qkv_matmul(attn_in, mat("qkv"), cosine, sine, gains[0], member, member_t, head)
    query, kv = fence("attend", query, kv)
    kv_r = swap(kv, "row")
    out_b, lse = attend(query, kv, kv_r, head)
    out_b = fence("out", out_b)
    att, hidden1, mlp_in = out_matmul(out_b, mat("out"), hidden0, [gate1, shift2, scale2])
    mlp_in = fence("gate", mlp_in)
    inner, gate_pre, up_pre = gate_up_matmul(mlp_in, mat("gate"), mat("up"))
    inner = fence("down", inner)
    mlp_out, hidden2 = down_matmul(inner, mat("down"), hidden1, gate2)
    cache = (hidden0, attn_in, raw, query, kv, kv_r, out_b, lse, att)
    cache += (hidden1, mlp_in, gate_pre, up_pre, inner, mlp_out)
    used = tuple(used[name] for name in ("qkv", "out", "gate", "up", "down"))
    return hidden2, cache, used


class Sum:
    value = None


def block_backward(grad2, cache, mods, mats, gains, tabs, comm, tag, plan):
    (hidden0, attn_in, raw, query, kv, kv_r, out_b, lse, att) = cache[:9]
    (hidden1, mlp_in, gate_pre, up_pre, inner, mlp_out) = cache[9:]
    shift1, scale1, gate1, shift2, scale2, gate2 = mods
    qkv_w, out_w, gate_w, up_w, down_w = mats
    cosine, sine, member, member_t, head = tabs
    flight, agenda, orders, paths, coords = comm
    n_data = lax.axis_size("dp")
    bits = (n_data - 1).bit_length()
    block = down_w.height // (4 * n_data)

    def fence(point, *values):
        values = flight.fence(values, plan.get(point, ()))
        return values if len(values) > 1 else values[0]

    def grad_of(left, name, right, tile):
        return ordered_grad(left, orders[name], [right], tile)

    def watch(name, task):
        agenda.tasks[name + tag] = task
        flight.watch(task, "value")

    def begin(name, value):
        path = paths[name][1:]
        watch(name[0], Share(value, path, path))

    def begin_halves(name, value, cut):
        path = paths[name][1:]
        other = [path[1], path[0]] + path[2:]
        held = Sum()
        held.value = value
        flight.watch(held, "value")
        agenda.tasks[name[0] + "a" + tag] = Share(Slice(held, slice(0, cut)), path, path)
        agenda.tasks[name[0] + "b" + tag] = Share(Slice(held, slice(cut, None)), path, other)

    def begin_down(value):
        order = ["row"] + list(reversed(range(bits))) + ["col"]
        if tag == "0":
            watch("d", BlockShare(value, order, paths["down"], coords))
            return
        watch("d", BlockShare(value, order, ["row"], coords))

    grad_mlp = (grad2 * plain(gate2)).astype(low)
    dgate2 = grad2 * mlp_out.astype(full)
    if gate2.shape[0] == 1:
        dgate2 = jnp.sum(dgate2, axis=0, keepdims=True)
    begin_down(grad_blocks(inner, grad_mlp, bits, block))
    grad2, grad_mlp = fence("start", grad2, grad_mlp)
    grad_gate, grad_up = down_back(grad_mlp, down_w, gate_pre, up_pre)
    w_gate = grad_of(mlp_in, "gate", grad_gate, 1024)
    w_up = grad_of(mlp_in, "up", grad_up, 1024)
    grad_gate, grad_up, w_gate, w_up = fence("gate", grad_gate, grad_up, w_gate, w_up)
    r_gate = row_sum(w_gate)
    r_up = row_sum(w_up)
    grad1, grad_att, dshift2, dscale2, dgate1 = mlp_back(
        [grad_gate, grad_up], [gate_w, up_w], grad2, hidden1, att, [scale2, gate1]
    )
    grad_att = fence("out", grad_att)
    w_out = grad_of(out_b, "out", grad_att, 384)
    grad_ob = out_back(grad_att, out_w)
    begin("gate", r_gate)
    begin("up", r_up)
    grad_ob, w_out = fence("attend", grad_ob, w_out)
    r_out = row_sum(w_out)
    dq, dkv, dkv_r = attend_back(query, kv, kv_r, grad_ob, out_b, lse, head)
    begin("out", r_out)
    dq, dkv_r = fence("qk", dq, dkv_r)
    grad_qkv, gain_rows = qk_back(dq, dkv, swap(dkv_r, "row"), raw, cosine, sine, gains[1], member, member_t, head)
    w_qkv = grad_of(attn_in, "qkv", grad_qkv, 1152)
    grad_qkv, w_qkv = fence("qkv", grad_qkv, w_qkv)
    r_qkv = row_sum(w_qkv)
    grad0, dshift1, dscale1 = qkv_back(grad_qkv, qkv_w, grad1, hidden0, scale1)
    dmods = [dshift1, dscale1, dgate1, dshift2, dscale2, dgate2]
    begin_halves("qkv", r_qkv, r_qkv.shape[1] // 256 * 128)
    return grad0, dmods, gain_rows[:2], begin_halves


def per_device(
    latents,
    levels,
    timesteps,
    patch_weight,
    patch_bias,
    ada_weight,
    ada_bias,
    qkv_weight,
    qk_gains,
    out_weight,
    gate_weight,
    up_weight,
    down_weight,
    cotangent,
):
    images, slots, chans, rows_loc, cols_loc = latents.shape
    n_data = lax.axis_size("dp")
    assert images == 1 and slots == 2
    assert lax.axis_size("row") == 2 and lax.axis_size("col") == 2
    row = lax.axis_index("row")
    col = lax.axis_index("col")
    data = lax.axis_index("dp")
    bits = (n_data - 1).bit_length()
    left = col == 0
    coords = {"row": row, "col": col}
    place = (row, col, coords)
    for k in range(bits):
        coords[k] = (data >> k) & 1
    grid_rows = rows_loc // 2
    grid_cols = cols_loc
    half_cols = grid_cols // 2
    tokens = grid_rows * grid_cols
    width = cotangent.shape[-1]
    head = qk_gains.shape[2]
    heads = width // head
    pvals = chans * 4
    shard = width // 4
    me = data * 4 + row * 2 + col
    own_rows = width // (4 * n_data)

    def pair(own, other, axis):
        return jnp.concatenate([jnp.where(left, own, other), jnp.where(left, other, own)], axis=axis)

    own = {}
    for name, s in (
        ("qkv", qkv_weight),
        ("out", out_weight),
        ("gate", gate_weight),
        ("up", up_weight),
        ("down", down_weight),
        ("ada", ada_weight),
    ):
        own[name] = lax.all_gather(s, "row", axis=0)
    shards = {"qkv": qkv_weight, "out": out_weight, "gate": gate_weight, "up": up_weight, "down": down_weight}
    shards["ada"] = ada_weight

    def bundle(which, relay_bit, *parts):
        return Bundle(place, own, shards, parts, which, relay_bit)

    ff = gate_weight.shape[2]
    b_q0 = bundle(0, 0, ("qkv", 0, width))
    b_kv0 = bundle(0, 1, ("qkv", width, 2 * width))
    b_out0 = bundle(0, 0, ("out", 0, width))
    b_gate0 = bundle(0, 0, ("gate", 0, ff))
    b_up0 = bundle(0, 1, ("up", 0, ff))
    b_down0 = bundle(0, 0, ("down", 0, width))
    b_ada_a = bundle(1, 1, ("ada", 0, 3 * width))
    b_ada_b = bundle(1, 0, ("ada", 3 * width, 3 * width))
    b_qkv1 = bundle(1, 1, ("qkv", 0, 3 * width))
    b_og1 = bundle(1, 0, ("out", 0, width), ("gate", 0, ff))
    b_up1 = bundle(1, 1, ("up", 0, ff))
    b_down1 = bundle(1, 0, ("down", 0, width))
    enc_mats = {
        "qkv": lambda: weight_of("qkv", b_q0, b_kv0),
        "out": lambda: weight_of("out", b_out0),
        "gate": lambda: weight_of("gate", b_gate0),
        "up": lambda: weight_of("up", b_up0),
        "down": lambda: weight_of("down", b_down0),
    }
    dec_mats = {
        "qkv": lambda: weight_of("qkv", b_qkv1),
        "out": lambda: weight_of("out", b_og1),
        "gate": lambda: weight_of("gate", b_og1),
        "up": lambda: weight_of("up", b_up1),
        "down": lambda: weight_of("down", b_down1),
    }

    small = jnp.concatenate(
        [jnp.swapaxes(patch_weight, 1, 2).reshape(2 * pvals, shard), patch_bias, ada_bias.reshape(12, shard)], axis=0
    )
    small_other = swap(small, "col")
    blk = latents[0]
    blk_other = swap(blk, "col")
    flight = Flight(small)

    class Start:
        pass

    Start.small, Start.blk = small_other, blk_other
    flight.watch(Start, "small")
    flight.watch(Start, "blk")
    (blk,) = flight.fence([blk])
    small = pair(small[None], Start.small[None], 0)
    wide = pair(blk, Start.blk, 3)
    flight.send(small, "row", Start, "small")
    flight.send(wide[:, :, rows_loc - 1 :], "row", Start, "top")
    small, wide = flight.fence([small, wide], [b_q0.over_col, b_kv0.over_col])
    temb = time_features(tie(timesteps, wide)[0], width)
    small = jnp.where(row == 0, jnp.stack([small, Start.small]), jnp.stack([Start.small, small]))
    small = small.reshape(4, 2 * pvals + 14, shard)
    patch_w = small[:, : 2 * pvals].transpose(1, 0, 2).reshape(2, pvals, width)
    patch_b = small[:, 2 * pvals : 2 * pvals + 2].transpose(1, 0, 2).reshape(2, width).astype(full)
    ada_b = small[:, 2 * pvals + 2 :].reshape(4, 2, 6 * shard).transpose(1, 0, 2).reshape(2, 6, width).astype(full)

    framed = jnp.concatenate([Start.top, wide[:, :, : rows_loc - 1]], axis=2)
    framed = jnp.concatenate([framed[..., -1:], framed[..., :-1]], axis=3)
    patches = (
        framed.reshape(slots, chans, grid_rows, 2, grid_cols, 2).transpose(0, 2, 4, 1, 3, 5).reshape(slots, tokens, pvals)
    )
    enc_patches = patches[0]
    dec_patches = jnp.where(left, patches[0], patches[1])

    sil0 = jax.nn.silu(temb[:1]).astype(low)
    temb_own = jnp.where(left, temb[:1], temb[1:])
    part = mod_partial(lax.dynamic_slice(sil0, (0, (2 * row + col) * shard), (1, shard)), ada_weight, width)

    cot_own = jnp.where(left, cotangent[0, 0], cotangent[0, 1])

    class Cotangent:
        got = None

    def send_cotangent(flight):
        flight.send(jnp.where(left, cotangent[0, 1], cotangent[0, 0]), "col", Cotangent, "got")

    quarter = head // 4
    lanes = tie(jnp.arange(width), flight.token)
    within = lanes % head
    section = within // quarter
    lane_freq = jnp.exp(-math.log(10000.0) * (within % quarter).astype(full) / quarter)
    row_pos = (row * grid_rows + jnp.arange(grid_rows)).astype(full)
    col_pos = jnp.arange(grid_cols).astype(full)
    row_angle = row_pos[:, None] * lane_freq[None, :]
    col_angle = col_pos[:, None] * lane_freq[None, :]
    by_row = section < 2
    sign = jnp.where(section % 2 == 0, -1.0, 1.0).astype(full)

    def table(fun):
        return jnp.where(by_row, fun(row_angle)[:, None, :], fun(col_angle)[None, :, :]).reshape(tokens, width)

    cosine = table(jnp.cos)
    sine = table(jnp.sin) * sign
    member = (lanes[:, None] // head == jnp.arange(128)[None, :]).astype(low)
    tabs = (cosine, sine, member, member.T, head)
    gain_rows = jnp.tile(qk_gains.astype(full), (1, 1, heads))
    even = jnp.broadcast_to((section % 2 == 0).astype(full), (2, 1, width))
    temper = head ** (-0.5) * math.log2(math.e)
    scaled = jnp.concatenate([gain_rows[:, :1] * temper, gain_rows[:, 1:], even], axis=1)
    gain_rows = jnp.concatenate([gain_rows, even], axis=1)
    gain_rows = [(scaled[k], gain_rows[k]) for k in range(2)]

    rest = list(range(2, bits))
    path_y = ["row", "col", 0, 1] + rest
    path_x = ["row", 0, "col", 1] + rest
    path_z = ["row", 1, "col", 0] + rest
    path_w = ["row", 1, 0, "col"] + rest
    paths = {"down": path_z, "gate": path_y, "up": path_x, "out": path_x, "qkv": path_y, "ada": path_y}
    perm = {}
    orders = {}
    for name in ("gate", "up", "out", "qkv", "ada"):
        key = tuple(paths[name])
        if key not in perm:
            source = halving_order(paths[name], width, own_rows, me)
            perm[key] = lax.optimization_barrier((source[:, None] == lanes[None, :]).astype(low))
        orders[name] = perm[key]

    enc_h0 = matmul(enc_patches, patch_w[0]) + patch_b[0]
    starts = [b_q0.relay, b_kv0.relay, b_out0.over_col, b_q0.first_row, b_kv0.first_row]
    enc_h0, part, cosine, sine = flight.fence([enc_h0, part, cosine, sine], starts)
    part = part + swap(part, "row")
    part = part + swap(part, "col")
    enc_mod = part + ada_b[0]
    enc_mods = [enc_mod[k : k + 1] for k in range(6)]
    tabs = (cosine, sine) + tabs[2:]
    points = {
        "qkv": [b_q0.second_row, b_kv0.second_row, b_gate0.over_col, b_out0.relay],
        "attend": [b_up0.over_col, b_gate0.relay, b_out0.first_row],
        "out": [b_out0.second_row, b_up0.relay, b_down0.over_col, b_gate0.rows_both],
        "gate": [b_up0.rows_both, b_ada_a.over_col, b_down0.relay],
        "down": [b_down0.rows_both, b_qkv1.over_col, b_ada_a.relay],
    }
    encoded, enc_cache, enc_mats = block_forward(enc_h0, enc_mods, enc_mats, gain_rows[0], tabs, flight, points)
    dec_h0 = matmul(dec_patches, patch_w[1]) + patch_b[1]
    cond = encoded + temb_own
    dec_sil = jax.nn.silu(cond).astype(low)
    (dec_sil,) = flight.fence([dec_sil], [b_ada_a.rows_both, b_ada_b.over_col, b_qkv1.relay])
    ada_bias1 = ada_b[1].reshape(1, 6 * width)
    mod_a = ada_matmul(dec_sil, weight_of("ada", b_ada_a), ada_bias1[:, : 3 * width])
    dec_mods = [Cols(mod_a, k * width, width) for k in range(3)]
    held = Sum()

    def second_mods(flight):
        held.value = ada_matmul(tie(dec_sil, flight.token), weight_of("ada", b_ada_b), ada_bias1[:, 3 * width :])
        flight.watch(held, "value")

    dec_mods += [Cols(held, k * width, width) for k in range(3)]
    points = {
        "qkv": [b_qkv1.rows_both, b_og1.over_col, b_ada_b.relay],
        "attend": [b_ada_b.rows_both, second_mods, b_up1.over_col, b_og1.relay],
        "out": [b_og1.rows_both, b_down1.over_col, b_up1.relay],
        "gate": [b_up1.rows_both, b_down1.relay, send_cotangent],
        "down": [b_down1.rows_both],
    }
    decoded, dec_cache, dec_mats = block_forward(dec_h0, dec_mods, dec_mats, gain_rows[1], tabs, flight, points)
    live = (col < levels[0]).astype(full)
    result = (decoded * live).astype(low).reshape(grid_rows, grid_cols, width)
    near = jnp.where(left, result[:, :half_cols], result[:, half_cols:])
    far = jnp.where(left, result[:, half_cols:], result[:, :half_cols])

    class Away:
        got = None

    def send_result(flight):
        flight.send(far, "col", Away, "got")


    agenda = Agenda()
    go = agenda.go
    comm = (flight, agenda, orders, paths, coords)
    cot = pair(cot_own, Cotangent.got, 1).reshape(tokens, width)
    dec_grad2 = cot.astype(full) * live

    def split_down(flight):
        value = agenda.tasks["d1"].value
        order = list(reversed(range(bits))) + ["col"]
        path = paths["qkv"][1:]
        cut = value.shape[-1] // 256 * 128
        agenda.tasks["da1"] = BlockShare(value[..., :cut], order, path, coords)
        agenda.tasks["db1"] = BlockShare(value[..., cut:], order, [path[1], path[0]] + path[2:], coords)

    plan = {
        "start": [send_result, go("d1")],
        "gate": [split_down, go("da1"), go("db1")],
        "out": [go("da1"), go("db1")],
        "attend": [go("g1"), go("u1"), go("da1", "db1")],
        "qk": [go("g1"), go("u1"), go("da1", "db1")],
        "qkv": [go("o1"), go("g1", "u1")],
    }
    dec_grad0, dec_dmods, dec_gains, begin_halves = block_backward(
        dec_grad2, dec_cache, dec_mods, dec_mats, gain_rows[1], tabs, comm, "1", plan
    )
    away = Away.got
    result = jnp.stack([jnp.where(left, near, away), jnp.where(left, away, near)])[None]
    dec_dmods = [piece.astype(low) for piece in dec_dmods]
    w_ada = ordered_grad(dec_sil, orders["ada"], dec_dmods, width)
    starts = [go("qa1"), go("qb1"), go("o1"), go("g1", "u1")]
    w_ada, *dec_dmods = flight.fence([w_ada] + dec_dmods, starts)
    r_ada = row_sum(w_ada)
    dec_bada = jnp.stack([jnp.sum(piece.astype(full), axis=0) for piece in dec_dmods])
    enc_grad2 = ada_back(dec_dmods, weight_of("ada", b_ada_a, b_ada_b), cond)

    def patch_rows(patch, grad):
        ones = jnp.ones((tokens, 1), low)
        return outer_sum(jnp.concatenate([patch, ones], axis=1), grad)

    total = jnp.concatenate([patch_rows(dec_patches, dec_grad0), dec_bada, dec_gains], axis=0)
    agenda.tasks["s"] = Total(total, ["row", "col"] + list(range(bits)))

    begin_halves("ada", r_ada, r_ada.shape[1] // 2)
    plan = {
        "start": [go("s"), go("d0"), go("aa1"), go("ab1")],
        "gate": [go("aa1"), go("ab1"), go("qa1"), go("qb1")],
        "out": [go("s"), go("aa1", "ab1")],
        "attend": [go("s"), go("g0"), go("u0"), go("d0")],
        "qk": [go("s"), go("g0"), go("u0"), go("aa1", "ab1")],
        "qkv": [go("s"), go("d0"), go("o0"), go("qa1", "qb1", "o1")],
    }
    enc_grad0, enc_dmods, enc_gains, _ = block_backward(
        enc_grad2, enc_cache, enc_mods, enc_mats, gain_rows[0], tabs, comm, "0", plan
    )
    dmod_enc = jnp.concatenate(enc_dmods, axis=0)
    total = jnp.concatenate([patch_rows(enc_patches, enc_grad0), enc_gains, dmod_enc], axis=0)
    def image(dpatch):
        return (
            dpatch.reshape(grid_rows, grid_cols, chans, 2, 2).transpose(2, 0, 3, 1, 4).reshape(chans, rows_loc, 2 * cols_loc)
        )

    enc_image = image(matmul_t(enc_grad0, patch_w[0]))
    dec_image = image(matmul_t(dec_grad0, patch_w[1]))
    zero = jnp.zeros_like(dec_image)
    grads = jnp.stack([enc_image + jnp.where(left, dec_image, zero), jnp.where(left, zero, dec_image)])
    grads = jnp.concatenate([grads[..., 1:], grads[..., :1]], axis=3)

    class Last:
        pass

    total, grads = flight.fence([total, grads])
    flight.send(total, "row", Last, "total")
    flight.send(grads[:, :, :1], "row", Last, "below")
    total, grads = flight.fence([total, grads], [go("qa0"), go("qb0"), go("g0", "u0"), go("qa1", "qb1", "o1")])
    total = total + Last.total
    flight.send(total, "col", Last, "total")
    grads = jnp.concatenate([grads[:, :, 1:], Last.below], axis=2)
    one = grads[..., :cols_loc]
    two = grads[..., cols_loc:]
    flight.send(jnp.where(left, two, one), "col", Last, "image")
    count = pvals + 3
    tiny = TotalAndRows(None, count, list(range(bits)))
    agenda.tasks["t"] = tiny

    def begin_tiny(flight):
        tiny.value = jnp.concatenate([total + Last.total, sil0.astype(full)], axis=0)
        go("t")(flight)

    flight.fence([total], [begin_tiny, go("qa0"), go("qb0"), go("o0"), go("g0", "u0")])
    latent_grad = (jnp.where(left, one, two) + Last.image)[None]
    flight.fence([total], [go("t"), go("qa0", "qb0", "o0"), go("d0")])
    flight.fence([total], [go("t"), go("qa0", "qb0", "o0"), go("d0")])
    flight.fence([total])
    while any(task.path for task in agenda.tasks.values()):
        flight.fence([total], [go(name) for name, task in agenda.tasks.items() if task.path])
        flight.fence([total])
    dec_small = agenda.tasks["s"].value
    total = tiny.value[:count]
    dmod_all = tiny.value[count:]
    dmod_all = dmod_all.reshape(n_data, 7, width)
    enc_small = total
    enc_ada = jnp.dot(
        lax.dynamic_slice(dmod_all, (0, 6, me * own_rows), (n_data, 1, own_rows))[:, 0].T,
        dmod_all[:, :6].reshape(n_data, 6 * width),
        precision=highest,
        preferred_element_type=full,
    )
    enc_bada = jnp.sum(dmod_all[:, :6], axis=0)

    def own_lanes(value):
        return lax.dynamic_slice(value, (0, me * own_rows), (value.shape[0], own_rows))

    enc_patch = own_lanes(enc_small[: pvals + 1])
    dec_patch = own_lanes(dec_small[: pvals + 1])
    g_patch = jnp.stack([enc_patch[:pvals].T, dec_patch[:pvals].T])
    g_patch_b = jnp.stack([enc_patch[pvals], dec_patch[pvals]])
    bada = jnp.stack([enc_bada.reshape(-1), dec_small[pvals + 1 : pvals + 7].reshape(-1)])
    own_bada = 6 * own_rows
    g_bada = lax.dynamic_slice(bada, (0, me * own_bada), (2, own_bada))
    gains = jnp.stack([enc_small[pvals + 1 :], dec_small[pvals + 7 :]])
    gains = gains.reshape(2, 2, heads, head).sum(axis=2)
    def both(name):
        parts = [agenda.tasks[name + tag].value.astype(full) for tag in "01"]
        return jnp.stack(parts)

    for task in agenda.tasks.values():
        assert not task.path
    g_ada = jnp.concatenate([agenda.tasks["aa1"].value, agenda.tasks["ab1"].value], axis=1)
    g_ada_all = jnp.stack([enc_ada, g_ada.astype(full)])
    g_qkv = jnp.concatenate([both("qa"), both("qb")], axis=2)
    down1 = jnp.concatenate([agenda.tasks["da1"].value, agenda.tasks["db1"].value], axis=1)
    g_down = jnp.stack([agenda.tasks["d0"].value.astype(full), down1.astype(full)])
    stacked = [g_qkv, both("o"), both("g"), both("u"), g_down]
    return (
        result,
        latent_grad,
        g_patch,
        g_patch_b,
        g_ada_all,
        g_bada,
        stacked[0],
        gains,
        stacked[1],
        stacked[2],
        stacked[3],
        stacked[4],
    )


def solution(mesh):
    tile = ("row", "col")
    every = ("dp", "row", "col")
    return jax.shard_map(
        per_device,
        mesh=mesh,
        in_specs=(
            P("dp", None, None, "row", "col"),
            P("dp"),
            P("dp", None),
            P(None, tile, None),
            P(None, tile),
            P(None, tile, None),
            P(None, tile),
            P(None, tile, None),
            P(),
            P(None, tile, None),
            P(None, tile, None),
            P(None, tile, None),
            P(None, tile, None),
            P("dp", None, "row", "col", None),
        ),
        out_specs=(
            P("dp", None, "row", "col", None),
            P("dp", None, None, "row", "col"),
            P(None, every, None),
            P(None, every),
            P(None, every, None),
            P(None, every),
            P(None, every, None),
            P(),
            P(None, every, None),
            P(None, every, None),
            P(None, every, None),
            P(None, every, None),
        ),
        check_vma=False,
    )
```

```python
import functools
import math

import jax
import jax.numpy as jnp
from jax import lax
from jax.experimental import pallas as pl
from jax.experimental.pallas import tpu as pltpu
from jax.sharding import PartitionSpec as P

epsilon = 1e-06
highest = lax.Precision.HIGHEST
low = jnp.bfloat16
full = jnp.float32
WINDOW = 256
MIB = 1 << 20


def matmul(left, right):
    return jnp.dot(left, right, preferred_element_type=full)


def matmul_t(left, right):
    return lax.dot_general(left, right, (((1,), (1,)), ((), ())), preferred_element_type=full)


def outer_sum(left, right):
    return lax.dot_general(left, right, (((0,), (0,)), ((), ())), preferred_element_type=full)


def rms_scale(value):
    return lax.rsqrt(jnp.mean(value * value, axis=-1, keepdims=True) + epsilon)


def rms_back(value, inverse, grad):
    return inverse * grad - value * inverse**3 * jnp.mean(value * grad, axis=-1, keepdims=True)


def swap(value, item):
    if isinstance(item, str):
        return lax.ppermute(value, item, [(0, 1), (1, 0)])
    size = lax.axis_size("dp")
    return lax.ppermute(value, "dp", [(i, i ^ (1 << item)) for i in range(size)])


def time_features(steps, width):
    half = width // 2
    freqs = jnp.exp(-math.log(10000.0) * jnp.arange(half).astype(full) / half)
    angles = steps.astype(full)[:, None] * freqs[None, :]
    return jnp.concatenate([jnp.cos(angles), jnp.sin(angles)], axis=-1)


def whole(shape):
    return pl.BlockSpec(shape, lambda *_: (0,) * len(shape))


def params(mib):
    return pltpu.CompilerParams(vmem_limit_bytes=mib * MIB)


def head_mean(value, member, head):
    return matmul(value.astype(low), member) * (1.0 / head)


def split_dot(value, onehot):
    top = value.astype(low)
    rest = (value - top.astype(full)).astype(low)
    return matmul(top, onehot) + matmul(rest, onehot)


def turned(value, cosine, sine, even, quarter):
    width = value.shape[-1]
    ahead = pltpu.roll(value, width - quarter, axis=1)
    behind = pltpu.roll(value, quarter, axis=1)
    return value * cosine + jnp.where(even, ahead, behind) * sine


def even_lanes(gain_ref, shape):
    return jnp.broadcast_to(gain_ref[2:3, :] > 0.5, shape)


def qk_back_body(head, dq_ref, dkv_ref, dkvx_ref, qkv_ref, cos_ref, sin_ref, gain_ref, mem_ref, memt_ref, out_ref, gg_ref):
    width = dq_ref.shape[-1]

    @pl.when(pl.program_id(0) == 0)
    def _():
        gg_ref[...] = jnp.zeros_like(gg_ref)

    cosine = cos_ref[...]
    sine = -sin_ref[...]
    even = even_lanes(gain_ref, cosine.shape)
    member = mem_ref[...]
    member_t = memt_ref[...]
    grads = (dq_ref[...], dkv_ref[:, :width] + dkvx_ref[:, :width].astype(full))
    for part in (0, 1):
        value = qkv_ref[:, part * width : (part + 1) * width]
        mean = head_mean(value * value, member, head)
        inverse_h = lax.rsqrt(mean + epsilon)
        inverse = split_dot(inverse_h, member_t)
        grad_n = turned(grads[part], cosine, sine, even, head // 4)
        normed = value * inverse
        gg_ref[part : part + 1, :] += jnp.sum(grad_n * normed, axis=0, keepdims=True)
        weighted = grad_n * gain_ref[part : part + 1, :]
        dots = head_mean(value * weighted, member, head) * inverse_h * inverse_h
        back = inverse * weighted - normed * split_dot(dots, member_t)
        out_ref[:, part * width : (part + 1) * width] = back.astype(low)
    out_ref[:, 2 * width :] = (dkv_ref[:, width:] + dkvx_ref[:, width:].astype(full)).astype(low)


def qk_back(dq, dkv, dkvx, raw, cosine, sine, gains, member, member_t, head):
    tokens, width = dq.shape
    step = 256
    rows = lambda n: pl.BlockSpec((step, n), lambda i: (i, 0))
    return pl.pallas_call(
        functools.partial(qk_back_body, head),
        grid=(tokens // step,),
        in_specs=[rows(width)]
        + [rows(2 * width)] * 3
        + [rows(width), rows(width), whole(gains.shape), whole(member.shape), whole(member_t.shape)],
        out_specs=[rows(3 * width), whole((8, width))],
        out_shape=[jax.ShapeDtypeStruct((tokens, 3 * width), low), jax.ShapeDtypeStruct((8, width), full)],
        compiler_params=params(60),
        cost_estimate=pl.CostEstimate(flops=60 * raw.size, bytes_accessed=18 * raw.size, transcendentals=0),
        name="qk_back",
    )(dq, dkv, dkvx, raw, cosine, sine, gains, member, member_t)


def head_window(head, width):
    index = pl.program_id(0)
    start = index * head
    base = jnp.minimum(lax.div(start, 128) * 128, width - WINDOW)
    return index, pl.multiple_of(base, 128), start - base


def window_mask(shape, offset, head):
    lane = lax.broadcasted_iota(jnp.int32, shape, 1)
    return jnp.logical_and(lane >= offset, lane < offset + head)


def attend_body(head, q_ref, kvl_ref, kvr_ref, o_ref, lse_ref, acc_ref):
    tokens, width = q_ref.shape
    index, base, offset = head_window(head, width)
    cols = pl.ds(base, WINDOW)
    vals = pl.ds(pl.multiple_of(width + base, 128), WINDOW)

    @pl.when(index == 0)
    def _():
        acc_ref[...] = jnp.zeros_like(acc_ref)
        lse_ref[...] = jnp.zeros_like(lse_ref)

    step = 256
    mask_k = window_mask((tokens, WINDOW), offset, head)
    one = jnp.ones((), low)
    value_l = jnp.where(mask_k, kvl_ref[:, vals], one)
    value_r = jnp.where(mask_k, kvr_ref[:, vals], one)
    mask = window_mask((step, WINDOW), offset, head)
    lane = lax.broadcasted_iota(jnp.int32, (step, lse_ref.shape[1]), 1)
    for first in range(0, tokens, step):
        rows = slice(first, first + step)
        query = jnp.where(mask, q_ref[rows, cols], jnp.zeros((), low))
        left = jnp.exp2(matmul_t(query, kvl_ref[:, cols])).astype(low)
        right = jnp.exp2(matmul_t(query, kvr_ref[:, cols])).astype(low)
        out = matmul(left, value_l) + matmul(right, value_r)
        total = jnp.max(jnp.where(mask, 0.0, out), axis=1, keepdims=True)
        acc_ref[rows, cols] += jnp.where(mask, out * (1.0 / total), 0.0)
        lse_ref[rows, :] += jnp.where(lane == index, jnp.log2(total), 0.0)

    @pl.when(index == pl.num_programs(0) - 1)
    def _():
        o_ref[...] = acc_ref[...].astype(low)


def attend(query, kv_l, kv_r, head):
    tokens, width = query.shape
    heads = width // head
    return pl.pallas_call(
        functools.partial(attend_body, head),
        grid=(heads,),
        in_specs=[whole((tokens, width))] + [whole((tokens, 2 * width))] * 2,
        out_specs=[whole((tokens, width)), whole((tokens, 128))],
        out_shape=[jax.ShapeDtypeStruct((tokens, width), low), jax.ShapeDtypeStruct((tokens, 128), full)],
        scratch_shapes=[pltpu.VMEM((tokens, width), full)],
        compiler_params=params(56),
        cost_estimate=pl.CostEstimate(
            flops=8 * tokens * tokens * WINDOW * heads, bytes_accessed=14 * tokens * width, transcendentals=2 * tokens * tokens * heads
        ),
        name="attend",
    )(query, kv_l, kv_r)


def in_three(column):
    top = column.astype(low)
    rest = column - top.astype(full)
    middle = rest.astype(low)
    return top, middle, (rest - middle.astype(full)).astype(low)


def attend_back_body(head, q_ref, kvl_ref, kvr_ref, do_ref, o_ref, lse_ref, dq_ref, dl_ref, dr_ref, dr_acc):
    tokens, width = q_ref.shape
    index, base, offset = head_window(head, width)
    cols = pl.ds(base, WINDOW)
    vals = pl.ds(pl.multiple_of(width + base, 128), WINDOW)
    temper = head ** (-0.5)

    @pl.when(index == 0)
    def _():
        for ref in (dq_ref, dl_ref, dr_acc):
            ref[...] = jnp.zeros_like(ref)

    shape = (tokens, WINDOW)
    mask = window_mask(shape, offset, head)
    lane = lax.broadcasted_iota(jnp.int32, shape, 1)
    spare = jnp.where(offset >= 3, 0, WINDOW - 3)
    zero = jnp.zeros((), low)
    minus = jnp.where(jnp.logical_and(lane >= spare, lane < spare + 3), -jnp.ones((), low), zero)
    query = jnp.where(mask, q_ref[:, cols], zero)
    grad = jnp.where(mask, do_ref[:, cols], zero)
    delta = jnp.sum(grad.astype(full) * o_ref[:, cols].astype(full), axis=1, keepdims=True)
    small = lax.broadcasted_iota(jnp.int32, lse_ref.shape, 1)
    level = jnp.sum(jnp.where(small == index, lse_ref[...], 0.0), axis=1, keepdims=True)
    query_x = query
    grad_x = grad
    for k, (a, b) in enumerate(zip(in_three(level), in_three(delta))):
        at = lane == spare + k
        query_x = jnp.where(at, a, query_x)
        grad_x = jnp.where(at, b, grad_x)
    grad_q = 0.0
    for ref, acc in ((kvl_ref, dl_ref), (kvr_ref, dr_acc)):
        key = jnp.where(mask, ref[:, cols], minus)
        value = jnp.where(mask, ref[:, vals], minus)
        prob = jnp.exp2(matmul_t(key, query_x))
        grad_s = (prob * matmul_t(value, grad_x)).astype(low)
        acc[:, vals] += matmul(prob.astype(low), grad)
        acc[:, cols] += matmul(grad_s, query)
        grad_q = grad_q + outer_sum(grad_s, key)
    dq_ref[:, cols] += jnp.where(mask, grad_q * temper, 0.0)

    @pl.when(index == pl.num_programs(0) - 1)
    def _():
        back = math.log(2.0)
        dl_ref[:, :width] = dl_ref[:, :width] * back
        dr_ref[:, :width] = (dr_acc[:, :width] * back).astype(low)
        dr_ref[:, width:] = dr_acc[:, width:].astype(low)


def attend_back(query, kv_l, kv_r, grad, out, levels, head):
    tokens, width = query.shape
    heads = width // head
    both = (tokens, 2 * width)
    one = (tokens, width)
    return pl.pallas_call(
        functools.partial(attend_back_body, head),
        grid=(heads,),
        in_specs=[whole(one), whole(both), whole(both), whole(one), whole(one), whole(levels.shape)],
        out_specs=[whole(one), whole(both), whole(both)],
        out_shape=[like(one, full), like(both, full), like(both, low)],
        scratch_shapes=[pltpu.VMEM(both, full)],
        compiler_params=params(62),
        cost_estimate=pl.CostEstimate(
            flops=20 * tokens * tokens * WINDOW * heads, bytes_accessed=28 * tokens * width, transcendentals=2 * tokens * tokens * heads
        ),
        name="attend_back",
    )(query, kv_l, kv_r, grad, out, levels)


class Weight:
    def __init__(self, segments):
        self.segments = segments
        self.columns = sum(columns for _, _, columns in segments)
        self.plan = [piece[1:] for piece in segments[0][1]]
        self.height = sum(rows for _, _, rows in self.plan)
        for _, pieces, _ in segments:
            assert [piece[3] for piece in pieces] == [rows for _, _, rows in self.plan]


def piece_source(ref, lead, first, count):
    for index in lead:
        ref = ref.at[index]
    return ref.at[:, pl.ds(first, count)]


class Cols:
    def __init__(self, array, first, count):
        self.source = array
        self.first = first
        self.count = count

    @property
    def array(self):
        return self.source if isinstance(self.source, jax.Array) else self.source.value

    @property
    def shape(self):
        return (self.array.shape[0], self.count)

    @property
    def dtype(self):
        return self.array.dtype

    @property
    def size(self):
        return self.array.shape[0] * self.count

    def value(self):
        return self.array[:, self.first : self.first + self.shape[1]]


def plain(value):
    return value.value() if isinstance(value, Cols) else value


def anywhere(count):
    return [pl.BlockSpec(memory_space=pl.ANY)] * count


class Stream:
    def __init__(self, weights, tile, late):
        self.weights = weights
        self.tile = tile
        self.late = late
        self.steps = weights[0].columns // tile

    def pieces_of(self):
        return [pieces for w in self.weights for _, pieces, _ in w.segments]

    def specs(self):
        return [pl.BlockSpec(memory_space=pltpu.SMEM)] + anywhere(sum(len(p) for p in self.pieces_of()) + len(self.late))

    def operands(self):
        offsets = jnp.concatenate([offs for w in self.weights for offs, _, _ in w.segments])
        arrays = [piece[0] for pieces in self.pieces_of() for piece in pieces]
        return [offsets] + arrays + [v.array if isinstance(v, Cols) else v for v in self.late]

    def scratch(self):
        shapes = []
        for w in self.weights:
            shapes += [pltpu.VMEM((2, w.height, self.tile), low), pltpu.SemaphoreType.DMA((2, len(w.plan)))]
        for value in self.late:
            shapes += [pltpu.VMEM(value.shape, value.dtype), pltpu.SemaphoreType.DMA((1,))]
        return shapes

    def bind(self, operand_refs, scratch_refs):
        self.offs = operand_refs[0]
        refs = list(operand_refs[1:])
        self.refs = []
        for w in self.weights:
            mine = []
            for _, pieces, _ in w.segments:
                mine.append(refs[: len(pieces)])
                refs = refs[len(pieces) :]
            self.refs.append(mine)
        self.buffers = scratch_refs[0 : 2 * len(self.weights) : 2]
        self.sems = scratch_refs[1 : 2 * len(self.weights) : 2]
        rest = scratch_refs[2 * len(self.weights) :]
        self.late_bufs = rest[0::2]
        self.late_copies = []
        for value, ref, buf, sem in zip(self.late, refs, rest[0::2], rest[1::2]):
            if isinstance(value, Cols):
                ref = ref.at[:, pl.ds(value.first, value.shape[1])]
            self.late_copies.append(pltpu.make_async_copy(ref, buf, sem.at[0]))

    def segment_copies(self, index, number, column, slot):
        w = self.weights[index]
        base = sum(len(x.plan) * len(x.segments) for x in self.weights[:index]) + number * len(w.plan)
        out = []
        for at, (_, lead, first, rows) in enumerate(w.segments[number][1]):
            source = piece_source(self.refs[index][number][at], lead, pl.multiple_of(first + column, 128), self.tile)
            start = pl.multiple_of(self.offs[base + at], 16)
            target = self.buffers[index].at[slot, pl.ds(start, rows), :]
            out.append(pltpu.make_async_copy(source, target, self.sems[index].at[slot, at]))
        return out

    def copies(self, step, slot):
        return [copy for index in range(len(self.weights)) for copy in self.segment_copies(index, 0, step * self.tile, slot)]

    def start_tile(self, step, slot):
        for index, w in enumerate(self.weights):
            first = 0
            for number, (_, _, columns) in enumerate(w.segments):
                count = columns // self.tile

                def start():
                    for copy in self.segment_copies(index, number, (step - first) * self.tile, slot):
                        copy.start()

                if len(w.segments) == 1:
                    start()
                else:
                    pl.when(jnp.logical_and(step >= first, step < first + count))(start)
                first += count

    def wait_tile(self, slot):
        for index in range(len(self.weights)):
            for copy in self.segment_copies(index, 0, 0, slot):
                copy.wait()

    def advance(self):
        step = pl.program_id(0)
        slot = lax.rem(step, 2)

        @pl.when(step == 0)
        def _():
            self.start_tile(jnp.int32(0), 0)
            for copy in self.late_copies:
                copy.start()

        @pl.when(step + 1 < self.steps)
        def _():
            self.start_tile(step + 1, 1 - slot)

        self.wait_tile(slot)
        return step, [buf.at[slot] for buf in self.buffers]

    def wait_late(self):
        for copy in self.late_copies:
            copy.wait()
        return self.late_bufs


def stream_call(name, stream, body, ins, in_specs, outs, out_specs, scratch, flops, mib=58):
    operands = stream.operands()
    frame = stream.scratch()

    def kernel(*refs):
        count = len(operands)
        ops, refs = refs[:count], refs[count:]
        inputs, refs = refs[: len(ins)], refs[len(ins) :]
        outputs, refs = refs[: len(outs)], refs[len(outs) :]
        stream.bind(ops, refs[: len(frame)])
        body(stream, inputs, outputs, refs[len(frame) :])

    moved = sum(v.size * v.dtype.itemsize for v in list(ins) + list(stream.late) + list(outs))
    moved += sum(2 * w.height * w.columns for w in stream.weights)
    return pl.pallas_call(
        kernel,
        grid=(stream.steps,),
        in_specs=stream.specs() + in_specs,
        out_specs=out_specs,
        out_shape=outs,
        scratch_shapes=frame + scratch,
        compiler_params=params(mib),
        cost_estimate=pl.CostEstimate(flops=flops, bytes_accessed=moved, transcendentals=0),
        name=name,
    )(*operands, *ins)


def by_rows(tokens, fun, step=128):
    @pl.loop(0, tokens // step)
    def _(i):
        fun(pl.ds(pl.multiple_of(i * step, step), step))


def take(ref, rows):
    return ref[rows, :] if ref.shape[0] > 1 else ref[...]


def give(ref, rows, value):
    if ref.shape[0] > 1:
        ref[rows, :] = value.astype(ref.dtype)
    else:
        ref[...] += jnp.sum(value, axis=0, keepdims=True)


def like(shape, dtype):
    return jax.ShapeDtypeStruct(shape, dtype)


def ada_matmul(value, weight, bias):
    tokens = value.shape[0]
    tile = weight.height
    stream = Stream([weight], tile, [])

    def body(stream, ins, outs, scratch):
        _, (w,) = stream.advance()
        outs[0][...] = matmul(ins[0][...], w[...]) + ins[1][...]

    return stream_call(
        "ada",
        stream,
        body,
        [value, bias],
        [whole(value.shape), pl.BlockSpec((1, tile), lambda j: (0, j))],
        [like((tokens, weight.columns), full)],
        [pl.BlockSpec((tokens, tile), lambda j: (0, j))],
        [],
        2 * tokens * weight.height * weight.columns,
    )[0]


def mod_partial(row, weight, width):
    shard = weight.shape[1]
    tall = jnp.broadcast_to(row, (16, shard))

    def body(x_ref, w_ref, out_ref):
        out_ref[0] = matmul(x_ref[...], w_ref[...])[:8]

    out = pl.pallas_call(
        body,
        grid=(6,),
        in_specs=[whole(tall.shape), pl.BlockSpec((None, shard, width), lambda j: (0, 0, j))],
        out_specs=pl.BlockSpec((1, 8, width), lambda j: (j, 0, 0)),
        out_shape=like((6, 8, width), full),
        compiler_params=params(60),
        cost_estimate=pl.CostEstimate(flops=0, bytes_accessed=12 * shard * width, transcendentals=0),
        name="modpart",
    )(tall, weight)
    return out[:, 0]


def qkv_matmul(value, weight, cosine, sine, gains, member, member_t, head):
    tokens, width = value.shape
    stream = Stream([weight], width, [cosine, sine])

    def body(stream, ins, outs, scratch):
        x_ref, gain_ref, mem_ref, memt_ref = ins
        q_ref, kv_ref, raw_ref = outs
        (acc_ref,) = scratch
        step, (w,) = stream.advance()
        cos_ref, sin_ref = stream.late_bufs
        acc_ref[...] = matmul(x_ref[...], w[...])

        @pl.when(step == 0)
        def _():
            stream.wait_late()

        def head_norm(part, out, cols):
            def rows_of(rows):
                raw = acc_ref[rows, :]
                raw_ref[rows, :] = raw
                mean = head_mean(raw * raw, mem_ref[...], head)
                inverse = split_dot(lax.rsqrt(mean + epsilon), memt_ref[...])
                normed = raw * inverse * gain_ref[part : part + 1, :]
                even = even_lanes(gain_ref, raw.shape)
                out[rows, cols] = turned(normed, cos_ref[rows, :], sin_ref[rows, :], even, head // 4).astype(low)

            by_rows(tokens, rows_of, 256)

        @pl.when(step == 0)
        def _():
            head_norm(0, q_ref, slice(0, width))

        @pl.when(step == 1)
        def _():
            head_norm(1, kv_ref, slice(0, width))

        @pl.when(step == 2)
        def _():
            kv_ref[:, width:] = acc_ref[...].astype(low)

    flat = like((tokens, width), low)
    return stream_call(
        "qkv",
        stream,
        body,
        [value, gains, member, member_t],
        [whole(v.shape) for v in (value, gains, member, member_t)],
        [flat, like((tokens, 2 * width), low), like((tokens, 2 * width), full)],
        [whole((tokens, width)), whole((tokens, 2 * width)), pl.BlockSpec((tokens, width), lambda j: (0, jnp.minimum(j, 1)))],
        [pltpu.VMEM((tokens, width), full)],
        2 * tokens * weight.height * weight.columns,
    )


def out_matmul(value, weight, hidden0, mods):
    tokens, width = value.shape
    stream = Stream([weight], 384, [hidden0] + mods)

    def body(stream, ins, outs, scratch):
        att_ref, h1_ref, b_ref = outs
        (acc_ref,) = scratch
        step, (w,) = stream.advance()
        acc_ref[step] = matmul(ins[0][...], w[...])

        @pl.when(step == stream.steps - 1)
        def _():
            h0_ref, gate_ref, shift_ref, scale_ref = stream.wait_late()

            def rows_of(rows):
                att = jnp.concatenate([acc_ref[k, rows, :] for k in range(stream.steps)], axis=1)
                hidden1 = h0_ref[rows, :] + take(gate_ref, rows) * att
                normed = hidden1 * rms_scale(hidden1)
                att_ref[rows, :] = att.astype(low)
                h1_ref[rows, :] = hidden1
                b_ref[rows, :] = (normed * (1.0 + take(scale_ref, rows)) + take(shift_ref, rows)).astype(low)

            by_rows(tokens, rows_of)

    return stream_call(
        "attout",
        stream,
        body,
        [value],
        [whole(value.shape)],
        [like((tokens, width), low), like((tokens, width), full), like((tokens, width), low)],
        [whole((tokens, width))] * 3,
        [pltpu.VMEM((stream.steps, tokens, 384), full)],
        2 * tokens * weight.height * weight.columns,
    )


def gate_up_matmul(value, gate, up):
    tokens, width = value.shape
    tile = 1024
    stream = Stream([gate, up], tile, [])

    def body(stream, ins, outs, scratch):
        hid_ref, g_ref, u_ref = outs
        _, (wg, wu) = stream.advance()
        g = matmul(ins[0][...], wg[...])
        u = matmul(ins[0][...], wu[...])
        g_ref[...] = g.astype(low)
        u_ref[...] = u.astype(low)
        hid_ref[...] = (g * jax.nn.sigmoid(g) * u).astype(low)

    flat = like((tokens, gate.columns), low)
    return stream_call(
        "gateup",
        stream,
        body,
        [value],
        [whole(value.shape)],
        [flat] * 3,
        [pl.BlockSpec((tokens, tile), lambda j: (0, j))] * 3,
        [],
        4 * tokens * gate.height * gate.columns,
    )


def down_matmul(value, weight, hidden1, gate):
    tokens, depth = value.shape
    width = weight.columns
    stream = Stream([weight], width, [hidden1, gate])

    def body(stream, ins, outs, scratch):
        mlp_ref, h2_ref = outs
        (acc_ref,) = scratch
        hid_ref = ins[0]
        at = 0
        copies = stream.copies(0, 0)
        for copy in copies + stream.late_copies:
            copy.start()
        for k, (_, _, rows) in enumerate(weight.plan):
            copies[k].wait()
            first = stream.offs[k]
            left = hid_ref[:, pl.ds(pl.multiple_of(first, 128), rows)]
            part = matmul(left, stream.buffers[0][0, pl.ds(pl.multiple_of(first, 128), rows), :])
            if k == 0:
                acc_ref[...] = part
            else:
                acc_ref[...] += part
        h1_ref, gate_ref = stream.wait_late()

        def rows_of(rows):
            mlp = acc_ref[rows, :]
            mlp_ref[rows, :] = mlp.astype(low)
            h2_ref[rows, :] = h1_ref[rows, :] + take(gate_ref, rows) * mlp

        by_rows(tokens, rows_of)

    return stream_call(
        "down",
        stream,
        body,
        [value],
        [whole(value.shape)],
        [like((tokens, width), low), like((tokens, width), full)],
        [whole((tokens, width))] * 2,
        [pltpu.VMEM((tokens, width), full)],
        2 * tokens * depth * width,
    )


def down_back(grad, weight, gate_pre, up_pre):
    tokens, width = grad.shape
    depth = weight.height
    stream = Stream([weight], width, [gate_pre, up_pre])

    def body(stream, ins, outs, scratch):
        dg_ref, du_ref = outs
        copies = stream.copies(0, 0)
        for copy in copies + stream.late_copies:
            copy.start()
        for k, (_, _, count) in enumerate(weight.plan):
            copies[k].wait()
            if k == 0:
                g_ref, u_ref = stream.wait_late()
            first = pl.multiple_of(stream.offs[k], 128)
            for at in range(0, count, 384):
                cols = pl.ds(pl.multiple_of(first + at, 128), 384)
                inner = matmul_t(ins[0][...], stream.buffers[0][0, cols, :])
                g = g_ref[:, cols].astype(full)
                u = u_ref[:, cols].astype(full)
                sigma = jax.nn.sigmoid(g)
                active = g * sigma
                dg_ref[:, cols] = (inner * u * (sigma + active * (1.0 - sigma))).astype(low)
                du_ref[:, cols] = (inner * active).astype(low)

    flat = like((tokens, depth), low)
    return stream_call(
        "downback",
        stream,
        body,
        [grad],
        [whole(grad.shape)],
        [flat, flat],
        [whole((tokens, depth))] * 2,
        [],
        2 * tokens * depth * width,
    )


def back_matmul(name, grads, weights, tile, late, outs, finish):
    tokens = grads[0].shape[0]
    width = weights[0].height
    stream = Stream(weights, tile, late)

    def body(stream, ins, outs, scratch):
        (acc_ref,) = scratch
        step, tiles = stream.advance()
        part = matmul_t(ins[0][...], tiles[0][...])
        for value, w in zip(ins[1:], tiles[1:]):
            part = part + matmul_t(value[...], w[...])

        @pl.when(step == 0)
        def _():
            acc_ref[...] = part

        @pl.when(step > 0)
        def _():
            acc_ref[...] += part

        @pl.when(step == stream.steps - 1)
        def _():
            refs = stream.wait_late()
            for ref in outs:
                if ref.shape[0] == 1:
                    ref[...] = jnp.zeros_like(ref)
            by_rows(tokens, lambda rows: finish(rows, acc_ref[rows, :], refs, outs))

    return stream_call(
        name,
        stream,
        body,
        list(grads),
        [pl.BlockSpec((tokens, tile), lambda j: (0, j))] * len(grads),
        outs,
        [whole(value.shape) for value in outs],
        [pltpu.VMEM((tokens, width), full)],
        2 * tokens * width * weights[0].columns * len(weights),
    )


def mlp_back(grads, weights, grad2, hidden1, att, mods):
    tokens, width = grad2.shape
    lead = mods[0].shape[0]

    def finish(rows, db, refs, outs):
        dh2_ref, h1_ref, att_ref, scale_ref, gate_ref = refs
        hidden1 = h1_ref[rows, :]
        inverse = rms_scale(hidden1)
        normed = hidden1 * inverse
        weighted = db * (1.0 + take(scale_ref, rows))
        back = inverse * (weighted - normed * jnp.mean(normed * weighted, axis=-1, keepdims=True))
        grad1 = dh2_ref[rows, :] + back
        outs[0][rows, :] = grad1
        outs[1][rows, :] = (grad1 * take(gate_ref, rows)).astype(low)
        give(outs[2], rows, db)
        give(outs[3], rows, db * normed)
        give(outs[4], rows, grad1 * att_ref[rows, :].astype(full))

    outs = [like((tokens, width), full), like((tokens, width), low)]
    outs += [like((lead, width), low if lead > 1 else full)] * 3
    return back_matmul("mlpback", grads, weights, 1024, [grad2, hidden1, att] + mods, outs, finish)


def qkv_back(grad, weight, grad1, hidden0, scale):
    tokens, width = grad1.shape
    lead = scale.shape[0]

    def finish(rows, da, refs, outs):
        dh1_ref, h0_ref, scale_ref = refs
        hidden0 = h0_ref[rows, :]
        inverse = rms_scale(hidden0)
        normed = hidden0 * inverse
        weighted = da * (1.0 + take(scale_ref, rows))
        back = inverse * (weighted - normed * jnp.mean(normed * weighted, axis=-1, keepdims=True))
        outs[0][rows, :] = (dh1_ref[rows, :] + back).astype(low)
        give(outs[1], rows, da)
        give(outs[2], rows, da * normed)

    outs = [like((tokens, width), low)] + [like((lead, width), low if lead > 1 else full)] * 2
    return back_matmul("qkvback", [grad], [weight], width, [grad1, hidden0, scale], outs, finish)


def out_back(grad, weight):
    def finish(rows, value, refs, outs):
        outs[0][rows, :] = value.astype(low)

    return back_matmul("outback", [grad], [weight], 1152, [], [like(grad.shape, low)], finish)[0]


def ada_back(grads, weight, cond):
    tokens, width = cond.shape
    tile = weight.height
    stream = Stream([weight], tile, [cond])

    def body(stream, ins, outs, scratch):
        (acc_ref,) = scratch
        step, (w,) = stream.advance()
        for k, grad in enumerate(ins):

            @pl.when(step == k)
            def _():
                part = matmul_t(grad[...], w[...])
                acc_ref[...] = part if k == 0 else acc_ref[...] + part

        @pl.when(step == stream.steps - 1)
        def _():
            (cond_ref,) = stream.wait_late()

            def rows_of(rows):
                cond = cond_ref[rows, :]
                sigma = jax.nn.sigmoid(cond)
                outs[0][rows, :] = acc_ref[rows, :] * sigma * (1.0 + cond * (1.0 - sigma))

            by_rows(tokens, rows_of)

    return stream_call(
        "adaback",
        stream,
        body,
        list(grads),
        [whole(grad.shape) for grad in grads],
        [like((tokens, width), full)],
        [whole((tokens, width))],
        [pltpu.VMEM((tokens, width), full)],
        2 * tokens * width * weight.columns,
    )[0]


def ordered_grad(left, order, rights, tile):
    tokens, width = left.shape
    many = len(rights) > 1
    columns = sum(right.shape[1] for right in rights)
    steps = columns // tile

    def body(order_ref, left_ref, *refs):
        ys, out_ref, turned_ref = refs[: len(rights)], refs[-2], refs[-1]
        step = pl.program_id(0)

        @pl.when(step == 0)
        def _():
            turned_ref[...] = matmul_t(order_ref[...], left_ref[...]).astype(low)

        if not many:
            out_ref[...] = matmul(turned_ref[...], ys[0][...]).astype(low)
            return
        for k, y in enumerate(ys):

            @pl.when(step == k)
            def _():
                out_ref[...] = matmul(turned_ref[...], y[...]).astype(low)

    tiles = [whole(right.shape) for right in rights] if many else [pl.BlockSpec((tokens, tile), lambda j: (0, j))]
    return pl.pallas_call(
        body,
        grid=(steps,),
        in_specs=[whole(order.shape), whole(left.shape)] + tiles,
        out_specs=pl.BlockSpec((width, tile), lambda j: (0, j)),
        out_shape=like((width, columns), low),
        scratch_shapes=[pltpu.VMEM((width, tokens), low)],
        compiler_params=params(56),
        cost_estimate=pl.CostEstimate(
            flops=2 * tokens * width * (columns + width), bytes_accessed=2 * width * (columns + 2 * width), transcendentals=0
        ),
        name="wgrad",
    )(order, left, *rights)


def down_grad(left, right, groups):
    tokens, depth = left.shape
    columns = right.shape[1]
    tile = depth // groups

    def body(left_ref, right_ref, out_ref):
        value = outer_sum(left_ref[...], right_ref[...]).astype(low)
        out_ref[0, 0] = value[: tile // 2]
        out_ref[1, 0] = value[tile // 2 :]

    return pl.pallas_call(
        body,
        grid=(groups,),
        in_specs=[pl.BlockSpec((tokens, tile), lambda j: (0, j)), whole(right.shape)],
        out_specs=pl.BlockSpec((2, 1, tile // 2, columns), lambda j: (0, j, 0, 0)),
        out_shape=like((2, groups, tile // 2, columns), low),
        compiler_params=params(40),
        cost_estimate=pl.CostEstimate(
            flops=2 * tokens * depth * columns, bytes_accessed=2 * depth * (columns + tokens), transcendentals=0
        ),
        name="wdown",
    )(left, right)


def tie(value, *others):
    others = [v for v in others if v is not None]
    if not others:
        return value
    return lax.optimization_barrier((value, *others))[0]


class Flight:
    def __init__(self, token):
        self.token = token
        self.held = []
        self.todo = []
        self.later = []

    def send(self, value, item, holder, name):
        setattr(holder, name, swap(tie(value, self.token), item))
        self.held.append((holder, name))

    def watch(self, holder, name):
        self.held.append((holder, name))

    def then(self, action):
        self.todo.append(action)

    def fence(self, values, starts=()):
        values = list(values)
        held, todo = self.held, self.todo
        self.held, self.todo = [], []
        held += [(holder, name) for left, holder, name in self.later if left == 0]
        self.later = [(left - 1, holder, name) for left, holder, name in self.later if left > 0]
        arrays = values + [getattr(holder, name) for holder, name in held]
        arrays = lax.optimization_barrier(tuple(arrays))
        self.token = arrays[0]
        for (holder, name), value in zip(held, arrays[len(values) :]):
            setattr(holder, name, value)
        for action in todo:
            action()
        for start in starts:
            start(self)
        return arrays[: len(values)]


class Bundle:
    def __init__(self, place, own, shards, parts, which, relay_bit):
        self.row, self.col, coords = place
        self.own = own
        self.shards = shards
        self.parts = parts
        self.which = which
        self.relay_bit = relay_bit
        self.rows = shards[parts[0][0]].shape[1]
        self.half = self.rows // 2
        self.at = coords[relay_bit] * self.half

    def over_col(self, flight):
        at = tie(self.at, flight.token)
        mine = [
            lax.dynamic_slice(self.shards[name], (self.which, at, first), (1, self.half, n))[0]
            for name, first, n in self.parts
        ]
        flight.send(jnp.concatenate(mine, axis=1), "col", self, "first")

    def relay(self, flight):
        flight.send(self.first, self.relay_bit, self, "second")

    def first_row(self, flight):
        flight.send(self.first, "row", self, "first_s")

    def second_row(self, flight):
        flight.send(self.second, "row", self, "second_s")

    def rows_both(self, flight):
        self.first_row(flight)
        self.second_row(flight)

    def segment(self, wanted):
        row, col, rows, half, at = self.row, self.col, self.rows, self.half, self.at
        other = (2 * row + 1 - col) * rows
        other_s = (2 * (1 - row) + 1 - col) * rows
        offsets = [col * rows, (col + 2) * rows, other + at, other_s + at]
        offsets += [other + (half - at), other_s + (half - at)]
        offsets = jnp.stack(offsets).astype(jnp.int32)
        begin = 0
        for name, first, n in self.parts:
            if name == wanted:
                own_all = self.own[name]
                lead = () if own_all.ndim == 3 else (self.which,)
                pieces = [(own_all, (0,) + lead, first, rows), (own_all, (1,) + lead, first, rows)]
                got = [self.first, self.first_s, self.second, self.second_s]
                pieces += [(value, (), begin, half) for value in got]
                return (offsets, pieces, n)
            begin += n
        raise KeyError(wanted)


def weight_of(name, *bundles):
    return Weight([bundle.segment(name) for bundle in bundles])


def item_weight(item):
    return {"row": 2, "col": 1}.get(item) or 4 << item


def halving_order(path, width, block, me, bits):
    at = jnp.arange(width)
    position = at // block
    owner = me
    for item in reversed(path):
        if item == "hi":
            mask = (1 << (bits - 1)) - 1
            owner = (owner & 7) | ((position & mask) << 3)
            position = position >> (bits - 1)
            continue
        bit = position & 1
        position = position >> 1
        if item == "row":
            owner = (owner & ~2) | (2 * bit)
        else:
            owner = owner ^ (bit * item_weight(item))
    return owner * block + at % block


class Slice:
    def __init__(self, held, columns, name="value"):
        self.held = held
        self.columns = columns
        self.name = name

    def get(self):
        return getattr(self.held, self.name)[..., self.columns]


class Share:
    def __init__(self, value, order, path):
        self.terms = [(value, list(order))]
        self.order = list(order)
        self.path = list(path)
        self.done = []
        self.result = None
        self.columns = None

    def pick(self, value, order, choice):
        order = list(order)
        while order and any(item in choice for item in order[:2]):
            rows, columns = value.shape
            if order[0] in choice:
                at = choice[order.pop(0)] * (rows // 2)
                value = value[at : at + rows // 2]
            else:
                at = choice[order.pop(1)]
                value = value.reshape(2, 2, rows // 4, columns)[:, at].reshape(rows // 2, columns)
        return value

    def collect(self, last=None):
        choice = {item: 0 for item in self.done}
        if last is not None:
            choice[last] = 1
        total = None
        for value, order in self.terms:
            value = value.get() if isinstance(value, Slice) else value
            part = self.pick(value, order, choice).astype(full)
            total = part if total is None else total + part
        return total

    def send(self, item):
        away = self.collect(item).astype(low)
        self.done.append(item)
        self.order = [other for other in self.order if other != item]
        return away

    def arrive(self, got):
        self.terms.append((got, self.order))

    @property
    def value(self):
        return self.collect() if self.result is None else self.result.get().astype(full)

    @property
    def base(self):
        return self.terms[0][0]

    @base.setter
    def base(self, value):
        self.terms[0] = (value, self.terms[0][1])


class BlockShare(Share):
    def __init__(self, value, order, path, coords):
        super().__init__(value, order, path)
        self.coords = coords

    def pick(self, value, order, choice):
        starts = [jnp.bitwise_xor(self.coords[item], choice[item]) if item in choice else 0 for item in order] + [0, 0]
        sizes = [1 if item in choice else 2 for item in order] + list(value.shape[-2:])
        if self.columns is not None and value.shape[-1] != self.columns[1]:
            starts[-1], sizes[-1] = self.columns
        value = lax.dynamic_slice(value, starts, sizes)
        return value.reshape([size for size in sizes[:-2] if size > 1] + list(sizes[-2:]))


class Total:
    def __init__(self, value, path):
        self.value = value
        self.path = list(path)

    def send(self, item):
        return self.value.astype(low)

    def arrive(self, got):
        self.value = self.value + got.astype(full)


class TotalAndRows(Total):
    def __init__(self, value, count, path):
        super().__init__(value, path)
        self.count = count

    def arrive(self, got):
        n = self.count
        value = self.value
        got = got.astype(full)
        self.value = jnp.concatenate([value[:n] + got[:n], value[n:], got[n:]], axis=0)


class Parcel:
    got = None


def last_share(value, bits):
    groups = [[2 * k + low_bit for k in range(1 << (bits - 1))] for low_bit in (0, 1)]
    return lax.psum_scatter(value, "dp", scatter_dimension=0, axis_index_groups=groups, tiled=False)


class Agenda:
    def __init__(self):
        self.tasks = {}

    def scatter(self, bits, windows, *names):
        def action(flight):
            tasks = [self.tasks[name] for name in names]
            parts = [task.collect().astype(low) for task in tasks]
            height = 1 << (bits - 1)
            block = parts[0].shape[-2] if isinstance(tasks[0], BlockShare) else parts[0].shape[0] // height
            value = parts[0] if len(parts) == 1 else jnp.concatenate(parts, axis=-1)
            value = value.reshape(height, block, value.shape[-1])
            parcel = Parcel()
            parcel.got = last_share(tie(value, flight.token), bits)
            flight.later.append((windows, parcel, "got"))
            at = 0
            for task, part in zip(tasks, parts):
                assert task.path.pop(0) == "hi"
                n = part.shape[-1]
                task.result = Slice(parcel, slice(at, at + n), "got")
                at += n

        return action

    def go(self, *names):
        def action(flight):
            tasks = [self.tasks[name] for name in names]
            items = [task.path.pop(0) for task in tasks]
            assert len(set(items)) == 1
            sent = [task.send(items[0]) for task in tasks]
            parcel = Parcel()
            away = sent[0] if len(sent) == 1 else jnp.concatenate(sent, axis=-1)
            flight.send(away, items[0], parcel, "got")

            def arrive():
                at = 0
                for task, value in zip(tasks, sent):
                    n = value.shape[-1]
                    task.arrive(parcel.got if len(tasks) == 1 else parcel.got[..., at : at + n])
                    at += n

            flight.then(arrive)

        return action


def row_sum(value):
    return lax.psum_scatter(value, "row", scatter_dimension=0, tiled=True)


def grad_blocks(left, right, bits, block):
    if (4 * block) % 128 == 0:
        value = down_grad(left, right, 2**bits)
    else:
        value = outer_sum(left, right).astype(low).reshape(2**bits, 2, 2 * block, right.shape[1])
        value = jnp.swapaxes(value, 0, 1)
    return value.reshape((2,) * (bits + 2) + (block, right.shape[1]))


def block_forward(hidden0, mods, mats, gains, tabs, flight, points):
    shift1, scale1, gate1, shift2, scale2, gate2 = mods
    cosine, sine, member, member_t, head = tabs
    used = {}

    def mat(name):
        used[name] = mats[name]()
        return used[name]

    def fence(point, *values):
        if point not in points:
            return values if len(values) > 1 else values[0]
        values = flight.fence(values, points[point])
        return values if len(values) > 1 else values[0]

    attn_in = (hidden0 * rms_scale(hidden0) * (1.0 + plain(scale1)) + plain(shift1)).astype(low)
    attn_in = fence("qkv", attn_in)
    query, kv, raw = qkv_matmul(attn_in, mat("qkv"), cosine, sine, gains[0], member, member_t, head)
    query, kv = fence("attend", query, kv)
    kv_r = swap(kv, "row")
    out_b, lse = attend(query, kv, kv_r, head)
    out_b = fence("out", out_b)
    att, hidden1, mlp_in = out_matmul(out_b, mat("out"), hidden0, [gate1, shift2, scale2])
    mlp_in = fence("gate", mlp_in)
    inner, gate_pre, up_pre = gate_up_matmul(mlp_in, mat("gate"), mat("up"))
    inner = fence("down", inner)
    mlp_out, hidden2 = down_matmul(inner, mat("down"), hidden1, gate2)
    cache = (hidden0, attn_in, raw, query, kv, kv_r, out_b, lse, att)
    cache += (hidden1, mlp_in, gate_pre, up_pre, inner, mlp_out)
    used = tuple(used[name] for name in ("qkv", "out", "gate", "up", "down"))
    return hidden2, cache, used


class Sum:
    value = None


def block_backward(grad2, cache, mods, mats, gains, tabs, comm, tag, plan):
    (hidden0, attn_in, raw, query, kv, kv_r, out_b, lse, att) = cache[:9]
    (hidden1, mlp_in, gate_pre, up_pre, inner, mlp_out) = cache[9:]
    shift1, scale1, gate1, shift2, scale2, gate2 = mods
    qkv_w, out_w, gate_w, up_w, down_w = mats
    cosine, sine, member, member_t, head = tabs
    flight, agenda, orders, paths, coords = comm
    n_data = lax.axis_size("dp")
    bits = (n_data - 1).bit_length()
    block = down_w.height // (4 * n_data)

    def fence(point, *values):
        values = flight.fence(values, plan.get(point, ()))
        return values if len(values) > 1 else values[0]

    def grad_of(left, name, right, tile):
        return ordered_grad(left, orders[name], [right], tile)

    def watch(name, task):
        agenda.tasks[name + tag] = task
        flight.watch(task, "base")

    def begin(name, value):
        path = paths[name][1:]
        watch(name[0], Share(value, path, path))

    def begin_halves(name, value, cut):
        path = paths[name][1:]
        other = [path[1], path[0]] + path[2:]
        held = Sum()
        held.value = value
        flight.watch(held, "value")
        agenda.tasks[name[0] + "a" + tag] = Share(Slice(held, slice(0, cut)), path, path)
        agenda.tasks[name[0] + "b" + tag] = Share(Slice(held, slice(cut, None)), path, other)

    def begin_down(value):
        order = ["row"] + list(reversed(range(bits))) + ["col"]
        if tag == "0":
            watch("d", BlockShare(value, order, paths["down"], coords))
            return
        watch("d", BlockShare(value, order, ["row"], coords))

    grad_mlp = (grad2 * plain(gate2)).astype(low)
    dgate2 = grad2 * mlp_out.astype(full)
    if gate2.shape[0] == 1:
        dgate2 = jnp.sum(dgate2, axis=0, keepdims=True)
    begin_down(grad_blocks(inner, grad_mlp, bits, block))
    grad2, grad_mlp = fence("start", grad2, grad_mlp)
    grad_gate, grad_up = down_back(grad_mlp, down_w, gate_pre, up_pre)
    w_gate = grad_of(mlp_in, "gate", grad_gate, 1024)
    w_up = grad_of(mlp_in, "up", grad_up, 1024)
    grad_gate, grad_up, w_gate, w_up = fence("gate", grad_gate, grad_up, w_gate, w_up)
    r_gate = row_sum(w_gate)
    r_up = row_sum(w_up)
    grad1, grad_att, dshift2, dscale2, dgate1 = mlp_back(
        [grad_gate, grad_up], [gate_w, up_w], grad2, hidden1, att, [scale2, gate1]
    )
    grad_att = fence("out", grad_att)
    w_out = grad_of(out_b, "out", grad_att, 384)
    grad_ob = out_back(grad_att, out_w)
    begin("gate", r_gate)
    begin("up", r_up)
    grad_ob, w_out = fence("attend", grad_ob, w_out)
    r_out = row_sum(w_out)
    dq, dkv, dkv_r = attend_back(query, kv, kv_r, grad_ob, out_b, lse, head)
    begin("out", r_out)
    dq, dkv_r = fence("qk", dq, dkv_r)
    grad_qkv, gain_rows = qk_back(dq, dkv, swap(dkv_r, "row"), raw, cosine, sine, gains[1], member, member_t, head)
    w_qkv = grad_of(attn_in, "qkv", grad_qkv, 1152)
    grad_qkv, w_qkv = fence("qkv", grad_qkv, w_qkv)
    r_qkv = row_sum(w_qkv)
    grad0, dshift1, dscale1 = qkv_back(grad_qkv, qkv_w, grad1, hidden0, scale1)
    dmods = [dshift1, dscale1, dgate1, dshift2, dscale2, dgate2]
    begin_halves("qkv", r_qkv, r_qkv.shape[1] // 256 * 128)
    return grad0, dmods, gain_rows[:2], begin_halves


def per_device(
    latents,
    levels,
    timesteps,
    patch_weight,
    patch_bias,
    ada_weight,
    ada_bias,
    qkv_weight,
    qk_gains,
    out_weight,
    gate_weight,
    up_weight,
    down_weight,
    cotangent,
):
    images, slots, chans, rows_loc, cols_loc = latents.shape
    n_data = lax.axis_size("dp")
    assert images == 1 and slots == 2
    assert lax.axis_size("row") == 2 and lax.axis_size("col") == 2
    row = lax.axis_index("row")
    col = lax.axis_index("col")
    data = lax.axis_index("dp")
    bits = (n_data - 1).bit_length()
    left = col == 0
    coords = {"row": row, "col": col}
    place = (row, col, coords)
    for k in range(bits):
        coords[k] = (data >> k) & 1
    grid_rows = rows_loc // 2
    grid_cols = cols_loc
    half_cols = grid_cols // 2
    tokens = grid_rows * grid_cols
    width = cotangent.shape[-1]
    head = qk_gains.shape[2]
    heads = width // head
    pvals = chans * 4
    shard = width // 4
    me = data * 4 + row * 2 + col
    own_rows = width // (4 * n_data)

    def pair(own, other, axis):
        return jnp.concatenate([jnp.where(left, own, other), jnp.where(left, other, own)], axis=axis)

    own = {}
    for name, s in (
        ("qkv", qkv_weight),
        ("out", out_weight),
        ("gate", gate_weight),
        ("up", up_weight),
        ("down", down_weight),
        ("ada", ada_weight),
    ):
        own[name] = lax.all_gather(s, "row", axis=0)
    shards = {"qkv": qkv_weight, "out": out_weight, "gate": gate_weight, "up": up_weight, "down": down_weight}
    shards["ada"] = ada_weight

    def bundle(which, relay_bit, *parts):
        return Bundle(place, own, shards, parts, which, relay_bit)

    ff = gate_weight.shape[2]
    b_q0 = bundle(0, 0, ("qkv", 0, width))
    b_kv0 = bundle(0, 1, ("qkv", width, 2 * width))
    b_out0 = bundle(0, 0, ("out", 0, width))
    b_gate0 = bundle(0, 0, ("gate", 0, ff))
    b_up0 = bundle(0, 1, ("up", 0, ff))
    b_down0 = bundle(0, 0, ("down", 0, width))
    b_ada_a = bundle(1, 1, ("ada", 0, 3 * width))
    b_ada_b = bundle(1, 0, ("ada", 3 * width, 3 * width))
    b_qkv1 = bundle(1, 1, ("qkv", 0, 3 * width))
    b_og1 = bundle(1, 0, ("out", 0, width), ("gate", 0, ff))
    b_up1 = bundle(1, 1, ("up", 0, ff))
    b_down1 = bundle(1, 0, ("down", 0, width))
    enc_mats = {
        "qkv": lambda: weight_of("qkv", b_q0, b_kv0),
        "out": lambda: weight_of("out", b_out0),
        "gate": lambda: weight_of("gate", b_gate0),
        "up": lambda: weight_of("up", b_up0),
        "down": lambda: weight_of("down", b_down0),
    }
    dec_mats = {
        "qkv": lambda: weight_of("qkv", b_qkv1),
        "out": lambda: weight_of("out", b_og1),
        "gate": lambda: weight_of("gate", b_og1),
        "up": lambda: weight_of("up", b_up1),
        "down": lambda: weight_of("down", b_down1),
    }

    small = jnp.concatenate(
        [jnp.swapaxes(patch_weight, 1, 2).reshape(2 * pvals, shard), patch_bias, ada_bias.reshape(12, shard)], axis=0
    )
    small_other = swap(small, "col")
    blk = latents[0]
    blk_other = swap(blk, "col")
    flight = Flight(small)

    class Start:
        pass

    Start.small, Start.blk = small_other, blk_other
    flight.watch(Start, "small")
    flight.watch(Start, "blk")
    (blk,) = flight.fence([blk])
    small = pair(small[None], Start.small[None], 0)
    wide = pair(blk, Start.blk, 3)
    flight.send(small, "row", Start, "small")
    flight.send(wide[:, :, rows_loc - 1 :], "row", Start, "top")
    small, wide = flight.fence([small, wide], [b_q0.over_col, b_kv0.over_col])
    temb = time_features(tie(timesteps, wide)[0], width)
    small = jnp.where(row == 0, jnp.stack([small, Start.small]), jnp.stack([Start.small, small]))
    small = small.reshape(4, 2 * pvals + 14, shard)
    patch_w = small[:, : 2 * pvals].transpose(1, 0, 2).reshape(2, pvals, width)
    patch_b = small[:, 2 * pvals : 2 * pvals + 2].transpose(1, 0, 2).reshape(2, width).astype(full)
    ada_b = small[:, 2 * pvals + 2 :].reshape(4, 2, 6 * shard).transpose(1, 0, 2).reshape(2, 6, width).astype(full)

    framed = jnp.concatenate([Start.top, wide[:, :, : rows_loc - 1]], axis=2)
    framed = jnp.concatenate([framed[..., -1:], framed[..., :-1]], axis=3)
    patches = (
        framed.reshape(slots, chans, grid_rows, 2, grid_cols, 2).transpose(0, 2, 4, 1, 3, 5).reshape(slots, tokens, pvals)
    )
    enc_patches = patches[0]
    dec_patches = jnp.where(left, patches[0], patches[1])

    sil0 = jax.nn.silu(temb[:1]).astype(low)
    temb_own = jnp.where(left, temb[:1], temb[1:])
    part = mod_partial(lax.dynamic_slice(sil0, (0, (2 * row + col) * shard), (1, shard)), ada_weight, width)

    cot_own = jnp.where(left, cotangent[0, 0], cotangent[0, 1])

    class Cotangent:
        got = None

    def send_cotangent(flight):
        flight.send(jnp.where(left, cotangent[0, 1], cotangent[0, 0]), "col", Cotangent, "got")

    quarter = head // 4
    lanes = tie(jnp.arange(width), flight.token)
    within = lanes % head
    section = within // quarter
    lane_freq = jnp.exp(-math.log(10000.0) * (within % quarter).astype(full) / quarter)
    row_pos = (row * grid_rows + jnp.arange(grid_rows)).astype(full)
    col_pos = jnp.arange(grid_cols).astype(full)
    row_angle = row_pos[:, None] * lane_freq[None, :]
    col_angle = col_pos[:, None] * lane_freq[None, :]
    by_row = section < 2
    sign = jnp.where(section % 2 == 0, -1.0, 1.0).astype(full)

    def table(fun):
        return jnp.where(by_row, fun(row_angle)[:, None, :], fun(col_angle)[None, :, :]).reshape(tokens, width)

    cosine = table(jnp.cos)
    sine = table(jnp.sin) * sign
    member = (lanes[:, None] // head == jnp.arange(128)[None, :]).astype(low)
    tabs = (cosine, sine, member, member.T, head)
    gain_rows = jnp.tile(qk_gains.astype(full), (1, 1, heads))
    even = jnp.broadcast_to((section % 2 == 0).astype(full), (2, 1, width))
    temper = head ** (-0.5) * math.log2(math.e)
    scaled = jnp.concatenate([gain_rows[:, :1] * temper, gain_rows[:, 1:], even], axis=1)
    gain_rows = jnp.concatenate([gain_rows, even], axis=1)
    gain_rows = [(scaled[k], gain_rows[k]) for k in range(2)]

    rest = list(range(2, bits))
    path_y = ["row", "col", 0, "hi"]
    path_x = ["row", 0, "col", "hi"]
    path_s = ["row", "col", 0, 1] + rest
    path_z = ["row", 1, "col", 0] + rest
    paths = {"down": path_z, "gate": path_y, "up": path_x, "out": path_x, "qkv": path_y, "ada": path_s}
    perm = {}
    orders = {}
    for name in ("gate", "up", "out", "qkv", "ada"):
        key = tuple(paths[name])
        if key not in perm:
            source = halving_order(paths[name], width, own_rows, me, bits)
            perm[key] = lax.optimization_barrier((source[:, None] == lanes[None, :]).astype(low))
        orders[name] = perm[key]

    enc_h0 = matmul(enc_patches, patch_w[0]) + patch_b[0]
    starts = [b_q0.relay, b_kv0.relay, b_out0.over_col, b_q0.first_row, b_kv0.first_row]
    enc_h0, part, cosine, sine = flight.fence([enc_h0, part, cosine, sine], starts)
    part = part + swap(part, "row")
    part = part + swap(part, "col")
    enc_mod = part + ada_b[0]
    enc_mods = [enc_mod[k : k + 1] for k in range(6)]
    tabs = (cosine, sine) + tabs[2:]
    points = {
        "qkv": [b_q0.second_row, b_kv0.second_row, b_gate0.over_col, b_out0.relay],
        "attend": [b_up0.over_col, b_gate0.relay, b_out0.first_row],
        "out": [b_out0.second_row, b_up0.relay, b_down0.over_col, b_gate0.rows_both],
        "gate": [b_up0.rows_both, b_ada_a.over_col, b_down0.relay],
        "down": [b_down0.rows_both, b_qkv1.over_col, b_ada_a.relay],
    }
    encoded, enc_cache, enc_mats = block_forward(enc_h0, enc_mods, enc_mats, gain_rows[0], tabs, flight, points)
    dec_h0 = matmul(dec_patches, patch_w[1]) + patch_b[1]
    cond = encoded + temb_own
    dec_sil = jax.nn.silu(cond).astype(low)
    (dec_sil,) = flight.fence([dec_sil], [b_ada_a.rows_both, b_ada_b.over_col, b_qkv1.relay])
    ada_bias1 = ada_b[1].reshape(1, 6 * width)
    mod_a = ada_matmul(dec_sil, weight_of("ada", b_ada_a), ada_bias1[:, : 3 * width])
    dec_mods = [Cols(mod_a, k * width, width) for k in range(3)]
    held = Sum()

    def second_mods(flight):
        held.value = ada_matmul(tie(dec_sil, flight.token), weight_of("ada", b_ada_b), ada_bias1[:, 3 * width :])
        flight.watch(held, "value")

    dec_mods += [Cols(held, k * width, width) for k in range(3)]
    points = {
        "qkv": [b_qkv1.rows_both, b_og1.over_col, b_ada_b.relay],
        "attend": [b_ada_b.rows_both, second_mods, b_up1.over_col, b_og1.relay],
        "out": [b_og1.rows_both, b_down1.over_col, b_up1.relay],
        "gate": [b_up1.rows_both, b_down1.relay, send_cotangent],
        "down": [b_down1.rows_both],
    }
    decoded, dec_cache, dec_mats = block_forward(dec_h0, dec_mods, dec_mats, gain_rows[1], tabs, flight, points)
    live = (col < levels[0]).astype(full)
    result = (decoded * live).astype(low).reshape(grid_rows, grid_cols, width)
    near = jnp.where(left, result[:, :half_cols], result[:, half_cols:])
    far = jnp.where(left, result[:, half_cols:], result[:, :half_cols])

    class Away:
        got = None

    def send_result(flight):
        flight.send(far, "col", Away, "got")


    agenda = Agenda()
    go = agenda.go
    scatter = functools.partial(agenda.scatter, bits)
    comm = (flight, agenda, orders, paths, coords)
    cot = pair(cot_own, Cotangent.got, 1).reshape(tokens, width)
    dec_grad2 = cot.astype(full) * live

    def split_down(flight):
        whole_sum = agenda.tasks["d1"]
        path = paths["qkv"][1:]
        cut = width // 256 * 128
        for name, columns, way in (
            ("da1", (0, cut), path),
            ("db1", (cut, width - cut), [path[1], path[0]] + path[2:]),
        ):
            part = BlockShare(None, whole_sum.order, way, coords)
            part.terms = list(whole_sum.terms)
            part.done = list(whole_sum.done)
            part.columns = columns
            agenda.tasks[name] = part

    plan = {
        "start": [send_result, go("d1")],
        "gate": [split_down, go("da1"), go("db1")],
        "out": [go("da1"), go("db1")],
        "attend": [go("g1"), go("u1"), scatter(1, "da1", "db1")],
        "qk": [go("g1"), go("u1")],
        "qkv": [go("o1")],
    }
    dec_grad0, dec_dmods, dec_gains, begin_halves = block_backward(
        dec_grad2, dec_cache, dec_mods, dec_mats, gain_rows[1], tabs, comm, "1", plan
    )
    away = Away.got
    result = jnp.stack([jnp.where(left, near, away), jnp.where(left, away, near)])[None]
    dec_dmods = [piece.astype(low) for piece in dec_dmods]
    w_ada = ordered_grad(dec_sil, orders["ada"], dec_dmods, width)
    starts = [go("qa1"), go("qb1"), go("o1")]
    w_ada, *dec_dmods = flight.fence([w_ada] + dec_dmods, starts)
    r_ada = row_sum(w_ada)
    dec_bada = jnp.stack([jnp.sum(piece.astype(full), axis=0) for piece in dec_dmods])
    enc_grad2 = ada_back(dec_dmods, weight_of("ada", b_ada_a, b_ada_b), cond)

    def patch_rows(patch, grad):
        ones = jnp.ones((tokens, 1), low)
        return outer_sum(jnp.concatenate([patch, ones], axis=1), grad)

    total = jnp.concatenate([patch_rows(dec_patches, dec_grad0), dec_bada, dec_gains], axis=0)
    agenda.tasks["s"] = Total(total, ["row", "col"] + list(range(bits)))

    begin_halves("ada", r_ada, r_ada.shape[1] // 2)
    plan = {
        "start": [go("s"), go("d0"), go("aa1"), go("ab1"), scatter(0, "g1", "u1")],
        "gate": [go("s"), go("aa1"), go("ab1"), go("qa1"), go("qb1")],
        "out": [go("s")],
        "attend": [go("s"), go("g0"), go("u0"), go("d0"), scatter(1, "qa1", "qb1", "o1")],
        "qk": [go("s"), go("g0"), go("u0"), go("aa1", "ab1")],
        "qkv": [go("d0"), go("o0"), go("aa1", "ab1")],
    }
    enc_grad0, enc_dmods, enc_gains, _ = block_backward(
        enc_grad2, enc_cache, enc_mods, enc_mats, gain_rows[0], tabs, comm, "0", plan
    )
    dmod_enc = jnp.concatenate(enc_dmods, axis=0)
    total = jnp.concatenate([patch_rows(enc_patches, enc_grad0), enc_gains, dmod_enc], axis=0)
    def image(dpatch):
        return (
            dpatch.reshape(grid_rows, grid_cols, chans, 2, 2).transpose(2, 0, 3, 1, 4).reshape(chans, rows_loc, 2 * cols_loc)
        )

    enc_image = image(matmul_t(enc_grad0, patch_w[0]))
    dec_image = image(matmul_t(dec_grad0, patch_w[1]))
    zero = jnp.zeros_like(dec_image)
    grads = jnp.stack([enc_image + jnp.where(left, dec_image, zero), jnp.where(left, zero, dec_image)])
    grads = jnp.concatenate([grads[..., 1:], grads[..., :1]], axis=3)

    class Last:
        pass

    total, grads = flight.fence([total, grads])
    flight.send(total, "row", Last, "total")
    flight.send(grads[:, :, :1], "row", Last, "below")
    total, grads = flight.fence([total, grads], [go("qa0"), go("qb0"), scatter(1, "g0", "u0")])
    total = total + Last.total
    flight.send(total, "col", Last, "total")
    grads = jnp.concatenate([grads[:, :, 1:], Last.below], axis=2)
    one = grads[..., :cols_loc]
    two = grads[..., cols_loc:]
    flight.send(jnp.where(left, two, one), "col", Last, "image")
    count = pvals + 3
    tiny = TotalAndRows(None, count, list(range(bits)))
    agenda.tasks["t"] = tiny

    def begin_tiny(flight):
        tiny.value = jnp.concatenate([total + Last.total, sil0.astype(full)], axis=0)
        go("t")(flight)

    flight.fence([total], [begin_tiny, go("qa0"), go("qb0"), go("o0"), go("d0")])
    latent_grad = (jnp.where(left, one, two) + Last.image)[None]
    flight.fence([total], [scatter(1, "qa0", "qb0", "o0"), go("t"), go("d0")])
    flight.fence([total], [go("t")])
    flight.fence([total])
    while any(task.path for task in agenda.tasks.values()):
        flight.fence([total], [go(name) for name, task in agenda.tasks.items() if task.path])
        flight.fence([total])
    dec_small = agenda.tasks["s"].value
    total = tiny.value[:count]
    dmod_all = tiny.value[count:]
    dmod_all = dmod_all.reshape(n_data, 7, width)
    enc_small = total
    enc_ada = jnp.dot(
        lax.dynamic_slice(dmod_all, (0, 6, me * own_rows), (n_data, 1, own_rows))[:, 0].T,
        dmod_all[:, :6].reshape(n_data, 6 * width),
        precision=highest,
        preferred_element_type=full,
    )
    enc_bada = jnp.sum(dmod_all[:, :6], axis=0)

    def own_lanes(value):
        return lax.dynamic_slice(value, (0, me * own_rows), (value.shape[0], own_rows))

    enc_patch = own_lanes(enc_small[: pvals + 1])
    dec_patch = own_lanes(dec_small[: pvals + 1])
    g_patch = jnp.stack([enc_patch[:pvals].T, dec_patch[:pvals].T])
    g_patch_b = jnp.stack([enc_patch[pvals], dec_patch[pvals]])
    bada = jnp.stack([enc_bada.reshape(-1), dec_small[pvals + 1 : pvals + 7].reshape(-1)])
    own_bada = 6 * own_rows
    g_bada = lax.dynamic_slice(bada, (0, me * own_bada), (2, own_bada))
    gains = jnp.stack([enc_small[pvals + 1 :], dec_small[pvals + 7 :]])
    gains = gains.reshape(2, 2, heads, head).sum(axis=2)
    def both(name):
        parts = [agenda.tasks[name + tag].value.astype(full) for tag in "01"]
        return jnp.stack(parts)

    for task in agenda.tasks.values():
        assert not task.path
    g_ada = jnp.concatenate([agenda.tasks["aa1"].value, agenda.tasks["ab1"].value], axis=1)
    g_ada_all = jnp.stack([enc_ada, g_ada.astype(full)])
    g_qkv = jnp.concatenate([both("qa"), both("qb")], axis=2)
    down1 = jnp.concatenate([agenda.tasks["da1"].value, agenda.tasks["db1"].value], axis=1)
    g_down = jnp.stack([agenda.tasks["d0"].value.astype(full), down1.astype(full)])
    stacked = [g_qkv, both("o"), both("g"), both("u"), g_down]
    return (
        result,
        latent_grad,
        g_patch,
        g_patch_b,
        g_ada_all,
        g_bada,
        stacked[0],
        gains,
        stacked[1],
        stacked[2],
        stacked[3],
        stacked[4],
    )


def solution(mesh):
    tile = ("row", "col")
    every = ("dp", "row", "col")
    return jax.shard_map(
        per_device,
        mesh=mesh,
        in_specs=(
            P("dp", None, None, "row", "col"),
            P("dp"),
            P("dp", None),
            P(None, tile, None),
            P(None, tile),
            P(None, tile, None),
            P(None, tile),
            P(None, tile, None),
            P(),
            P(None, tile, None),
            P(None, tile, None),
            P(None, tile, None),
            P(None, tile, None),
            P("dp", None, "row", "col", None),
        ),
        out_specs=(
            P("dp", None, "row", "col", None),
            P("dp", None, None, "row", "col"),
            P(None, every, None),
            P(None, every),
            P(None, every, None),
            P(None, every),
            P(None, every, None),
            P(),
            P(None, every, None),
            P(None, every, None),
            P(None, every, None),
            P(None, every, None),
        ),
        check_vma=False,
    )
```

```python
import functools
import math

import jax
import jax.numpy as jnp
from jax import lax
from jax.experimental import pallas as pl
from jax.experimental.pallas import tpu as pltpu
from jax.sharding import PartitionSpec as P

epsilon = 1e-06
highest = lax.Precision.HIGHEST
low = jnp.bfloat16
full = jnp.float32
WINDOW = 256
PAIR = 2
MIB = 1 << 20


def matmul(left, right):
    return jnp.dot(left, right, preferred_element_type=full)


def matmul_t(left, right):
    return lax.dot_general(left, right, (((1,), (1,)), ((), ())), preferred_element_type=full)


def outer_sum(left, right):
    return lax.dot_general(left, right, (((0,), (0,)), ((), ())), preferred_element_type=full)


def rms_scale(value):
    return lax.rsqrt(jnp.mean(value * value, axis=-1, keepdims=True) + epsilon)


def rms_back(value, inverse, grad):
    return inverse * grad - value * inverse**3 * jnp.mean(value * grad, axis=-1, keepdims=True)


def swap(value, item):
    if isinstance(item, str):
        return lax.ppermute(value, item, [(0, 1), (1, 0)])
    size = lax.axis_size("dp")
    return lax.ppermute(value, "dp", [(i, i ^ (1 << item)) for i in range(size)])


def time_features(steps, width):
    half = width // 2
    freqs = jnp.exp(-math.log(10000.0) * jnp.arange(half).astype(full) / half)
    angles = steps.astype(full)[:, None] * freqs[None, :]
    return jnp.concatenate([jnp.cos(angles), jnp.sin(angles)], axis=-1)


def whole(shape):
    return pl.BlockSpec(shape, lambda *_: (0,) * len(shape))


def params(mib):
    return pltpu.CompilerParams(vmem_limit_bytes=mib * MIB)


def head_mean(value, member, head):
    return matmul(value.astype(low), member) * (1.0 / head)


def split_dot(value, onehot):
    top = value.astype(low)
    rest = (value - top.astype(full)).astype(low)
    return matmul(top, onehot) + matmul(rest, onehot)


def turned(value, cosine, sine, even, quarter):
    width = value.shape[-1]
    ahead = pltpu.roll(value, width - quarter, axis=1)
    behind = pltpu.roll(value, quarter, axis=1)
    return value * cosine + jnp.where(even, ahead, behind) * sine


def even_lanes(gain_ref, shape):
    return jnp.broadcast_to(gain_ref[2:3, :] > 0.5, shape)


def qk_back_body(head, dq_ref, dkv_ref, dkvx_ref, qkv_ref, cos_ref, sin_ref, gain_ref, mem_ref, memt_ref, out_ref, gg_ref):
    width = dq_ref.shape[-1]

    @pl.when(pl.program_id(0) == 0)
    def _():
        gg_ref[...] = jnp.zeros_like(gg_ref)

    cosine = cos_ref[...]
    sine = -sin_ref[...]
    even = even_lanes(gain_ref, cosine.shape)
    member = mem_ref[...]
    member_t = memt_ref[...]
    grads = (dq_ref[...], dkv_ref[:, :width] + dkvx_ref[:, :width].astype(full))
    for part in (0, 1):
        value = qkv_ref[:, part * width : (part + 1) * width]
        mean = head_mean(value * value, member, head)
        inverse_h = lax.rsqrt(mean + epsilon)
        inverse = split_dot(inverse_h, member_t)
        grad_n = turned(grads[part], cosine, sine, even, head // 4)
        normed = value * inverse
        gg_ref[part : part + 1, :] += jnp.sum(grad_n * normed, axis=0, keepdims=True)
        weighted = grad_n * gain_ref[part : part + 1, :]
        dots = head_mean(value * weighted, member, head) * inverse_h * inverse_h
        back = inverse * weighted - normed * split_dot(dots, member_t)
        out_ref[:, part * width : (part + 1) * width] = back.astype(low)
    out_ref[:, 2 * width :] = (dkv_ref[:, width:] + dkvx_ref[:, width:].astype(full)).astype(low)


def qk_back(dq, dkv, dkvx, raw, cosine, sine, gains, member, member_t, head):
    tokens, width = dq.shape
    step = 256
    rows = lambda n: pl.BlockSpec((step, n), lambda i: (i, 0))
    return pl.pallas_call(
        functools.partial(qk_back_body, head),
        grid=(tokens // step,),
        in_specs=[rows(width)]
        + [rows(2 * width)] * 3
        + [rows(width), rows(width), whole(gains.shape), whole(member.shape), whole(member_t.shape)],
        out_specs=[rows(3 * width), whole((8, width))],
        out_shape=[jax.ShapeDtypeStruct((tokens, 3 * width), low), jax.ShapeDtypeStruct((8, width), full)],
        compiler_params=params(60),
        cost_estimate=pl.CostEstimate(flops=60 * raw.size, bytes_accessed=18 * raw.size, transcendentals=0),
        name="qk_back",
    )(dq, dkv, dkvx, raw, cosine, sine, gains, member, member_t)


def head_window(head, width, part):
    index = pl.program_id(0) * PAIR + part
    start = index * head
    base = jnp.minimum(lax.div(start, 128) * 128, width - WINDOW)
    return index, pl.multiple_of(base, 128), start - base


def window_mask(shape, offset, head):
    lane = lax.broadcasted_iota(jnp.int32, shape, 1)
    return jnp.logical_and(lane >= offset, lane < offset + head)


def attend_body(head, q_ref, kvl_ref, kvr_ref, o_ref, lse_ref, acc_ref):
    tokens, width = q_ref.shape

    @pl.when(pl.program_id(0) == 0)
    def _():
        acc_ref[...] = jnp.zeros_like(acc_ref)
        lse_ref[...] = jnp.zeros_like(lse_ref)

    step = 256
    one = jnp.ones((), low)
    lane = lax.broadcasted_iota(jnp.int32, (step, lse_ref.shape[1]), 1)
    for part in range(PAIR):
        index, base, offset = head_window(head, width, part)
        cols = pl.ds(base, WINDOW)
        vals = pl.ds(pl.multiple_of(width + base, 128), WINDOW)
        mask_k = window_mask((tokens, WINDOW), offset, head)
        value_l = jnp.where(mask_k, kvl_ref[:, vals], one)
        value_r = jnp.where(mask_k, kvr_ref[:, vals], one)
        mask = window_mask((step, WINDOW), offset, head)
        for first in range(0, tokens, step):
            rows = slice(first, first + step)
            query = jnp.where(mask, q_ref[rows, cols], jnp.zeros((), low))
            left = jnp.exp2(matmul_t(query, kvl_ref[:, cols])).astype(low)
            right = jnp.exp2(matmul_t(query, kvr_ref[:, cols])).astype(low)
            out = matmul(left, value_l) + matmul(right, value_r)
            total = jnp.max(jnp.where(mask, 0.0, out), axis=1, keepdims=True)
            acc_ref[rows, cols] += jnp.where(mask, out * (1.0 / total), 0.0)
            lse_ref[rows, :] += jnp.where(lane == index, jnp.log2(total), 0.0)

    @pl.when(pl.program_id(0) == pl.num_programs(0) - 1)
    def _():
        o_ref[...] = acc_ref[...].astype(low)


def attend(query, kv_l, kv_r, head):
    tokens, width = query.shape
    heads = width // head
    return pl.pallas_call(
        functools.partial(attend_body, head),
        grid=(heads // PAIR,),
        in_specs=[whole((tokens, width))] + [whole((tokens, 2 * width))] * 2,
        out_specs=[whole((tokens, width)), whole((tokens, 128))],
        out_shape=[jax.ShapeDtypeStruct((tokens, width), low), jax.ShapeDtypeStruct((tokens, 128), full)],
        scratch_shapes=[pltpu.VMEM((tokens, width), full)],
        compiler_params=params(56),
        cost_estimate=pl.CostEstimate(
            flops=8 * tokens * tokens * WINDOW * heads, bytes_accessed=14 * tokens * width, transcendentals=2 * tokens * tokens * heads
        ),
        name="attend",
    )(query, kv_l, kv_r)


def in_three(column):
    top = column.astype(low)
    rest = column - top.astype(full)
    middle = rest.astype(low)
    return top, middle, (rest - middle.astype(full)).astype(low)


def attend_back_body(head, q_ref, kvl_ref, kvr_ref, do_ref, o_ref, lse_ref, dq_ref, dl_ref, dr_ref, dr_acc):
    tokens, width = q_ref.shape
    temper = head ** (-0.5)

    @pl.when(pl.program_id(0) == 0)
    def _():
        for ref in (dq_ref, dl_ref, dr_acc):
            ref[...] = jnp.zeros_like(ref)

    shape = (tokens, WINDOW)
    lane = lax.broadcasted_iota(jnp.int32, shape, 1)
    small = lax.broadcasted_iota(jnp.int32, lse_ref.shape, 1)
    zero = jnp.zeros((), low)
    for part in range(PAIR):
        index, base, offset = head_window(head, width, part)
        cols = pl.ds(base, WINDOW)
        vals = pl.ds(pl.multiple_of(width + base, 128), WINDOW)
        mask = window_mask(shape, offset, head)
        spare = jnp.where(offset >= 3, 0, WINDOW - 3)
        minus = jnp.where(jnp.logical_and(lane >= spare, lane < spare + 3), -jnp.ones((), low), zero)
        query = jnp.where(mask, q_ref[:, cols], zero)
        grad = jnp.where(mask, do_ref[:, cols], zero)
        delta = jnp.sum(grad.astype(full) * o_ref[:, cols].astype(full), axis=1, keepdims=True)
        level = jnp.sum(jnp.where(small == index, lse_ref[...], 0.0), axis=1, keepdims=True)
        query_x = query
        grad_x = grad
        for k, (a, b) in enumerate(zip(in_three(level), in_three(delta))):
            at = lane == spare + k
            query_x = jnp.where(at, a, query_x)
            grad_x = jnp.where(at, b, grad_x)
        grad_q = 0.0
        for ref, acc in ((kvl_ref, dl_ref), (kvr_ref, dr_acc)):
            key = jnp.where(mask, ref[:, cols], minus)
            value = jnp.where(mask, ref[:, vals], minus)
            prob = jnp.exp2(matmul_t(key, query_x))
            grad_s = (prob * matmul_t(value, grad_x)).astype(low)
            acc[:, vals] += matmul(prob.astype(low), grad)
            acc[:, cols] += matmul(grad_s, query)
            grad_q = grad_q + outer_sum(grad_s, key)
        dq_ref[:, cols] += jnp.where(mask, grad_q * temper, 0.0)

    @pl.when(pl.program_id(0) == pl.num_programs(0) - 1)
    def _():
        back = math.log(2.0)
        dl_ref[:, :width] = dl_ref[:, :width] * back
        dr_ref[:, :width] = (dr_acc[:, :width] * back).astype(low)
        dr_ref[:, width:] = dr_acc[:, width:].astype(low)


def attend_back(query, kv_l, kv_r, grad, out, levels, head):
    tokens, width = query.shape
    heads = width // head
    both = (tokens, 2 * width)
    one = (tokens, width)
    return pl.pallas_call(
        functools.partial(attend_back_body, head),
        grid=(heads // PAIR,),
        in_specs=[whole(one), whole(both), whole(both), whole(one), whole(one), whole(levels.shape)],
        out_specs=[whole(one), whole(both), whole(both)],
        out_shape=[like(one, full), like(both, full), like(both, low)],
        scratch_shapes=[pltpu.VMEM(both, full)],
        compiler_params=params(62),
        cost_estimate=pl.CostEstimate(
            flops=20 * tokens * tokens * WINDOW * heads, bytes_accessed=28 * tokens * width, transcendentals=2 * tokens * tokens * heads
        ),
        name="attend_back",
    )(query, kv_l, kv_r, grad, out, levels)


class Weight:
    def __init__(self, segments):
        self.segments = segments
        self.columns = sum(columns for _, _, columns in segments)
        self.plan = [piece[1:] for piece in segments[0][1]]
        self.height = sum(rows for _, _, rows in self.plan)
        for _, pieces, _ in segments:
            assert [piece[3] for piece in pieces] == [rows for _, _, rows in self.plan]


def piece_source(ref, lead, first, count):
    for index in lead:
        ref = ref.at[index]
    return ref.at[:, pl.ds(first, count)]


class Cols:
    def __init__(self, array, first, count):
        self.source = array
        self.first = first
        self.count = count

    @property
    def array(self):
        return self.source if isinstance(self.source, jax.Array) else self.source.value

    @property
    def shape(self):
        return (self.array.shape[0], self.count)

    @property
    def dtype(self):
        return self.array.dtype

    @property
    def size(self):
        return self.array.shape[0] * self.count

    def value(self):
        return self.array[:, self.first : self.first + self.shape[1]]


def plain(value):
    return value.value() if isinstance(value, Cols) else value


def anywhere(count):
    return [pl.BlockSpec(memory_space=pl.ANY)] * count


class Stream:
    def __init__(self, weights, tile, late):
        self.weights = weights
        self.tile = tile
        self.late = late
        self.steps = weights[0].columns // tile

    def pieces_of(self):
        return [pieces for w in self.weights for _, pieces, _ in w.segments]

    def specs(self):
        return [pl.BlockSpec(memory_space=pltpu.SMEM)] + anywhere(sum(len(p) for p in self.pieces_of()) + len(self.late))

    def operands(self):
        offsets = jnp.concatenate([offs for w in self.weights for offs, _, _ in w.segments])
        arrays = [piece[0] for pieces in self.pieces_of() for piece in pieces]
        return [offsets] + arrays + [v.array if isinstance(v, Cols) else v for v in self.late]

    def scratch(self):
        shapes = []
        for w in self.weights:
            shapes += [pltpu.VMEM((2, w.height, self.tile), low), pltpu.SemaphoreType.DMA((2, len(w.plan)))]
        for value in self.late:
            shapes += [pltpu.VMEM(value.shape, value.dtype), pltpu.SemaphoreType.DMA((1,))]
        return shapes

    def bind(self, operand_refs, scratch_refs):
        self.offs = operand_refs[0]
        refs = list(operand_refs[1:])
        self.refs = []
        for w in self.weights:
            mine = []
            for _, pieces, _ in w.segments:
                mine.append(refs[: len(pieces)])
                refs = refs[len(pieces) :]
            self.refs.append(mine)
        self.buffers = scratch_refs[0 : 2 * len(self.weights) : 2]
        self.sems = scratch_refs[1 : 2 * len(self.weights) : 2]
        rest = scratch_refs[2 * len(self.weights) :]
        self.late_bufs = rest[0::2]
        self.late_copies = []
        for value, ref, buf, sem in zip(self.late, refs, rest[0::2], rest[1::2]):
            if isinstance(value, Cols):
                ref = ref.at[:, pl.ds(value.first, value.shape[1])]
            self.late_copies.append(pltpu.make_async_copy(ref, buf, sem.at[0]))

    def segment_copies(self, index, number, column, slot):
        w = self.weights[index]
        base = sum(len(x.plan) * len(x.segments) for x in self.weights[:index]) + number * len(w.plan)
        out = []
        for at, (_, lead, first, rows) in enumerate(w.segments[number][1]):
            source = piece_source(self.refs[index][number][at], lead, pl.multiple_of(first + column, 128), self.tile)
            start = pl.multiple_of(self.offs[base + at], 16)
            target = self.buffers[index].at[slot, pl.ds(start, rows), :]
            out.append(pltpu.make_async_copy(source, target, self.sems[index].at[slot, at]))
        return out

    def copies(self, step, slot):
        return [copy for index in range(len(self.weights)) for copy in self.segment_copies(index, 0, step * self.tile, slot)]

    def start_tile(self, step, slot):
        for index, w in enumerate(self.weights):
            first = 0
            for number, (_, _, columns) in enumerate(w.segments):
                count = columns // self.tile

                def start():
                    for copy in self.segment_copies(index, number, (step - first) * self.tile, slot):
                        copy.start()

                if len(w.segments) == 1:
                    start()
                else:
                    pl.when(jnp.logical_and(step >= first, step < first + count))(start)
                first += count

    def wait_tile(self, slot):
        for index in range(len(self.weights)):
            for copy in self.segment_copies(index, 0, 0, slot):
                copy.wait()

    def advance(self):
        step = pl.program_id(0)
        slot = lax.rem(step, 2)

        @pl.when(step == 0)
        def _():
            self.start_tile(jnp.int32(0), 0)
            for copy in self.late_copies:
                copy.start()

        @pl.when(step + 1 < self.steps)
        def _():
            self.start_tile(step + 1, 1 - slot)

        self.wait_tile(slot)
        return step, [buf.at[slot] for buf in self.buffers]

    def wait_late(self):
        for copy in self.late_copies:
            copy.wait()
        return self.late_bufs


def stream_call(name, stream, body, ins, in_specs, outs, out_specs, scratch, flops, mib=58):
    operands = stream.operands()
    frame = stream.scratch()

    def kernel(*refs):
        count = len(operands)
        ops, refs = refs[:count], refs[count:]
        inputs, refs = refs[: len(ins)], refs[len(ins) :]
        outputs, refs = refs[: len(outs)], refs[len(outs) :]
        stream.bind(ops, refs[: len(frame)])
        body(stream, inputs, outputs, refs[len(frame) :])

    moved = sum(v.size * v.dtype.itemsize for v in list(ins) + list(stream.late) + list(outs))
    moved += sum(2 * w.height * w.columns for w in stream.weights)
    return pl.pallas_call(
        kernel,
        grid=(stream.steps,),
        in_specs=stream.specs() + in_specs,
        out_specs=out_specs,
        out_shape=outs,
        scratch_shapes=frame + scratch,
        compiler_params=params(mib),
        cost_estimate=pl.CostEstimate(flops=flops, bytes_accessed=moved, transcendentals=0),
        name=name,
    )(*operands, *ins)


def by_rows(tokens, fun, step=128):
    @pl.loop(0, tokens // step)
    def _(i):
        fun(pl.ds(pl.multiple_of(i * step, step), step))


def take(ref, rows):
    return ref[rows, :] if ref.shape[0] > 1 else ref[...]


def give(ref, rows, value):
    if ref.shape[0] > 1:
        ref[rows, :] = value.astype(ref.dtype)
    else:
        ref[...] += jnp.sum(value, axis=0, keepdims=True)


def like(shape, dtype):
    return jax.ShapeDtypeStruct(shape, dtype)


def ada_matmul(value, weight, bias):
    tokens = value.shape[0]
    tile = weight.height
    stream = Stream([weight], tile, [])

    def body(stream, ins, outs, scratch):
        _, (w,) = stream.advance()
        outs[0][...] = matmul(ins[0][...], w[...]) + ins[1][...]

    return stream_call(
        "ada",
        stream,
        body,
        [value, bias],
        [whole(value.shape), pl.BlockSpec((1, tile), lambda j: (0, j))],
        [like((tokens, weight.columns), full)],
        [pl.BlockSpec((tokens, tile), lambda j: (0, j))],
        [],
        2 * tokens * weight.height * weight.columns,
    )[0]


def mod_partial(row, weight, width):
    shard = weight.shape[1]
    tall = jnp.broadcast_to(row, (16, shard))

    def body(x_ref, w_ref, out_ref):
        out_ref[0] = matmul(x_ref[...], w_ref[...])[:8]

    out = pl.pallas_call(
        body,
        grid=(6,),
        in_specs=[whole(tall.shape), pl.BlockSpec((None, shard, width), lambda j: (0, 0, j))],
        out_specs=pl.BlockSpec((1, 8, width), lambda j: (j, 0, 0)),
        out_shape=like((6, 8, width), full),
        compiler_params=params(60),
        cost_estimate=pl.CostEstimate(flops=0, bytes_accessed=12 * shard * width, transcendentals=0),
        name="modpart",
    )(tall, weight)
    return out[:, 0]


def qkv_matmul(value, weight, cosine, sine, gains, member, member_t, head):
    tokens, width = value.shape
    stream = Stream([weight], width, [cosine, sine])

    def body(stream, ins, outs, scratch):
        x_ref, gain_ref, mem_ref, memt_ref = ins
        q_ref, kv_ref, raw_ref = outs
        (acc_ref,) = scratch
        step, (w,) = stream.advance()
        cos_ref, sin_ref = stream.late_bufs
        acc_ref[...] = matmul(x_ref[...], w[...])

        @pl.when(step == 0)
        def _():
            stream.wait_late()

        def head_norm(part, out, cols):
            def rows_of(rows):
                raw = acc_ref[rows, :]
                raw_ref[rows, :] = raw
                mean = head_mean(raw * raw, mem_ref[...], head)
                inverse = split_dot(lax.rsqrt(mean + epsilon), memt_ref[...])
                normed = raw * inverse * gain_ref[part : part + 1, :]
                even = even_lanes(gain_ref, raw.shape)
                out[rows, cols] = turned(normed, cos_ref[rows, :], sin_ref[rows, :], even, head // 4).astype(low)

            by_rows(tokens, rows_of, 256)

        @pl.when(step == 0)
        def _():
            head_norm(0, q_ref, slice(0, width))

        @pl.when(step == 1)
        def _():
            head_norm(1, kv_ref, slice(0, width))

        @pl.when(step == 2)
        def _():
            kv_ref[:, width:] = acc_ref[...].astype(low)

    flat = like((tokens, width), low)
    return stream_call(
        "qkv",
        stream,
        body,
        [value, gains, member, member_t],
        [whole(v.shape) for v in (value, gains, member, member_t)],
        [flat, like((tokens, 2 * width), low), like((tokens, 2 * width), full)],
        [whole((tokens, width)), whole((tokens, 2 * width)), pl.BlockSpec((tokens, width), lambda j: (0, jnp.minimum(j, 1)))],
        [pltpu.VMEM((tokens, width), full)],
        2 * tokens * weight.height * weight.columns,
    )


def out_matmul(value, weight, hidden0, mods):
    tokens, width = value.shape
    stream = Stream([weight], 384, [hidden0] + mods)

    def body(stream, ins, outs, scratch):
        att_ref, h1_ref, b_ref = outs
        (acc_ref,) = scratch
        step, (w,) = stream.advance()
        acc_ref[step] = matmul(ins[0][...], w[...])

        @pl.when(step == stream.steps - 1)
        def _():
            h0_ref, gate_ref, shift_ref, scale_ref = stream.wait_late()

            def rows_of(rows):
                att = jnp.concatenate([acc_ref[k, rows, :] for k in range(stream.steps)], axis=1)
                hidden1 = h0_ref[rows, :] + take(gate_ref, rows) * att
                normed = hidden1 * rms_scale(hidden1)
                att_ref[rows, :] = att.astype(low)
                h1_ref[rows, :] = hidden1
                b_ref[rows, :] = (normed * (1.0 + take(scale_ref, rows)) + take(shift_ref, rows)).astype(low)

            by_rows(tokens, rows_of)

    return stream_call(
        "attout",
        stream,
        body,
        [value],
        [whole(value.shape)],
        [like((tokens, width), low), like((tokens, width), full), like((tokens, width), low)],
        [whole((tokens, width))] * 3,
        [pltpu.VMEM((stream.steps, tokens, 384), full)],
        2 * tokens * weight.height * weight.columns,
    )


def gate_up_matmul(value, gate, up):
    tokens, width = value.shape
    tile = 1024
    stream = Stream([gate, up], tile, [])

    def body(stream, ins, outs, scratch):
        hid_ref, g_ref, u_ref = outs
        _, (wg, wu) = stream.advance()
        g = matmul(ins[0][...], wg[...])
        u = matmul(ins[0][...], wu[...])
        g_ref[...] = g.astype(low)
        u_ref[...] = u.astype(low)
        hid_ref[...] = (g * jax.nn.sigmoid(g) * u).astype(low)

    flat = like((tokens, gate.columns), low)
    return stream_call(
        "gateup",
        stream,
        body,
        [value],
        [whole(value.shape)],
        [flat] * 3,
        [pl.BlockSpec((tokens, tile), lambda j: (0, j))] * 3,
        [],
        4 * tokens * gate.height * gate.columns,
    )


def down_matmul(value, weight, hidden1, gate):
    tokens, depth = value.shape
    width = weight.columns
    stream = Stream([weight], width, [hidden1, gate])

    def body(stream, ins, outs, scratch):
        mlp_ref, h2_ref = outs
        (acc_ref,) = scratch
        hid_ref = ins[0]
        at = 0
        copies = stream.copies(0, 0)
        for copy in copies + stream.late_copies:
            copy.start()
        for k, (_, _, rows) in enumerate(weight.plan):
            copies[k].wait()
            first = stream.offs[k]
            left = hid_ref[:, pl.ds(pl.multiple_of(first, 128), rows)]
            part = matmul(left, stream.buffers[0][0, pl.ds(pl.multiple_of(first, 128), rows), :])
            if k == 0:
                acc_ref[...] = part
            else:
                acc_ref[...] += part
        h1_ref, gate_ref = stream.wait_late()

        def rows_of(rows):
            mlp = acc_ref[rows, :]
            mlp_ref[rows, :] = mlp.astype(low)
            h2_ref[rows, :] = h1_ref[rows, :] + take(gate_ref, rows) * mlp

        by_rows(tokens, rows_of)

    return stream_call(
        "down",
        stream,
        body,
        [value],
        [whole(value.shape)],
        [like((tokens, width), low), like((tokens, width), full)],
        [whole((tokens, width))] * 2,
        [pltpu.VMEM((tokens, width), full)],
        2 * tokens * depth * width,
    )


def down_back(grad, weight, gate_pre, up_pre):
    tokens, width = grad.shape
    depth = weight.height
    stream = Stream([weight], width, [gate_pre, up_pre])

    def body(stream, ins, outs, scratch):
        dg_ref, du_ref = outs
        copies = stream.copies(0, 0)
        for copy in copies + stream.late_copies:
            copy.start()
        for k, (_, _, count) in enumerate(weight.plan):
            copies[k].wait()
            if k == 0:
                g_ref, u_ref = stream.wait_late()
            first = pl.multiple_of(stream.offs[k], 128)
            for at in range(0, count, 384):
                cols = pl.ds(pl.multiple_of(first + at, 128), 384)
                inner = matmul_t(ins[0][...], stream.buffers[0][0, cols, :])
                g = g_ref[:, cols].astype(full)
                u = u_ref[:, cols].astype(full)
                sigma = jax.nn.sigmoid(g)
                active = g * sigma
                dg_ref[:, cols] = (inner * u * (sigma + active * (1.0 - sigma))).astype(low)
                du_ref[:, cols] = (inner * active).astype(low)

    flat = like((tokens, depth), low)
    return stream_call(
        "downback",
        stream,
        body,
        [grad],
        [whole(grad.shape)],
        [flat, flat],
        [whole((tokens, depth))] * 2,
        [],
        2 * tokens * depth * width,
    )


def back_matmul(name, grads, weights, tile, late, outs, finish):
    tokens = grads[0].shape[0]
    width = weights[0].height
    stream = Stream(weights, tile, late)

    def body(stream, ins, outs, scratch):
        (acc_ref,) = scratch
        step, tiles = stream.advance()
        part = matmul_t(ins[0][...], tiles[0][...])
        for value, w in zip(ins[1:], tiles[1:]):
            part = part + matmul_t(value[...], w[...])

        @pl.when(step == 0)
        def _():
            acc_ref[...] = part

        @pl.when(step > 0)
        def _():
            acc_ref[...] += part

        @pl.when(step == stream.steps - 1)
        def _():
            refs = stream.wait_late()
            for ref in outs:
                if ref.shape[0] == 1:
                    ref[...] = jnp.zeros_like(ref)
            by_rows(tokens, lambda rows: finish(rows, acc_ref[rows, :], refs, outs))

    return stream_call(
        name,
        stream,
        body,
        list(grads),
        [pl.BlockSpec((tokens, tile), lambda j: (0, j))] * len(grads),
        outs,
        [whole(value.shape) for value in outs],
        [pltpu.VMEM((tokens, width), full)],
        2 * tokens * width * weights[0].columns * len(weights),
    )


def mlp_back(grads, weights, grad2, hidden1, att, mods):
    tokens, width = grad2.shape
    lead = mods[0].shape[0]

    def finish(rows, db, refs, outs):
        dh2_ref, h1_ref, att_ref, scale_ref, gate_ref = refs
        hidden1 = h1_ref[rows, :]
        inverse = rms_scale(hidden1)
        normed = hidden1 * inverse
        weighted = db * (1.0 + take(scale_ref, rows))
        back = inverse * (weighted - normed * jnp.mean(normed * weighted, axis=-1, keepdims=True))
        grad1 = dh2_ref[rows, :] + back
        outs[0][rows, :] = grad1
        outs[1][rows, :] = (grad1 * take(gate_ref, rows)).astype(low)
        give(outs[2], rows, db)
        give(outs[3], rows, db * normed)
        give(outs[4], rows, grad1 * att_ref[rows, :].astype(full))

    outs = [like((tokens, width), full), like((tokens, width), low)]
    outs += [like((lead, width), low if lead > 1 else full)] * 3
    return back_matmul("mlpback", grads, weights, 1024, [grad2, hidden1, att] + mods, outs, finish)


def qkv_back(grad, weight, grad1, hidden0, scale):
    tokens, width = grad1.shape
    lead = scale.shape[0]

    def finish(rows, da, refs, outs):
        dh1_ref, h0_ref, scale_ref = refs
        hidden0 = h0_ref[rows, :]
        inverse = rms_scale(hidden0)
        normed = hidden0 * inverse
        weighted = da * (1.0 + take(scale_ref, rows))
        back = inverse * (weighted - normed * jnp.mean(normed * weighted, axis=-1, keepdims=True))
        outs[0][rows, :] = (dh1_ref[rows, :] + back).astype(low)
        give(outs[1], rows, da)
        give(outs[2], rows, da * normed)

    outs = [like((tokens, width), low)] + [like((lead, width), low if lead > 1 else full)] * 2
    return back_matmul("qkvback", [grad], [weight], width, [grad1, hidden0, scale], outs, finish)


def out_back(grad, weight):
    def finish(rows, value, refs, outs):
        outs[0][rows, :] = value.astype(low)

    return back_matmul("outback", [grad], [weight], 1152, [], [like(grad.shape, low)], finish)[0]


def ada_back(grads, weight, cond):
    tokens, width = cond.shape
    tile = weight.height
    stream = Stream([weight], tile, [cond])

    def body(stream, ins, outs, scratch):
        (acc_ref,) = scratch
        step, (w,) = stream.advance()
        for k, grad in enumerate(ins):

            @pl.when(step == k)
            def _():
                part = matmul_t(grad[...], w[...])
                acc_ref[...] = part if k == 0 else acc_ref[...] + part

        @pl.when(step == stream.steps - 1)
        def _():
            (cond_ref,) = stream.wait_late()

            def rows_of(rows):
                cond = cond_ref[rows, :]
                sigma = jax.nn.sigmoid(cond)
                outs[0][rows, :] = acc_ref[rows, :] * sigma * (1.0 + cond * (1.0 - sigma))

            by_rows(tokens, rows_of)

    return stream_call(
        "adaback",
        stream,
        body,
        list(grads),
        [whole(grad.shape) for grad in grads],
        [like((tokens, width), full)],
        [whole((tokens, width))],
        [pltpu.VMEM((tokens, width), full)],
        2 * tokens * width * weight.columns,
    )[0]


def ordered_grad(left, order, rights, tile):
    tokens, width = left.shape
    many = len(rights) > 1
    columns = sum(right.shape[1] for right in rights)
    steps = columns // tile

    def body(order_ref, left_ref, *refs):
        ys, out_ref, turned_ref = refs[: len(rights)], refs[-2], refs[-1]
        step = pl.program_id(0)

        @pl.when(step == 0)
        def _():
            turned_ref[...] = matmul_t(order_ref[...], left_ref[...]).astype(low)

        if not many:
            out_ref[...] = matmul(turned_ref[...], ys[0][...]).astype(low)
            return
        for k, y in enumerate(ys):

            @pl.when(step == k)
            def _():
                out_ref[...] = matmul(turned_ref[...], y[...]).astype(low)

    tiles = [whole(right.shape) for right in rights] if many else [pl.BlockSpec((tokens, tile), lambda j: (0, j))]
    return pl.pallas_call(
        body,
        grid=(steps,),
        in_specs=[whole(order.shape), whole(left.shape)] + tiles,
        out_specs=pl.BlockSpec((width, tile), lambda j: (0, j)),
        out_shape=like((width, columns), low),
        scratch_shapes=[pltpu.VMEM((width, tokens), low)],
        compiler_params=params(56),
        cost_estimate=pl.CostEstimate(
            flops=2 * tokens * width * (columns + width), bytes_accessed=2 * width * (columns + 2 * width), transcendentals=0
        ),
        name="wgrad",
    )(order, left, *rights)


def down_grad(left, right, groups):
    tokens, depth = left.shape
    columns = right.shape[1]
    tile = depth // groups

    def body(left_ref, right_ref, out_ref):
        value = outer_sum(left_ref[...], right_ref[...]).astype(low)
        out_ref[0, 0] = value[: tile // 2]
        out_ref[1, 0] = value[tile // 2 :]

    return pl.pallas_call(
        body,
        grid=(groups,),
        in_specs=[pl.BlockSpec((tokens, tile), lambda j: (0, j)), whole(right.shape)],
        out_specs=pl.BlockSpec((2, 1, tile // 2, columns), lambda j: (0, j, 0, 0)),
        out_shape=like((2, groups, tile // 2, columns), low),
        compiler_params=params(40),
        cost_estimate=pl.CostEstimate(
            flops=2 * tokens * depth * columns, bytes_accessed=2 * depth * (columns + tokens), transcendentals=0
        ),
        name="wdown",
    )(left, right)


def tie(value, *others):
    others = [v for v in others if v is not None]
    if not others:
        return value
    return lax.optimization_barrier((value, *others))[0]


class Flight:
    def __init__(self, token):
        self.token = token
        self.held = []
        self.todo = []
        self.later = []

    def send(self, value, item, holder, name):
        setattr(holder, name, swap(tie(value, self.token), item))
        self.held.append((holder, name))

    def watch(self, holder, name):
        self.held.append((holder, name))

    def then(self, action):
        self.todo.append(action)

    def fence(self, values, starts=()):
        values = list(values)
        held, todo = self.held, self.todo
        self.held, self.todo = [], []
        held += [(holder, name) for left, holder, name in self.later if left == 0]
        self.later = [(left - 1, holder, name) for left, holder, name in self.later if left > 0]
        arrays = values + [getattr(holder, name) for holder, name in held]
        arrays = lax.optimization_barrier(tuple(arrays))
        self.token = arrays[0]
        for (holder, name), value in zip(held, arrays[len(values) :]):
            setattr(holder, name, value)
        for action in todo:
            action()
        for start in starts:
            start(self)
        return arrays[: len(values)]


class Bundle:
    def __init__(self, place, own, shards, parts, which, relay_bit):
        self.row, self.col, coords = place
        self.own = own
        self.shards = shards
        self.parts = parts
        self.which = which
        self.relay_bit = relay_bit
        self.rows = shards[parts[0][0]].shape[1]
        self.half = self.rows // 2
        self.at = coords[relay_bit] * self.half

    def prepare(self, flight):
        at = tie(self.at, flight.token)
        mine = [
            lax.dynamic_slice(self.shards[name], (self.which, at, first), (1, self.half, n))[0]
            for name, first, n in self.parts
        ]
        self.mine = jnp.concatenate(mine, axis=1)
        flight.watch(self, "mine")

    def over_col(self, flight):
        flight.send(self.mine, "col", self, "first")

    def relay(self, flight):
        flight.send(self.first, self.relay_bit, self, "second")

    def first_row(self, flight):
        flight.send(self.first, "row", self, "first_s")

    def second_row(self, flight):
        flight.send(self.second, "row", self, "second_s")

    def rows_both(self, flight):
        self.first_row(flight)
        self.second_row(flight)

    def segment(self, wanted):
        row, col, rows, half, at = self.row, self.col, self.rows, self.half, self.at
        other = (2 * row + 1 - col) * rows
        other_s = (2 * (1 - row) + 1 - col) * rows
        offsets = [col * rows, (col + 2) * rows, other + at, other_s + at]
        offsets += [other + (half - at), other_s + (half - at)]
        offsets = jnp.stack(offsets).astype(jnp.int32)
        begin = 0
        for name, first, n in self.parts:
            if name == wanted:
                own_all = self.own[name]
                lead = () if own_all.ndim == 3 else (self.which,)
                pieces = [(own_all, (0,) + lead, first, rows), (own_all, (1,) + lead, first, rows)]
                got = [self.first, self.first_s, self.second, self.second_s]
                pieces += [(value, (), begin, half) for value in got]
                return (offsets, pieces, n)
            begin += n
        raise KeyError(wanted)


def weight_of(name, *bundles):
    return Weight([bundle.segment(name) for bundle in bundles])


def item_weight(item):
    return {"row": 2, "col": 1}.get(item) or 4 << item


def halving_order(path, width, block, me, bits):
    at = jnp.arange(width)
    position = at // block
    owner = me
    for item in reversed(path):
        if item == "hi":
            mask = (1 << (bits - 1)) - 1
            owner = (owner & 7) | ((position & mask) << 3)
            position = position >> (bits - 1)
            continue
        bit = position & 1
        position = position >> 1
        if item == "row":
            owner = (owner & ~2) | (2 * bit)
        else:
            owner = owner ^ (bit * item_weight(item))
    return owner * block + at % block


class Slice:
    def __init__(self, held, columns, name="value"):
        self.held = held
        self.columns = columns
        self.name = name

    def get(self):
        return getattr(self.held, self.name)[..., self.columns]


class Share:
    def __init__(self, value, order, path):
        self.terms = [(value, list(order))]
        self.order = list(order)
        self.path = list(path)
        self.done = []
        self.result = None
        self.columns = None

    def pick(self, value, order, choice):
        order = list(order)
        while order and any(item in choice for item in order[:2]):
            rows, columns = value.shape
            if order[0] in choice:
                at = choice[order.pop(0)] * (rows // 2)
                value = value[at : at + rows // 2]
            else:
                at = choice[order.pop(1)]
                value = value.reshape(2, 2, rows // 4, columns)[:, at].reshape(rows // 2, columns)
        return value

    def collect(self, last=None):
        choice = {item: 0 for item in self.done}
        if last is not None:
            choice[last] = 1
        total = None
        for value, order in self.terms:
            value = value.get() if isinstance(value, Slice) else value
            part = self.pick(value, order, choice).astype(full)
            total = part if total is None else total + part
        return total

    def send(self, item):
        away = self.collect(item).astype(low)
        self.done.append(item)
        self.order = [other for other in self.order if other != item]
        return away

    def arrive(self, got):
        self.terms.append((got, self.order))

    @property
    def value(self):
        return self.collect() if self.result is None else self.result.get().astype(full)

    @property
    def base(self):
        return self.terms[0][0]

    @base.setter
    def base(self, value):
        self.terms[0] = (value, self.terms[0][1])


class BlockShare(Share):
    def __init__(self, value, order, path, coords):
        super().__init__(value, order, path)
        self.coords = coords

    def pick(self, value, order, choice):
        starts = [jnp.bitwise_xor(self.coords[item], choice[item]) if item in choice else 0 for item in order] + [0, 0]
        sizes = [1 if item in choice else 2 for item in order] + list(value.shape[-2:])
        if self.columns is not None and value.shape[-1] != self.columns[1]:
            starts[-1], sizes[-1] = self.columns
        value = lax.dynamic_slice(value, starts, sizes)
        return value.reshape([size for size in sizes[:-2] if size > 1] + list(sizes[-2:]))


class Total:
    def __init__(self, value, path):
        self.value = value
        self.path = list(path)

    def send(self, item):
        return self.value.astype(low)

    def arrive(self, got):
        self.value = self.value + got.astype(full)


class TotalAndRows(Total):
    def __init__(self, value, count, path):
        super().__init__(value, path)
        self.count = count

    def arrive(self, got):
        n = self.count
        value = self.value
        got = got.astype(full)
        self.value = jnp.concatenate([value[:n] + got[:n], value[n:], got[n:]], axis=0)


class Parcel:
    got = None


def last_share(value, bits):
    groups = [[2 * k + low_bit for k in range(1 << (bits - 1))] for low_bit in (0, 1)]
    return lax.psum_scatter(value, "dp", scatter_dimension=0, axis_index_groups=groups, tiled=False)


class Agenda:
    def __init__(self):
        self.tasks = {}

    def scatter(self, bits, windows, *names):
        def action(flight):
            tasks = [self.tasks[name] for name in names]
            parts = [task.collect().astype(low) for task in tasks]
            height = 1 << (bits - 1)
            block = parts[0].shape[-2] if isinstance(tasks[0], BlockShare) else parts[0].shape[0] // height
            value = parts[0] if len(parts) == 1 else jnp.concatenate(parts, axis=-1)
            value = value.reshape(height, block, value.shape[-1])
            parcel = Parcel()
            parcel.got = last_share(tie(value, flight.token), bits)
            flight.later.append((windows, parcel, "got"))
            at = 0
            for task, part in zip(tasks, parts):
                assert task.path.pop(0) == "hi"
                n = part.shape[-1]
                task.result = Slice(parcel, slice(at, at + n), "got")
                at += n

        return action

    def go(self, *names):
        def action(flight):
            tasks = [self.tasks[name] for name in names]
            items = [task.path.pop(0) for task in tasks]
            assert len(set(items)) == 1
            sent = [task.send(items[0]) for task in tasks]
            parcel = Parcel()
            away = sent[0] if len(sent) == 1 else jnp.concatenate(sent, axis=-1)
            flight.send(away, items[0], parcel, "got")

            def arrive():
                at = 0
                for task, value in zip(tasks, sent):
                    n = value.shape[-1]
                    task.arrive(parcel.got if len(tasks) == 1 else parcel.got[..., at : at + n])
                    at += n

            flight.then(arrive)

        return action


def row_sum(value):
    return lax.psum_scatter(value, "row", scatter_dimension=0, tiled=True)


def grad_blocks(left, right, bits, block):
    if (4 * block) % 128 == 0:
        value = down_grad(left, right, 2**bits)
    else:
        value = outer_sum(left, right).astype(low).reshape(2**bits, 2, 2 * block, right.shape[1])
        value = jnp.swapaxes(value, 0, 1)
    return value.reshape((2,) * (bits + 2) + (block, right.shape[1]))


def block_forward(hidden0, mods, mats, gains, tabs, flight, points):
    shift1, scale1, gate1, shift2, scale2, gate2 = mods
    cosine, sine, member, member_t, head = tabs
    used = {}

    def mat(name):
        used[name] = mats[name]()
        return used[name]

    def fence(point, *values):
        if point not in points:
            return values if len(values) > 1 else values[0]
        values = flight.fence(values, points[point])
        return values if len(values) > 1 else values[0]

    attn_in = (hidden0 * rms_scale(hidden0) * (1.0 + plain(scale1)) + plain(shift1)).astype(low)
    attn_in = fence("qkv", attn_in)
    query, kv, raw = qkv_matmul(attn_in, mat("qkv"), cosine, sine, gains[0], member, member_t, head)
    query, kv = fence("attend", query, kv)
    kv_r = swap(kv, "row")
    out_b, lse = attend(query, kv, kv_r, head)
    out_b = fence("out", out_b)
    att, hidden1, mlp_in = out_matmul(out_b, mat("out"), hidden0, [gate1, shift2, scale2])
    mlp_in = fence("gate", mlp_in)
    inner, gate_pre, up_pre = gate_up_matmul(mlp_in, mat("gate"), mat("up"))
    inner = fence("down", inner)
    mlp_out, hidden2 = down_matmul(inner, mat("down"), hidden1, gate2)
    cache = (hidden0, attn_in, raw, query, kv, kv_r, out_b, lse, att)
    cache += (hidden1, mlp_in, gate_pre, up_pre, inner, mlp_out)
    used = tuple(used[name] for name in ("qkv", "out", "gate", "up", "down"))
    return hidden2, cache, used


class Sum:
    value = None


def block_backward(grad2, cache, mods, mats, gains, tabs, comm, tag, plan):
    (hidden0, attn_in, raw, query, kv, kv_r, out_b, lse, att) = cache[:9]
    (hidden1, mlp_in, gate_pre, up_pre, inner, mlp_out) = cache[9:]
    shift1, scale1, gate1, shift2, scale2, gate2 = mods
    qkv_w, out_w, gate_w, up_w, down_w = mats
    cosine, sine, member, member_t, head = tabs
    flight, agenda, orders, paths, coords = comm
    n_data = lax.axis_size("dp")
    bits = (n_data - 1).bit_length()
    block = down_w.height // (4 * n_data)

    def fence(point, *values):
        values = flight.fence(values, plan.get(point, ()))
        return values if len(values) > 1 else values[0]

    def grad_of(left, name, right, tile):
        return ordered_grad(left, orders[name], [right], tile)

    def watch(name, task):
        agenda.tasks[name + tag] = task
        flight.watch(task, "base")

    def begin(name, value):
        path = paths[name][1:]
        watch(name[0], Share(value, path, path))

    def begin_halves(name, value, cut):
        path = paths[name][1:]
        other = [path[1], path[0]] + path[2:]
        held = Sum()
        held.value = value
        flight.watch(held, "value")
        agenda.tasks[name[0] + "a" + tag] = Share(Slice(held, slice(0, cut)), path, path)
        agenda.tasks[name[0] + "b" + tag] = Share(Slice(held, slice(cut, None)), path, other)

    def begin_down(value):
        order = ["row"] + list(reversed(range(bits))) + ["col"]
        watch("d", BlockShare(value, order, ["row"], coords))

    grad_mlp = (grad2 * plain(gate2)).astype(low)
    dgate2 = grad2 * mlp_out.astype(full)
    if gate2.shape[0] == 1:
        dgate2 = jnp.sum(dgate2, axis=0, keepdims=True)
    begin_down(grad_blocks(inner, grad_mlp, bits, block))
    grad2, grad_mlp = fence("start", grad2, grad_mlp)
    grad_gate, grad_up = down_back(grad_mlp, down_w, gate_pre, up_pre)
    w_gate = grad_of(mlp_in, "gate", grad_gate, 1024)
    w_up = grad_of(mlp_in, "up", grad_up, 1024)
    grad_gate, grad_up, w_gate, w_up = fence("gate", grad_gate, grad_up, w_gate, w_up)
    r_gate = row_sum(w_gate)
    r_up = row_sum(w_up)
    grad1, grad_att, dshift2, dscale2, dgate1 = mlp_back(
        [grad_gate, grad_up], [gate_w, up_w], grad2, hidden1, att, [scale2, gate1]
    )
    grad_att = fence("out", grad_att)
    w_out = grad_of(out_b, "out", grad_att, 384)
    grad_ob = out_back(grad_att, out_w)
    begin("gate", r_gate)
    begin("up", r_up)
    grad_ob, w_out = fence("attend", grad_ob, w_out)
    r_out = row_sum(w_out)
    dq, dkv, dkv_r = attend_back(query, kv, kv_r, grad_ob, out_b, lse, head)
    begin("out", r_out)
    dq, dkv_r = fence("qk", dq, dkv_r)
    grad_qkv, gain_rows = qk_back(dq, dkv, swap(dkv_r, "row"), raw, cosine, sine, gains[1], member, member_t, head)
    w_qkv = grad_of(attn_in, "qkv", grad_qkv, 1152)
    grad_qkv, w_qkv = fence("qkv", grad_qkv, w_qkv)
    r_qkv = row_sum(w_qkv)
    grad0, dshift1, dscale1 = qkv_back(grad_qkv, qkv_w, grad1, hidden0, scale1)
    dmods = [dshift1, dscale1, dgate1, dshift2, dscale2, dgate2]
    begin_halves("qkv", r_qkv, r_qkv.shape[1] // 256 * 128)
    return grad0, dmods, gain_rows[:2], begin_halves


def per_device(
    latents,
    levels,
    timesteps,
    patch_weight,
    patch_bias,
    ada_weight,
    ada_bias,
    qkv_weight,
    qk_gains,
    out_weight,
    gate_weight,
    up_weight,
    down_weight,
    cotangent,
):
    images, slots, chans, rows_loc, cols_loc = latents.shape
    n_data = lax.axis_size("dp")
    assert images == 1 and slots == 2
    assert lax.axis_size("row") == 2 and lax.axis_size("col") == 2
    row = lax.axis_index("row")
    col = lax.axis_index("col")
    data = lax.axis_index("dp")
    bits = (n_data - 1).bit_length()
    left = col == 0
    coords = {"row": row, "col": col}
    place = (row, col, coords)
    for k in range(bits):
        coords[k] = (data >> k) & 1
    grid_rows = rows_loc // 2
    grid_cols = cols_loc
    half_cols = grid_cols // 2
    tokens = grid_rows * grid_cols
    width = cotangent.shape[-1]
    head = qk_gains.shape[2]
    heads = width // head
    pvals = chans * 4
    shard = width // 4
    me = data * 4 + row * 2 + col
    own_rows = width // (4 * n_data)

    def pair(own, other, axis):
        return jnp.concatenate([jnp.where(left, own, other), jnp.where(left, other, own)], axis=axis)

    own = {}
    for name, s in (
        ("qkv", qkv_weight),
        ("out", out_weight),
        ("gate", gate_weight),
        ("up", up_weight),
        ("down", down_weight),
        ("ada", ada_weight),
    ):
        own[name] = lax.all_gather(s, "row", axis=0)
    shards = {"qkv": qkv_weight, "out": out_weight, "gate": gate_weight, "up": up_weight, "down": down_weight}
    shards["ada"] = ada_weight

    def bundle(which, relay_bit, *parts):
        return Bundle(place, own, shards, parts, which, relay_bit)

    ff = gate_weight.shape[2]
    b_q0 = bundle(0, 0, ("qkv", 0, width))
    b_kv0 = bundle(0, 1, ("qkv", width, 2 * width))
    b_out0 = bundle(0, 0, ("out", 0, width))
    b_gate0 = bundle(0, 0, ("gate", 0, ff))
    b_up0 = bundle(0, 1, ("up", 0, ff))
    b_down0 = bundle(0, 0, ("down", 0, width))
    b_ada_a = bundle(1, 1, ("ada", 0, 3 * width))
    b_ada_b = bundle(1, 0, ("ada", 3 * width, 3 * width))
    b_qkv1 = bundle(1, 1, ("qkv", 0, 3 * width))
    b_og1 = bundle(1, 0, ("out", 0, width), ("gate", 0, ff))
    b_up1 = bundle(1, 1, ("up", 0, ff))
    b_down1 = bundle(1, 0, ("down", 0, width))
    enc_mats = {
        "qkv": lambda: weight_of("qkv", b_q0, b_kv0),
        "out": lambda: weight_of("out", b_out0),
        "gate": lambda: weight_of("gate", b_gate0),
        "up": lambda: weight_of("up", b_up0),
        "down": lambda: weight_of("down", b_down0),
    }
    dec_mats = {
        "qkv": lambda: weight_of("qkv", b_qkv1),
        "out": lambda: weight_of("out", b_og1),
        "gate": lambda: weight_of("gate", b_og1),
        "up": lambda: weight_of("up", b_up1),
        "down": lambda: weight_of("down", b_down1),
    }

    small = jnp.concatenate(
        [jnp.swapaxes(patch_weight, 1, 2).reshape(2 * pvals, shard), patch_bias, ada_bias.reshape(12, shard)], axis=0
    )
    small_other = swap(small, "col")
    blk = latents[0]
    blk_other = swap(blk, "col")
    flight = Flight(small)

    class Start:
        pass

    Start.small, Start.blk = small_other, blk_other
    flight.watch(Start, "small")
    flight.watch(Start, "blk")
    (blk,) = flight.fence([blk], [b_q0.prepare, b_kv0.prepare])
    small = pair(small[None], Start.small[None], 0)
    wide = pair(blk, Start.blk, 3)
    flight.send(small, "row", Start, "small")
    flight.send(wide[:, :, rows_loc - 1 :], "row", Start, "top")
    small, wide = flight.fence([small, wide], [b_q0.over_col, b_kv0.over_col, b_out0.prepare])
    temb = time_features(tie(timesteps, wide)[0], width)
    small = jnp.where(row == 0, jnp.stack([small, Start.small]), jnp.stack([Start.small, small]))
    small = small.reshape(4, 2 * pvals + 14, shard)
    patch_w = small[:, : 2 * pvals].transpose(1, 0, 2).reshape(2, pvals, width)
    patch_b = small[:, 2 * pvals : 2 * pvals + 2].transpose(1, 0, 2).reshape(2, width).astype(full)
    ada_b = small[:, 2 * pvals + 2 :].reshape(4, 2, 6 * shard).transpose(1, 0, 2).reshape(2, 6, width).astype(full)

    framed = jnp.concatenate([Start.top, wide[:, :, : rows_loc - 1]], axis=2)
    framed = jnp.concatenate([framed[..., -1:], framed[..., :-1]], axis=3)
    patches = (
        framed.reshape(slots, chans, grid_rows, 2, grid_cols, 2).transpose(0, 2, 4, 1, 3, 5).reshape(slots, tokens, pvals)
    )
    enc_patches = patches[0]
    dec_patches = jnp.where(left, patches[0], patches[1])

    sil0 = jax.nn.silu(temb[:1]).astype(low)
    temb_own = jnp.where(left, temb[:1], temb[1:])
    part = mod_partial(lax.dynamic_slice(sil0, (0, (2 * row + col) * shard), (1, shard)), ada_weight, width)

    cot_own = jnp.where(left, cotangent[0, 0], cotangent[0, 1])

    class Cotangent:
        got = None

    def send_cotangent(flight):
        flight.send(jnp.where(left, cotangent[0, 1], cotangent[0, 0]), "col", Cotangent, "got")

    quarter = head // 4
    lanes = tie(jnp.arange(width), flight.token)
    within = lanes % head
    section = within // quarter
    lane_freq = jnp.exp(-math.log(10000.0) * (within % quarter).astype(full) / quarter)
    row_pos = (row * grid_rows + jnp.arange(grid_rows)).astype(full)
    col_pos = jnp.arange(grid_cols).astype(full)
    row_angle = row_pos[:, None] * lane_freq[None, :]
    col_angle = col_pos[:, None] * lane_freq[None, :]
    by_row = section < 2
    sign = jnp.where(section % 2 == 0, -1.0, 1.0).astype(full)

    def table(fun):
        return jnp.where(by_row, fun(row_angle)[:, None, :], fun(col_angle)[None, :, :]).reshape(tokens, width)

    cosine = table(jnp.cos)
    sine = table(jnp.sin) * sign
    member = (lanes[:, None] // head == jnp.arange(128)[None, :]).astype(low)
    tabs = (cosine, sine, member, member.T, head)
    gain_rows = jnp.tile(qk_gains.astype(full), (1, 1, heads))
    even = jnp.broadcast_to((section % 2 == 0).astype(full), (2, 1, width))
    temper = head ** (-0.5) * math.log2(math.e)
    scaled = jnp.concatenate([gain_rows[:, :1] * temper, gain_rows[:, 1:], even], axis=1)
    gain_rows = jnp.concatenate([gain_rows, even], axis=1)
    gain_rows = [(scaled[k], gain_rows[k]) for k in range(2)]

    rest = list(range(2, bits))
    path_y = ["row", "col", 0, "hi"]
    path_x = ["row", 0, "col", "hi"]
    path_s = ["row", "col", 0, 1] + rest
    paths = {"gate": path_y, "up": path_x, "out": path_x, "qkv": path_y, "ada": path_s}
    perm = {}
    orders = {}
    for name in ("gate", "up", "out", "qkv", "ada"):
        key = tuple(paths[name])
        if key not in perm:
            source = halving_order(paths[name], width, own_rows, me, bits)
            perm[key] = lax.optimization_barrier((source[:, None] == lanes[None, :]).astype(low))
        orders[name] = perm[key]

    enc_h0 = matmul(enc_patches, patch_w[0]) + patch_b[0]
    starts = [b_q0.relay, b_kv0.relay, b_out0.over_col, b_q0.first_row, b_kv0.first_row, b_gate0.prepare]
    enc_h0, part, cosine, sine = flight.fence([enc_h0, part, cosine, sine], starts)
    part = part + swap(part, "row")
    part = part + swap(part, "col")
    enc_mod = part + ada_b[0]
    enc_mods = [enc_mod[k : k + 1] for k in range(6)]
    tabs = (cosine, sine) + tabs[2:]
    points = {
        "qkv": [b_q0.second_row, b_kv0.second_row, b_gate0.over_col, b_out0.relay, b_up0.prepare],
        "attend": [b_up0.over_col, b_gate0.relay, b_out0.first_row, b_down0.prepare],
        "out": [b_out0.second_row, b_up0.relay, b_down0.over_col, b_gate0.rows_both, b_ada_a.prepare],
        "gate": [b_up0.rows_both, b_ada_a.over_col, b_down0.relay, b_qkv1.prepare],
        "down": [b_down0.rows_both, b_qkv1.over_col, b_ada_a.relay, b_ada_b.prepare],
    }
    encoded, enc_cache, enc_mats = block_forward(enc_h0, enc_mods, enc_mats, gain_rows[0], tabs, flight, points)
    dec_h0 = matmul(dec_patches, patch_w[1]) + patch_b[1]
    cond = encoded + temb_own
    dec_sil = jax.nn.silu(cond).astype(low)
    starts = [b_ada_a.rows_both, b_ada_b.over_col, b_qkv1.relay, b_og1.prepare]
    keys = list(perm)
    dec_sil, *made = flight.fence([dec_sil] + [perm[key] for key in keys], starts)
    perm = dict(zip(keys, made))
    orders = {name: perm[tuple(paths[name])] for name in orders}
    ada_bias1 = ada_b[1].reshape(1, 6 * width)
    mod_a = ada_matmul(dec_sil, weight_of("ada", b_ada_a), ada_bias1[:, : 3 * width])
    dec_mods = [Cols(mod_a, k * width, width) for k in range(3)]
    held = Sum()

    def second_mods(flight):
        held.value = ada_matmul(tie(dec_sil, flight.token), weight_of("ada", b_ada_b), ada_bias1[:, 3 * width :])
        flight.watch(held, "value")

    dec_mods += [Cols(held, k * width, width) for k in range(3)]
    points = {
        "qkv": [b_qkv1.rows_both, b_og1.over_col, b_ada_b.relay, b_up1.prepare],
        "attend": [b_ada_b.rows_both, second_mods, b_up1.over_col, b_og1.relay, b_down1.prepare],
        "out": [b_og1.rows_both, b_down1.over_col, b_up1.relay],
        "gate": [b_up1.rows_both, b_down1.relay, send_cotangent],
        "down": [b_down1.rows_both],
    }
    decoded, dec_cache, dec_mats = block_forward(dec_h0, dec_mods, dec_mats, gain_rows[1], tabs, flight, points)
    live = (col < levels[0]).astype(full)
    result = (decoded * live).astype(low).reshape(grid_rows, grid_cols, width)
    near = jnp.where(left, result[:, :half_cols], result[:, half_cols:])
    far = jnp.where(left, result[:, half_cols:], result[:, :half_cols])

    class Away:
        got = None

    def send_result(flight):
        flight.send(far, "col", Away, "got")


    agenda = Agenda()
    go = agenda.go
    scatter = functools.partial(agenda.scatter, bits)
    comm = (flight, agenda, orders, paths, coords)
    cot = pair(cot_own, Cotangent.got, 1).reshape(tokens, width)
    dec_grad2 = cot.astype(full) * live

    def split_down(tag, way_a, way_b, flight):
        whole_sum = agenda.tasks["d" + tag]
        cut = width // 256 * 128
        for name, columns, way in (("da" + tag, (0, cut), way_a), ("db" + tag, (cut, width - cut), way_b)):
            part = BlockShare(None, whole_sum.order, way, coords)
            part.terms = list(whole_sum.terms)
            part.done = list(whole_sum.done)
            part.columns = columns
            agenda.tasks[name] = part

    plan = {
        "start": [send_result, go("d1")],
        "gate": [functools.partial(split_down, "1", ["col", 0, "hi"], [0, "col", "hi"]), go("da1"), go("db1")],
        "out": [go("da1"), go("db1")],
        "attend": [go("g1"), go("u1"), scatter(1, "da1", "db1")],
        "qk": [go("g1"), go("u1")],
        "qkv": [go("o1")],
    }
    dec_grad0, dec_dmods, dec_gains, begin_halves = block_backward(
        dec_grad2, dec_cache, dec_mods, dec_mats, gain_rows[1], tabs, comm, "1", plan
    )
    away = Away.got
    result = jnp.stack([jnp.where(left, near, away), jnp.where(left, away, near)])[None]
    dec_dmods = [piece.astype(low) for piece in dec_dmods]
    w_ada = ordered_grad(dec_sil, orders["ada"], dec_dmods, width)
    starts = [go("qa1"), go("qb1"), go("o1")]
    w_ada, *dec_dmods = flight.fence([w_ada] + dec_dmods, starts)
    r_ada = row_sum(w_ada)
    dec_bada = jnp.stack([jnp.sum(piece.astype(full), axis=0) for piece in dec_dmods])
    enc_grad2 = ada_back(dec_dmods, weight_of("ada", b_ada_a, b_ada_b), cond)

    def patch_rows(patch, grad):
        ones = jnp.ones((tokens, 1), low)
        return outer_sum(jnp.concatenate([patch, ones], axis=1), grad)

    total = jnp.concatenate([patch_rows(dec_patches, dec_grad0), dec_bada, dec_gains], axis=0)
    agenda.tasks["s"] = Total(total, ["row", "col"] + list(range(bits)))

    begin_halves("ada", r_ada, r_ada.shape[1] // 2)
    plan = {
        "start": [go("s"), go("d0"), go("aa1"), go("ab1"), scatter(0, "g1", "u1")],
        "gate": [
            functools.partial(split_down, "0", [1, "col", 0] + rest, [1, 0, "col"] + rest),
            go("aa1"),
            go("ab1"),
            go("qa1"),
            go("qb1"),
            go("da0"),
        ],
        "out": [go("s"), go("db0")],
        "attend": [go("s"), go("g0"), go("u0"), go("aa1", "ab1")],
        "qk": [go("g0"), go("u0"), go("da0"), go("db0"), scatter(0, "qa1", "qb1", "o1")],
        "qkv": [go("s"), go("o0"), go("da0"), go("db0"), go("aa1", "ab1")],
    }
    enc_grad0, enc_dmods, enc_gains, _ = block_backward(
        enc_grad2, enc_cache, enc_mods, enc_mats, gain_rows[0], tabs, comm, "0", plan
    )
    dmod_enc = jnp.concatenate(enc_dmods, axis=0)
    total = jnp.concatenate([patch_rows(enc_patches, enc_grad0), enc_gains, dmod_enc], axis=0)
    def image(dpatch):
        return (
            dpatch.reshape(grid_rows, grid_cols, chans, 2, 2).transpose(2, 0, 3, 1, 4).reshape(chans, rows_loc, 2 * cols_loc)
        )

    enc_image = image(matmul_t(enc_grad0, patch_w[0]))
    dec_image = image(matmul_t(dec_grad0, patch_w[1]))
    zero = jnp.zeros_like(dec_image)
    grads = jnp.stack([enc_image + jnp.where(left, dec_image, zero), jnp.where(left, zero, dec_image)])
    grads = jnp.concatenate([grads[..., 1:], grads[..., :1]], axis=3)

    class Last:
        pass

    total, grads = flight.fence([total, grads])
    flight.send(total, "row", Last, "total")
    flight.send(grads[:, :, :1], "row", Last, "below")
    total, grads = flight.fence([total, grads], [go("qa0"), go("qb0"), scatter(1, "g0", "u0")])
    total = total + Last.total
    flight.send(total, "col", Last, "total")
    grads = jnp.concatenate([grads[:, :, 1:], Last.below], axis=2)
    one = grads[..., :cols_loc]
    two = grads[..., cols_loc:]
    flight.send(jnp.where(left, two, one), "col", Last, "image")
    count = pvals + 3
    tiny = TotalAndRows(None, count, list(range(bits)))
    agenda.tasks["t"] = tiny

    def begin_tiny(flight):
        tiny.value = jnp.concatenate([total + Last.total, sil0.astype(full)], axis=0)
        go("t")(flight)

    flight.fence([total], [begin_tiny, go("qa0"), go("qb0"), go("o0"), go("s")])
    latent_grad = (jnp.where(left, one, two) + Last.image)[None]
    flight.fence([total], [scatter(1, "qa0", "qb0", "o0"), go("t"), go("da0", "db0")])
    flight.fence([total], [go("t")])
    flight.fence([total])
    while any(task.path for task in agenda.tasks.values()):
        flight.fence([total], [go(name) for name, task in agenda.tasks.items() if task.path])
        flight.fence([total])
    dec_small = agenda.tasks["s"].value
    total = tiny.value[:count]
    dmod_all = tiny.value[count:]
    dmod_all = dmod_all.reshape(n_data, 7, width)
    enc_small = total
    enc_ada = jnp.dot(
        lax.dynamic_slice(dmod_all, (0, 6, me * own_rows), (n_data, 1, own_rows))[:, 0].T,
        dmod_all[:, :6].reshape(n_data, 6 * width),
        precision=highest,
        preferred_element_type=full,
    )
    enc_bada = jnp.sum(dmod_all[:, :6], axis=0)

    def own_lanes(value):
        return lax.dynamic_slice(value, (0, me * own_rows), (value.shape[0], own_rows))

    enc_patch = own_lanes(enc_small[: pvals + 1])
    dec_patch = own_lanes(dec_small[: pvals + 1])
    g_patch = jnp.stack([enc_patch[:pvals].T, dec_patch[:pvals].T])
    g_patch_b = jnp.stack([enc_patch[pvals], dec_patch[pvals]])
    bada = jnp.stack([enc_bada.reshape(-1), dec_small[pvals + 1 : pvals + 7].reshape(-1)])
    own_bada = 6 * own_rows
    g_bada = lax.dynamic_slice(bada, (0, me * own_bada), (2, own_bada))
    gains = jnp.stack([enc_small[pvals + 1 :], dec_small[pvals + 7 :]])
    gains = gains.reshape(2, 2, heads, head).sum(axis=2)
    def both(name):
        parts = [agenda.tasks[name + tag].value.astype(full) for tag in "01"]
        return jnp.stack(parts)

    for task in agenda.tasks.values():
        assert not task.path
    g_ada = jnp.concatenate([agenda.tasks["aa1"].value, agenda.tasks["ab1"].value], axis=1)
    g_ada_all = jnp.stack([enc_ada, g_ada.astype(full)])
    g_qkv = jnp.concatenate([both("qa"), both("qb")], axis=2)
    g_down = jnp.concatenate([both("da"), both("db")], axis=2)
    stacked = [g_qkv, both("o"), both("g"), both("u"), g_down]
    return (
        result,
        latent_grad,
        g_patch,
        g_patch_b,
        g_ada_all,
        g_bada,
        stacked[0],
        gains,
        stacked[1],
        stacked[2],
        stacked[3],
        stacked[4],
    )


def solution(mesh):
    tile = ("row", "col")
    every = ("dp", "row", "col")
    return jax.shard_map(
        per_device,
        mesh=mesh,
        in_specs=(
            P("dp", None, None, "row", "col"),
            P("dp"),
            P("dp", None),
            P(None, tile, None),
            P(None, tile),
            P(None, tile, None),
            P(None, tile),
            P(None, tile, None),
            P(),
            P(None, tile, None),
            P(None, tile, None),
            P(None, tile, None),
            P(None, tile, None),
            P("dp", None, "row", "col", None),
        ),
        out_specs=(
            P("dp", None, "row", "col", None),
            P("dp", None, None, "row", "col"),
            P(None, every, None),
            P(None, every),
            P(None, every, None),
            P(None, every),
            P(None, every, None),
            P(),
            P(None, every, None),
            P(None, every, None),
            P(None, every, None),
            P(None, every, None),
        ),
        check_vma=False,
    )
```

```python
import functools
import math

import jax
import jax.numpy as jnp
from jax import lax
from jax.experimental import pallas as pl
from jax.experimental.pallas import tpu as pltpu
from jax.sharding import PartitionSpec as P

epsilon = 1e-06
highest = lax.Precision.HIGHEST
low = jnp.bfloat16
full = jnp.float32
WINDOW = 256
PAIR = 4
MIB = 1 << 20


def matmul(left, right):
    return jnp.dot(left, right, preferred_element_type=full)


def matmul_t(left, right):
    return lax.dot_general(left, right, (((1,), (1,)), ((), ())), preferred_element_type=full)


def outer_sum(left, right):
    return lax.dot_general(left, right, (((0,), (0,)), ((), ())), preferred_element_type=full)


def rms_scale(value):
    return lax.rsqrt(jnp.mean(value * value, axis=-1, keepdims=True) + epsilon)


def rms_back(value, inverse, grad):
    return inverse * grad - value * inverse**3 * jnp.mean(value * grad, axis=-1, keepdims=True)


def swap(value, item):
    if isinstance(item, str):
        return lax.ppermute(value, item, [(0, 1), (1, 0)])
    size = lax.axis_size("dp")
    return lax.ppermute(value, "dp", [(i, i ^ (1 << item)) for i in range(size)])


def time_features(steps, width):
    half = width // 2
    freqs = jnp.exp(-math.log(10000.0) * jnp.arange(half).astype(full) / half)
    angles = steps.astype(full)[:, None] * freqs[None, :]
    return jnp.concatenate([jnp.cos(angles), jnp.sin(angles)], axis=-1)


def whole(shape):
    return pl.BlockSpec(shape, lambda *_: (0,) * len(shape))


def params(mib):
    return pltpu.CompilerParams(vmem_limit_bytes=mib * MIB)


def head_mean(value, member, head):
    return matmul(value.astype(low), member) * (1.0 / head)


def split_dot(value, onehot):
    top = value.astype(low)
    rest = (value - top.astype(full)).astype(low)
    return matmul(top, onehot) + matmul(rest, onehot)


def turned(value, cosine, sine, even, quarter):
    width = value.shape[-1]
    ahead = pltpu.roll(value, width - quarter, axis=1)
    behind = pltpu.roll(value, quarter, axis=1)
    return value * cosine + jnp.where(even, ahead, behind) * sine


def even_lanes(gain_ref, shape):
    return jnp.broadcast_to(gain_ref[2:3, :] > 0.5, shape)


def qk_back_body(head, dq_ref, dkv_ref, dkvx_ref, qkv_ref, cos_ref, sin_ref, gain_ref, mem_ref, memt_ref, out_ref, gg_ref):
    width = dq_ref.shape[-1]

    @pl.when(pl.program_id(0) == 0)
    def _():
        gg_ref[...] = jnp.zeros_like(gg_ref)

    cosine = cos_ref[...]
    sine = -sin_ref[...]
    even = even_lanes(gain_ref, cosine.shape)
    member = mem_ref[...]
    member_t = memt_ref[...]
    grads = (dq_ref[...], dkv_ref[:, :width] + dkvx_ref[:, :width].astype(full))
    for part in (0, 1):
        value = qkv_ref[:, part * width : (part + 1) * width]
        mean = head_mean(value * value, member, head)
        inverse_h = lax.rsqrt(mean + epsilon)
        inverse = split_dot(inverse_h, member_t)
        grad_n = turned(grads[part], cosine, sine, even, head // 4)
        normed = value * inverse
        gg_ref[part : part + 1, :] += jnp.sum(grad_n * normed, axis=0, keepdims=True)
        weighted = grad_n * gain_ref[part : part + 1, :]
        dots = head_mean(value * weighted, member, head) * inverse_h * inverse_h
        back = inverse * weighted - normed * split_dot(dots, member_t)
        out_ref[:, part * width : (part + 1) * width] = back.astype(low)
    out_ref[:, 2 * width :] = (dkv_ref[:, width:] + dkvx_ref[:, width:].astype(full)).astype(low)


def qk_back(dq, dkv, dkvx, raw, cosine, sine, gains, member, member_t, head):
    tokens, width = dq.shape
    step = 256
    rows = lambda n: pl.BlockSpec((step, n), lambda i: (i, 0))
    return pl.pallas_call(
        functools.partial(qk_back_body, head),
        grid=(tokens // step,),
        in_specs=[rows(width)]
        + [rows(2 * width)] * 3
        + [rows(width), rows(width), whole(gains.shape), whole(member.shape), whole(member_t.shape)],
        out_specs=[rows(3 * width), whole((8, width))],
        out_shape=[jax.ShapeDtypeStruct((tokens, 3 * width), low), jax.ShapeDtypeStruct((8, width), full)],
        compiler_params=params(60),
        cost_estimate=pl.CostEstimate(flops=60 * raw.size, bytes_accessed=18 * raw.size, transcendentals=0),
        name="qk_back",
    )(dq, dkv, dkvx, raw, cosine, sine, gains, member, member_t)


def head_window(head, width, part):
    index = pl.program_id(0) * PAIR + part
    start = index * head
    base = jnp.minimum(lax.div(start, 128) * 128, width - WINDOW)
    return index, pl.multiple_of(base, 128), start - base


def window_mask(shape, offset, head):
    lane = lax.broadcasted_iota(jnp.int32, shape, 1)
    return jnp.logical_and(lane >= offset, lane < offset + head)


def attend_body(head, q_ref, kvl_ref, kvr_ref, o_ref, lse_ref, acc_ref):
    tokens, width = q_ref.shape

    @pl.when(pl.program_id(0) == 0)
    def _():
        acc_ref[...] = jnp.zeros_like(acc_ref)
        lse_ref[...] = jnp.zeros_like(lse_ref)

    step = 256
    one = jnp.ones((), low)
    lane = lax.broadcasted_iota(jnp.int32, (step, lse_ref.shape[1]), 1)
    for part in range(PAIR):
        index, base, offset = head_window(head, width, part)
        cols = pl.ds(base, WINDOW)
        vals = pl.ds(pl.multiple_of(width + base, 128), WINDOW)
        mask_k = window_mask((tokens, WINDOW), offset, head)
        value_l = jnp.where(mask_k, kvl_ref[:, vals], one)
        value_r = jnp.where(mask_k, kvr_ref[:, vals], one)
        mask = window_mask((step, WINDOW), offset, head)
        for first in range(0, tokens, step):
            rows = slice(first, first + step)
            query = jnp.where(mask, q_ref[rows, cols], jnp.zeros((), low))
            left = jnp.exp2(matmul_t(query, kvl_ref[:, cols])).astype(low)
            right = jnp.exp2(matmul_t(query, kvr_ref[:, cols])).astype(low)
            out = matmul(left, value_l) + matmul(right, value_r)
            total = jnp.max(jnp.where(mask, 0.0, out), axis=1, keepdims=True)
            acc_ref[rows, cols] += jnp.where(mask, out * (1.0 / total), 0.0)
            lse_ref[rows, :] += jnp.where(lane == index, jnp.log2(total), 0.0)

    @pl.when(pl.program_id(0) == pl.num_programs(0) - 1)
    def _():
        o_ref[...] = acc_ref[...].astype(low)


def attend(query, kv_l, kv_r, head):
    tokens, width = query.shape
    heads = width // head
    return pl.pallas_call(
        functools.partial(attend_body, head),
        grid=(heads // PAIR,),
        in_specs=[whole((tokens, width))] + [whole((tokens, 2 * width))] * 2,
        out_specs=[whole((tokens, width)), whole((tokens, 128))],
        out_shape=[jax.ShapeDtypeStruct((tokens, width), low), jax.ShapeDtypeStruct((tokens, 128), full)],
        scratch_shapes=[pltpu.VMEM((tokens, width), full)],
        compiler_params=params(56),
        cost_estimate=pl.CostEstimate(
            flops=8 * tokens * tokens * WINDOW * heads, bytes_accessed=14 * tokens * width, transcendentals=2 * tokens * tokens * heads
        ),
        name="attend",
    )(query, kv_l, kv_r)


def in_three(column):
    top = column.astype(low)
    rest = column - top.astype(full)
    middle = rest.astype(low)
    return top, middle, (rest - middle.astype(full)).astype(low)


def attend_back_body(head, q_ref, kvl_ref, kvr_ref, do_ref, o_ref, lse_ref, dq_ref, dl_ref, dr_ref, dr_acc):
    tokens, width = q_ref.shape
    temper = head ** (-0.5)

    @pl.when(pl.program_id(0) == 0)
    def _():
        for ref in (dq_ref, dl_ref, dr_acc):
            ref[...] = jnp.zeros_like(ref)

    shape = (tokens, WINDOW)
    lane = lax.broadcasted_iota(jnp.int32, shape, 1)
    small = lax.broadcasted_iota(jnp.int32, lse_ref.shape, 1)
    zero = jnp.zeros((), low)
    for part in range(PAIR):
        index, base, offset = head_window(head, width, part)
        cols = pl.ds(base, WINDOW)
        vals = pl.ds(pl.multiple_of(width + base, 128), WINDOW)
        mask = window_mask(shape, offset, head)
        spare = jnp.where(offset >= 3, 0, WINDOW - 3)
        minus = jnp.where(jnp.logical_and(lane >= spare, lane < spare + 3), -jnp.ones((), low), zero)
        query = jnp.where(mask, q_ref[:, cols], zero)
        grad = jnp.where(mask, do_ref[:, cols], zero)
        delta = jnp.sum(grad.astype(full) * o_ref[:, cols].astype(full), axis=1, keepdims=True)
        level = jnp.sum(jnp.where(small == index, lse_ref[...], 0.0), axis=1, keepdims=True)
        query_x = query
        grad_x = grad
        for k, (a, b) in enumerate(zip(in_three(level), in_three(delta))):
            at = lane == spare + k
            query_x = jnp.where(at, a, query_x)
            grad_x = jnp.where(at, b, grad_x)
        grad_q = 0.0
        for ref, acc in ((kvl_ref, dl_ref), (kvr_ref, dr_acc)):
            key = jnp.where(mask, ref[:, cols], minus)
            value = jnp.where(mask, ref[:, vals], minus)
            prob = jnp.exp2(matmul_t(key, query_x))
            grad_s = (prob * matmul_t(value, grad_x)).astype(low)
            acc[:, vals] += matmul(prob.astype(low), grad)
            acc[:, cols] += matmul(grad_s, query)
            grad_q = grad_q + outer_sum(grad_s, key)
        dq_ref[:, cols] += jnp.where(mask, grad_q * temper, 0.0)

    @pl.when(pl.program_id(0) == pl.num_programs(0) - 1)
    def _():
        back = math.log(2.0)
        dl_ref[:, :width] = dl_ref[:, :width] * back
        dr_ref[:, :width] = (dr_acc[:, :width] * back).astype(low)
        dr_ref[:, width:] = dr_acc[:, width:].astype(low)


def attend_back(query, kv_l, kv_r, grad, out, levels, head):
    tokens, width = query.shape
    heads = width // head
    both = (tokens, 2 * width)
    one = (tokens, width)
    return pl.pallas_call(
        functools.partial(attend_back_body, head),
        grid=(heads // PAIR,),
        in_specs=[whole(one), whole(both), whole(both), whole(one), whole(one), whole(levels.shape)],
        out_specs=[whole(one), whole(both), whole(both)],
        out_shape=[like(one, full), like(both, full), like(both, low)],
        scratch_shapes=[pltpu.VMEM(both, full)],
        compiler_params=params(62),
        cost_estimate=pl.CostEstimate(
            flops=20 * tokens * tokens * WINDOW * heads, bytes_accessed=28 * tokens * width, transcendentals=2 * tokens * tokens * heads
        ),
        name="attend_back",
    )(query, kv_l, kv_r, grad, out, levels)


class Weight:
    def __init__(self, segments):
        self.segments = segments
        self.columns = sum(columns for _, _, columns in segments)
        self.plan = [piece[1:] for piece in segments[0][1]]
        self.height = sum(rows for _, _, rows in self.plan)
        for _, pieces, _ in segments:
            assert [piece[3] for piece in pieces] == [rows for _, _, rows in self.plan]


def piece_source(ref, lead, first, count):
    for index in lead:
        ref = ref.at[index]
    return ref.at[:, pl.ds(first, count)]


class Cols:
    def __init__(self, array, first, count):
        self.source = array
        self.first = first
        self.count = count

    @property
    def array(self):
        return self.source if isinstance(self.source, jax.Array) else self.source.value

    @property
    def shape(self):
        return (self.array.shape[0], self.count)

    @property
    def dtype(self):
        return self.array.dtype

    @property
    def size(self):
        return self.array.shape[0] * self.count

    def value(self):
        return self.array[:, self.first : self.first + self.shape[1]]


def plain(value):
    return value.value() if isinstance(value, Cols) else value


def anywhere(count):
    return [pl.BlockSpec(memory_space=pl.ANY)] * count


class Stream:
    def __init__(self, weights, tile, late):
        self.weights = weights
        self.tile = tile
        self.late = late
        self.steps = weights[0].columns // tile

    def pieces_of(self):
        return [pieces for w in self.weights for _, pieces, _ in w.segments]

    def specs(self):
        return [pl.BlockSpec(memory_space=pltpu.SMEM)] + anywhere(sum(len(p) for p in self.pieces_of()) + len(self.late))

    def operands(self):
        offsets = jnp.concatenate([offs for w in self.weights for offs, _, _ in w.segments])
        arrays = [piece[0] for pieces in self.pieces_of() for piece in pieces]
        return [offsets] + arrays + [v.array if isinstance(v, Cols) else v for v in self.late]

    def scratch(self):
        shapes = []
        for w in self.weights:
            shapes += [pltpu.VMEM((2, w.height, self.tile), low), pltpu.SemaphoreType.DMA((2, len(w.plan)))]
        for value in self.late:
            shapes += [pltpu.VMEM(value.shape, value.dtype), pltpu.SemaphoreType.DMA((1,))]
        return shapes

    def bind(self, operand_refs, scratch_refs):
        self.offs = operand_refs[0]
        refs = list(operand_refs[1:])
        self.refs = []
        for w in self.weights:
            mine = []
            for _, pieces, _ in w.segments:
                mine.append(refs[: len(pieces)])
                refs = refs[len(pieces) :]
            self.refs.append(mine)
        self.buffers = scratch_refs[0 : 2 * len(self.weights) : 2]
        self.sems = scratch_refs[1 : 2 * len(self.weights) : 2]
        rest = scratch_refs[2 * len(self.weights) :]
        self.late_bufs = rest[0::2]
        self.late_copies = []
        for value, ref, buf, sem in zip(self.late, refs, rest[0::2], rest[1::2]):
            if isinstance(value, Cols):
                ref = ref.at[:, pl.ds(value.first, value.shape[1])]
            self.late_copies.append(pltpu.make_async_copy(ref, buf, sem.at[0]))

    def segment_copies(self, index, number, column, slot):
        w = self.weights[index]
        base = sum(len(x.plan) * len(x.segments) for x in self.weights[:index]) + number * len(w.plan)
        out = []
        for at, (_, lead, first, rows) in enumerate(w.segments[number][1]):
            source = piece_source(self.refs[index][number][at], lead, pl.multiple_of(first + column, 128), self.tile)
            start = pl.multiple_of(self.offs[base + at], 16)
            target = self.buffers[index].at[slot, pl.ds(start, rows), :]
            out.append(pltpu.make_async_copy(source, target, self.sems[index].at[slot, at]))
        return out

    def copies(self, step, slot):
        return [copy for index in range(len(self.weights)) for copy in self.segment_copies(index, 0, step * self.tile, slot)]

    def start_tile(self, step, slot):
        for index, w in enumerate(self.weights):
            first = 0
            for number, (_, _, columns) in enumerate(w.segments):
                count = columns // self.tile

                def start():
                    for copy in self.segment_copies(index, number, (step - first) * self.tile, slot):
                        copy.start()

                if len(w.segments) == 1:
                    start()
                else:
                    pl.when(jnp.logical_and(step >= first, step < first + count))(start)
                first += count

    def wait_tile(self, slot):
        for index in range(len(self.weights)):
            for copy in self.segment_copies(index, 0, 0, slot):
                copy.wait()

    def advance(self):
        step = pl.program_id(0)
        slot = lax.rem(step, 2)

        @pl.when(step == 0)
        def _():
            self.start_tile(jnp.int32(0), 0)
            for copy in self.late_copies:
                copy.start()

        @pl.when(step + 1 < self.steps)
        def _():
            self.start_tile(step + 1, 1 - slot)

        self.wait_tile(slot)
        return step, [buf.at[slot] for buf in self.buffers]

    def wait_late(self):
        for copy in self.late_copies:
            copy.wait()
        return self.late_bufs


def stream_call(name, stream, body, ins, in_specs, outs, out_specs, scratch, flops, mib=58):
    operands = stream.operands()
    frame = stream.scratch()

    def kernel(*refs):
        count = len(operands)
        ops, refs = refs[:count], refs[count:]
        inputs, refs = refs[: len(ins)], refs[len(ins) :]
        outputs, refs = refs[: len(outs)], refs[len(outs) :]
        stream.bind(ops, refs[: len(frame)])
        body(stream, inputs, outputs, refs[len(frame) :])

    moved = sum(v.size * v.dtype.itemsize for v in list(ins) + list(stream.late) + list(outs))
    moved += sum(2 * w.height * w.columns for w in stream.weights)
    return pl.pallas_call(
        kernel,
        grid=(stream.steps,),
        in_specs=stream.specs() + in_specs,
        out_specs=out_specs,
        out_shape=outs,
        scratch_shapes=frame + scratch,
        compiler_params=params(mib),
        cost_estimate=pl.CostEstimate(flops=flops, bytes_accessed=moved, transcendentals=0),
        name=name,
    )(*operands, *ins)


def by_rows(tokens, fun, step=128):
    @pl.loop(0, tokens // step)
    def _(i):
        fun(pl.ds(pl.multiple_of(i * step, step), step))


def take(ref, rows):
    return ref[rows, :] if ref.shape[0] > 1 else ref[...]


def give(ref, rows, value):
    if ref.shape[0] > 1:
        ref[rows, :] = value.astype(ref.dtype)
    else:
        ref[...] += jnp.sum(value, axis=0, keepdims=True)


def like(shape, dtype):
    return jax.ShapeDtypeStruct(shape, dtype)


def ada_matmul(value, weight, bias):
    tokens = value.shape[0]
    tile = weight.height
    stream = Stream([weight], tile, [])

    def body(stream, ins, outs, scratch):
        _, (w,) = stream.advance()
        outs[0][...] = matmul(ins[0][...], w[...]) + ins[1][...]

    return stream_call(
        "ada",
        stream,
        body,
        [value, bias],
        [whole(value.shape), pl.BlockSpec((1, tile), lambda j: (0, j))],
        [like((tokens, weight.columns), full)],
        [pl.BlockSpec((tokens, tile), lambda j: (0, j))],
        [],
        2 * tokens * weight.height * weight.columns,
    )[0]


def mod_partial(row, weight, width):
    shard = weight.shape[1]
    tall = jnp.broadcast_to(row, (16, shard))

    def body(x_ref, w_ref, out_ref):
        out_ref[0] = matmul(x_ref[...], w_ref[...])[:8]

    out = pl.pallas_call(
        body,
        grid=(6,),
        in_specs=[whole(tall.shape), pl.BlockSpec((None, shard, width), lambda j: (0, 0, j))],
        out_specs=pl.BlockSpec((1, 8, width), lambda j: (j, 0, 0)),
        out_shape=like((6, 8, width), full),
        compiler_params=params(60),
        cost_estimate=pl.CostEstimate(flops=0, bytes_accessed=12 * shard * width, transcendentals=0),
        name="modpart",
    )(tall, weight)
    return out[:, 0]


def qkv_matmul(value, weight, cosine, sine, gains, member, member_t, head):
    tokens, width = value.shape
    stream = Stream([weight], width, [cosine, sine])

    def body(stream, ins, outs, scratch):
        x_ref, gain_ref, mem_ref, memt_ref = ins
        q_ref, kv_ref, raw_ref = outs
        (acc_ref,) = scratch
        step, (w,) = stream.advance()
        cos_ref, sin_ref = stream.late_bufs
        acc_ref[...] = matmul(x_ref[...], w[...])

        @pl.when(step == 0)
        def _():
            stream.wait_late()

        def head_norm(part, out, cols):
            def rows_of(rows):
                raw = acc_ref[rows, :]
                raw_ref[rows, :] = raw
                mean = head_mean(raw * raw, mem_ref[...], head)
                inverse = split_dot(lax.rsqrt(mean + epsilon), memt_ref[...])
                normed = raw * inverse * gain_ref[part : part + 1, :]
                even = even_lanes(gain_ref, raw.shape)
                out[rows, cols] = turned(normed, cos_ref[rows, :], sin_ref[rows, :], even, head // 4).astype(low)

            by_rows(tokens, rows_of, 256)

        @pl.when(step == 0)
        def _():
            head_norm(0, q_ref, slice(0, width))

        @pl.when(step == 1)
        def _():
            head_norm(1, kv_ref, slice(0, width))

        @pl.when(step == 2)
        def _():
            kv_ref[:, width:] = acc_ref[...].astype(low)

    flat = like((tokens, width), low)
    return stream_call(
        "qkv",
        stream,
        body,
        [value, gains, member, member_t],
        [whole(v.shape) for v in (value, gains, member, member_t)],
        [flat, like((tokens, 2 * width), low), like((tokens, 2 * width), full)],
        [whole((tokens, width)), whole((tokens, 2 * width)), pl.BlockSpec((tokens, width), lambda j: (0, jnp.minimum(j, 1)))],
        [pltpu.VMEM((tokens, width), full)],
        2 * tokens * weight.height * weight.columns,
    )


def out_matmul(value, weight, hidden0, mods):
    tokens, width = value.shape
    stream = Stream([weight], 384, [hidden0] + mods)

    def body(stream, ins, outs, scratch):
        att_ref, h1_ref, b_ref = outs
        (acc_ref,) = scratch
        step, (w,) = stream.advance()
        acc_ref[step] = matmul(ins[0][...], w[...])

        @pl.when(step == stream.steps - 1)
        def _():
            h0_ref, gate_ref, shift_ref, scale_ref = stream.wait_late()

            def rows_of(rows):
                att = jnp.concatenate([acc_ref[k, rows, :] for k in range(stream.steps)], axis=1)
                hidden1 = h0_ref[rows, :] + take(gate_ref, rows) * att
                normed = hidden1 * rms_scale(hidden1)
                att_ref[rows, :] = att.astype(low)
                h1_ref[rows, :] = hidden1
                b_ref[rows, :] = (normed * (1.0 + take(scale_ref, rows)) + take(shift_ref, rows)).astype(low)

            by_rows(tokens, rows_of)

    return stream_call(
        "attout",
        stream,
        body,
        [value],
        [whole(value.shape)],
        [like((tokens, width), low), like((tokens, width), full), like((tokens, width), low)],
        [whole((tokens, width))] * 3,
        [pltpu.VMEM((stream.steps, tokens, 384), full)],
        2 * tokens * weight.height * weight.columns,
    )


def gate_up_matmul(value, gate, up):
    tokens, width = value.shape
    tile = 1024
    stream = Stream([gate, up], tile, [])

    def body(stream, ins, outs, scratch):
        hid_ref, g_ref, u_ref = outs
        _, (wg, wu) = stream.advance()
        g = matmul(ins[0][...], wg[...])
        u = matmul(ins[0][...], wu[...])
        g_ref[...] = g.astype(low)
        u_ref[...] = u.astype(low)
        hid_ref[...] = (g * jax.nn.sigmoid(g) * u).astype(low)

    flat = like((tokens, gate.columns), low)
    return stream_call(
        "gateup",
        stream,
        body,
        [value],
        [whole(value.shape)],
        [flat] * 3,
        [pl.BlockSpec((tokens, tile), lambda j: (0, j))] * 3,
        [],
        4 * tokens * gate.height * gate.columns,
    )


def down_matmul(value, weight, hidden1, gate):
    tokens, depth = value.shape
    width = weight.columns
    stream = Stream([weight], width, [hidden1, gate])

    def body(stream, ins, outs, scratch):
        mlp_ref, h2_ref = outs
        (acc_ref,) = scratch
        hid_ref = ins[0]
        at = 0
        copies = stream.copies(0, 0)
        for copy in copies + stream.late_copies:
            copy.start()
        for k, (_, _, rows) in enumerate(weight.plan):
            copies[k].wait()
            first = stream.offs[k]
            left = hid_ref[:, pl.ds(pl.multiple_of(first, 128), rows)]
            part = matmul(left, stream.buffers[0][0, pl.ds(pl.multiple_of(first, 128), rows), :])
            if k == 0:
                acc_ref[...] = part
            else:
                acc_ref[...] += part
        h1_ref, gate_ref = stream.wait_late()

        def rows_of(rows):
            mlp = acc_ref[rows, :]
            mlp_ref[rows, :] = mlp.astype(low)
            h2_ref[rows, :] = h1_ref[rows, :] + take(gate_ref, rows) * mlp

        by_rows(tokens, rows_of)

    return stream_call(
        "down",
        stream,
        body,
        [value],
        [whole(value.shape)],
        [like((tokens, width), low), like((tokens, width), full)],
        [whole((tokens, width))] * 2,
        [pltpu.VMEM((tokens, width), full)],
        2 * tokens * depth * width,
    )


def down_back(grad, weight, gate_pre, up_pre):
    tokens, width = grad.shape
    depth = weight.height
    stream = Stream([weight], width, [gate_pre, up_pre])

    def body(stream, ins, outs, scratch):
        dg_ref, du_ref = outs
        copies = stream.copies(0, 0)
        for copy in copies + stream.late_copies:
            copy.start()
        for k, (_, _, count) in enumerate(weight.plan):
            copies[k].wait()
            if k == 0:
                g_ref, u_ref = stream.wait_late()
            first = pl.multiple_of(stream.offs[k], 128)
            for at in range(0, count, 384):
                cols = pl.ds(pl.multiple_of(first + at, 128), 384)
                inner = matmul_t(ins[0][...], stream.buffers[0][0, cols, :])
                g = g_ref[:, cols].astype(full)
                u = u_ref[:, cols].astype(full)
                sigma = jax.nn.sigmoid(g)
                active = g * sigma
                dg_ref[:, cols] = (inner * u * (sigma + active * (1.0 - sigma))).astype(low)
                du_ref[:, cols] = (inner * active).astype(low)

    flat = like((tokens, depth), low)
    return stream_call(
        "downback",
        stream,
        body,
        [grad],
        [whole(grad.shape)],
        [flat, flat],
        [whole((tokens, depth))] * 2,
        [],
        2 * tokens * depth * width,
    )


def back_matmul(name, grads, weights, tile, late, outs, finish):
    tokens = grads[0].shape[0]
    width = weights[0].height
    stream = Stream(weights, tile, late)

    def body(stream, ins, outs, scratch):
        (acc_ref,) = scratch
        step, tiles = stream.advance()
        part = matmul_t(ins[0][...], tiles[0][...])
        for value, w in zip(ins[1:], tiles[1:]):
            part = part + matmul_t(value[...], w[...])

        @pl.when(step == 0)
        def _():
            acc_ref[...] = part

        @pl.when(step > 0)
        def _():
            acc_ref[...] += part

        @pl.when(step == stream.steps - 1)
        def _():
            refs = stream.wait_late()
            for ref in outs:
                if ref.shape[0] == 1:
                    ref[...] = jnp.zeros_like(ref)
            by_rows(tokens, lambda rows: finish(rows, acc_ref[rows, :], refs, outs))

    return stream_call(
        name,
        stream,
        body,
        list(grads),
        [pl.BlockSpec((tokens, tile), lambda j: (0, j))] * len(grads),
        outs,
        [whole(value.shape) for value in outs],
        [pltpu.VMEM((tokens, width), full)],
        2 * tokens * width * weights[0].columns * len(weights),
    )


def mlp_back(grads, weights, grad2, hidden1, att, mods):
    tokens, width = grad2.shape
    lead = mods[0].shape[0]

    def finish(rows, db, refs, outs):
        dh2_ref, h1_ref, att_ref, scale_ref, gate_ref = refs
        hidden1 = h1_ref[rows, :]
        inverse = rms_scale(hidden1)
        normed = hidden1 * inverse
        weighted = db * (1.0 + take(scale_ref, rows))
        back = inverse * (weighted - normed * jnp.mean(normed * weighted, axis=-1, keepdims=True))
        grad1 = dh2_ref[rows, :] + back
        outs[0][rows, :] = grad1
        outs[1][rows, :] = (grad1 * take(gate_ref, rows)).astype(low)
        give(outs[2], rows, db)
        give(outs[3], rows, db * normed)
        give(outs[4], rows, grad1 * att_ref[rows, :].astype(full))

    outs = [like((tokens, width), full), like((tokens, width), low)]
    outs += [like((lead, width), low if lead > 1 else full)] * 3
    return back_matmul("mlpback", grads, weights, 1024, [grad2, hidden1, att] + mods, outs, finish)


def qkv_back(grad, weight, grad1, hidden0, scale):
    tokens, width = grad1.shape
    lead = scale.shape[0]

    def finish(rows, da, refs, outs):
        dh1_ref, h0_ref, scale_ref = refs
        hidden0 = h0_ref[rows, :]
        inverse = rms_scale(hidden0)
        normed = hidden0 * inverse
        weighted = da * (1.0 + take(scale_ref, rows))
        back = inverse * (weighted - normed * jnp.mean(normed * weighted, axis=-1, keepdims=True))
        outs[0][rows, :] = (dh1_ref[rows, :] + back).astype(low)
        give(outs[1], rows, da)
        give(outs[2], rows, da * normed)

    outs = [like((tokens, width), low)] + [like((lead, width), low if lead > 1 else full)] * 2
    return back_matmul("qkvback", [grad], [weight], width, [grad1, hidden0, scale], outs, finish)


def out_back(grad, weight):
    def finish(rows, value, refs, outs):
        outs[0][rows, :] = value.astype(low)

    return back_matmul("outback", [grad], [weight], 1152, [], [like(grad.shape, low)], finish)[0]


def ada_back(grads, weight, cond):
    tokens, width = cond.shape
    tile = weight.height
    stream = Stream([weight], tile, [cond])

    def body(stream, ins, outs, scratch):
        (acc_ref,) = scratch
        step, (w,) = stream.advance()
        for k, grad in enumerate(ins):

            @pl.when(step == k)
            def _():
                part = matmul_t(grad[...], w[...])
                acc_ref[...] = part if k == 0 else acc_ref[...] + part

        @pl.when(step == stream.steps - 1)
        def _():
            (cond_ref,) = stream.wait_late()

            def rows_of(rows):
                cond = cond_ref[rows, :]
                sigma = jax.nn.sigmoid(cond)
                outs[0][rows, :] = acc_ref[rows, :] * sigma * (1.0 + cond * (1.0 - sigma))

            by_rows(tokens, rows_of)

    return stream_call(
        "adaback",
        stream,
        body,
        list(grads),
        [whole(grad.shape) for grad in grads],
        [like((tokens, width), full)],
        [whole((tokens, width))],
        [pltpu.VMEM((tokens, width), full)],
        2 * tokens * width * weight.columns,
    )[0]


def ordered_grad(left, order, rights, tile):
    tokens, width = left.shape
    counts = [right.shape[1] // tile for right in rights]
    firsts = [sum(counts[:k]) for k in range(len(rights))]
    columns = sum(right.shape[1] for right in rights)

    def body(order_ref, left_ref, *refs):
        ys, out_ref, turned_ref = refs[: len(rights)], refs[-2], refs[-1]
        step = pl.program_id(0)

        @pl.when(step == 0)
        def _():
            turned_ref[...] = matmul_t(order_ref[...], left_ref[...]).astype(low)

        if len(rights) == 1:
            out_ref[...] = matmul(turned_ref[...], ys[0][...]).astype(low)
            return
        for y, first, count in zip(ys, firsts, counts):

            @pl.when(jnp.logical_and(step >= first, step < first + count))
            def _():
                out_ref[...] = matmul(turned_ref[...], y[...]).astype(low)

    def tile_of(first, count):
        return pl.BlockSpec((tokens, tile), lambda j: (0, jnp.clip(j - first, 0, count - 1)))

    return pl.pallas_call(
        body,
        grid=(columns // tile,),
        in_specs=[whole(order.shape), whole(left.shape)] + [tile_of(f, c) for f, c in zip(firsts, counts)],
        out_specs=pl.BlockSpec((width, tile), lambda j: (0, j)),
        out_shape=like((width, columns), low),
        scratch_shapes=[pltpu.VMEM((width, tokens), low)],
        compiler_params=params(60),
        cost_estimate=pl.CostEstimate(
            flops=2 * tokens * width * (columns + width), bytes_accessed=2 * width * (columns + 2 * width), transcendentals=0
        ),
        name="wgrad",
    )(order, left, *rights)


def down_grad(left, right, groups):
    tokens, depth = left.shape
    columns = right.shape[1]
    tile = depth // groups

    def body(left_ref, right_ref, out_ref):
        value = outer_sum(left_ref[...], right_ref[...]).astype(low)
        out_ref[0, 0] = value[: tile // 2]
        out_ref[1, 0] = value[tile // 2 :]

    return pl.pallas_call(
        body,
        grid=(groups,),
        in_specs=[pl.BlockSpec((tokens, tile), lambda j: (0, j)), whole(right.shape)],
        out_specs=pl.BlockSpec((2, 1, tile // 2, columns), lambda j: (0, j, 0, 0)),
        out_shape=like((2, groups, tile // 2, columns), low),
        compiler_params=params(60),
        cost_estimate=pl.CostEstimate(
            flops=2 * tokens * depth * columns, bytes_accessed=2 * depth * (columns + tokens), transcendentals=0
        ),
        name="wdown",
    )(left, right)


def tie(value, *others):
    others = [v for v in others if v is not None]
    if not others:
        return value
    return lax.optimization_barrier((value, *others))[0]


class Flight:
    def __init__(self, token):
        self.token = token
        self.held = []
        self.todo = []
        self.later = []

    def send(self, value, item, holder, name):
        setattr(holder, name, swap(tie(value, self.token), item))
        self.held.append((holder, name))

    def watch(self, holder, name):
        self.held.append((holder, name))

    def then(self, action):
        self.todo.append(action)

    def fence(self, values, starts=()):
        values = list(values)
        held, todo = self.held, self.todo
        self.held, self.todo = [], []
        held += [(holder, name) for left, holder, name in self.later if left == 0]
        self.later = [(left - 1, holder, name) for left, holder, name in self.later if left > 0]
        arrays = values + [getattr(holder, name) for holder, name in held]
        arrays = lax.optimization_barrier(tuple(arrays))
        self.token = arrays[0]
        for (holder, name), value in zip(held, arrays[len(values) :]):
            setattr(holder, name, value)
        for action in todo:
            action()
        for start in starts:
            start(self)
        return arrays[: len(values)]


class Bundle:
    def __init__(self, place, own, shards, parts, which, relay_bit):
        self.row, self.col, coords = place
        self.own = own
        self.shards = shards
        self.parts = parts
        self.which = which
        self.relay_bit = relay_bit
        self.rows = shards[parts[0][0]].shape[1]
        self.half = self.rows // 2
        self.at = coords[relay_bit] * self.half

    def prepare(self, flight):
        at = tie(self.at, flight.token)
        mine = [
            lax.dynamic_slice(self.shards[name], (self.which, at, first), (1, self.half, n))[0]
            for name, first, n in self.parts
        ]
        self.mine = jnp.concatenate(mine, axis=1)
        flight.watch(self, "mine")

    def over_col(self, flight):
        flight.send(self.mine, "col", self, "first")

    def relay(self, flight):
        flight.send(self.first, self.relay_bit, self, "second")

    def first_row(self, flight):
        flight.send(self.first, "row", self, "first_s")

    def second_row(self, flight):
        flight.send(self.second, "row", self, "second_s")

    def rows_both(self, flight):
        self.first_row(flight)
        self.second_row(flight)

    def segment(self, wanted):
        row, col, rows, half, at = self.row, self.col, self.rows, self.half, self.at
        other = (2 * row + 1 - col) * rows
        other_s = (2 * (1 - row) + 1 - col) * rows
        offsets = [col * rows, (col + 2) * rows, other + at, other_s + at]
        offsets += [other + (half - at), other_s + (half - at)]
        offsets = jnp.stack(offsets).astype(jnp.int32)
        begin = 0
        for name, first, n in self.parts:
            if name == wanted:
                own_all = self.own[name]
                lead = () if own_all.ndim == 3 else (self.which,)
                pieces = [(own_all, (0,) + lead, first, rows), (own_all, (1,) + lead, first, rows)]
                got = [self.first, self.first_s, self.second, self.second_s]
                pieces += [(value, (), begin, half) for value in got]
                return (offsets, pieces, n)
            begin += n
        raise KeyError(wanted)


def weight_of(name, *bundles):
    return Weight([bundle.segment(name) for bundle in bundles])


def item_weight(item):
    return {"row": 2, "col": 1}.get(item) or 4 << item


def halving_order(path, width, block, me, bits):
    at = jnp.arange(width)
    position = at // block
    owner = me
    for item in reversed(path):
        if item == "hi":
            mask = (1 << (bits - 1)) - 1
            owner = (owner & 7) | ((position & mask) << 3)
            position = position >> (bits - 1)
            continue
        bit = position & 1
        position = position >> 1
        if item == "row":
            owner = (owner & ~2) | (2 * bit)
        else:
            owner = owner ^ (bit * item_weight(item))
    return owner * block + at % block


class Slice:
    def __init__(self, held, columns, name="value"):
        self.held = held
        self.columns = columns
        self.name = name

    def get(self):
        return getattr(self.held, self.name)[..., self.columns]


class Term:
    def __init__(self, terms, at):
        self.terms = terms
        self.at = at

    @property
    def value(self):
        return self.terms[self.at][0]

    @value.setter
    def value(self, value):
        self.terms[self.at] = (value, self.terms[self.at][1])


class Share:
    def __init__(self, value, order, path):
        self.terms = [(value, list(order))]
        self.order = list(order)
        self.path = list(path)
        self.done = []
        self.result = None
        self.columns = None

    def pick(self, value, order, choice):
        order = list(order)
        while order and any(item in choice for item in order[:2]):
            rows, columns = value.shape
            if order[0] in choice:
                at = choice[order.pop(0)] * (rows // 2)
                value = value[at : at + rows // 2]
            else:
                at = choice[order.pop(1)]
                value = value.reshape(2, 2, rows // 4, columns)[:, at].reshape(rows // 2, columns)
        return value

    def collect(self, last=None):
        choice = {item: 0 for item in self.done}
        if last is not None:
            choice[last] = 1
        total = None
        for value, order in self.terms:
            value = value.get() if isinstance(value, Slice) else value
            part = self.pick(value, order, choice).astype(full)
            total = part if total is None else total + part
        return total

    def send(self, item):
        away = self.collect(item).astype(low)
        self.done.append(item)
        self.order = [other for other in self.order if other != item]
        return away

    def arrive(self, got):
        self.terms.append((got, self.order))

    @property
    def value(self):
        return self.collect() if self.result is None else self.result.get().astype(full)

    def hold(self, flight):
        if self.result is not None:
            flight.watch(self.result.held, self.result.name)
            return
        for at, (value, _) in enumerate(self.terms):
            if isinstance(value, Slice):
                flight.watch(value.held, value.name)
            else:
                flight.watch(Term(self.terms, at), "value")

    @property
    def base(self):
        return self.terms[0][0]

    @base.setter
    def base(self, value):
        self.terms[0] = (value, self.terms[0][1])


class BlockShare(Share):
    def __init__(self, value, order, path, coords):
        super().__init__(value, order, path)
        self.coords = coords

    def pick(self, value, order, choice):
        starts = [jnp.bitwise_xor(self.coords[item], choice[item]) if item in choice else 0 for item in order] + [0, 0]
        sizes = [1 if item in choice else 2 for item in order] + list(value.shape[-2:])
        if self.columns is not None and value.shape[-1] != self.columns[1]:
            starts[-1], sizes[-1] = self.columns
        value = lax.dynamic_slice(value, starts, sizes)
        return value.reshape([size for size in sizes[:-2] if size > 1] + list(sizes[-2:]))


class Total:
    def __init__(self, value, path):
        self.value = value
        self.path = list(path)

    def send(self, item):
        return self.value.astype(low)

    def arrive(self, got):
        self.value = self.value + got.astype(full)


class TotalAndRows(Total):
    def __init__(self, value, count, path):
        super().__init__(value, path)
        self.count = count

    def arrive(self, got):
        n = self.count
        value = self.value
        got = got.astype(full)
        self.value = jnp.concatenate([value[:n] + got[:n], value[n:], got[n:]], axis=0)


class Parcel:
    got = None


def last_share(value, bits):
    groups = [[2 * k + low_bit for k in range(1 << (bits - 1))] for low_bit in (0, 1)]
    return lax.psum_scatter(value, "dp", scatter_dimension=0, axis_index_groups=groups, tiled=False)


class Agenda:
    def __init__(self):
        self.tasks = {}

    def scatter(self, bits, windows, *names):
        def action(flight):
            tasks = [self.tasks[name] for name in names]
            parts = [task.collect().astype(low) for task in tasks]
            height = 1 << (bits - 1)
            block = parts[0].shape[-2] if isinstance(tasks[0], BlockShare) else parts[0].shape[0] // height
            value = parts[0] if len(parts) == 1 else jnp.concatenate(parts, axis=-1)
            value = value.reshape(height, block, value.shape[-1])
            parcel = Parcel()
            parcel.got = last_share(tie(value, flight.token), bits)
            flight.later.append((windows, parcel, "got"))
            at = 0
            for task, part in zip(tasks, parts):
                assert task.path.pop(0) == "hi"
                n = part.shape[-1]
                task.result = Slice(parcel, slice(at, at + n), "got")
                at += n

        return action

    def go(self, *names):
        def action(flight):
            tasks = [self.tasks[name] for name in names]
            items = [task.path.pop(0) for task in tasks]
            assert len(set(items)) == 1
            sent = [task.send(items[0]) for task in tasks]
            parcel = Parcel()
            away = sent[0] if len(sent) == 1 else jnp.concatenate(sent, axis=-1)
            flight.send(away, items[0], parcel, "got")

            def arrive():
                at = 0
                for task, value in zip(tasks, sent):
                    n = value.shape[-1]
                    task.arrive(parcel.got if len(tasks) == 1 else parcel.got[..., at : at + n])
                    at += n

            flight.then(arrive)

        return action


def row_sum(value):
    return lax.psum_scatter(value, "row", scatter_dimension=0, tiled=True)


def grad_blocks(left, right, bits, block):
    if (4 * block) % 128 == 0:
        value = down_grad(left, right, 2**bits)
    else:
        value = outer_sum(left, right).astype(low).reshape(2**bits, 2, 2 * block, right.shape[1])
        value = jnp.swapaxes(value, 0, 1)
    return value.reshape((2,) * (bits + 2) + (block, right.shape[1]))


def block_forward(hidden0, mods, mats, gains, tabs, flight, points):
    shift1, scale1, gate1, shift2, scale2, gate2 = mods
    cosine, sine, member, member_t, head = tabs
    used = {}

    def mat(name):
        used[name] = mats[name]()
        return used[name]

    def fence(point, *values):
        if point not in points:
            return values if len(values) > 1 else values[0]
        values = flight.fence(values, points[point])
        return values if len(values) > 1 else values[0]

    attn_in = (hidden0 * rms_scale(hidden0) * (1.0 + plain(scale1)) + plain(shift1)).astype(low)
    attn_in = fence("qkv", attn_in)
    query, kv, raw = qkv_matmul(attn_in, mat("qkv"), cosine, sine, gains[0], member, member_t, head)
    query, kv = fence("attend", query, kv)
    kv_r = swap(kv, "row")
    out_b, lse = attend(query, kv, kv_r, head)
    out_b = fence("out", out_b)
    att, hidden1, mlp_in = out_matmul(out_b, mat("out"), hidden0, [gate1, shift2, scale2])
    mlp_in = fence("gate", mlp_in)
    inner, gate_pre, up_pre = gate_up_matmul(mlp_in, mat("gate"), mat("up"))
    inner = fence("down", inner)
    mlp_out, hidden2 = down_matmul(inner, mat("down"), hidden1, gate2)
    cache = (hidden0, attn_in, raw, query, kv, kv_r, out_b, lse, att)
    cache += (hidden1, mlp_in, gate_pre, up_pre, inner, mlp_out)
    used = tuple(used[name] for name in ("qkv", "out", "gate", "up", "down"))
    return hidden2, cache, used


class Sum:
    value = None


def block_backward(grad2, cache, mods, mats, gains, tabs, comm, tag, plan):
    (hidden0, attn_in, raw, query, kv, kv_r, out_b, lse, att) = cache[:9]
    (hidden1, mlp_in, gate_pre, up_pre, inner, mlp_out) = cache[9:]
    shift1, scale1, gate1, shift2, scale2, gate2 = mods
    qkv_w, out_w, gate_w, up_w, down_w = mats
    cosine, sine, member, member_t, head = tabs
    flight, agenda, orders, paths, coords = comm
    n_data = lax.axis_size("dp")
    bits = (n_data - 1).bit_length()
    block = down_w.height // (4 * n_data)
    width = hidden0.shape[1]

    def fence(point, *values):
        values = flight.fence(values, plan.get(point, ()))
        return values if len(values) > 1 else values[0]

    def grad_of(left, name, rights, tile):
        return ordered_grad(left, orders[name], rights, tile)

    def watch(name, task):
        agenda.tasks[name + tag] = task
        flight.watch(task, "base")

    def begin(name, value):
        order = paths[name][1:]
        watch(name[0], Share(value, order, [order[1], order[0]] + order[2:]))

    def begin_halves(name, value, cut):
        path = paths[name][1:]
        other = [path[1], path[0]] + path[2:]
        held = Sum()
        held.value = value
        flight.watch(held, "value")
        agenda.tasks[name[0] + "a" + tag] = Share(Slice(held, slice(0, cut)), path, path)
        agenda.tasks[name[0] + "b" + tag] = Share(Slice(held, slice(cut, None)), path, other)

    def begin_down(value):
        order = ["row"] + list(reversed(range(bits))) + ["col"]
        watch("d", BlockShare(value, order, ["row"], coords))

    grad_mlp = (grad2 * plain(gate2)).astype(low)
    dgate2 = grad2 * mlp_out.astype(full)
    if gate2.shape[0] == 1:
        dgate2 = jnp.sum(dgate2, axis=0, keepdims=True)
    begin_down(grad_blocks(inner, grad_mlp, bits, block))
    grad2, grad_mlp = fence("start", grad2, grad_mlp)
    grad_gate, grad_up = down_back(grad_mlp, down_w, gate_pre, up_pre)
    w_gate = grad_of(mlp_in, "gate", [grad_gate, grad_up], 1024)
    grad_gate, grad_up, w_gate = fence("gate", grad_gate, grad_up, w_gate)
    r_gate = row_sum(w_gate)
    grad1, grad_att, dshift2, dscale2, dgate1 = mlp_back(
        [grad_gate, grad_up], [gate_w, up_w], grad2, hidden1, att, [scale2, gate1]
    )
    grad_att = fence("out", grad_att)
    w_out = grad_of(out_b, "out", [grad_att], 384)
    grad_ob = out_back(grad_att, out_w)
    begin_halves("gate", r_gate, grad_gate.shape[1])
    grad_ob, w_out = fence("attend", grad_ob, w_out)
    r_out = row_sum(w_out)
    dq, dkv, dkv_r = attend_back(query, kv, kv_r, grad_ob, out_b, lse, head)
    begin("out", r_out)
    dq, dkv_r = fence("qk", dq, dkv_r)
    grad_qkv, gain_rows = qk_back(dq, dkv, swap(dkv_r, "row"), raw, cosine, sine, gains[1], member, member_t, head)
    w_qkv = grad_of(attn_in, "qkv", [grad_qkv], width)
    grad_qkv, w_qkv = fence("qkv", grad_qkv, w_qkv)
    r_qkv = row_sum(w_qkv)
    grad0, dshift1, dscale1 = qkv_back(grad_qkv, qkv_w, grad1, hidden0, scale1)
    dmods = [dshift1, dscale1, dgate1, dshift2, dscale2, dgate2]
    begin_halves("qkv", r_qkv, r_qkv.shape[1] // 256 * 128)
    return grad0, dmods, gain_rows[:2], begin_halves


def per_device(
    latents,
    levels,
    timesteps,
    patch_weight,
    patch_bias,
    ada_weight,
    ada_bias,
    qkv_weight,
    qk_gains,
    out_weight,
    gate_weight,
    up_weight,
    down_weight,
    cotangent,
):
    images, slots, chans, rows_loc, cols_loc = latents.shape
    n_data = lax.axis_size("dp")
    assert images == 1 and slots == 2
    assert lax.axis_size("row") == 2 and lax.axis_size("col") == 2
    row = lax.axis_index("row")
    col = lax.axis_index("col")
    data = lax.axis_index("dp")
    bits = (n_data - 1).bit_length()
    left = col == 0
    coords = {"row": row, "col": col}
    place = (row, col, coords)
    for k in range(bits):
        coords[k] = (data >> k) & 1
    grid_rows = rows_loc // 2
    grid_cols = cols_loc
    half_cols = grid_cols // 2
    tokens = grid_rows * grid_cols
    width = cotangent.shape[-1]
    head = qk_gains.shape[2]
    heads = width // head
    pvals = chans * 4
    shard = width // 4
    me = data * 4 + row * 2 + col
    own_rows = width // (4 * n_data)

    def pair(own, other, axis):
        return jnp.concatenate([jnp.where(left, own, other), jnp.where(left, other, own)], axis=axis)

    own = {}
    for name, s in (
        ("qkv", qkv_weight),
        ("out", out_weight),
        ("gate", gate_weight),
        ("up", up_weight),
        ("down", down_weight),
        ("ada", ada_weight),
    ):
        own[name] = lax.all_gather(s, "row", axis=0)
    shards = {"qkv": qkv_weight, "out": out_weight, "gate": gate_weight, "up": up_weight, "down": down_weight}
    shards["ada"] = ada_weight

    def bundle(which, relay_bit, *parts):
        return Bundle(place, own, shards, parts, which, relay_bit)

    ff = gate_weight.shape[2]
    b_q0 = bundle(0, 0, ("qkv", 0, width))
    b_kv0 = bundle(0, 1, ("qkv", width, 2 * width))
    b_out0 = bundle(0, 0, ("out", 0, width))
    b_gate0 = bundle(0, 0, ("gate", 0, ff))
    b_up0 = bundle(0, 1, ("up", 0, ff))
    b_down0 = bundle(0, 0, ("down", 0, width))
    b_ada_a = bundle(1, 1, ("ada", 0, 3 * width))
    b_ada_b = bundle(1, 0, ("ada", 3 * width, 3 * width))
    b_qkv1 = bundle(1, 1, ("qkv", 0, 3 * width))
    b_og1 = bundle(1, 0, ("out", 0, width), ("gate", 0, ff))
    b_up1 = bundle(1, 1, ("up", 0, ff))
    b_down1 = bundle(1, 0, ("down", 0, width))
    enc_mats = {
        "qkv": lambda: weight_of("qkv", b_q0, b_kv0),
        "out": lambda: weight_of("out", b_out0),
        "gate": lambda: weight_of("gate", b_gate0),
        "up": lambda: weight_of("up", b_up0),
        "down": lambda: weight_of("down", b_down0),
    }
    dec_mats = {
        "qkv": lambda: weight_of("qkv", b_qkv1),
        "out": lambda: weight_of("out", b_og1),
        "gate": lambda: weight_of("gate", b_og1),
        "up": lambda: weight_of("up", b_up1),
        "down": lambda: weight_of("down", b_down1),
    }

    small = jnp.concatenate(
        [jnp.swapaxes(patch_weight, 1, 2).reshape(2 * pvals, shard), patch_bias, ada_bias.reshape(12, shard)], axis=0
    )
    small_other = swap(small, "col")
    blk = latents[0]
    blk_other = swap(blk, "col")
    flight = Flight(small)

    class Start:
        pass

    Start.small, Start.blk = small_other, blk_other
    flight.watch(Start, "small")
    flight.watch(Start, "blk")
    (blk,) = flight.fence([blk], [b_q0.prepare, b_kv0.prepare])
    small = pair(small[None], Start.small[None], 0)
    wide = pair(blk, Start.blk, 3)
    flight.send(small, "row", Start, "small")
    flight.send(wide[:, :, rows_loc - 1 :], "row", Start, "top")
    small, wide = flight.fence([small, wide], [b_q0.over_col, b_kv0.over_col, b_out0.prepare])
    temb = time_features(tie(timesteps, wide)[0], width)
    small = jnp.where(row == 0, jnp.stack([small, Start.small]), jnp.stack([Start.small, small]))
    small = small.reshape(4, 2 * pvals + 14, shard)
    patch_w = small[:, : 2 * pvals].transpose(1, 0, 2).reshape(2, pvals, width)
    patch_b = small[:, 2 * pvals : 2 * pvals + 2].transpose(1, 0, 2).reshape(2, width).astype(full)
    ada_b = small[:, 2 * pvals + 2 :].reshape(4, 2, 6 * shard).transpose(1, 0, 2).reshape(2, 6, width).astype(full)

    framed = jnp.concatenate([Start.top, wide[:, :, : rows_loc - 1]], axis=2)
    framed = jnp.concatenate([framed[..., -1:], framed[..., :-1]], axis=3)
    patches = (
        framed.reshape(slots, chans, grid_rows, 2, grid_cols, 2).transpose(0, 2, 4, 1, 3, 5).reshape(slots, tokens, pvals)
    )
    enc_patches = patches[0]
    dec_patches = jnp.where(left, patches[0], patches[1])

    sil0 = jax.nn.silu(temb[:1]).astype(low)
    temb_own = jnp.where(left, temb[:1], temb[1:])
    part = mod_partial(lax.dynamic_slice(sil0, (0, (2 * row + col) * shard), (1, shard)), ada_weight, width)

    cot_own = jnp.where(left, cotangent[0, 0], cotangent[0, 1])

    class Cotangent:
        got = None

    def send_cotangent(flight):
        flight.send(jnp.where(left, cotangent[0, 1], cotangent[0, 0]), "col", Cotangent, "got")

    quarter = head // 4
    lanes = tie(jnp.arange(width), flight.token)
    within = lanes % head
    section = within // quarter
    lane_freq = jnp.exp(-math.log(10000.0) * (within % quarter).astype(full) / quarter)
    row_pos = (row * grid_rows + jnp.arange(grid_rows)).astype(full)
    col_pos = jnp.arange(grid_cols).astype(full)
    row_angle = row_pos[:, None] * lane_freq[None, :]
    col_angle = col_pos[:, None] * lane_freq[None, :]
    by_row = section < 2
    sign = jnp.where(section % 2 == 0, -1.0, 1.0).astype(full)

    def table(fun):
        return jnp.where(by_row, fun(row_angle)[:, None, :], fun(col_angle)[None, :, :]).reshape(tokens, width)

    cosine = table(jnp.cos)
    sine = table(jnp.sin) * sign
    member = (lanes[:, None] // head == jnp.arange(128)[None, :]).astype(low)
    tabs = (cosine, sine, member, member.T, head)
    gain_rows = jnp.tile(qk_gains.astype(full), (1, 1, heads))
    even = jnp.broadcast_to((section % 2 == 0).astype(full), (2, 1, width))
    temper = head ** (-0.5) * math.log2(math.e)
    scaled = jnp.concatenate([gain_rows[:, :1] * temper, gain_rows[:, 1:], even], axis=1)
    gain_rows = jnp.concatenate([gain_rows, even], axis=1)
    gain_rows = [(scaled[k], gain_rows[k]) for k in range(2)]

    rest = list(range(2, bits))
    path_y = ["row", "col", 0, "hi"]
    path_s = ["row", "col", 0, 1] + rest
    paths = {"gate": path_y, "out": path_y, "qkv": path_y, "ada": path_s}
    perm = {}
    orders = {}
    for name in paths:
        key = tuple(paths[name])
        if key not in perm:
            source = halving_order(paths[name], width, own_rows, me, bits)
            perm[key] = lax.optimization_barrier((source[:, None] == lanes[None, :]).astype(low))
        orders[name] = perm[key]

    enc_h0 = matmul(enc_patches, patch_w[0]) + patch_b[0]
    starts = [b_q0.relay, b_kv0.relay, b_out0.over_col, b_q0.first_row, b_kv0.first_row, b_gate0.prepare]
    enc_h0, part, cosine, sine = flight.fence([enc_h0, part, cosine, sine], starts)
    part = part + swap(part, "row")
    part = part + swap(part, "col")
    enc_mod = part + ada_b[0]
    enc_mods = [enc_mod[k : k + 1] for k in range(6)]
    tabs = (cosine, sine) + tabs[2:]
    points = {
        "qkv": [b_q0.second_row, b_kv0.second_row, b_gate0.over_col, b_out0.relay, b_up0.prepare],
        "attend": [b_up0.over_col, b_gate0.relay, b_out0.first_row, b_down0.prepare],
        "out": [b_out0.second_row, b_up0.relay, b_down0.over_col, b_gate0.rows_both, b_ada_a.prepare],
        "gate": [b_up0.rows_both, b_ada_a.over_col, b_down0.relay, b_qkv1.prepare],
        "down": [b_down0.rows_both, b_qkv1.over_col, b_ada_a.relay, b_ada_b.prepare],
    }
    encoded, enc_cache, enc_mats = block_forward(enc_h0, enc_mods, enc_mats, gain_rows[0], tabs, flight, points)
    dec_h0 = matmul(dec_patches, patch_w[1]) + patch_b[1]
    cond = encoded + temb_own
    dec_sil = jax.nn.silu(cond).astype(low)
    starts = [b_ada_a.rows_both, b_ada_b.over_col, b_qkv1.relay, b_og1.prepare]
    keys = list(perm)
    dec_sil, *made = flight.fence([dec_sil] + [perm[key] for key in keys], starts)
    perm = dict(zip(keys, made))
    orders = {name: perm[tuple(paths[name])] for name in orders}
    ada_bias1 = ada_b[1].reshape(1, 6 * width)
    mod_a = ada_matmul(dec_sil, weight_of("ada", b_ada_a), ada_bias1[:, : 3 * width])
    dec_mods = [Cols(mod_a, k * width, width) for k in range(3)]
    held = Sum()

    def second_mods(flight):
        held.value = ada_matmul(tie(dec_sil, flight.token), weight_of("ada", b_ada_b), ada_bias1[:, 3 * width :])
        flight.watch(held, "value")

    dec_mods += [Cols(held, k * width, width) for k in range(3)]
    points = {
        "qkv": [b_qkv1.rows_both, b_og1.over_col, b_ada_b.relay, b_up1.prepare],
        "attend": [b_ada_b.rows_both, second_mods, b_up1.over_col, b_og1.relay, b_down1.prepare],
        "out": [b_og1.rows_both, b_down1.over_col, b_up1.relay],
        "gate": [b_up1.rows_both, b_down1.relay, send_cotangent],
        "down": [b_down1.rows_both],
    }
    decoded, dec_cache, dec_mats = block_forward(dec_h0, dec_mods, dec_mats, gain_rows[1], tabs, flight, points)
    live = (col < levels[0]).astype(full)
    result = (decoded * live).astype(low).reshape(grid_rows, grid_cols, width)
    near = jnp.where(left, result[:, :half_cols], result[:, half_cols:])
    far = jnp.where(left, result[:, half_cols:], result[:, :half_cols])

    class Away:
        got = None

    def send_result(flight):
        flight.send(far, "col", Away, "got")


    agenda = Agenda()
    go = agenda.go
    scatter = functools.partial(agenda.scatter, bits)
    comm = (flight, agenda, orders, paths, coords)
    cot = pair(cot_own, Cotangent.got, 1).reshape(tokens, width)
    dec_grad2 = cot.astype(full) * live

    def split_down(tag, way_a, way_b, flight):
        whole_sum = agenda.tasks["d" + tag]
        cut = width // 256 * 128
        for name, columns, way in (("da" + tag, (0, cut), way_a), ("db" + tag, (cut, width - cut), way_b)):
            part = BlockShare(None, whole_sum.order, way, coords)
            part.terms = list(whole_sum.terms)
            part.done = list(whole_sum.done)
            part.columns = columns
            agenda.tasks[name] = part

    plan = {
        "start": [send_result, go("d1")],
        "gate": [functools.partial(split_down, "1", ["col", 0, "hi"], [0, "col", "hi"]), go("da1"), go("db1")],
        "out": [go("da1"), go("db1")],
        "attend": [go("ga1"), go("gb1"), scatter(1, "da1", "db1")],
        "qk": [go("ga1"), go("gb1")],
        "qkv": [go("o1")],
    }
    dec_grad0, dec_dmods, dec_gains, begin_halves = block_backward(
        dec_grad2, dec_cache, dec_mods, dec_mats, gain_rows[1], tabs, comm, "1", plan
    )
    away = Away.got
    result = jnp.stack([jnp.where(left, near, away), jnp.where(left, away, near)])[None]
    dec_dmods = [piece.astype(low) for piece in dec_dmods]
    w_ada = ordered_grad(dec_sil, orders["ada"], dec_dmods, width)
    starts = [go("qa1"), go("qb1"), go("o1")]
    w_ada, *dec_dmods = flight.fence([w_ada] + dec_dmods, starts)
    r_ada = row_sum(w_ada)
    dec_bada = jnp.stack([jnp.sum(piece.astype(full), axis=0) for piece in dec_dmods])
    enc_grad2 = ada_back(dec_dmods, weight_of("ada", b_ada_a, b_ada_b), cond)

    def patch_rows(patch, grad):
        ones = jnp.ones((tokens, 1), low)
        return outer_sum(jnp.concatenate([patch, ones], axis=1), grad)

    total = jnp.concatenate([patch_rows(dec_patches, dec_grad0), dec_bada, dec_gains], axis=0)
    agenda.tasks["s"] = Total(total, ["row", "col"] + list(range(bits)))

    begin_halves("ada", r_ada, r_ada.shape[1] // 2)
    plan = {
        "start": [go("s"), go("d0"), go("aa1"), go("ab1"), scatter(0, "ga1", "gb1")],
        "gate": [
            functools.partial(split_down, "0", [1, "col", 0] + rest, [1, 0, "col"] + rest),
            go("aa1"),
            go("ab1"),
            go("qa1"),
            go("qb1"),
            go("da0"),
        ],
        "out": [go("s"), go("db0")],
        "attend": [go("s"), go("ga0"), go("gb0"), go("aa1", "ab1")],
        "qk": [go("ga0"), go("gb0"), go("da0"), go("db0"), scatter(0, "qa1", "qb1", "o1")],
        "qkv": [go("s"), go("o0"), go("da0"), go("db0"), go("aa1", "ab1")],
    }
    enc_grad0, enc_dmods, enc_gains, _ = block_backward(
        enc_grad2, enc_cache, enc_mods, enc_mats, gain_rows[0], tabs, comm, "0", plan
    )
    dmod_enc = jnp.concatenate(enc_dmods, axis=0)
    class Last:
        pass

    Last.result = result
    (enc_grad0,) = flight.fence([enc_grad0], [go("qa0"), go("qb0"), scatter(1, "ga0", "gb0")])
    total = jnp.concatenate([patch_rows(enc_patches, enc_grad0), enc_gains, dmod_enc], axis=0)

    def image(dpatch):
        return (
            dpatch.reshape(grid_rows, grid_cols, chans, 2, 2).transpose(2, 0, 3, 1, 4).reshape(chans, rows_loc, 2 * cols_loc)
        )

    enc_image = image(matmul_t(enc_grad0, patch_w[0]))
    dec_image = image(matmul_t(dec_grad0, patch_w[1]))
    zero = jnp.zeros_like(dec_image)
    grads = jnp.stack([enc_image + jnp.where(left, dec_image, zero), jnp.where(left, zero, dec_image)])
    grads = jnp.concatenate([grads[..., 1:], grads[..., :1]], axis=3)
    finished = [name for name, task in agenda.tasks.items() if not task.path and isinstance(task, Share)]
    for name in finished:
        agenda.tasks[name].hold(flight)
    flight.watch(Last, "result")
    total, grads = flight.fence([total, grads], [go("qa0"), go("qb0"), go("o0"), go("s")])
    flight.send(total, "row", Last, "total")
    flight.send(grads[:, :, :1], "row", Last, "below")
    total, grads = flight.fence([total, grads], [scatter(3, "qa0", "qb0", "o0"), go("da0", "db0")])
    total = total + Last.total
    flight.send(total, "col", Last, "total")
    grads = jnp.concatenate([grads[:, :, 1:], Last.below], axis=2)
    one = grads[..., :cols_loc]
    two = grads[..., cols_loc:]
    flight.send(jnp.where(left, two, one), "col", Last, "image")
    count = pvals + 3
    tiny = TotalAndRows(None, count, list(range(bits)))
    agenda.tasks["t"] = tiny

    def begin_tiny(flight):
        tiny.value = jnp.concatenate([total + Last.total, sil0.astype(full)], axis=0)
        go("t")(flight)

    flight.fence([total], [begin_tiny])
    latent_grad = (jnp.where(left, one, two) + Last.image)[None]
    flight.fence([total], [go("t")])
    flight.fence([total], [go("t")])
    flight.fence([total])
    result = Last.result
    while any(task.path for task in agenda.tasks.values()):
        flight.fence([total], [go(name) for name, task in agenda.tasks.items() if task.path])
        flight.fence([total])
    dec_small = agenda.tasks["s"].value
    total = tiny.value[:count]
    dmod_all = tiny.value[count:]
    dmod_all = dmod_all.reshape(n_data, 7, width)
    enc_small = total
    enc_ada = jnp.dot(
        lax.dynamic_slice(dmod_all, (0, 6, me * own_rows), (n_data, 1, own_rows))[:, 0].T,
        dmod_all[:, :6].reshape(n_data, 6 * width),
        precision=highest,
        preferred_element_type=full,
    )
    enc_bada = jnp.sum(dmod_all[:, :6], axis=0)

    def own_lanes(value):
        return lax.dynamic_slice(value, (0, me * own_rows), (value.shape[0], own_rows))

    enc_patch = own_lanes(enc_small[: pvals + 1])
    dec_patch = own_lanes(dec_small[: pvals + 1])
    g_patch = jnp.stack([enc_patch[:pvals].T, dec_patch[:pvals].T])
    g_patch_b = jnp.stack([enc_patch[pvals], dec_patch[pvals]])
    bada = jnp.stack([enc_bada.reshape(-1), dec_small[pvals + 1 : pvals + 7].reshape(-1)])
    own_bada = 6 * own_rows
    g_bada = lax.dynamic_slice(bada, (0, me * own_bada), (2, own_bada))
    gains = jnp.stack([enc_small[pvals + 1 :], dec_small[pvals + 7 :]])
    gains = gains.reshape(2, 2, heads, head).sum(axis=2)
    def both(name):
        parts = [agenda.tasks[name + tag].value.astype(full) for tag in "01"]
        return jnp.stack(parts)

    for task in agenda.tasks.values():
        assert not task.path
    g_ada = jnp.concatenate([agenda.tasks["aa1"].value, agenda.tasks["ab1"].value], axis=1)
    g_ada_all = jnp.stack([enc_ada, g_ada.astype(full)])
    g_qkv = jnp.concatenate([both("qa"), both("qb")], axis=2)
    g_down = jnp.concatenate([both("da"), both("db")], axis=2)
    stacked = [g_qkv, both("o"), both("ga"), both("gb"), g_down]
    return (
        result,
        latent_grad,
        g_patch,
        g_patch_b,
        g_ada_all,
        g_bada,
        stacked[0],
        gains,
        stacked[1],
        stacked[2],
        stacked[3],
        stacked[4],
    )


def solution(mesh):
    tile = ("row", "col")
    every = ("dp", "row", "col")
    return jax.shard_map(
        per_device,
        mesh=mesh,
        in_specs=(
            P("dp", None, None, "row", "col"),
            P("dp"),
            P("dp", None),
            P(None, tile, None),
            P(None, tile),
            P(None, tile, None),
            P(None, tile),
            P(None, tile, None),
            P(),
            P(None, tile, None),
            P(None, tile, None),
            P(None, tile, None),
            P(None, tile, None),
            P("dp", None, "row", "col", None),
        ),
        out_specs=(
            P("dp", None, "row", "col", None),
            P("dp", None, None, "row", "col"),
            P(None, every, None),
            P(None, every),
            P(None, every, None),
            P(None, every),
            P(None, every, None),
            P(),
            P(None, every, None),
            P(None, every, None),
            P(None, every, None),
            P(None, every, None),
        ),
        check_vma=False,
    )
```

```python
import functools
import math

import jax
import jax.numpy as jnp
from jax import lax
from jax.experimental import pallas as pl
from jax.experimental.pallas import tpu as pltpu
from jax.sharding import PartitionSpec as P

epsilon = 1e-06
highest = lax.Precision.HIGHEST
low = jnp.bfloat16
full = jnp.float32
WINDOW = 256
PAIR = 4
MIB = 1 << 20


def matmul(left, right):
    return jnp.dot(left, right, preferred_element_type=full)


def matmul_t(left, right):
    return lax.dot_general(left, right, (((1,), (1,)), ((), ())), preferred_element_type=full)


def outer_sum(left, right):
    return lax.dot_general(left, right, (((0,), (0,)), ((), ())), preferred_element_type=full)


def rms_scale(value):
    return lax.rsqrt(jnp.mean(value * value, axis=-1, keepdims=True) + epsilon)


def rms_back(value, inverse, grad):
    return inverse * grad - value * inverse**3 * jnp.mean(value * grad, axis=-1, keepdims=True)


def swap(value, item):
    if isinstance(item, str):
        return lax.ppermute(value, item, [(0, 1), (1, 0)])
    size = lax.axis_size("dp")
    return lax.ppermute(value, "dp", [(i, i ^ (1 << item)) for i in range(size)])


def time_features(steps, width):
    half = width // 2
    freqs = jnp.exp(-math.log(10000.0) * jnp.arange(half).astype(full) / half)
    angles = steps.astype(full)[:, None] * freqs[None, :]
    return jnp.concatenate([jnp.cos(angles), jnp.sin(angles)], axis=-1)


def whole(shape):
    return pl.BlockSpec(shape, lambda *_: (0,) * len(shape))


def params(mib):
    return pltpu.CompilerParams(vmem_limit_bytes=mib * MIB)


def head_mean(value, member, head):
    return matmul(value.astype(low), member) * (1.0 / head)


def split_dot(value, onehot):
    top = value.astype(low)
    rest = (value - top.astype(full)).astype(low)
    return matmul(top, onehot) + matmul(rest, onehot)


def turned(value, cosine, sine, even, quarter):
    width = value.shape[-1]
    ahead = pltpu.roll(value, width - quarter, axis=1)
    behind = pltpu.roll(value, quarter, axis=1)
    return value * cosine + jnp.where(even, ahead, behind) * sine


def even_lanes(gain_ref, shape):
    return jnp.broadcast_to(gain_ref[2:3, :] > 0.5, shape)


def qk_back_body(head, dq_ref, dkv_ref, dkvx_ref, qkv_ref, cos_ref, sin_ref, gain_ref, mem_ref, memt_ref, out_ref, gg_ref):
    width = dq_ref.shape[-1]

    @pl.when(pl.program_id(0) == 0)
    def _():
        gg_ref[...] = jnp.zeros_like(gg_ref)

    cosine = cos_ref[...]
    sine = -sin_ref[...]
    even = even_lanes(gain_ref, cosine.shape)
    member = mem_ref[...]
    member_t = memt_ref[...]
    grads = (dq_ref[...], dkv_ref[:, :width] + dkvx_ref[:, :width].astype(full))
    for part in (0, 1):
        value = qkv_ref[:, part * width : (part + 1) * width]
        mean = head_mean(value * value, member, head)
        inverse_h = lax.rsqrt(mean + epsilon)
        inverse = split_dot(inverse_h, member_t)
        grad_n = turned(grads[part], cosine, sine, even, head // 4)
        normed = value * inverse
        gg_ref[part : part + 1, :] += jnp.sum(grad_n * normed, axis=0, keepdims=True)
        weighted = grad_n * gain_ref[part : part + 1, :]
        dots = head_mean(value * weighted, member, head) * inverse_h * inverse_h
        back = inverse * weighted - normed * split_dot(dots, member_t)
        out_ref[:, part * width : (part + 1) * width] = back.astype(low)
    out_ref[:, 2 * width :] = (dkv_ref[:, width:] + dkvx_ref[:, width:].astype(full)).astype(low)


def qk_back(dq, dkv, dkvx, raw, cosine, sine, gains, member, member_t, head):
    tokens, width = dq.shape
    step = 256
    rows = lambda n: pl.BlockSpec((step, n), lambda i: (i, 0))
    return pl.pallas_call(
        functools.partial(qk_back_body, head),
        grid=(tokens // step,),
        in_specs=[rows(width)]
        + [rows(2 * width)] * 3
        + [rows(width), rows(width), whole(gains.shape), whole(member.shape), whole(member_t.shape)],
        out_specs=[rows(3 * width), whole((8, width))],
        out_shape=[jax.ShapeDtypeStruct((tokens, 3 * width), low), jax.ShapeDtypeStruct((8, width), full)],
        compiler_params=params(60),
        cost_estimate=pl.CostEstimate(flops=60 * raw.size, bytes_accessed=18 * raw.size, transcendentals=0),
        name="qk_back",
    )(dq, dkv, dkvx, raw, cosine, sine, gains, member, member_t)


def head_window(head, width, part):
    index = pl.program_id(0) * PAIR + part
    start = index * head
    base = jnp.minimum(lax.div(start, 128) * 128, width - WINDOW)
    return index, pl.multiple_of(base, 128), start - base


def window_mask(shape, offset, head):
    lane = lax.broadcasted_iota(jnp.int32, shape, 1)
    return jnp.logical_and(lane >= offset, lane < offset + head)


def attend_body(head, q_ref, kvl_ref, kvr_ref, o_ref, lse_ref, acc_ref):
    tokens, width = q_ref.shape

    @pl.when(pl.program_id(0) == 0)
    def _():
        acc_ref[...] = jnp.zeros_like(acc_ref)
        lse_ref[...] = jnp.zeros_like(lse_ref)

    step = 256
    one = jnp.ones((), low)
    lane = lax.broadcasted_iota(jnp.int32, (step, lse_ref.shape[1]), 1)
    for part in range(PAIR):
        index, base, offset = head_window(head, width, part)
        cols = pl.ds(base, WINDOW)
        vals = pl.ds(pl.multiple_of(width + base, 128), WINDOW)
        mask_k = window_mask((tokens, WINDOW), offset, head)
        value_l = jnp.where(mask_k, kvl_ref[:, vals], one)
        value_r = jnp.where(mask_k, kvr_ref[:, vals], one)
        mask = window_mask((step, WINDOW), offset, head)
        for first in range(0, tokens, step):
            rows = slice(first, first + step)
            query = jnp.where(mask, q_ref[rows, cols], jnp.zeros((), low))
            left = jnp.exp2(matmul_t(query, kvl_ref[:, cols])).astype(low)
            right = jnp.exp2(matmul_t(query, kvr_ref[:, cols])).astype(low)
            out = matmul(left, value_l) + matmul(right, value_r)
            total = jnp.max(jnp.where(mask, 0.0, out), axis=1, keepdims=True)
            acc_ref[rows, cols] += jnp.where(mask, out * (1.0 / total), 0.0)
            lse_ref[rows, :] += jnp.where(lane == index, jnp.log2(total), 0.0)

    @pl.when(pl.program_id(0) == pl.num_programs(0) - 1)
    def _():
        o_ref[...] = acc_ref[...].astype(low)


def attend(query, kv_l, kv_r, head):
    tokens, width = query.shape
    heads = width // head
    return pl.pallas_call(
        functools.partial(attend_body, head),
        grid=(heads // PAIR,),
        in_specs=[whole((tokens, width))] + [whole((tokens, 2 * width))] * 2,
        out_specs=[whole((tokens, width)), whole((tokens, 128))],
        out_shape=[jax.ShapeDtypeStruct((tokens, width), low), jax.ShapeDtypeStruct((tokens, 128), full)],
        scratch_shapes=[pltpu.VMEM((tokens, width), full)],
        compiler_params=params(56),
        cost_estimate=pl.CostEstimate(
            flops=8 * tokens * tokens * WINDOW * heads, bytes_accessed=14 * tokens * width, transcendentals=2 * tokens * tokens * heads
        ),
        name="attend",
    )(query, kv_l, kv_r)


def in_three(column):
    top = column.astype(low)
    rest = column - top.astype(full)
    middle = rest.astype(low)
    return top, middle, (rest - middle.astype(full)).astype(low)


def attend_back_body(head, q_ref, kvl_ref, kvr_ref, do_ref, o_ref, lse_ref, dq_ref, dl_ref, dr_ref, dr_acc):
    tokens, width = q_ref.shape
    temper = head ** (-0.5)

    @pl.when(pl.program_id(0) == 0)
    def _():
        for ref in (dq_ref, dl_ref, dr_acc):
            ref[...] = jnp.zeros_like(ref)

    shape = (tokens, WINDOW)
    lane = lax.broadcasted_iota(jnp.int32, shape, 1)
    small = lax.broadcasted_iota(jnp.int32, lse_ref.shape, 1)
    zero = jnp.zeros((), low)
    for part in range(PAIR):
        index, base, offset = head_window(head, width, part)
        cols = pl.ds(base, WINDOW)
        vals = pl.ds(pl.multiple_of(width + base, 128), WINDOW)
        mask = window_mask(shape, offset, head)
        spare = jnp.where(offset >= 3, 0, WINDOW - 3)
        minus = jnp.where(jnp.logical_and(lane >= spare, lane < spare + 3), -jnp.ones((), low), zero)
        query = jnp.where(mask, q_ref[:, cols], zero)
        grad = jnp.where(mask, do_ref[:, cols], zero)
        delta = jnp.sum(grad.astype(full) * o_ref[:, cols].astype(full), axis=1, keepdims=True)
        level = jnp.sum(jnp.where(small == index, lse_ref[...], 0.0), axis=1, keepdims=True)
        query_x = query
        grad_x = grad
        for k, (a, b) in enumerate(zip(in_three(level), in_three(delta))):
            at = lane == spare + k
            query_x = jnp.where(at, a, query_x)
            grad_x = jnp.where(at, b, grad_x)
        grad_q = 0.0
        for ref, acc in ((kvl_ref, dl_ref), (kvr_ref, dr_acc)):
            key = jnp.where(mask, ref[:, cols], minus)
            value = jnp.where(mask, ref[:, vals], minus)
            prob = jnp.exp2(matmul_t(key, query_x))
            grad_s = (prob * matmul_t(value, grad_x)).astype(low)
            acc[:, vals] += matmul(prob.astype(low), grad)
            acc[:, cols] += matmul(grad_s, query)
            grad_q = grad_q + outer_sum(grad_s, key)
        dq_ref[:, cols] += jnp.where(mask, grad_q * temper, 0.0)

    @pl.when(pl.program_id(0) == pl.num_programs(0) - 1)
    def _():
        back = math.log(2.0)
        dl_ref[:, :width] = dl_ref[:, :width] * back
        dr_ref[:, :width] = (dr_acc[:, :width] * back).astype(low)
        dr_ref[:, width:] = dr_acc[:, width:].astype(low)


def attend_back(query, kv_l, kv_r, grad, out, levels, head):
    tokens, width = query.shape
    heads = width // head
    both = (tokens, 2 * width)
    one = (tokens, width)
    return pl.pallas_call(
        functools.partial(attend_back_body, head),
        grid=(heads // PAIR,),
        in_specs=[whole(one), whole(both), whole(both), whole(one), whole(one), whole(levels.shape)],
        out_specs=[whole(one), whole(both), whole(both)],
        out_shape=[like(one, full), like(both, full), like(both, low)],
        scratch_shapes=[pltpu.VMEM(both, full)],
        compiler_params=params(62),
        cost_estimate=pl.CostEstimate(
            flops=20 * tokens * tokens * WINDOW * heads, bytes_accessed=28 * tokens * width, transcendentals=2 * tokens * tokens * heads
        ),
        name="attend_back",
    )(query, kv_l, kv_r, grad, out, levels)


class Weight:
    def __init__(self, segments):
        self.segments = segments
        self.columns = sum(columns for _, _, columns in segments)
        self.plan = [piece[1:] for piece in segments[0][1]]
        self.height = sum(rows for _, _, rows in self.plan)
        for _, pieces, _ in segments:
            assert [piece[3] for piece in pieces] == [rows for _, _, rows in self.plan]


def piece_source(ref, lead, first, count):
    for index in lead:
        ref = ref.at[index]
    return ref.at[:, pl.ds(first, count)]


class Cols:
    def __init__(self, array, first, count):
        self.source = array
        self.first = first
        self.count = count

    @property
    def array(self):
        return self.source if isinstance(self.source, jax.Array) else self.source.value

    @property
    def shape(self):
        return (self.array.shape[0], self.count)

    @property
    def dtype(self):
        return self.array.dtype

    @property
    def size(self):
        return self.array.shape[0] * self.count

    def value(self):
        return self.array[:, self.first : self.first + self.shape[1]]


def plain(value):
    return value.value().astype(full) if isinstance(value, Cols) else value


def anywhere(count):
    return [pl.BlockSpec(memory_space=pl.ANY)] * count


class Stream:
    def __init__(self, weights, tile, late):
        self.weights = weights
        self.tile = tile
        self.late = late
        self.steps = weights[0].columns // tile

    def pieces_of(self):
        return [pieces for w in self.weights for _, pieces, _ in w.segments]

    def specs(self):
        return [pl.BlockSpec(memory_space=pltpu.SMEM)] + anywhere(sum(len(p) for p in self.pieces_of()) + len(self.late))

    def operands(self):
        offsets = jnp.concatenate([offs for w in self.weights for offs, _, _ in w.segments])
        arrays = [piece[0] for pieces in self.pieces_of() for piece in pieces]
        return [offsets] + arrays + [v.array if isinstance(v, Cols) else v for v in self.late]

    def scratch(self):
        shapes = []
        for w in self.weights:
            shapes += [pltpu.VMEM((2, w.height, self.tile), low), pltpu.SemaphoreType.DMA((2, len(w.plan)))]
        for value in self.late:
            shapes += [pltpu.VMEM(value.shape, value.dtype), pltpu.SemaphoreType.DMA((1,))]
        return shapes

    def bind(self, operand_refs, scratch_refs):
        self.offs = operand_refs[0]
        refs = list(operand_refs[1:])
        self.refs = []
        for w in self.weights:
            mine = []
            for _, pieces, _ in w.segments:
                mine.append(refs[: len(pieces)])
                refs = refs[len(pieces) :]
            self.refs.append(mine)
        self.buffers = scratch_refs[0 : 2 * len(self.weights) : 2]
        self.sems = scratch_refs[1 : 2 * len(self.weights) : 2]
        rest = scratch_refs[2 * len(self.weights) :]
        self.late_bufs = rest[0::2]
        self.late_copies = []
        for value, ref, buf, sem in zip(self.late, refs, rest[0::2], rest[1::2]):
            if isinstance(value, Cols):
                ref = ref.at[:, pl.ds(value.first, value.shape[1])]
            self.late_copies.append(pltpu.make_async_copy(ref, buf, sem.at[0]))

    def segment_copies(self, index, number, column, slot):
        w = self.weights[index]
        base = sum(len(x.plan) * len(x.segments) for x in self.weights[:index]) + number * len(w.plan)
        out = []
        for at, (_, lead, first, rows) in enumerate(w.segments[number][1]):
            source = piece_source(self.refs[index][number][at], lead, pl.multiple_of(first + column, 128), self.tile)
            start = pl.multiple_of(self.offs[base + at], 16)
            target = self.buffers[index].at[slot, pl.ds(start, rows), :]
            out.append(pltpu.make_async_copy(source, target, self.sems[index].at[slot, at]))
        return out

    def copies(self, step, slot):
        return [copy for index in range(len(self.weights)) for copy in self.segment_copies(index, 0, step * self.tile, slot)]

    def start_tile(self, step, slot):
        for index, w in enumerate(self.weights):
            first = 0
            for number, (_, _, columns) in enumerate(w.segments):
                count = columns // self.tile

                def start():
                    for copy in self.segment_copies(index, number, (step - first) * self.tile, slot):
                        copy.start()

                if len(w.segments) == 1:
                    start()
                else:
                    pl.when(jnp.logical_and(step >= first, step < first + count))(start)
                first += count

    def wait_tile(self, slot):
        for index in range(len(self.weights)):
            for copy in self.segment_copies(index, 0, 0, slot):
                copy.wait()

    def advance(self):
        step = pl.program_id(0)
        slot = lax.rem(step, 2)

        @pl.when(step == 0)
        def _():
            self.start_tile(jnp.int32(0), 0)
            for copy in self.late_copies:
                copy.start()

        @pl.when(step + 1 < self.steps)
        def _():
            self.start_tile(step + 1, 1 - slot)

        self.wait_tile(slot)
        return step, [buf.at[slot] for buf in self.buffers]

    def wait_late(self):
        for copy in self.late_copies:
            copy.wait()
        return self.late_bufs


def stream_call(name, stream, body, ins, in_specs, outs, out_specs, scratch, flops, mib=58):
    operands = stream.operands()
    frame = stream.scratch()

    def kernel(*refs):
        count = len(operands)
        ops, refs = refs[:count], refs[count:]
        inputs, refs = refs[: len(ins)], refs[len(ins) :]
        outputs, refs = refs[: len(outs)], refs[len(outs) :]
        stream.bind(ops, refs[: len(frame)])
        body(stream, inputs, outputs, refs[len(frame) :])

    moved = sum(v.size * v.dtype.itemsize for v in list(ins) + list(stream.late) + list(outs))
    moved += sum(2 * w.height * w.columns for w in stream.weights)
    return pl.pallas_call(
        kernel,
        grid=(stream.steps,),
        in_specs=stream.specs() + in_specs,
        out_specs=out_specs,
        out_shape=outs,
        scratch_shapes=frame + scratch,
        compiler_params=params(mib),
        cost_estimate=pl.CostEstimate(flops=flops, bytes_accessed=moved, transcendentals=0),
        name=name,
    )(*operands, *ins)


def by_rows(tokens, fun, step=128):
    @pl.loop(0, tokens // step)
    def _(i):
        fun(pl.ds(pl.multiple_of(i * step, step), step))


def take(ref, rows):
    return (ref[rows, :] if ref.shape[0] > 1 else ref[...]).astype(full)


def give(ref, rows, value):
    if ref.shape[0] > 1:
        ref[rows, :] = value.astype(ref.dtype)
    else:
        ref[...] += jnp.sum(value, axis=0, keepdims=True)


def like(shape, dtype):
    return jax.ShapeDtypeStruct(shape, dtype)


def ada_matmul(value, weight, bias):
    tokens = value.shape[0]
    tile = weight.height
    stream = Stream([weight], tile, [])

    def body(stream, ins, outs, scratch):
        _, (w,) = stream.advance()
        outs[0][...] = (matmul(ins[0][...], w[...]) + ins[1][...]).astype(low)

    return stream_call(
        "ada",
        stream,
        body,
        [value, bias],
        [whole(value.shape), pl.BlockSpec((1, tile), lambda j: (0, j))],
        [like((tokens, weight.columns), low)],
        [pl.BlockSpec((tokens, tile), lambda j: (0, j))],
        [],
        2 * tokens * weight.height * weight.columns,
    )[0]


def mod_partial(row, weight, width):
    shard = weight.shape[1]
    tall = jnp.broadcast_to(row, (16, shard))

    def body(x_ref, w_ref, out_ref):
        out_ref[0] = matmul(x_ref[...], w_ref[...])[:8]

    out = pl.pallas_call(
        body,
        grid=(6,),
        in_specs=[whole(tall.shape), pl.BlockSpec((None, shard, width), lambda j: (0, 0, j))],
        out_specs=pl.BlockSpec((1, 8, width), lambda j: (j, 0, 0)),
        out_shape=like((6, 8, width), full),
        compiler_params=params(60),
        cost_estimate=pl.CostEstimate(flops=0, bytes_accessed=12 * shard * width, transcendentals=0),
        name="modpart",
    )(tall, weight)
    return out[:, 0]


def qkv_matmul(value, weight, cosine, sine, gains, member, member_t, head):
    tokens, width = value.shape
    stream = Stream([weight], width, [cosine, sine])

    def body(stream, ins, outs, scratch):
        x_ref, gain_ref, mem_ref, memt_ref = ins
        q_ref, kv_ref, raw_ref = outs
        (acc_ref,) = scratch
        step, (w,) = stream.advance()
        cos_ref, sin_ref = stream.late_bufs
        acc_ref[...] = matmul(x_ref[...], w[...])

        @pl.when(step == 0)
        def _():
            stream.wait_late()

        def head_norm(part, out, cols):
            def rows_of(rows):
                raw = acc_ref[rows, :]
                raw_ref[rows, :] = raw
                mean = head_mean(raw * raw, mem_ref[...], head)
                inverse = split_dot(lax.rsqrt(mean + epsilon), memt_ref[...])
                normed = raw * inverse * gain_ref[part : part + 1, :]
                even = even_lanes(gain_ref, raw.shape)
                out[rows, cols] = turned(normed, cos_ref[rows, :], sin_ref[rows, :], even, head // 4).astype(low)

            by_rows(tokens, rows_of, 256)

        @pl.when(step == 0)
        def _():
            head_norm(0, q_ref, slice(0, width))

        @pl.when(step == 1)
        def _():
            head_norm(1, kv_ref, slice(0, width))

        @pl.when(step == 2)
        def _():
            kv_ref[:, width:] = acc_ref[...].astype(low)

    flat = like((tokens, width), low)
    return stream_call(
        "qkv",
        stream,
        body,
        [value, gains, member, member_t],
        [whole(v.shape) for v in (value, gains, member, member_t)],
        [flat, like((tokens, 2 * width), low), like((tokens, 2 * width), full)],
        [whole((tokens, width)), whole((tokens, 2 * width)), pl.BlockSpec((tokens, width), lambda j: (0, jnp.minimum(j, 1)))],
        [pltpu.VMEM((tokens, width), full)],
        2 * tokens * weight.height * weight.columns,
    )


def out_matmul(value, weight, hidden0, mods):
    tokens, width = value.shape
    stream = Stream([weight], 384, [hidden0] + mods)

    def body(stream, ins, outs, scratch):
        att_ref, h1_ref, b_ref = outs
        (acc_ref,) = scratch
        step, (w,) = stream.advance()
        acc_ref[step] = matmul(ins[0][...], w[...])

        @pl.when(step == stream.steps - 1)
        def _():
            h0_ref, gate_ref, shift_ref, scale_ref = stream.wait_late()

            def rows_of(rows):
                att = jnp.concatenate([acc_ref[k, rows, :] for k in range(stream.steps)], axis=1)
                hidden1 = h0_ref[rows, :] + take(gate_ref, rows) * att
                normed = hidden1 * rms_scale(hidden1)
                att_ref[rows, :] = att.astype(low)
                h1_ref[rows, :] = hidden1
                b_ref[rows, :] = (normed * (1.0 + take(scale_ref, rows)) + take(shift_ref, rows)).astype(low)

            by_rows(tokens, rows_of)

    return stream_call(
        "attout",
        stream,
        body,
        [value],
        [whole(value.shape)],
        [like((tokens, width), low), like((tokens, width), full), like((tokens, width), low)],
        [whole((tokens, width))] * 3,
        [pltpu.VMEM((stream.steps, tokens, 384), full)],
        2 * tokens * weight.height * weight.columns,
    )


def gate_up_matmul(value, gate, up):
    tokens, width = value.shape
    tile = 1024
    stream = Stream([gate, up], tile, [])

    def body(stream, ins, outs, scratch):
        hid_ref, g_ref, u_ref = outs
        _, (wg, wu) = stream.advance()
        g = matmul(ins[0][...], wg[...])
        u = matmul(ins[0][...], wu[...])
        g_ref[...] = g.astype(low)
        u_ref[...] = u.astype(low)
        hid_ref[...] = (g * jax.nn.sigmoid(g) * u).astype(low)

    flat = like((tokens, gate.columns), low)
    return stream_call(
        "gateup",
        stream,
        body,
        [value],
        [whole(value.shape)],
        [flat] * 3,
        [pl.BlockSpec((tokens, tile), lambda j: (0, j))] * 3,
        [],
        4 * tokens * gate.height * gate.columns,
    )


def down_matmul(value, weight, hidden1, gate):
    tokens, depth = value.shape
    width = weight.columns
    stream = Stream([weight], width, [hidden1, gate])

    def body(stream, ins, outs, scratch):
        mlp_ref, h2_ref = outs
        (acc_ref,) = scratch
        hid_ref = ins[0]
        at = 0
        copies = stream.copies(0, 0)
        for copy in copies + stream.late_copies:
            copy.start()
        for k, (_, _, rows) in enumerate(weight.plan):
            copies[k].wait()
            first = stream.offs[k]
            left = hid_ref[:, pl.ds(pl.multiple_of(first, 128), rows)]
            part = matmul(left, stream.buffers[0][0, pl.ds(pl.multiple_of(first, 128), rows), :])
            if k == 0:
                acc_ref[...] = part
            else:
                acc_ref[...] += part
        h1_ref, gate_ref = stream.wait_late()

        def rows_of(rows):
            mlp = acc_ref[rows, :]
            mlp_ref[rows, :] = mlp.astype(low)
            h2_ref[rows, :] = h1_ref[rows, :] + take(gate_ref, rows) * mlp

        by_rows(tokens, rows_of)

    return stream_call(
        "down",
        stream,
        body,
        [value],
        [whole(value.shape)],
        [like((tokens, width), low), like((tokens, width), full)],
        [whole((tokens, width))] * 2,
        [pltpu.VMEM((tokens, width), full)],
        2 * tokens * depth * width,
    )


def down_back(grad, weight, gate_pre, up_pre):
    tokens, width = grad.shape
    depth = weight.height
    stream = Stream([weight], width, [gate_pre, up_pre])

    def body(stream, ins, outs, scratch):
        dg_ref, du_ref = outs
        copies = stream.copies(0, 0)
        for copy in copies + stream.late_copies:
            copy.start()
        for k, (_, _, count) in enumerate(weight.plan):
            copies[k].wait()
            if k == 0:
                g_ref, u_ref = stream.wait_late()
            first = pl.multiple_of(stream.offs[k], 128)
            for at in range(0, count, 384):
                cols = pl.ds(pl.multiple_of(first + at, 128), 384)
                inner = matmul_t(ins[0][...], stream.buffers[0][0, cols, :])
                g = g_ref[:, cols].astype(full)
                u = u_ref[:, cols].astype(full)
                sigma = jax.nn.sigmoid(g)
                active = g * sigma
                dg_ref[:, cols] = (inner * u * (sigma + active * (1.0 - sigma))).astype(low)
                du_ref[:, cols] = (inner * active).astype(low)

    flat = like((tokens, depth), low)
    return stream_call(
        "downback",
        stream,
        body,
        [grad],
        [whole(grad.shape)],
        [flat, flat],
        [whole((tokens, depth))] * 2,
        [],
        2 * tokens * depth * width,
    )


def back_matmul(name, grads, weights, tile, late, outs, finish):
    tokens = grads[0].shape[0]
    width = weights[0].height
    stream = Stream(weights, tile, late)

    def body(stream, ins, outs, scratch):
        (acc_ref,) = scratch
        step, tiles = stream.advance()
        part = matmul_t(ins[0][...], tiles[0][...])
        for value, w in zip(ins[1:], tiles[1:]):
            part = part + matmul_t(value[...], w[...])

        @pl.when(step == 0)
        def _():
            acc_ref[...] = part

        @pl.when(step > 0)
        def _():
            acc_ref[...] += part

        @pl.when(step == stream.steps - 1)
        def _():
            refs = stream.wait_late()
            for ref in outs:
                if ref.shape[0] == 1:
                    ref[...] = jnp.zeros_like(ref)
            by_rows(tokens, lambda rows: finish(rows, acc_ref[rows, :], refs, outs))

    return stream_call(
        name,
        stream,
        body,
        list(grads),
        [pl.BlockSpec((tokens, tile), lambda j: (0, j))] * len(grads),
        outs,
        [whole(value.shape) for value in outs],
        [pltpu.VMEM((tokens, width), full)],
        2 * tokens * width * weights[0].columns * len(weights),
    )


def mlp_back(grads, weights, grad2, hidden1, att, mods):
    tokens, width = grad2.shape
    lead = mods[0].shape[0]

    def finish(rows, db, refs, outs):
        dh2_ref, h1_ref, att_ref, scale_ref, gate_ref = refs
        hidden1 = h1_ref[rows, :]
        inverse = rms_scale(hidden1)
        normed = hidden1 * inverse
        weighted = db * (1.0 + take(scale_ref, rows))
        back = inverse * (weighted - normed * jnp.mean(normed * weighted, axis=-1, keepdims=True))
        grad1 = dh2_ref[rows, :] + back
        outs[0][rows, :] = grad1
        outs[1][rows, :] = (grad1 * take(gate_ref, rows)).astype(low)
        give(outs[2], rows, db)
        give(outs[3], rows, db * normed)
        give(outs[4], rows, grad1 * att_ref[rows, :].astype(full))

    outs = [like((tokens, width), full), like((tokens, width), low)]
    outs += [like((lead, width), low if lead > 1 else full)] * 3
    return back_matmul("mlpback", grads, weights, 1024, [grad2, hidden1, att] + mods, outs, finish)


def qkv_back(grad, weight, grad1, hidden0, scale):
    tokens, width = grad1.shape
    lead = scale.shape[0]

    def finish(rows, da, refs, outs):
        dh1_ref, h0_ref, scale_ref = refs
        hidden0 = h0_ref[rows, :]
        inverse = rms_scale(hidden0)
        normed = hidden0 * inverse
        weighted = da * (1.0 + take(scale_ref, rows))
        back = inverse * (weighted - normed * jnp.mean(normed * weighted, axis=-1, keepdims=True))
        outs[0][rows, :] = (dh1_ref[rows, :] + back).astype(low)
        give(outs[1], rows, da)
        give(outs[2], rows, da * normed)

    outs = [like((tokens, width), low)] + [like((lead, width), low if lead > 1 else full)] * 2
    return back_matmul("qkvback", [grad], [weight], width, [grad1, hidden0, scale], outs, finish)


def out_back(grad, weight):
    def finish(rows, value, refs, outs):
        outs[0][rows, :] = value.astype(low)

    return back_matmul("outback", [grad], [weight], 1152, [], [like(grad.shape, low)], finish)[0]


def ada_back(grads, weight, cond):
    tokens, width = cond.shape
    tile = weight.height
    stream = Stream([weight], tile, [cond])

    def body(stream, ins, outs, scratch):
        (acc_ref,) = scratch
        step, (w,) = stream.advance()
        for k, grad in enumerate(ins):

            @pl.when(step == k)
            def _():
                part = matmul_t(grad[...], w[...])
                acc_ref[...] = part if k == 0 else acc_ref[...] + part

        @pl.when(step == stream.steps - 1)
        def _():
            (cond_ref,) = stream.wait_late()

            def rows_of(rows):
                cond = cond_ref[rows, :]
                sigma = jax.nn.sigmoid(cond)
                outs[0][rows, :] = acc_ref[rows, :] * sigma * (1.0 + cond * (1.0 - sigma))

            by_rows(tokens, rows_of)

    return stream_call(
        "adaback",
        stream,
        body,
        list(grads),
        [whole(grad.shape) for grad in grads],
        [like((tokens, width), full)],
        [whole((tokens, width))],
        [pltpu.VMEM((tokens, width), full)],
        2 * tokens * width * weight.columns,
    )[0]


def ordered_grad(left, order, rights, tile):
    tokens, width = left.shape
    counts = [right.shape[1] // tile for right in rights]
    firsts = [sum(counts[:k]) for k in range(len(rights))]
    columns = sum(right.shape[1] for right in rights)

    def body(order_ref, left_ref, *refs):
        ys, out_ref, turned_ref = refs[: len(rights)], refs[-2], refs[-1]
        step = pl.program_id(0)

        @pl.when(step == 0)
        def _():
            turned_ref[...] = matmul_t(order_ref[...], left_ref[...]).astype(low)

        if len(rights) == 1:
            out_ref[...] = matmul(turned_ref[...], ys[0][...]).astype(low)
            return
        for y, first, count in zip(ys, firsts, counts):

            @pl.when(jnp.logical_and(step >= first, step < first + count))
            def _():
                out_ref[...] = matmul(turned_ref[...], y[...]).astype(low)

    def tile_of(first, count):
        return pl.BlockSpec((tokens, tile), lambda j: (0, jnp.clip(j - first, 0, count - 1)))

    return pl.pallas_call(
        body,
        grid=(columns // tile,),
        in_specs=[whole(order.shape), whole(left.shape)] + [tile_of(f, c) for f, c in zip(firsts, counts)],
        out_specs=pl.BlockSpec((width, tile), lambda j: (0, j)),
        out_shape=like((width, columns), low),
        scratch_shapes=[pltpu.VMEM((width, tokens), low)],
        compiler_params=params(60),
        cost_estimate=pl.CostEstimate(
            flops=2 * tokens * width * (columns + width), bytes_accessed=2 * width * (columns + 2 * width), transcendentals=0
        ),
        name="wgrad",
    )(order, left, *rights)


def down_grad(left, right, groups):
    tokens, depth = left.shape
    columns = right.shape[1]
    tile = depth // groups

    def body(left_ref, right_ref, out_ref):
        value = outer_sum(left_ref[...], right_ref[...]).astype(low)
        out_ref[0, 0] = value[: tile // 2]
        out_ref[1, 0] = value[tile // 2 :]

    return pl.pallas_call(
        body,
        grid=(groups,),
        in_specs=[pl.BlockSpec((tokens, tile), lambda j: (0, j)), whole(right.shape)],
        out_specs=pl.BlockSpec((2, 1, tile // 2, columns), lambda j: (0, j, 0, 0)),
        out_shape=like((2, groups, tile // 2, columns), low),
        compiler_params=params(40),
        cost_estimate=pl.CostEstimate(
            flops=2 * tokens * depth * columns, bytes_accessed=2 * depth * (columns + tokens), transcendentals=0
        ),
        name="wdown",
    )(left, right)


def tie(value, *others):
    others = [v for v in others if v is not None]
    if not others:
        return value
    return lax.optimization_barrier((value, *others))[0]


class Flight:
    def __init__(self, token):
        self.token = token
        self.held = []
        self.todo = []
        self.later = []

    def send(self, value, item, holder, name):
        setattr(holder, name, swap(tie(value, self.token), item))
        self.held.append((holder, name))

    def watch(self, holder, name):
        self.held.append((holder, name))

    def then(self, action):
        self.todo.append(action)

    def fence(self, values, starts=()):
        values = list(values)
        held, todo = self.held, self.todo
        self.held, self.todo = [], []
        held += [(holder, name) for left, holder, name in self.later if left == 0]
        self.later = [(left - 1, holder, name) for left, holder, name in self.later if left > 0]
        arrays = values + [getattr(holder, name) for holder, name in held]
        arrays = lax.optimization_barrier(tuple(arrays))
        self.token = arrays[0]
        for (holder, name), value in zip(held, arrays[len(values) :]):
            setattr(holder, name, value)
        for action in todo:
            action()
        for start in starts:
            start(self)
        return arrays[: len(values)]


class Bundle:
    def __init__(self, place, own, shards, parts, which, relay_bit):
        self.row, self.col, coords = place
        self.own = own
        self.shards = shards
        self.parts = parts
        self.which = which
        self.relay_bit = relay_bit
        self.rows = shards[parts[0][0]].shape[1]
        self.half = self.rows // 2
        self.at = coords[relay_bit] * self.half

    def prepare(self, flight):
        at = tie(self.at, flight.token)
        mine = [
            lax.dynamic_slice(self.shards[name], (self.which, at, first), (1, self.half, n))[0]
            for name, first, n in self.parts
        ]
        self.mine = jnp.concatenate(mine, axis=1)
        flight.watch(self, "mine")

    def over_col(self, flight):
        flight.send(self.mine, "col", self, "first")

    def relay(self, flight):
        flight.send(self.first, self.relay_bit, self, "second")

    def first_row(self, flight):
        flight.send(self.first, "row", self, "first_s")

    def second_row(self, flight):
        flight.send(self.second, "row", self, "second_s")

    def rows_both(self, flight):
        self.first_row(flight)
        self.second_row(flight)

    def segment(self, wanted):
        row, col, rows, half, at = self.row, self.col, self.rows, self.half, self.at
        other = (2 * row + 1 - col) * rows
        other_s = (2 * (1 - row) + 1 - col) * rows
        offsets = [col * rows, (col + 2) * rows, other + at, other_s + at]
        offsets += [other + (half - at), other_s + (half - at)]
        offsets = jnp.stack(offsets).astype(jnp.int32)
        begin = 0
        for name, first, n in self.parts:
            if name == wanted:
                own_all = self.own[name]
                lead = () if own_all.ndim == 3 else (self.which,)
                pieces = [(own_all, (0,) + lead, first, rows), (own_all, (1,) + lead, first, rows)]
                got = [self.first, self.first_s, self.second, self.second_s]
                pieces += [(value, (), begin, half) for value in got]
                return (offsets, pieces, n)
            begin += n
        raise KeyError(wanted)


def weight_of(name, *bundles):
    return Weight([bundle.segment(name) for bundle in bundles])


def item_weight(item):
    return {"row": 2, "col": 1}.get(item) or 4 << item


def halving_order(path, width, block, me, bits):
    at = jnp.arange(width)
    position = at // block
    owner = me
    for item in reversed(path):
        if item == "hi":
            mask = (1 << (bits - 1)) - 1
            owner = (owner & 7) | ((position & mask) << 3)
            position = position >> (bits - 1)
            continue
        bit = position & 1
        position = position >> 1
        if item == "row":
            owner = (owner & ~2) | (2 * bit)
        else:
            owner = owner ^ (bit * item_weight(item))
    return owner * block + at % block


class Slice:
    def __init__(self, held, columns, name="value"):
        self.held = held
        self.columns = columns
        self.name = name

    def get(self):
        return getattr(self.held, self.name)[..., self.columns]


class Term:
    def __init__(self, terms, at):
        self.terms = terms
        self.at = at

    @property
    def value(self):
        return self.terms[self.at][0]

    @value.setter
    def value(self, value):
        self.terms[self.at] = (value, self.terms[self.at][1])


class Share:
    def __init__(self, value, order, path):
        self.terms = [(value, list(order))]
        self.order = list(order)
        self.path = list(path)
        self.done = []
        self.result = None
        self.columns = None

    def pick(self, value, order, choice):
        order = list(order)
        while order and any(item in choice for item in order[:2]):
            rows, columns = value.shape
            if order[0] in choice:
                at = choice[order.pop(0)] * (rows // 2)
                value = value[at : at + rows // 2]
            else:
                at = choice[order.pop(1)]
                value = value.reshape(2, 2, rows // 4, columns)[:, at].reshape(rows // 2, columns)
        return value

    def collect(self, last=None):
        choice = {item: 0 for item in self.done}
        if last is not None:
            choice[last] = 1
        total = None
        for value, order in self.terms:
            value = value.get() if isinstance(value, Slice) else value
            part = self.pick(value, order, choice).astype(full)
            total = part if total is None else total + part
        return total

    def send(self, item):
        away = self.collect(item).astype(low)
        self.done.append(item)
        self.order = [other for other in self.order if other != item]
        return away

    def arrive(self, got):
        self.terms.append((got, self.order))

    @property
    def value(self):
        return self.collect() if self.result is None else self.result.get().astype(full)

    def hold(self, flight):
        if self.result is not None:
            flight.watch(self.result.held, self.result.name)
            return
        for at, (value, _) in enumerate(self.terms):
            if isinstance(value, Slice):
                flight.watch(value.held, value.name)
            else:
                flight.watch(Term(self.terms, at), "value")

    @property
    def base(self):
        return self.terms[0][0]

    @base.setter
    def base(self, value):
        self.terms[0] = (value, self.terms[0][1])


class BlockShare(Share):
    def __init__(self, value, order, path, coords):
        super().__init__(value, order, path)
        self.coords = coords

    def pick(self, value, order, choice):
        starts = [jnp.bitwise_xor(self.coords[item], choice[item]) if item in choice else 0 for item in order] + [0, 0]
        sizes = [1 if item in choice else 2 for item in order] + list(value.shape[-2:])
        if self.columns is not None and value.shape[-1] != self.columns[1]:
            starts[-1], sizes[-1] = self.columns
        value = lax.dynamic_slice(value, starts, sizes)
        return value.reshape([size for size in sizes[:-2] if size > 1] + list(sizes[-2:]))


class Total:
    def __init__(self, value, path):
        self.value = value
        self.path = list(path)

    def send(self, item):
        return self.value.astype(low)

    def arrive(self, got):
        self.value = self.value + got.astype(full)


class TotalAndRows(Total):
    def __init__(self, value, count, path):
        super().__init__(value, path)
        self.count = count

    def arrive(self, got):
        n = self.count
        value = self.value
        got = got.astype(full)
        self.value = jnp.concatenate([value[:n] + got[:n], value[n:], got[n:]], axis=0)


class Parcel:
    got = None


def last_share(value, bits):
    groups = [[2 * k + low_bit for k in range(1 << (bits - 1))] for low_bit in (0, 1)]
    return lax.psum_scatter(value, "dp", scatter_dimension=0, axis_index_groups=groups, tiled=False)


class Agenda:
    def __init__(self):
        self.tasks = {}
        self.packed = {}

    def scatter(self, bits, windows, *names):
        def action(flight):
            if names not in self.packed:
                self.pack(bits, *names)(flight)
            parcel, widths = self.packed[names]
            parcel.got = last_share(tie(parcel.got, flight.token), bits)
            flight.later.append((windows, parcel, "got"))
            at = 0
            for name, n in zip(names, widths):
                task = self.tasks[name]
                assert task.path.pop(0) == "hi"
                task.result = Slice(parcel, slice(at, at + n), "got")
                at += n

        return action

    def pack(self, bits, *names):
        def action(flight):
            tasks = [self.tasks[name] for name in names]
            parts = [task.collect().astype(low) for task in tasks]
            height = 1 << (bits - 1)
            block = parts[0].shape[-2] if isinstance(tasks[0], BlockShare) else parts[0].shape[0] // height
            value = parts[0] if len(parts) == 1 else jnp.concatenate(parts, axis=-1)
            parcel = Parcel()
            parcel.got = value.reshape(height, block, value.shape[-1])
            flight.watch(parcel, "got")
            self.packed[names] = (parcel, [part.shape[-1] for part in parts])

        return action

    def go(self, *names):
        def action(flight):
            tasks = [self.tasks[name] for name in names]
            items = [task.path.pop(0) for task in tasks]
            assert len(set(items)) == 1
            sent = [task.send(items[0]) for task in tasks]
            parcel = Parcel()
            away = sent[0] if len(sent) == 1 else jnp.concatenate(sent, axis=-1)
            flight.send(away, items[0], parcel, "got")

            def arrive():
                at = 0
                for task, value in zip(tasks, sent):
                    n = value.shape[-1]
                    task.arrive(parcel.got if len(tasks) == 1 else parcel.got[..., at : at + n])
                    at += n

            flight.then(arrive)

        return action


def row_sum(value):
    return lax.psum_scatter(value, "row", scatter_dimension=0, tiled=True)


def grad_blocks(left, right, bits, block):
    if (4 * block) % 128 == 0:
        value = down_grad(left, right, 2**bits)
    else:
        value = outer_sum(left, right).astype(low).reshape(2**bits, 2, 2 * block, right.shape[1])
        value = jnp.swapaxes(value, 0, 1)
    return value.reshape((2,) * (bits + 2) + (block, right.shape[1]))


def block_forward(hidden0, mods, mats, gains, tabs, flight, points):
    shift1, scale1, gate1, shift2, scale2, gate2 = mods
    cosine, sine, member, member_t, head = tabs
    used = {}

    def mat(name):
        used[name] = mats[name]()
        return used[name]

    def fence(point, *values):
        if point not in points:
            return values if len(values) > 1 else values[0]
        values = flight.fence(values, points[point])
        return values if len(values) > 1 else values[0]

    attn_in = (hidden0 * rms_scale(hidden0) * (1.0 + plain(scale1)) + plain(shift1)).astype(low)
    attn_in = fence("qkv", attn_in)
    query, kv, raw = qkv_matmul(attn_in, mat("qkv"), cosine, sine, gains[0], member, member_t, head)
    query, kv = fence("attend", query, kv)
    kv_r = swap(kv, "row")
    out_b, lse = attend(query, kv, kv_r, head)
    out_b = fence("out", out_b)
    att, hidden1, mlp_in = out_matmul(out_b, mat("out"), hidden0, [gate1, shift2, scale2])
    mlp_in = fence("gate", mlp_in)
    inner, gate_pre, up_pre = gate_up_matmul(mlp_in, mat("gate"), mat("up"))
    inner = fence("down", inner)
    mlp_out, hidden2 = down_matmul(inner, mat("down"), hidden1, gate2)
    cache = (hidden0, attn_in, raw, query, kv, kv_r, out_b, lse, att)
    cache += (hidden1, mlp_in, gate_pre, up_pre, inner, mlp_out)
    used = tuple(used[name] for name in ("qkv", "out", "gate", "up", "down"))
    return hidden2, cache, used


class Sum:
    value = None


def block_backward(grad2, cache, mods, mats, gains, tabs, comm, tag, plan):
    (hidden0, attn_in, raw, query, kv, kv_r, out_b, lse, att) = cache[:9]
    (hidden1, mlp_in, gate_pre, up_pre, inner, mlp_out) = cache[9:]
    shift1, scale1, gate1, shift2, scale2, gate2 = mods
    qkv_w, out_w, gate_w, up_w, down_w = mats
    cosine, sine, member, member_t, head = tabs
    flight, agenda, orders, paths, coords = comm
    n_data = lax.axis_size("dp")
    bits = (n_data - 1).bit_length()
    block = down_w.height // (4 * n_data)
    width = hidden0.shape[1]

    def fence(point, *values):
        values = flight.fence(values, plan.get(point, ()))
        return values if len(values) > 1 else values[0]

    def grad_of(left, name, rights, tile):
        return ordered_grad(left, orders[name], rights, tile)

    def watch(name, task):
        agenda.tasks[name + tag] = task
        flight.watch(task, "base")

    def begin(name, value):
        order = paths[name][1:]
        watch(name[0], Share(value, order, [order[1], order[0]] + order[2:]))

    def begin_halves(name, value, cut):
        path = paths[name][1:]
        other = [path[1], path[0]] + path[2:]
        held = Sum()
        held.value = value
        flight.watch(held, "value")
        agenda.tasks[name[0] + "a" + tag] = Share(Slice(held, slice(0, cut)), path, path)
        agenda.tasks[name[0] + "b" + tag] = Share(Slice(held, slice(cut, None)), path, other)

    def begin_down(value):
        order = ["row"] + list(reversed(range(bits))) + ["col"]
        watch("d", BlockShare(value, order, ["row"], coords))

    grad_mlp = (grad2 * plain(gate2)).astype(low)
    dgate2 = grad2 * mlp_out.astype(full)
    if gate2.shape[0] == 1:
        dgate2 = jnp.sum(dgate2, axis=0, keepdims=True)
    begin_down(grad_blocks(inner, grad_mlp, bits, block))
    grad2, grad_mlp = fence("start", grad2, grad_mlp)
    grad_gate, grad_up = down_back(grad_mlp, down_w, gate_pre, up_pre)
    w_gate = grad_of(mlp_in, "gate", [grad_gate, grad_up], 1024)
    grad_gate, grad_up, w_gate = fence("gate", grad_gate, grad_up, w_gate)
    r_gate = row_sum(w_gate)
    grad1, grad_att, dshift2, dscale2, dgate1 = mlp_back(
        [grad_gate, grad_up], [gate_w, up_w], grad2, hidden1, att, [scale2, gate1]
    )
    grad_att = fence("out", grad_att)
    w_out = grad_of(out_b, "out", [grad_att], 384)
    grad_ob = out_back(grad_att, out_w)
    begin_halves("gate", r_gate, grad_gate.shape[1])
    grad_ob, w_out = fence("attend", grad_ob, w_out)
    r_out = row_sum(w_out)
    dq, dkv, dkv_r = attend_back(query, kv, kv_r, grad_ob, out_b, lse, head)
    begin("out", r_out)
    dq, dkv_r = fence("qk", dq, dkv_r)
    grad_qkv, gain_rows = qk_back(dq, dkv, swap(dkv_r, "row"), raw, cosine, sine, gains[1], member, member_t, head)
    w_qkv = grad_of(attn_in, "qkv", [grad_qkv], width)
    grad_qkv, w_qkv = fence("qkv", grad_qkv, w_qkv)
    r_qkv = row_sum(w_qkv)
    grad0, dshift1, dscale1 = qkv_back(grad_qkv, qkv_w, grad1, hidden0, scale1)
    dmods = [dshift1, dscale1, dgate1, dshift2, dscale2, dgate2]
    begin_halves("qkv", r_qkv, r_qkv.shape[1] // 256 * 128)
    return grad0, dmods, gain_rows[:2], begin_halves


def per_device(
    latents,
    levels,
    timesteps,
    patch_weight,
    patch_bias,
    ada_weight,
    ada_bias,
    qkv_weight,
    qk_gains,
    out_weight,
    gate_weight,
    up_weight,
    down_weight,
    cotangent,
):
    images, slots, chans, rows_loc, cols_loc = latents.shape
    n_data = lax.axis_size("dp")
    assert images == 1 and slots == 2
    assert lax.axis_size("row") == 2 and lax.axis_size("col") == 2
    row = lax.axis_index("row")
    col = lax.axis_index("col")
    data = lax.axis_index("dp")
    bits = (n_data - 1).bit_length()
    left = col == 0
    coords = {"row": row, "col": col}
    place = (row, col, coords)
    for k in range(bits):
        coords[k] = (data >> k) & 1
    grid_rows = rows_loc // 2
    grid_cols = cols_loc
    half_cols = grid_cols // 2
    tokens = grid_rows * grid_cols
    width = cotangent.shape[-1]
    head = qk_gains.shape[2]
    heads = width // head
    pvals = chans * 4
    shard = width // 4
    me = data * 4 + row * 2 + col
    own_rows = width // (4 * n_data)

    def pair(own, other, axis):
        return jnp.concatenate([jnp.where(left, own, other), jnp.where(left, other, own)], axis=axis)

    own = {}
    for name, s in (
        ("qkv", qkv_weight),
        ("out", out_weight),
        ("gate", gate_weight),
        ("up", up_weight),
        ("down", down_weight),
        ("ada", ada_weight),
    ):
        own[name] = lax.all_gather(s, "row", axis=0)
    shards = {"qkv": qkv_weight, "out": out_weight, "gate": gate_weight, "up": up_weight, "down": down_weight}
    shards["ada"] = ada_weight

    def bundle(which, relay_bit, *parts):
        return Bundle(place, own, shards, parts, which, relay_bit)

    ff = gate_weight.shape[2]
    b_q0 = bundle(0, 0, ("qkv", 0, width))
    b_kv0 = bundle(0, 1, ("qkv", width, 2 * width))
    b_out0 = bundle(0, 0, ("out", 0, width))
    b_gate0 = bundle(0, 0, ("gate", 0, ff))
    b_up0 = bundle(0, 1, ("up", 0, ff))
    b_down0 = bundle(0, 0, ("down", 0, width))
    b_ada_a = bundle(1, 1, ("ada", 0, 3 * width))
    b_ada_b = bundle(1, 0, ("ada", 3 * width, 3 * width))
    b_qkv1 = bundle(1, 1, ("qkv", 0, 3 * width))
    b_og1 = bundle(1, 0, ("out", 0, width), ("gate", 0, ff))
    b_up1 = bundle(1, 1, ("up", 0, ff))
    b_down1 = bundle(1, 0, ("down", 0, width))
    enc_mats = {
        "qkv": lambda: weight_of("qkv", b_q0, b_kv0),
        "out": lambda: weight_of("out", b_out0),
        "gate": lambda: weight_of("gate", b_gate0),
        "up": lambda: weight_of("up", b_up0),
        "down": lambda: weight_of("down", b_down0),
    }
    dec_mats = {
        "qkv": lambda: weight_of("qkv", b_qkv1),
        "out": lambda: weight_of("out", b_og1),
        "gate": lambda: weight_of("gate", b_og1),
        "up": lambda: weight_of("up", b_up1),
        "down": lambda: weight_of("down", b_down1),
    }

    small = jnp.concatenate(
        [jnp.swapaxes(patch_weight, 1, 2).reshape(2 * pvals, shard), patch_bias, ada_bias.reshape(12, shard)], axis=0
    )
    small_other = swap(small, "col")
    blk = latents[0]
    blk_other = swap(blk, "col")
    flight = Flight(small)

    class Start:
        pass

    Start.small, Start.blk = small_other, blk_other
    flight.watch(Start, "small")
    flight.watch(Start, "blk")
    (blk,) = flight.fence([blk], [b_q0.prepare, b_kv0.prepare])
    small = pair(small[None], Start.small[None], 0)
    wide = pair(blk, Start.blk, 3)
    flight.send(small, "row", Start, "small")
    flight.send(wide[:, :, rows_loc - 1 :], "row", Start, "top")
    small, wide = flight.fence([small, wide], [b_q0.over_col, b_kv0.over_col, b_out0.prepare])
    temb = time_features(tie(timesteps, wide)[0], width)
    small = jnp.where(row == 0, jnp.stack([small, Start.small]), jnp.stack([Start.small, small]))
    small = small.reshape(4, 2 * pvals + 14, shard)
    patch_w = small[:, : 2 * pvals].transpose(1, 0, 2).reshape(2, pvals, width)
    patch_b = small[:, 2 * pvals : 2 * pvals + 2].transpose(1, 0, 2).reshape(2, width).astype(full)
    ada_b = small[:, 2 * pvals + 2 :].reshape(4, 2, 6 * shard).transpose(1, 0, 2).reshape(2, 6, width).astype(full)

    framed = jnp.concatenate([Start.top, wide[:, :, : rows_loc - 1]], axis=2)
    framed = jnp.concatenate([framed[..., -1:], framed[..., :-1]], axis=3)
    patches = (
        framed.reshape(slots, chans, grid_rows, 2, grid_cols, 2).transpose(0, 2, 4, 1, 3, 5).reshape(slots, tokens, pvals)
    )
    enc_patches = patches[0]
    dec_patches = jnp.where(left, patches[0], patches[1])

    sil0 = jax.nn.silu(temb[:1]).astype(low)
    temb_own = jnp.where(left, temb[:1], temb[1:])
    part = mod_partial(lax.dynamic_slice(sil0, (0, (2 * row + col) * shard), (1, shard)), ada_weight, width)

    cot_own = jnp.where(left, cotangent[0, 0], cotangent[0, 1])

    class Cotangent:
        got = None

    def send_cotangent(flight):
        flight.send(jnp.where(left, cotangent[0, 1], cotangent[0, 0]), "col", Cotangent, "got")

    quarter = head // 4
    lanes = tie(jnp.arange(width), flight.token)
    within = lanes % head
    section = within // quarter
    lane_freq = jnp.exp(-math.log(10000.0) * (within % quarter).astype(full) / quarter)
    row_pos = (row * grid_rows + jnp.arange(grid_rows)).astype(full)
    col_pos = jnp.arange(grid_cols).astype(full)
    row_angle = row_pos[:, None] * lane_freq[None, :]
    col_angle = col_pos[:, None] * lane_freq[None, :]
    by_row = section < 2
    sign = jnp.where(section % 2 == 0, -1.0, 1.0).astype(full)

    def table(fun):
        return jnp.where(by_row, fun(row_angle)[:, None, :], fun(col_angle)[None, :, :]).reshape(tokens, width)

    cosine = table(jnp.cos)
    sine = table(jnp.sin) * sign
    member = (lanes[:, None] // head == jnp.arange(128)[None, :]).astype(low)
    tabs = (cosine, sine, member, member.T, head)
    gain_rows = jnp.tile(qk_gains.astype(full), (1, 1, heads))
    even = jnp.broadcast_to((section % 2 == 0).astype(full), (2, 1, width))
    temper = head ** (-0.5) * math.log2(math.e)
    scaled = jnp.concatenate([gain_rows[:, :1] * temper, gain_rows[:, 1:], even], axis=1)
    gain_rows = jnp.concatenate([gain_rows, even], axis=1)
    gain_rows = [(scaled[k], gain_rows[k]) for k in range(2)]

    rest = list(range(2, bits))
    path_y = ["row", "col", 0, "hi"]
    path_s = ["row", "col", 0, 1] + rest
    paths = {"gate": path_y, "out": path_y, "qkv": path_y, "ada": path_s}
    perm = {}
    orders = {}
    for name in paths:
        key = tuple(paths[name])
        if key not in perm:
            source = halving_order(paths[name], width, own_rows, me, bits)
            perm[key] = lax.optimization_barrier((source[:, None] == lanes[None, :]).astype(low))
        orders[name] = perm[key]

    enc_h0 = matmul(enc_patches, patch_w[0]) + patch_b[0]
    starts = [b_q0.relay, b_kv0.relay, b_out0.over_col, b_q0.first_row, b_kv0.first_row, b_gate0.prepare]
    enc_h0, part, cosine, sine = flight.fence([enc_h0, part, cosine, sine], starts)
    part = part + swap(part, "row")
    part = part + swap(part, "col")
    enc_mod = part + ada_b[0]
    enc_mods = [enc_mod[k : k + 1] for k in range(6)]
    tabs = (cosine, sine) + tabs[2:]
    points = {
        "qkv": [b_q0.second_row, b_kv0.second_row, b_gate0.over_col, b_out0.relay, b_up0.prepare],
        "attend": [b_up0.over_col, b_gate0.relay, b_out0.first_row, b_down0.prepare],
        "out": [b_out0.second_row, b_up0.relay, b_down0.over_col, b_gate0.rows_both, b_ada_a.prepare],
        "gate": [b_up0.rows_both, b_ada_a.over_col, b_down0.relay, b_qkv1.prepare],
        "down": [b_down0.rows_both, b_qkv1.over_col, b_ada_a.relay, b_ada_b.prepare],
    }
    encoded, enc_cache, enc_mats = block_forward(enc_h0, enc_mods, enc_mats, gain_rows[0], tabs, flight, points)
    dec_h0 = matmul(dec_patches, patch_w[1]) + patch_b[1]
    cond = encoded + temb_own
    dec_sil = jax.nn.silu(cond).astype(low)
    starts = [b_ada_a.rows_both, b_ada_b.over_col, b_qkv1.relay, b_og1.prepare]
    keys = list(perm)
    dec_sil, *made = flight.fence([dec_sil] + [perm[key] for key in keys], starts)
    perm = dict(zip(keys, made))
    orders = {name: perm[tuple(paths[name])] for name in orders}
    ada_bias1 = ada_b[1].reshape(1, 6 * width)
    mod_a = ada_matmul(dec_sil, weight_of("ada", b_ada_a), ada_bias1[:, : 3 * width])
    dec_mods = [Cols(mod_a, k * width, width) for k in range(3)]
    held = Sum()

    def second_mods(flight):
        held.value = ada_matmul(tie(dec_sil, flight.token), weight_of("ada", b_ada_b), ada_bias1[:, 3 * width :])
        flight.watch(held, "value")

    dec_mods += [Cols(held, k * width, width) for k in range(3)]
    points = {
        "qkv": [b_qkv1.rows_both, b_og1.over_col, b_ada_b.relay, b_up1.prepare],
        "attend": [b_ada_b.rows_both, second_mods, b_up1.over_col, b_og1.relay, b_down1.prepare],
        "out": [b_og1.rows_both, b_down1.over_col, b_up1.relay],
        "gate": [b_up1.rows_both, b_down1.relay, send_cotangent],
        "down": [b_down1.rows_both],
    }
    decoded, dec_cache, dec_mats = block_forward(dec_h0, dec_mods, dec_mats, gain_rows[1], tabs, flight, points)
    live = (col < levels[0]).astype(full)
    result = (decoded * live).astype(low).reshape(grid_rows, grid_cols, width)
    near = jnp.where(left, result[:, :half_cols], result[:, half_cols:])
    far = jnp.where(left, result[:, half_cols:], result[:, :half_cols])

    class Away:
        got = None

    def send_result(flight):
        flight.send(far, "col", Away, "got")


    agenda = Agenda()
    go = agenda.go
    scatter = functools.partial(agenda.scatter, bits)
    comm = (flight, agenda, orders, paths, coords)
    cot = pair(cot_own, Cotangent.got, 1).reshape(tokens, width)
    dec_grad2 = cot.astype(full) * live

    def split_down(tag, way_a, way_b, flight):
        whole_sum = agenda.tasks["d" + tag]
        cut = width // 256 * 128
        for name, columns, way in (("da" + tag, (0, cut), way_a), ("db" + tag, (cut, width - cut), way_b)):
            part = BlockShare(None, whole_sum.order, way, coords)
            part.terms = list(whole_sum.terms)
            part.done = list(whole_sum.done)
            part.columns = columns
            agenda.tasks[name] = part

    plan = {
        "start": [send_result, go("d1")],
        "gate": [functools.partial(split_down, "1", ["col", 0, "hi"], [0, "col", "hi"]), go("da1"), go("db1")],
        "out": [go("da1"), go("db1")],
        "attend": [go("ga1"), go("gb1"), scatter(1, "da1", "db1")],
        "qk": [go("ga1"), go("gb1")],
        "qkv": [go("o1")],
    }
    dec_grad0, dec_dmods, dec_gains, begin_halves = block_backward(
        dec_grad2, dec_cache, dec_mods, dec_mats, gain_rows[1], tabs, comm, "1", plan
    )
    away = Away.got
    result = jnp.stack([jnp.where(left, near, away), jnp.where(left, away, near)])[None]
    dec_dmods = [piece.astype(low) for piece in dec_dmods]
    w_ada = ordered_grad(dec_sil, orders["ada"], dec_dmods, width)
    starts = [go("qa1"), go("qb1"), go("o1")]
    w_ada, *dec_dmods = flight.fence([w_ada] + dec_dmods, starts)
    r_ada = row_sum(w_ada)
    dec_bada = jnp.stack([jnp.sum(piece.astype(full), axis=0) for piece in dec_dmods])
    enc_grad2 = ada_back(dec_dmods, weight_of("ada", b_ada_a, b_ada_b), cond)

    def patch_rows(patch, grad):
        ones = jnp.ones((tokens, 1), low)
        return outer_sum(jnp.concatenate([patch, ones], axis=1), grad)

    total = jnp.concatenate([patch_rows(dec_patches, dec_grad0), dec_bada, dec_gains], axis=0)
    agenda.tasks["s"] = Total(total, ["row", "col"] + list(range(bits)))

    begin_halves("ada", r_ada, r_ada.shape[1] // 2)
    plan = {
        "start": [go("s"), go("d0"), go("aa1"), go("ab1"), scatter(0, "ga1", "gb1")],
        "gate": [
            functools.partial(split_down, "0", [1, "col", 0] + rest, [1, 0, "col"] + rest),
            go("aa1"),
            go("ab1"),
            go("qa1"),
            go("qb1"),
            go("da0"),
        ],
        "out": [go("s"), go("db0")],
        "attend": [go("s"), go("ga0"), go("gb0"), go("aa1", "ab1")],
        "qk": [go("ga0"), go("gb0"), go("da0"), go("db0"), scatter(0, "qa1", "qb1", "o1")],
        "qkv": [go("s"), go("o0"), go("da0"), go("db0"), go("aa1", "ab1")],
    }
    enc_grad0, enc_dmods, enc_gains, _ = block_backward(
        enc_grad2, enc_cache, enc_mods, enc_mats, gain_rows[0], tabs, comm, "0", plan
    )
    dmod_enc = jnp.concatenate(enc_dmods, axis=0)
    total = jnp.concatenate([patch_rows(enc_patches, enc_grad0), enc_gains, dmod_enc], axis=0)
    def image(dpatch):
        return (
            dpatch.reshape(grid_rows, grid_cols, chans, 2, 2).transpose(2, 0, 3, 1, 4).reshape(chans, rows_loc, 2 * cols_loc)
        )

    enc_image = image(matmul_t(enc_grad0, patch_w[0]))
    dec_image = image(matmul_t(dec_grad0, patch_w[1]))
    zero = jnp.zeros_like(dec_image)
    grads = jnp.stack([enc_image + jnp.where(left, dec_image, zero), jnp.where(left, zero, dec_image)])
    grads = jnp.concatenate([grads[..., 1:], grads[..., :1]], axis=3)

    class Last:
        pass

    total, grads = flight.fence([total, grads])
    flight.send(total, "row", Last, "total")
    flight.send(grads[:, :, :1], "row", Last, "below")
    total, grads = flight.fence([total, grads], [go("qa0"), go("qb0"), scatter(1, "ga0", "gb0")])
    total = total + Last.total
    flight.send(total, "col", Last, "total")
    grads = jnp.concatenate([grads[:, :, 1:], Last.below], axis=2)
    one = grads[..., :cols_loc]
    two = grads[..., cols_loc:]
    flight.send(jnp.where(left, two, one), "col", Last, "image")
    count = pvals + 3
    tiny = TotalAndRows(None, count, list(range(bits)))
    agenda.tasks["t"] = tiny

    def begin_tiny(flight):
        tiny.value = jnp.concatenate([total + Last.total, sil0.astype(full)], axis=0)
        go("t")(flight)

    flight.fence([total], [begin_tiny, go("qa0"), go("qb0"), go("o0"), go("s")])
    latent_grad = (jnp.where(left, one, two) + Last.image)[None]
    flight.fence([total], [scatter(1, "qa0", "qb0", "o0"), go("t"), go("da0", "db0")])
    flight.fence([total], [go("t")])
    flight.fence([total])
    while any(task.path for task in agenda.tasks.values()):
        flight.fence([total], [go(name) for name, task in agenda.tasks.items() if task.path])
        flight.fence([total])
    dec_small = agenda.tasks["s"].value
    total = tiny.value[:count]
    dmod_all = tiny.value[count:]
    dmod_all = dmod_all.reshape(n_data, 7, width)
    enc_small = total
    enc_ada = jnp.dot(
        lax.dynamic_slice(dmod_all, (0, 6, me * own_rows), (n_data, 1, own_rows))[:, 0].T,
        dmod_all[:, :6].reshape(n_data, 6 * width),
        precision=highest,
        preferred_element_type=full,
    )
    enc_bada = jnp.sum(dmod_all[:, :6], axis=0)

    def own_lanes(value):
        return lax.dynamic_slice(value, (0, me * own_rows), (value.shape[0], own_rows))

    enc_patch = own_lanes(enc_small[: pvals + 1])
    dec_patch = own_lanes(dec_small[: pvals + 1])
    g_patch = jnp.stack([enc_patch[:pvals].T, dec_patch[:pvals].T])
    g_patch_b = jnp.stack([enc_patch[pvals], dec_patch[pvals]])
    bada = jnp.stack([enc_bada.reshape(-1), dec_small[pvals + 1 : pvals + 7].reshape(-1)])
    own_bada = 6 * own_rows
    g_bada = lax.dynamic_slice(bada, (0, me * own_bada), (2, own_bada))
    gains = jnp.stack([enc_small[pvals + 1 :], dec_small[pvals + 7 :]])
    gains = gains.reshape(2, 2, heads, head).sum(axis=2)
    def both(name):
        parts = [agenda.tasks[name + tag].value.astype(full) for tag in "01"]
        return jnp.stack(parts)

    for task in agenda.tasks.values():
        assert not task.path
    g_ada = jnp.concatenate([agenda.tasks["aa1"].value, agenda.tasks["ab1"].value], axis=1)
    g_ada_all = jnp.stack([enc_ada, g_ada.astype(full)])
    g_qkv = jnp.concatenate([both("qa"), both("qb")], axis=2)
    g_down = jnp.concatenate([both("da"), both("db")], axis=2)
    stacked = [g_qkv, both("o"), both("ga"), both("gb"), g_down]
    return (
        result,
        latent_grad,
        g_patch,
        g_patch_b,
        g_ada_all,
        g_bada,
        stacked[0],
        gains,
        stacked[1],
        stacked[2],
        stacked[3],
        stacked[4],
    )


def solution(mesh):
    tile = ("row", "col")
    every = ("dp", "row", "col")
    return jax.shard_map(
        per_device,
        mesh=mesh,
        in_specs=(
            P("dp", None, None, "row", "col"),
            P("dp"),
            P("dp", None),
            P(None, tile, None),
            P(None, tile),
            P(None, tile, None),
            P(None, tile),
            P(None, tile, None),
            P(),
            P(None, tile, None),
            P(None, tile, None),
            P(None, tile, None),
            P(None, tile, None),
            P("dp", None, "row", "col", None),
        ),
        out_specs=(
            P("dp", None, "row", "col", None),
            P("dp", None, None, "row", "col"),
            P(None, every, None),
            P(None, every),
            P(None, every, None),
            P(None, every),
            P(None, every, None),
            P(),
            P(None, every, None),
            P(None, every, None),
            P(None, every, None),
            P(None, every, None),
        ),
        check_vma=False,
    )
```

```python
import functools
import math

import jax
import jax.numpy as jnp
from jax import lax
from jax.experimental import pallas as pl
from jax.experimental.pallas import tpu as pltpu
from jax.sharding import PartitionSpec as P

epsilon = 1e-06
highest = lax.Precision.HIGHEST
low = jnp.bfloat16
full = jnp.float32
WINDOW = 256
PAIR = 4
MIB = 1 << 20


def matmul(left, right):
    return jnp.dot(left, right, preferred_element_type=full)


def matmul_t(left, right):
    return lax.dot_general(left, right, (((1,), (1,)), ((), ())), preferred_element_type=full)


def outer_sum(left, right):
    return lax.dot_general(left, right, (((0,), (0,)), ((), ())), preferred_element_type=full)


def rms_scale(value):
    return lax.rsqrt(jnp.mean(value * value, axis=-1, keepdims=True) + epsilon)


def rms_back(value, inverse, grad):
    return inverse * grad - value * inverse**3 * jnp.mean(value * grad, axis=-1, keepdims=True)


def swap(value, item):
    if isinstance(item, str):
        return lax.ppermute(value, item, [(0, 1), (1, 0)])
    size = lax.axis_size("dp")
    return lax.ppermute(value, "dp", [(i, i ^ (1 << item)) for i in range(size)])


def time_features(steps, width):
    half = width // 2
    freqs = jnp.exp(-math.log(10000.0) * jnp.arange(half).astype(full) / half)
    angles = steps.astype(full)[:, None] * freqs[None, :]
    return jnp.concatenate([jnp.cos(angles), jnp.sin(angles)], axis=-1)


def whole(shape):
    return pl.BlockSpec(shape, lambda *_: (0,) * len(shape))


def params(mib):
    return pltpu.CompilerParams(vmem_limit_bytes=mib * MIB)


def head_mean(value, member, head):
    return matmul(value.astype(low), member) * (1.0 / head)


def split_dot(value, onehot):
    top = value.astype(low)
    rest = (value - top.astype(full)).astype(low)
    return matmul(top, onehot) + matmul(rest, onehot)


def turned(value, cosine, sine, even, quarter):
    width = value.shape[-1]
    ahead = pltpu.roll(value, width - quarter, axis=1)
    behind = pltpu.roll(value, quarter, axis=1)
    return value * cosine + jnp.where(even, ahead, behind) * sine


def even_lanes(gain_ref, shape):
    return jnp.broadcast_to(gain_ref[2:3, :] > 0.5, shape)


def qk_back_body(head, dq_ref, dkv_ref, dkvx_ref, qkv_ref, cos_ref, sin_ref, gain_ref, mem_ref, memt_ref, out_ref, gg_ref):
    width = dq_ref.shape[-1]

    @pl.when(pl.program_id(0) == 0)
    def _():
        gg_ref[...] = jnp.zeros_like(gg_ref)

    cosine = cos_ref[...]
    sine = -sin_ref[...]
    even = even_lanes(gain_ref, cosine.shape)
    member = mem_ref[...]
    member_t = memt_ref[...]
    grads = (dq_ref[...], dkv_ref[:, :width] + dkvx_ref[:, :width].astype(full))
    for part in (0, 1):
        value = qkv_ref[:, part * width : (part + 1) * width]
        mean = head_mean(value * value, member, head)
        inverse_h = lax.rsqrt(mean + epsilon)
        inverse = split_dot(inverse_h, member_t)
        grad_n = turned(grads[part], cosine, sine, even, head // 4)
        normed = value * inverse
        gg_ref[part : part + 1, :] += jnp.sum(grad_n * normed, axis=0, keepdims=True)
        weighted = grad_n * gain_ref[part : part + 1, :]
        dots = head_mean(value * weighted, member, head) * inverse_h * inverse_h
        back = inverse * weighted - normed * split_dot(dots, member_t)
        out_ref[:, part * width : (part + 1) * width] = back.astype(low)
    out_ref[:, 2 * width :] = (dkv_ref[:, width:] + dkvx_ref[:, width:].astype(full)).astype(low)


def qk_back(dq, dkv, dkvx, raw, cosine, sine, gains, member, member_t, head):
    tokens, width = dq.shape
    step = 256
    rows = lambda n: pl.BlockSpec((step, n), lambda i: (i, 0))
    return pl.pallas_call(
        functools.partial(qk_back_body, head),
        grid=(tokens // step,),
        in_specs=[rows(width)]
        + [rows(2 * width)] * 3
        + [rows(width), rows(width), whole(gains.shape), whole(member.shape), whole(member_t.shape)],
        out_specs=[rows(3 * width), whole((8, width))],
        out_shape=[jax.ShapeDtypeStruct((tokens, 3 * width), low), jax.ShapeDtypeStruct((8, width), full)],
        compiler_params=params(60),
        cost_estimate=pl.CostEstimate(flops=60 * raw.size, bytes_accessed=18 * raw.size, transcendentals=0),
        name="qk_back",
    )(dq, dkv, dkvx, raw, cosine, sine, gains, member, member_t)


def head_window(head, width, part):
    index = pl.program_id(0) * PAIR + part
    start = index * head
    base = jnp.minimum(lax.div(start, 128) * 128, width - WINDOW)
    return index, pl.multiple_of(base, 128), start - base


def window_mask(shape, offset, head):
    lane = lax.broadcasted_iota(jnp.int32, shape, 1)
    return jnp.logical_and(lane >= offset, lane < offset + head)


def attend_body(head, q_ref, kvl_ref, kvr_ref, o_ref, lse_ref, acc_ref):
    tokens, width = q_ref.shape

    @pl.when(pl.program_id(0) == 0)
    def _():
        acc_ref[...] = jnp.zeros_like(acc_ref)
        lse_ref[...] = jnp.zeros_like(lse_ref)

    step = 256
    one = jnp.ones((), low)
    lane = lax.broadcasted_iota(jnp.int32, (step, lse_ref.shape[1]), 1)
    for part in range(PAIR):
        index, base, offset = head_window(head, width, part)
        cols = pl.ds(base, WINDOW)
        vals = pl.ds(pl.multiple_of(width + base, 128), WINDOW)
        mask_k = window_mask((tokens, WINDOW), offset, head)
        value_l = jnp.where(mask_k, kvl_ref[:, vals], one)
        value_r = jnp.where(mask_k, kvr_ref[:, vals], one)
        mask = window_mask((step, WINDOW), offset, head)
        for first in range(0, tokens, step):
            rows = slice(first, first + step)
            query = jnp.where(mask, q_ref[rows, cols], jnp.zeros((), low))
            left = jnp.exp2(matmul_t(query, kvl_ref[:, cols])).astype(low)
            right = jnp.exp2(matmul_t(query, kvr_ref[:, cols])).astype(low)
            out = matmul(left, value_l) + matmul(right, value_r)
            total = jnp.max(jnp.where(mask, 0.0, out), axis=1, keepdims=True)
            acc_ref[rows, cols] += jnp.where(mask, out * (1.0 / total), 0.0)
            lse_ref[rows, :] += jnp.where(lane == index, jnp.log2(total), 0.0)

    @pl.when(pl.program_id(0) == pl.num_programs(0) - 1)
    def _():
        o_ref[...] = acc_ref[...].astype(low)


def attend(query, kv_l, kv_r, head):
    tokens, width = query.shape
    heads = width // head
    return pl.pallas_call(
        functools.partial(attend_body, head),
        grid=(heads // PAIR,),
        in_specs=[whole((tokens, width))] + [whole((tokens, 2 * width))] * 2,
        out_specs=[whole((tokens, width)), whole((tokens, 128))],
        out_shape=[jax.ShapeDtypeStruct((tokens, width), low), jax.ShapeDtypeStruct((tokens, 128), full)],
        scratch_shapes=[pltpu.VMEM((tokens, width), full)],
        compiler_params=params(56),
        cost_estimate=pl.CostEstimate(
            flops=8 * tokens * tokens * WINDOW * heads, bytes_accessed=14 * tokens * width, transcendentals=2 * tokens * tokens * heads
        ),
        name="attend",
    )(query, kv_l, kv_r)


def in_three(column):
    top = column.astype(low)
    rest = column - top.astype(full)
    middle = rest.astype(low)
    return top, middle, (rest - middle.astype(full)).astype(low)


def attend_back_body(head, q_ref, kvl_ref, kvr_ref, do_ref, o_ref, lse_ref, dq_ref, dl_ref, dr_ref, dr_acc):
    tokens, width = q_ref.shape
    temper = head ** (-0.5)

    @pl.when(pl.program_id(0) == 0)
    def _():
        for ref in (dq_ref, dl_ref, dr_acc):
            ref[...] = jnp.zeros_like(ref)

    shape = (tokens, WINDOW)
    lane = lax.broadcasted_iota(jnp.int32, shape, 1)
    small = lax.broadcasted_iota(jnp.int32, lse_ref.shape, 1)
    zero = jnp.zeros((), low)
    for part in range(PAIR):
        index, base, offset = head_window(head, width, part)
        cols = pl.ds(base, WINDOW)
        vals = pl.ds(pl.multiple_of(width + base, 128), WINDOW)
        mask = window_mask(shape, offset, head)
        spare = jnp.where(offset >= 3, 0, WINDOW - 3)
        minus = jnp.where(jnp.logical_and(lane >= spare, lane < spare + 3), -jnp.ones((), low), zero)
        query = jnp.where(mask, q_ref[:, cols], zero)
        grad = jnp.where(mask, do_ref[:, cols], zero)
        delta = jnp.sum(grad.astype(full) * o_ref[:, cols].astype(full), axis=1, keepdims=True)
        level = jnp.sum(jnp.where(small == index, lse_ref[...], 0.0), axis=1, keepdims=True)
        query_x = query
        grad_x = grad
        for k, (a, b) in enumerate(zip(in_three(level), in_three(delta))):
            at = lane == spare + k
            query_x = jnp.where(at, a, query_x)
            grad_x = jnp.where(at, b, grad_x)
        grad_q = 0.0
        for ref, acc in ((kvl_ref, dl_ref), (kvr_ref, dr_acc)):
            key = jnp.where(mask, ref[:, cols], minus)
            value = jnp.where(mask, ref[:, vals], minus)
            prob = jnp.exp2(matmul_t(key, query_x))
            grad_s = (prob * matmul_t(value, grad_x)).astype(low)
            acc[:, vals] += matmul(prob.astype(low), grad)
            acc[:, cols] += matmul(grad_s, query)
            grad_q = grad_q + outer_sum(grad_s, key)
        dq_ref[:, cols] += jnp.where(mask, grad_q * temper, 0.0)

    @pl.when(pl.program_id(0) == pl.num_programs(0) - 1)
    def _():
        back = math.log(2.0)
        dl_ref[:, :width] = dl_ref[:, :width] * back
        dr_ref[:, :width] = (dr_acc[:, :width] * back).astype(low)
        dr_ref[:, width:] = dr_acc[:, width:].astype(low)


def attend_back(query, kv_l, kv_r, grad, out, levels, head):
    tokens, width = query.shape
    heads = width // head
    both = (tokens, 2 * width)
    one = (tokens, width)
    return pl.pallas_call(
        functools.partial(attend_back_body, head),
        grid=(heads // PAIR,),
        in_specs=[whole(one), whole(both), whole(both), whole(one), whole(one), whole(levels.shape)],
        out_specs=[whole(one), whole(both), whole(both)],
        out_shape=[like(one, full), like(both, full), like(both, low)],
        scratch_shapes=[pltpu.VMEM(both, full)],
        compiler_params=params(62),
        cost_estimate=pl.CostEstimate(
            flops=20 * tokens * tokens * WINDOW * heads, bytes_accessed=28 * tokens * width, transcendentals=2 * tokens * tokens * heads
        ),
        name="attend_back",
    )(query, kv_l, kv_r, grad, out, levels)


class Weight:
    def __init__(self, segments):
        self.segments = segments
        self.columns = sum(columns for _, _, columns in segments)
        self.plan = [piece[1:] for piece in segments[0][1]]
        self.height = sum(rows for _, _, rows in self.plan)
        for _, pieces, _ in segments:
            assert [piece[3] for piece in pieces] == [rows for _, _, rows in self.plan]


def piece_source(ref, lead, first, count):
    for index in lead:
        ref = ref.at[index]
    return ref.at[:, pl.ds(first, count)]


class Cols:
    def __init__(self, array, first, count):
        self.source = array
        self.first = first
        self.count = count

    @property
    def array(self):
        return self.source if isinstance(self.source, jax.Array) else self.source.value

    @property
    def shape(self):
        return (self.array.shape[0], self.count)

    @property
    def dtype(self):
        return self.array.dtype

    @property
    def size(self):
        return self.array.shape[0] * self.count

    def value(self):
        return self.array[:, self.first : self.first + self.shape[1]]


def plain(value):
    return value.value().astype(full) if isinstance(value, Cols) else value


def anywhere(count):
    return [pl.BlockSpec(memory_space=pl.ANY)] * count


class Stream:
    def __init__(self, weights, tile, late):
        self.weights = weights
        self.tile = tile
        self.late = late
        self.steps = weights[0].columns // tile

    def pieces_of(self):
        return [pieces for w in self.weights for _, pieces, _ in w.segments]

    def specs(self):
        return [pl.BlockSpec(memory_space=pltpu.SMEM)] + anywhere(sum(len(p) for p in self.pieces_of()) + len(self.late))

    def operands(self):
        offsets = jnp.concatenate([offs for w in self.weights for offs, _, _ in w.segments])
        arrays = [piece[0] for pieces in self.pieces_of() for piece in pieces]
        return [offsets] + arrays + [v.array if isinstance(v, Cols) else v for v in self.late]

    def scratch(self):
        shapes = []
        for w in self.weights:
            shapes += [pltpu.VMEM((2, w.height, self.tile), low), pltpu.SemaphoreType.DMA((2, len(w.plan)))]
        for value in self.late:
            shapes += [pltpu.VMEM(value.shape, value.dtype), pltpu.SemaphoreType.DMA((1,))]
        return shapes

    def bind(self, operand_refs, scratch_refs):
        self.offs = operand_refs[0]
        refs = list(operand_refs[1:])
        self.refs = []
        for w in self.weights:
            mine = []
            for _, pieces, _ in w.segments:
                mine.append(refs[: len(pieces)])
                refs = refs[len(pieces) :]
            self.refs.append(mine)
        self.buffers = scratch_refs[0 : 2 * len(self.weights) : 2]
        self.sems = scratch_refs[1 : 2 * len(self.weights) : 2]
        rest = scratch_refs[2 * len(self.weights) :]
        self.late_bufs = rest[0::2]
        self.late_copies = []
        for value, ref, buf, sem in zip(self.late, refs, rest[0::2], rest[1::2]):
            if isinstance(value, Cols):
                ref = ref.at[:, pl.ds(value.first, value.shape[1])]
            self.late_copies.append(pltpu.make_async_copy(ref, buf, sem.at[0]))

    def segment_copies(self, index, number, column, slot):
        w = self.weights[index]
        base = sum(len(x.plan) * len(x.segments) for x in self.weights[:index]) + number * len(w.plan)
        out = []
        for at, (_, lead, first, rows) in enumerate(w.segments[number][1]):
            source = piece_source(self.refs[index][number][at], lead, pl.multiple_of(first + column, 128), self.tile)
            start = pl.multiple_of(self.offs[base + at], 16)
            target = self.buffers[index].at[slot, pl.ds(start, rows), :]
            out.append(pltpu.make_async_copy(source, target, self.sems[index].at[slot, at]))
        return out

    def copies(self, step, slot):
        return [copy for index in range(len(self.weights)) for copy in self.segment_copies(index, 0, step * self.tile, slot)]

    def start_tile(self, step, slot):
        for index, w in enumerate(self.weights):
            first = 0
            for number, (_, _, columns) in enumerate(w.segments):
                count = columns // self.tile

                def start():
                    for copy in self.segment_copies(index, number, (step - first) * self.tile, slot):
                        copy.start()

                if len(w.segments) == 1:
                    start()
                else:
                    pl.when(jnp.logical_and(step >= first, step < first + count))(start)
                first += count

    def wait_tile(self, slot):
        for index in range(len(self.weights)):
            for copy in self.segment_copies(index, 0, 0, slot):
                copy.wait()

    def advance(self):
        step = pl.program_id(0)
        slot = lax.rem(step, 2)

        @pl.when(step == 0)
        def _():
            self.start_tile(jnp.int32(0), 0)
            for copy in self.late_copies:
                copy.start()

        @pl.when(step + 1 < self.steps)
        def _():
            self.start_tile(step + 1, 1 - slot)

        self.wait_tile(slot)
        return step, [buf.at[slot] for buf in self.buffers]

    def wait_late(self):
        for copy in self.late_copies:
            copy.wait()
        return self.late_bufs


def stream_call(name, stream, body, ins, in_specs, outs, out_specs, scratch, flops, mib=58):
    operands = stream.operands()
    frame = stream.scratch()

    def kernel(*refs):
        count = len(operands)
        ops, refs = refs[:count], refs[count:]
        inputs, refs = refs[: len(ins)], refs[len(ins) :]
        outputs, refs = refs[: len(outs)], refs[len(outs) :]
        stream.bind(ops, refs[: len(frame)])
        body(stream, inputs, outputs, refs[len(frame) :])

    moved = sum(v.size * v.dtype.itemsize for v in list(ins) + list(stream.late) + list(outs))
    moved += sum(2 * w.height * w.columns for w in stream.weights)
    return pl.pallas_call(
        kernel,
        grid=(stream.steps,),
        in_specs=stream.specs() + in_specs,
        out_specs=out_specs,
        out_shape=outs,
        scratch_shapes=frame + scratch,
        compiler_params=params(mib),
        cost_estimate=pl.CostEstimate(flops=flops, bytes_accessed=moved, transcendentals=0),
        name=name,
    )(*operands, *ins)


def by_rows(tokens, fun, step=128):
    @pl.loop(0, tokens // step)
    def _(i):
        fun(pl.ds(pl.multiple_of(i * step, step), step))


def take(ref, rows):
    return (ref[rows, :] if ref.shape[0] > 1 else ref[...]).astype(full)


def give(ref, rows, value):
    if ref.shape[0] > 1:
        ref[rows, :] = value.astype(ref.dtype)
    else:
        ref[...] += jnp.sum(value, axis=0, keepdims=True)


def like(shape, dtype):
    return jax.ShapeDtypeStruct(shape, dtype)


def ada_matmul(value, weight, bias):
    tokens = value.shape[0]
    tile = weight.height
    stream = Stream([weight], tile, [])

    def body(stream, ins, outs, scratch):
        _, (w,) = stream.advance()
        outs[0][...] = (matmul(ins[0][...], w[...]) + ins[1][...]).astype(low)

    return stream_call(
        "ada",
        stream,
        body,
        [value, bias],
        [whole(value.shape), pl.BlockSpec((1, tile), lambda j: (0, j))],
        [like((tokens, weight.columns), low)],
        [pl.BlockSpec((tokens, tile), lambda j: (0, j))],
        [],
        2 * tokens * weight.height * weight.columns,
    )[0]


def mod_partial(row, weight, width):
    shard = weight.shape[1]
    tall = jnp.broadcast_to(row, (16, shard))

    def body(x_ref, w_ref, out_ref):
        out_ref[0] = matmul(x_ref[...], w_ref[...])[:8]

    out = pl.pallas_call(
        body,
        grid=(6,),
        in_specs=[whole(tall.shape), pl.BlockSpec((None, shard, width), lambda j: (0, 0, j))],
        out_specs=pl.BlockSpec((1, 8, width), lambda j: (j, 0, 0)),
        out_shape=like((6, 8, width), full),
        compiler_params=params(60),
        cost_estimate=pl.CostEstimate(flops=0, bytes_accessed=12 * shard * width, transcendentals=0),
        name="modpart",
    )(tall, weight)
    return out[:, 0]


def qkv_matmul(value, weight, cosine, sine, gains, member, member_t, head):
    tokens, width = value.shape
    stream = Stream([weight], width, [cosine, sine])

    def body(stream, ins, outs, scratch):
        x_ref, gain_ref, mem_ref, memt_ref = ins
        q_ref, kv_ref, raw_ref = outs
        (acc_ref,) = scratch
        step, (w,) = stream.advance()
        cos_ref, sin_ref = stream.late_bufs
        acc_ref[...] = matmul(x_ref[...], w[...])

        @pl.when(step == 0)
        def _():
            stream.wait_late()

        def head_norm(part, out, cols):
            def rows_of(rows):
                raw = acc_ref[rows, :]
                raw_ref[rows, :] = raw
                mean = head_mean(raw * raw, mem_ref[...], head)
                inverse = split_dot(lax.rsqrt(mean + epsilon), memt_ref[...])
                normed = raw * inverse * gain_ref[part : part + 1, :]
                even = even_lanes(gain_ref, raw.shape)
                out[rows, cols] = turned(normed, cos_ref[rows, :], sin_ref[rows, :], even, head // 4).astype(low)

            by_rows(tokens, rows_of, 256)

        @pl.when(step == 0)
        def _():
            head_norm(0, q_ref, slice(0, width))

        @pl.when(step == 1)
        def _():
            head_norm(1, kv_ref, slice(0, width))

        @pl.when(step == 2)
        def _():
            kv_ref[:, width:] = acc_ref[...].astype(low)

    flat = like((tokens, width), low)
    return stream_call(
        "qkv",
        stream,
        body,
        [value, gains, member, member_t],
        [whole(v.shape) for v in (value, gains, member, member_t)],
        [flat, like((tokens, 2 * width), low), like((tokens, 2 * width), full)],
        [whole((tokens, width)), whole((tokens, 2 * width)), pl.BlockSpec((tokens, width), lambda j: (0, jnp.minimum(j, 1)))],
        [pltpu.VMEM((tokens, width), full)],
        2 * tokens * weight.height * weight.columns,
    )


def out_matmul(value, weight, hidden0, mods):
    tokens, width = value.shape
    stream = Stream([weight], 384, [hidden0] + mods)

    def body(stream, ins, outs, scratch):
        att_ref, h1_ref, b_ref = outs
        (acc_ref,) = scratch
        step, (w,) = stream.advance()
        acc_ref[step] = matmul(ins[0][...], w[...])

        @pl.when(step == stream.steps - 1)
        def _():
            h0_ref, gate_ref, shift_ref, scale_ref = stream.wait_late()

            def rows_of(rows):
                att = jnp.concatenate([acc_ref[k, rows, :] for k in range(stream.steps)], axis=1)
                hidden1 = h0_ref[rows, :] + take(gate_ref, rows) * att
                normed = hidden1 * rms_scale(hidden1)
                att_ref[rows, :] = att.astype(low)
                h1_ref[rows, :] = hidden1
                b_ref[rows, :] = (normed * (1.0 + take(scale_ref, rows)) + take(shift_ref, rows)).astype(low)

            by_rows(tokens, rows_of)

    return stream_call(
        "attout",
        stream,
        body,
        [value],
        [whole(value.shape)],
        [like((tokens, width), low), like((tokens, width), full), like((tokens, width), low)],
        [whole((tokens, width))] * 3,
        [pltpu.VMEM((stream.steps, tokens, 384), full)],
        2 * tokens * weight.height * weight.columns,
    )


def gate_up_matmul(value, gate, up):
    tokens, width = value.shape
    tile = 1024
    stream = Stream([gate, up], tile, [])

    def body(stream, ins, outs, scratch):
        hid_ref, g_ref, u_ref = outs
        _, (wg, wu) = stream.advance()
        g = matmul(ins[0][...], wg[...])
        u = matmul(ins[0][...], wu[...])
        g_ref[...] = g.astype(low)
        u_ref[...] = u.astype(low)
        hid_ref[...] = (g * jax.nn.sigmoid(g) * u).astype(low)

    flat = like((tokens, gate.columns), low)
    return stream_call(
        "gateup",
        stream,
        body,
        [value],
        [whole(value.shape)],
        [flat] * 3,
        [pl.BlockSpec((tokens, tile), lambda j: (0, j))] * 3,
        [],
        4 * tokens * gate.height * gate.columns,
    )


def down_matmul(value, weight, hidden1, gate):
    tokens, depth = value.shape
    width = weight.columns
    stream = Stream([weight], width, [hidden1, gate])

    def body(stream, ins, outs, scratch):
        mlp_ref, h2_ref = outs
        (acc_ref,) = scratch
        hid_ref = ins[0]
        at = 0
        copies = stream.copies(0, 0)
        for copy in copies + stream.late_copies:
            copy.start()
        for k, (_, _, rows) in enumerate(weight.plan):
            copies[k].wait()
            first = stream.offs[k]
            left = hid_ref[:, pl.ds(pl.multiple_of(first, 128), rows)]
            part = matmul(left, stream.buffers[0][0, pl.ds(pl.multiple_of(first, 128), rows), :])
            if k == 0:
                acc_ref[...] = part
            else:
                acc_ref[...] += part
        h1_ref, gate_ref = stream.wait_late()

        def rows_of(rows):
            mlp = acc_ref[rows, :]
            mlp_ref[rows, :] = mlp.astype(low)
            h2_ref[rows, :] = h1_ref[rows, :] + take(gate_ref, rows) * mlp

        by_rows(tokens, rows_of)

    return stream_call(
        "down",
        stream,
        body,
        [value],
        [whole(value.shape)],
        [like((tokens, width), low), like((tokens, width), full)],
        [whole((tokens, width))] * 2,
        [pltpu.VMEM((tokens, width), full)],
        2 * tokens * depth * width,
    )


def down_back(grad, weight, gate_pre, up_pre):
    tokens, width = grad.shape
    depth = weight.height
    stream = Stream([weight], width, [gate_pre, up_pre])

    def body(stream, ins, outs, scratch):
        dg_ref, du_ref = outs
        copies = stream.copies(0, 0)
        for copy in copies + stream.late_copies:
            copy.start()
        for k, (_, _, count) in enumerate(weight.plan):
            copies[k].wait()
            if k == 0:
                g_ref, u_ref = stream.wait_late()
            first = pl.multiple_of(stream.offs[k], 128)
            for at in range(0, count, 384):
                cols = pl.ds(pl.multiple_of(first + at, 128), 384)
                inner = matmul_t(ins[0][...], stream.buffers[0][0, cols, :])
                g = g_ref[:, cols].astype(full)
                u = u_ref[:, cols].astype(full)
                sigma = jax.nn.sigmoid(g)
                active = g * sigma
                dg_ref[:, cols] = (inner * u * (sigma + active * (1.0 - sigma))).astype(low)
                du_ref[:, cols] = (inner * active).astype(low)

    flat = like((tokens, depth), low)
    return stream_call(
        "downback",
        stream,
        body,
        [grad],
        [whole(grad.shape)],
        [flat, flat],
        [whole((tokens, depth))] * 2,
        [],
        2 * tokens * depth * width,
    )


def back_matmul(name, grads, weights, tile, late, outs, finish):
    tokens = grads[0].shape[0]
    width = weights[0].height
    stream = Stream(weights, tile, late)

    def body(stream, ins, outs, scratch):
        (acc_ref,) = scratch
        step, tiles = stream.advance()
        part = matmul_t(ins[0][...], tiles[0][...])
        for value, w in zip(ins[1:], tiles[1:]):
            part = part + matmul_t(value[...], w[...])

        @pl.when(step == 0)
        def _():
            acc_ref[...] = part

        @pl.when(step > 0)
        def _():
            acc_ref[...] += part

        @pl.when(step == stream.steps - 1)
        def _():
            refs = stream.wait_late()
            for ref in outs:
                if ref.shape[0] == 1:
                    ref[...] = jnp.zeros_like(ref)
            by_rows(tokens, lambda rows: finish(rows, acc_ref[rows, :], refs, outs))

    return stream_call(
        name,
        stream,
        body,
        list(grads),
        [pl.BlockSpec((tokens, tile), lambda j: (0, j))] * len(grads),
        outs,
        [whole(value.shape) for value in outs],
        [pltpu.VMEM((tokens, width), full)],
        2 * tokens * width * weights[0].columns * len(weights),
    )


def mlp_back(grads, weights, grad2, hidden1, att, mods):
    tokens, width = grad2.shape
    lead = mods[0].shape[0]

    def finish(rows, db, refs, outs):
        dh2_ref, h1_ref, att_ref, scale_ref, gate_ref = refs
        hidden1 = h1_ref[rows, :]
        inverse = rms_scale(hidden1)
        normed = hidden1 * inverse
        weighted = db * (1.0 + take(scale_ref, rows))
        back = inverse * (weighted - normed * jnp.mean(normed * weighted, axis=-1, keepdims=True))
        grad1 = dh2_ref[rows, :] + back
        outs[0][rows, :] = grad1
        outs[1][rows, :] = (grad1 * take(gate_ref, rows)).astype(low)
        give(outs[2], rows, db)
        give(outs[3], rows, db * normed)
        give(outs[4], rows, grad1 * att_ref[rows, :].astype(full))

    outs = [like((tokens, width), full), like((tokens, width), low)]
    outs += [like((lead, width), low if lead > 1 else full)] * 3
    return back_matmul("mlpback", grads, weights, 1024, [grad2, hidden1, att] + mods, outs, finish)


def qkv_back(grad, weight, grad1, hidden0, scale):
    tokens, width = grad1.shape
    lead = scale.shape[0]

    def finish(rows, da, refs, outs):
        dh1_ref, h0_ref, scale_ref = refs
        hidden0 = h0_ref[rows, :]
        inverse = rms_scale(hidden0)
        normed = hidden0 * inverse
        weighted = da * (1.0 + take(scale_ref, rows))
        back = inverse * (weighted - normed * jnp.mean(normed * weighted, axis=-1, keepdims=True))
        outs[0][rows, :] = (dh1_ref[rows, :] + back).astype(low)
        give(outs[1], rows, da)
        give(outs[2], rows, da * normed)

    outs = [like((tokens, width), low)] + [like((lead, width), low if lead > 1 else full)] * 2
    return back_matmul("qkvback", [grad], [weight], width, [grad1, hidden0, scale], outs, finish)


def out_back(grad, weight):
    def finish(rows, value, refs, outs):
        outs[0][rows, :] = value.astype(low)

    return back_matmul("outback", [grad], [weight], 1152, [], [like(grad.shape, low)], finish)[0]


def ada_back(grads, weight, cond):
    tokens, width = cond.shape
    tile = weight.height
    stream = Stream([weight], tile, [cond])

    def body(stream, ins, outs, scratch):
        (acc_ref,) = scratch
        step, (w,) = stream.advance()
        for k, grad in enumerate(ins):

            @pl.when(step == k)
            def _():
                part = matmul_t(grad[...], w[...])
                acc_ref[...] = part if k == 0 else acc_ref[...] + part

        @pl.when(step == stream.steps - 1)
        def _():
            (cond_ref,) = stream.wait_late()

            def rows_of(rows):
                cond = cond_ref[rows, :]
                sigma = jax.nn.sigmoid(cond)
                outs[0][rows, :] = acc_ref[rows, :] * sigma * (1.0 + cond * (1.0 - sigma))

            by_rows(tokens, rows_of)

    return stream_call(
        "adaback",
        stream,
        body,
        list(grads),
        [whole(grad.shape) for grad in grads],
        [like((tokens, width), full)],
        [whole((tokens, width))],
        [pltpu.VMEM((tokens, width), full)],
        2 * tokens * width * weight.columns,
    )[0]


def ordered_grad(left, order, rights, tile):
    tokens, width = left.shape
    counts = [right.shape[1] // tile for right in rights]
    firsts = [sum(counts[:k]) for k in range(len(rights))]
    columns = sum(right.shape[1] for right in rights)

    def body(order_ref, left_ref, *refs):
        ys, out_ref, turned_ref = refs[: len(rights)], refs[-2], refs[-1]
        step = pl.program_id(0)

        @pl.when(step == 0)
        def _():
            turned_ref[...] = matmul_t(order_ref[...], left_ref[...]).astype(low)

        if len(rights) == 1:
            out_ref[...] = matmul(turned_ref[...], ys[0][...]).astype(low)
            return
        for y, first, count in zip(ys, firsts, counts):

            @pl.when(jnp.logical_and(step >= first, step < first + count))
            def _():
                out_ref[...] = matmul(turned_ref[...], y[...]).astype(low)

    def tile_of(first, count):
        return pl.BlockSpec((tokens, tile), lambda j: (0, jnp.clip(j - first, 0, count - 1)))

    return pl.pallas_call(
        body,
        grid=(columns // tile,),
        in_specs=[whole(order.shape), whole(left.shape)] + [tile_of(f, c) for f, c in zip(firsts, counts)],
        out_specs=pl.BlockSpec((width, tile), lambda j: (0, j)),
        out_shape=like((width, columns), low),
        scratch_shapes=[pltpu.VMEM((width, tokens), low)],
        compiler_params=params(60),
        cost_estimate=pl.CostEstimate(
            flops=2 * tokens * width * (columns + width), bytes_accessed=2 * width * (columns + 2 * width), transcendentals=0
        ),
        name="wgrad",
    )(order, left, *rights)


def down_grad(left, right, groups):
    tokens, depth = left.shape
    columns = right.shape[1]
    tile = depth // groups

    def body(left_ref, right_ref, out_ref):
        value = outer_sum(left_ref[...], right_ref[...]).astype(low)
        out_ref[0, 0] = value[: tile // 2]
        out_ref[1, 0] = value[tile // 2 :]

    return pl.pallas_call(
        body,
        grid=(groups,),
        in_specs=[pl.BlockSpec((tokens, tile), lambda j: (0, j)), whole(right.shape)],
        out_specs=pl.BlockSpec((2, 1, tile // 2, columns), lambda j: (0, j, 0, 0)),
        out_shape=like((2, groups, tile // 2, columns), low),
        compiler_params=params(40),
        cost_estimate=pl.CostEstimate(
            flops=2 * tokens * depth * columns, bytes_accessed=2 * depth * (columns + tokens), transcendentals=0
        ),
        name="wdown",
    )(left, right)


def tie(value, *others):
    others = [v for v in others if v is not None]
    if not others:
        return value
    return lax.optimization_barrier((value, *others))[0]


class Flight:
    def __init__(self, token):
        self.token = token
        self.held = []
        self.todo = []
        self.later = []

    def send(self, value, item, holder, name):
        setattr(holder, name, swap(tie(value, self.token), item))
        self.held.append((holder, name))

    def watch(self, holder, name):
        self.held.append((holder, name))

    def then(self, action):
        self.todo.append(action)

    def fence(self, values, starts=()):
        values = list(values)
        held, todo = self.held, self.todo
        self.held, self.todo = [], []
        held += [(holder, name) for left, holder, name in self.later if left == 0]
        self.later = [(left - 1, holder, name) for left, holder, name in self.later if left > 0]
        arrays = values + [getattr(holder, name) for holder, name in held]
        arrays = lax.optimization_barrier(tuple(arrays))
        self.token = arrays[0]
        for (holder, name), value in zip(held, arrays[len(values) :]):
            setattr(holder, name, value)
        for action in todo:
            action()
        for start in starts:
            start(self)
        return arrays[: len(values)]


class Bundle:
    def __init__(self, place, own, shards, parts, which, relay_bit):
        self.row, self.col, coords = place
        self.own = own
        self.shards = shards
        self.parts = parts
        self.which = which
        self.relay_bit = relay_bit
        self.rows = shards[parts[0][0]].shape[1]
        self.half = self.rows // 2
        self.at = coords[relay_bit] * self.half

    def prepare(self, flight):
        at = tie(self.at, flight.token)
        mine = [
            lax.dynamic_slice(self.shards[name], (self.which, at, first), (1, self.half, n))[0]
            for name, first, n in self.parts
        ]
        self.mine = jnp.concatenate(mine, axis=1)
        flight.watch(self, "mine")

    def over_col(self, flight):
        flight.send(self.mine, "col", self, "first")

    def relay(self, flight):
        flight.send(self.first, self.relay_bit, self, "second")

    def first_row(self, flight):
        flight.send(self.first, "row", self, "first_s")

    def second_row(self, flight):
        flight.send(self.second, "row", self, "second_s")

    def rows_both(self, flight):
        self.first_row(flight)
        self.second_row(flight)

    def segment(self, wanted):
        row, col, rows, half, at = self.row, self.col, self.rows, self.half, self.at
        other = (2 * row + 1 - col) * rows
        other_s = (2 * (1 - row) + 1 - col) * rows
        offsets = [col * rows, (col + 2) * rows, other + at, other_s + at]
        offsets += [other + (half - at), other_s + (half - at)]
        offsets = jnp.stack(offsets).astype(jnp.int32)
        begin = 0
        for name, first, n in self.parts:
            if name == wanted:
                own_all = self.own[name]
                lead = () if own_all.ndim == 3 else (self.which,)
                pieces = [(own_all, (0,) + lead, first, rows), (own_all, (1,) + lead, first, rows)]
                got = [self.first, self.first_s, self.second, self.second_s]
                pieces += [(value, (), begin, half) for value in got]
                return (offsets, pieces, n)
            begin += n
        raise KeyError(wanted)


def weight_of(name, *bundles):
    return Weight([bundle.segment(name) for bundle in bundles])


def item_weight(item):
    return {"row": 2, "col": 1}.get(item) or 4 << item


def halving_order(path, width, block, me, bits):
    at = jnp.arange(width)
    position = at // block
    owner = me
    for item in reversed(path):
        if item == "hi":
            mask = (1 << (bits - 1)) - 1
            owner = (owner & 7) | ((position & mask) << 3)
            position = position >> (bits - 1)
            continue
        bit = position & 1
        position = position >> 1
        if item == "row":
            owner = (owner & ~2) | (2 * bit)
        else:
            owner = owner ^ (bit * item_weight(item))
    return owner * block + at % block


class Slice:
    def __init__(self, held, columns, name="value"):
        self.held = held
        self.columns = columns
        self.name = name

    def get(self):
        return getattr(self.held, self.name)[..., self.columns]


class Term:
    def __init__(self, terms, at):
        self.terms = terms
        self.at = at

    @property
    def value(self):
        return self.terms[self.at][0]

    @value.setter
    def value(self, value):
        self.terms[self.at] = (value, self.terms[self.at][1])


class Share:
    def __init__(self, value, order, path):
        self.terms = [(value, list(order))]
        self.order = list(order)
        self.path = list(path)
        self.done = []
        self.result = None
        self.columns = None

    def pick(self, value, order, choice):
        order = list(order)
        while order and any(item in choice for item in order[:2]):
            rows, columns = value.shape
            if order[0] in choice:
                at = choice[order.pop(0)] * (rows // 2)
                value = value[at : at + rows // 2]
            else:
                at = choice[order.pop(1)]
                value = value.reshape(2, 2, rows // 4, columns)[:, at].reshape(rows // 2, columns)
        return value

    def collect(self, last=None):
        choice = {item: 0 for item in self.done}
        if last is not None:
            choice[last] = 1
        total = None
        for value, order in self.terms:
            value = value.get() if isinstance(value, Slice) else value
            part = self.pick(value, order, choice).astype(full)
            total = part if total is None else total + part
        return total

    def send(self, item):
        away = self.collect(item).astype(low)
        self.done.append(item)
        self.order = [other for other in self.order if other != item]
        return away

    def arrive(self, got):
        self.terms.append((got, self.order))

    @property
    def value(self):
        return self.collect() if self.result is None else self.result.get().astype(full)

    def hold(self, flight):
        if self.result is not None:
            flight.watch(self.result.held, self.result.name)
            return
        for at, (value, _) in enumerate(self.terms):
            if isinstance(value, Slice):
                flight.watch(value.held, value.name)
            else:
                flight.watch(Term(self.terms, at), "value")

    @property
    def base(self):
        return self.terms[0][0]

    @base.setter
    def base(self, value):
        self.terms[0] = (value, self.terms[0][1])


class BlockShare(Share):
    def __init__(self, value, order, path, coords):
        super().__init__(value, order, path)
        self.coords = coords

    def pick(self, value, order, choice):
        starts = [jnp.bitwise_xor(self.coords[item], choice[item]) if item in choice else 0 for item in order] + [0, 0]
        sizes = [1 if item in choice else 2 for item in order] + list(value.shape[-2:])
        if self.columns is not None and value.shape[-1] != self.columns[1]:
            starts[-1], sizes[-1] = self.columns
        value = lax.dynamic_slice(value, starts, sizes)
        return value.reshape([size for size in sizes[:-2] if size > 1] + list(sizes[-2:]))


class Total:
    def __init__(self, value, path):
        self.value = value
        self.path = list(path)

    def send(self, item):
        return self.value.astype(low)

    def arrive(self, got):
        self.value = self.value + got.astype(full)


class TotalAndRows(Total):
    def __init__(self, value, count, path):
        super().__init__(value, path)
        self.count = count

    def arrive(self, got):
        n = self.count
        value = self.value
        got = got.astype(full)
        self.value = jnp.concatenate([value[:n] + got[:n], value[n:], got[n:]], axis=0)


class Parcel:
    got = None


def last_share(value, bits):
    groups = [[2 * k + low_bit for k in range(1 << (bits - 1))] for low_bit in (0, 1)]
    return lax.psum_scatter(value, "dp", scatter_dimension=0, axis_index_groups=groups, tiled=False)


class Agenda:
    def __init__(self):
        self.tasks = {}
        self.packed = {}

    def scatter(self, bits, windows, *names):
        def action(flight):
            self.pack(bits, *names)
            parcel, widths = self.packed[names]
            parcel.got = last_share(tie(parcel.got, flight.token), bits)
            if windows is not None:
                flight.later.append((windows, parcel, "got"))
            at = 0
            for name, n in zip(names, widths):
                task = self.tasks[name]
                assert task.path.pop(0) == "hi"
                task.result = Slice(parcel, slice(at, at + n), "got")
                at += n

        return action

    def pack(self, bits, *names):
        tasks = [self.tasks[name] for name in names]
        parts = [task.collect().astype(low) for task in tasks]
        height = 1 << (bits - 1)
        block = parts[0].shape[-2] if isinstance(tasks[0], BlockShare) else parts[0].shape[0] // height
        value = parts[0] if len(parts) == 1 else jnp.concatenate(parts, axis=-1)
        parcel = Parcel()
        parcel.got = value.reshape(height, block, value.shape[-1])
        self.packed[names] = (parcel, [part.shape[-1] for part in parts])

    def go(self, *names):
        def action(flight):
            tasks = [self.tasks[name] for name in names]
            items = [task.path.pop(0) for task in tasks]
            assert len(set(items)) == 1
            sent = [task.send(items[0]) for task in tasks]
            parcel = Parcel()
            away = sent[0] if len(sent) == 1 else jnp.concatenate(sent, axis=-1)
            flight.send(away, items[0], parcel, "got")

            def arrive():
                at = 0
                for task, value in zip(tasks, sent):
                    n = value.shape[-1]
                    task.arrive(parcel.got if len(tasks) == 1 else parcel.got[..., at : at + n])
                    at += n

            flight.then(arrive)

        return action


def row_sum(value):
    return lax.psum_scatter(value, "row", scatter_dimension=0, tiled=True)


def grad_blocks(left, right, bits, block):
    if (4 * block) % 128 == 0:
        value = down_grad(left, right, 2**bits)
    else:
        value = outer_sum(left, right).astype(low).reshape(2**bits, 2, 2 * block, right.shape[1])
        value = jnp.swapaxes(value, 0, 1)
    return value.reshape((2,) * (bits + 2) + (block, right.shape[1]))


def block_forward(hidden0, mods, mats, gains, tabs, flight, points):
    shift1, scale1, gate1, shift2, scale2, gate2 = mods
    cosine, sine, member, member_t, head = tabs
    used = {}

    def mat(name):
        used[name] = mats[name]()
        return used[name]

    def fence(point, *values):
        if point not in points:
            return values if len(values) > 1 else values[0]
        values = flight.fence(values, points[point])
        return values if len(values) > 1 else values[0]

    attn_in = (hidden0 * rms_scale(hidden0) * (1.0 + plain(scale1)) + plain(shift1)).astype(low)
    attn_in = fence("qkv", attn_in)
    query, kv, raw = qkv_matmul(attn_in, mat("qkv"), cosine, sine, gains[0], member, member_t, head)
    query, kv = fence("attend", query, kv)
    kv_r = swap(kv, "row")
    out_b, lse = attend(query, kv, kv_r, head)
    out_b = fence("out", out_b)
    att, hidden1, mlp_in = out_matmul(out_b, mat("out"), hidden0, [gate1, shift2, scale2])
    mlp_in = fence("gate", mlp_in)
    inner, gate_pre, up_pre = gate_up_matmul(mlp_in, mat("gate"), mat("up"))
    inner = fence("down", inner)
    mlp_out, hidden2 = down_matmul(inner, mat("down"), hidden1, gate2)
    cache = (hidden0, attn_in, raw, query, kv, kv_r, out_b, lse, att)
    cache += (hidden1, mlp_in, gate_pre, up_pre, inner, mlp_out)
    used = tuple(used[name] for name in ("qkv", "out", "gate", "up", "down"))
    return hidden2, cache, used


class Sum:
    value = None


def block_backward(grad2, cache, mods, mats, gains, tabs, comm, tag, plan):
    (hidden0, attn_in, raw, query, kv, kv_r, out_b, lse, att) = cache[:9]
    (hidden1, mlp_in, gate_pre, up_pre, inner, mlp_out) = cache[9:]
    shift1, scale1, gate1, shift2, scale2, gate2 = mods
    qkv_w, out_w, gate_w, up_w, down_w = mats
    cosine, sine, member, member_t, head = tabs
    flight, agenda, orders, paths, coords = comm
    n_data = lax.axis_size("dp")
    bits = (n_data - 1).bit_length()
    block = down_w.height // (4 * n_data)
    width = hidden0.shape[1]

    def fence(point, *values):
        values = flight.fence(values, plan.get(point, ()))
        return values if len(values) > 1 else values[0]

    def grad_of(left, name, rights, tile):
        return ordered_grad(left, orders[name], rights, tile)

    def watch(name, task):
        agenda.tasks[name + tag] = task
        flight.watch(task, "base")

    def begin(name, value):
        order = paths[name][1:]
        watch(name[0], Share(value, order, [order[1], order[0]] + order[2:]))

    def begin_halves(name, value, cut):
        path = paths[name][1:]
        other = [path[1], path[0]] + path[2:]
        held = Sum()
        held.value = value
        flight.watch(held, "value")
        agenda.tasks[name[0] + "a" + tag] = Share(Slice(held, slice(0, cut)), path, path)
        agenda.tasks[name[0] + "b" + tag] = Share(Slice(held, slice(cut, None)), path, other)

    def begin_down(value):
        order = ["row"] + list(reversed(range(bits))) + ["col"]
        watch("d", BlockShare(value, order, ["row"], coords))

    grad_mlp = (grad2 * plain(gate2)).astype(low)
    dgate2 = grad2 * mlp_out.astype(full)
    if gate2.shape[0] == 1:
        dgate2 = jnp.sum(dgate2, axis=0, keepdims=True)
    begin_down(grad_blocks(inner, grad_mlp, bits, block))
    grad2, grad_mlp = fence("start", grad2, grad_mlp)
    grad_gate, grad_up = down_back(grad_mlp, down_w, gate_pre, up_pre)
    w_gate = grad_of(mlp_in, "gate", [grad_gate, grad_up], 1024)
    grad_gate, grad_up, w_gate = fence("gate", grad_gate, grad_up, w_gate)
    r_gate = row_sum(w_gate)
    grad1, grad_att, dshift2, dscale2, dgate1 = mlp_back(
        [grad_gate, grad_up], [gate_w, up_w], grad2, hidden1, att, [scale2, gate1]
    )
    grad_att = fence("out", grad_att)
    w_out = grad_of(out_b, "out", [grad_att], 384)
    grad_ob = out_back(grad_att, out_w)
    begin_halves("gate", r_gate, grad_gate.shape[1])
    grad_ob, w_out = fence("attend", grad_ob, w_out)
    r_out = row_sum(w_out)
    dq, dkv, dkv_r = attend_back(query, kv, kv_r, grad_ob, out_b, lse, head)
    begin("out", r_out)
    dq, dkv_r = fence("qk", dq, dkv_r)
    grad_qkv, gain_rows = qk_back(dq, dkv, swap(dkv_r, "row"), raw, cosine, sine, gains[1], member, member_t, head)
    w_qkv = grad_of(attn_in, "qkv", [grad_qkv], width)
    grad_qkv, w_qkv = fence("qkv", grad_qkv, w_qkv)
    r_qkv = row_sum(w_qkv)
    grad0, dshift1, dscale1 = qkv_back(grad_qkv, qkv_w, grad1, hidden0, scale1)
    dmods = [dshift1, dscale1, dgate1, dshift2, dscale2, dgate2]
    begin_halves("qkv", r_qkv, r_qkv.shape[1] // 256 * 128)
    return grad0, dmods, gain_rows[:2], begin_halves


def per_device(
    latents,
    levels,
    timesteps,
    patch_weight,
    patch_bias,
    ada_weight,
    ada_bias,
    qkv_weight,
    qk_gains,
    out_weight,
    gate_weight,
    up_weight,
    down_weight,
    cotangent,
):
    images, slots, chans, rows_loc, cols_loc = latents.shape
    n_data = lax.axis_size("dp")
    assert images == 1 and slots == 2
    assert lax.axis_size("row") == 2 and lax.axis_size("col") == 2
    row = lax.axis_index("row")
    col = lax.axis_index("col")
    data = lax.axis_index("dp")
    bits = (n_data - 1).bit_length()
    left = col == 0
    coords = {"row": row, "col": col}
    place = (row, col, coords)
    for k in range(bits):
        coords[k] = (data >> k) & 1
    grid_rows = rows_loc // 2
    grid_cols = cols_loc
    half_cols = grid_cols // 2
    tokens = grid_rows * grid_cols
    width = cotangent.shape[-1]
    head = qk_gains.shape[2]
    heads = width // head
    pvals = chans * 4
    shard = width // 4
    me = data * 4 + row * 2 + col
    own_rows = width // (4 * n_data)

    def pair(own, other, axis):
        return jnp.concatenate([jnp.where(left, own, other), jnp.where(left, other, own)], axis=axis)

    own = {}
    for name, s in (
        ("qkv", qkv_weight),
        ("out", out_weight),
        ("gate", gate_weight),
        ("up", up_weight),
        ("down", down_weight),
        ("ada", ada_weight),
    ):
        own[name] = lax.all_gather(s, "row", axis=0)
    shards = {"qkv": qkv_weight, "out": out_weight, "gate": gate_weight, "up": up_weight, "down": down_weight}
    shards["ada"] = ada_weight

    def bundle(which, relay_bit, *parts):
        return Bundle(place, own, shards, parts, which, relay_bit)

    ff = gate_weight.shape[2]
    b_q0 = bundle(0, 0, ("qkv", 0, width))
    b_kv0 = bundle(0, 1, ("qkv", width, 2 * width))
    b_out0 = bundle(0, 0, ("out", 0, width))
    b_gate0 = bundle(0, 0, ("gate", 0, ff))
    b_up0 = bundle(0, 1, ("up", 0, ff))
    b_down0 = bundle(0, 0, ("down", 0, width))
    b_ada_a = bundle(1, 1, ("ada", 0, 3 * width))
    b_ada_b = bundle(1, 0, ("ada", 3 * width, 3 * width))
    b_qkv1 = bundle(1, 1, ("qkv", 0, 3 * width))
    b_og1 = bundle(1, 0, ("out", 0, width), ("gate", 0, ff))
    b_up1 = bundle(1, 1, ("up", 0, ff))
    b_down1 = bundle(1, 0, ("down", 0, width))
    enc_mats = {
        "qkv": lambda: weight_of("qkv", b_q0, b_kv0),
        "out": lambda: weight_of("out", b_out0),
        "gate": lambda: weight_of("gate", b_gate0),
        "up": lambda: weight_of("up", b_up0),
        "down": lambda: weight_of("down", b_down0),
    }
    dec_mats = {
        "qkv": lambda: weight_of("qkv", b_qkv1),
        "out": lambda: weight_of("out", b_og1),
        "gate": lambda: weight_of("gate", b_og1),
        "up": lambda: weight_of("up", b_up1),
        "down": lambda: weight_of("down", b_down1),
    }

    small = jnp.concatenate(
        [jnp.swapaxes(patch_weight, 1, 2).reshape(2 * pvals, shard), patch_bias, ada_bias.reshape(12, shard)], axis=0
    )
    small_other = swap(small, "col")
    blk = latents[0]
    blk_other = swap(blk, "col")
    flight = Flight(small)

    class Start:
        pass

    Start.small, Start.blk = small_other, blk_other
    flight.watch(Start, "small")
    flight.watch(Start, "blk")
    (blk,) = flight.fence([blk], [b_q0.prepare, b_kv0.prepare])
    small = pair(small[None], Start.small[None], 0)
    wide = pair(blk, Start.blk, 3)
    flight.send(small, "row", Start, "small")
    flight.send(wide[:, :, rows_loc - 1 :], "row", Start, "top")
    small, wide = flight.fence([small, wide], [b_q0.over_col, b_kv0.over_col, b_out0.prepare])
    temb = time_features(tie(timesteps, wide)[0], width)
    small = jnp.where(row == 0, jnp.stack([small, Start.small]), jnp.stack([Start.small, small]))
    small = small.reshape(4, 2 * pvals + 14, shard)
    patch_w = small[:, : 2 * pvals].transpose(1, 0, 2).reshape(2, pvals, width)
    patch_b = small[:, 2 * pvals : 2 * pvals + 2].transpose(1, 0, 2).reshape(2, width).astype(full)
    ada_b = small[:, 2 * pvals + 2 :].reshape(4, 2, 6 * shard).transpose(1, 0, 2).reshape(2, 6, width).astype(full)

    framed = jnp.concatenate([Start.top, wide[:, :, : rows_loc - 1]], axis=2)
    framed = jnp.concatenate([framed[..., -1:], framed[..., :-1]], axis=3)
    patches = (
        framed.reshape(slots, chans, grid_rows, 2, grid_cols, 2).transpose(0, 2, 4, 1, 3, 5).reshape(slots, tokens, pvals)
    )
    enc_patches = patches[0]
    dec_patches = jnp.where(left, patches[0], patches[1])

    sil0 = jax.nn.silu(temb[:1]).astype(low)
    temb_own = jnp.where(left, temb[:1], temb[1:])
    part = mod_partial(lax.dynamic_slice(sil0, (0, (2 * row + col) * shard), (1, shard)), ada_weight, width)

    cot_own = jnp.where(left, cotangent[0, 0], cotangent[0, 1])

    class Cotangent:
        got = None

    def send_cotangent(flight):
        flight.send(jnp.where(left, cotangent[0, 1], cotangent[0, 0]), "col", Cotangent, "got")

    quarter = head // 4
    lanes = tie(jnp.arange(width), flight.token)
    within = lanes % head
    section = within // quarter
    lane_freq = jnp.exp(-math.log(10000.0) * (within % quarter).astype(full) / quarter)
    row_pos = (row * grid_rows + jnp.arange(grid_rows)).astype(full)
    col_pos = jnp.arange(grid_cols).astype(full)
    row_angle = row_pos[:, None] * lane_freq[None, :]
    col_angle = col_pos[:, None] * lane_freq[None, :]
    by_row = section < 2
    sign = jnp.where(section % 2 == 0, -1.0, 1.0).astype(full)

    def table(fun):
        return jnp.where(by_row, fun(row_angle)[:, None, :], fun(col_angle)[None, :, :]).reshape(tokens, width)

    cosine = table(jnp.cos)
    sine = table(jnp.sin) * sign
    member = (lanes[:, None] // head == jnp.arange(128)[None, :]).astype(low)
    tabs = (cosine, sine, member, member.T, head)
    gain_rows = jnp.tile(qk_gains.astype(full), (1, 1, heads))
    even = jnp.broadcast_to((section % 2 == 0).astype(full), (2, 1, width))
    temper = head ** (-0.5) * math.log2(math.e)
    scaled = jnp.concatenate([gain_rows[:, :1] * temper, gain_rows[:, 1:], even], axis=1)
    gain_rows = jnp.concatenate([gain_rows, even], axis=1)
    gain_rows = [(scaled[k], gain_rows[k]) for k in range(2)]

    rest = list(range(2, bits))
    path_y = ["row", "col", 0, "hi"]
    path_s = ["row", "col", 0, 1] + rest
    paths = {"gate": path_y, "out": path_y, "qkv": path_y, "ada": path_s}
    perm = {}
    orders = {}
    for name in paths:
        key = tuple(paths[name])
        if key not in perm:
            source = halving_order(paths[name], width, own_rows, me, bits)
            perm[key] = lax.optimization_barrier((source[:, None] == lanes[None, :]).astype(low))
        orders[name] = perm[key]

    enc_h0 = matmul(enc_patches, patch_w[0]) + patch_b[0]
    starts = [b_q0.relay, b_kv0.relay, b_out0.over_col, b_q0.first_row, b_kv0.first_row, b_gate0.prepare]
    enc_h0, part, cosine, sine = flight.fence([enc_h0, part, cosine, sine], starts)
    part = part + swap(part, "row")
    part = part + swap(part, "col")
    enc_mod = part + ada_b[0]
    enc_mods = [enc_mod[k : k + 1] for k in range(6)]
    tabs = (cosine, sine) + tabs[2:]
    points = {
        "qkv": [b_q0.second_row, b_kv0.second_row, b_gate0.over_col, b_out0.relay, b_up0.prepare],
        "attend": [b_up0.over_col, b_gate0.relay, b_out0.first_row, b_down0.prepare],
        "out": [b_out0.second_row, b_up0.relay, b_down0.over_col, b_gate0.rows_both, b_ada_a.prepare],
        "gate": [b_up0.rows_both, b_ada_a.over_col, b_down0.relay, b_qkv1.prepare],
        "down": [b_down0.rows_both, b_qkv1.over_col, b_ada_a.relay, b_ada_b.prepare],
    }
    encoded, enc_cache, enc_mats = block_forward(enc_h0, enc_mods, enc_mats, gain_rows[0], tabs, flight, points)
    dec_h0 = matmul(dec_patches, patch_w[1]) + patch_b[1]
    cond = encoded + temb_own
    dec_sil = jax.nn.silu(cond).astype(low)
    starts = [b_ada_a.rows_both, b_ada_b.over_col, b_qkv1.relay, b_og1.prepare]
    keys = list(perm)
    dec_sil, *made = flight.fence([dec_sil] + [perm[key] for key in keys], starts)
    perm = dict(zip(keys, made))
    orders = {name: perm[tuple(paths[name])] for name in orders}
    ada_bias1 = ada_b[1].reshape(1, 6 * width)
    mod_a = ada_matmul(dec_sil, weight_of("ada", b_ada_a), ada_bias1[:, : 3 * width])
    dec_mods = [Cols(mod_a, k * width, width) for k in range(3)]
    held = Sum()

    def second_mods(flight):
        held.value = ada_matmul(tie(dec_sil, flight.token), weight_of("ada", b_ada_b), ada_bias1[:, 3 * width :])
        flight.watch(held, "value")

    dec_mods += [Cols(held, k * width, width) for k in range(3)]
    points = {
        "qkv": [b_qkv1.rows_both, b_og1.over_col, b_ada_b.relay, b_up1.prepare],
        "attend": [b_ada_b.rows_both, second_mods, b_up1.over_col, b_og1.relay, b_down1.prepare],
        "out": [b_og1.rows_both, b_down1.over_col, b_up1.relay],
        "gate": [b_up1.rows_both, b_down1.relay, send_cotangent],
        "down": [b_down1.rows_both],
    }
    decoded, dec_cache, dec_mats = block_forward(dec_h0, dec_mods, dec_mats, gain_rows[1], tabs, flight, points)
    live = (col < levels[0]).astype(full)
    result = (decoded * live).astype(low).reshape(grid_rows, grid_cols, width)
    near = jnp.where(left, result[:, :half_cols], result[:, half_cols:])
    far = jnp.where(left, result[:, half_cols:], result[:, :half_cols])

    class Away:
        got = None

    def send_result(flight):
        flight.send(far, "col", Away, "got")


    agenda = Agenda()
    go = agenda.go
    scatter = functools.partial(agenda.scatter, bits)
    comm = (flight, agenda, orders, paths, coords)
    cot = pair(cot_own, Cotangent.got, 1).reshape(tokens, width)
    dec_grad2 = cot.astype(full) * live

    def split_down(tag, way_a, way_b, flight):
        whole_sum = agenda.tasks["d" + tag]
        cut = width // 256 * 128
        for name, columns, way in (("da" + tag, (0, cut), way_a), ("db" + tag, (cut, width - cut), way_b)):
            part = BlockShare(None, whole_sum.order, way, coords)
            part.terms = list(whole_sum.terms)
            part.done = list(whole_sum.done)
            part.columns = columns
            agenda.tasks[name] = part

    plan = {
        "start": [send_result, go("d1")],
        "gate": [functools.partial(split_down, "1", ["col", 0, "hi"], [0, "col", "hi"]), go("da1"), go("db1")],
        "out": [go("da1"), go("db1")],
        "attend": [go("ga1"), go("gb1"), scatter(1, "da1", "db1")],
        "qk": [go("ga1"), go("gb1")],
        "qkv": [go("o1")],
    }
    dec_grad0, dec_dmods, dec_gains, begin_halves = block_backward(
        dec_grad2, dec_cache, dec_mods, dec_mats, gain_rows[1], tabs, comm, "1", plan
    )
    away = Away.got
    result = jnp.stack([jnp.where(left, near, away), jnp.where(left, away, near)])[None]
    dec_dmods = [piece.astype(low) for piece in dec_dmods]
    w_ada = ordered_grad(dec_sil, orders["ada"], dec_dmods, width)
    starts = [go("qa1"), go("qb1"), go("o1")]
    w_ada, *dec_dmods = flight.fence([w_ada] + dec_dmods, starts)
    r_ada = row_sum(w_ada)
    dec_bada = jnp.stack([jnp.sum(piece.astype(full), axis=0) for piece in dec_dmods])
    enc_grad2 = ada_back(dec_dmods, weight_of("ada", b_ada_a, b_ada_b), cond)

    def patch_rows(patch, grad):
        ones = jnp.ones((tokens, 1), low)
        return outer_sum(jnp.concatenate([patch, ones], axis=1), grad)

    total = jnp.concatenate([patch_rows(dec_patches, dec_grad0), dec_bada, dec_gains], axis=0)
    agenda.tasks["s"] = Total(total, ["row", "col"] + list(range(bits)))

    begin_halves("ada", r_ada, r_ada.shape[1] // 2)
    plan = {
        "start": [go("s"), go("d0"), go("aa1"), go("ab1"), scatter(0, "ga1", "gb1")],
        "gate": [
            functools.partial(split_down, "0", [1, "col", 0] + rest, [1, 0, "col"] + rest),
            go("aa1"),
            go("ab1"),
            go("qa1"),
            go("qb1"),
            go("da0"),
        ],
        "out": [go("s"), go("db0")],
        "attend": [go("s"), go("ga0"), go("gb0"), go("aa1", "ab1")],
        "qk": [go("ga0"), go("gb0"), go("da0"), go("db0"), scatter(0, "qa1", "qb1", "o1")],
        "qkv": [go("s"), go("o0"), go("da0"), go("db0"), go("aa1", "ab1")],
    }
    enc_grad0, enc_dmods, enc_gains, _ = block_backward(
        enc_grad2, enc_cache, enc_mods, enc_mats, gain_rows[0], tabs, comm, "0", plan
    )
    dmod_enc = jnp.concatenate(enc_dmods, axis=0)
    class Last:
        pass

    starts = [go("qa0"), go("qb0"), go("s"), scatter(1, "ga0", "gb0")]
    (enc_grad0,) = flight.fence([enc_grad0], starts)
    total = jnp.concatenate([patch_rows(enc_patches, enc_grad0), enc_gains, dmod_enc], axis=0)

    def image(dpatch):
        return (
            dpatch.reshape(grid_rows, grid_cols, chans, 2, 2).transpose(2, 0, 3, 1, 4).reshape(chans, rows_loc, 2 * cols_loc)
        )

    enc_image = image(matmul_t(enc_grad0, patch_w[0]))
    dec_image = image(matmul_t(dec_grad0, patch_w[1]))
    zero = jnp.zeros_like(dec_image)
    grads = jnp.stack([enc_image + jnp.where(left, dec_image, zero), jnp.where(left, zero, dec_image)])
    grads = jnp.concatenate([grads[..., 1:], grads[..., :1]], axis=3)
    total, grads = flight.fence([total, grads], [go("qa0"), go("qb0"), go("o0"), go("da0", "db0")])
    flight.send(total, "row", Last, "total")
    flight.send(grads[:, :, :1], "row", Last, "below")
    total, grads = flight.fence([total, grads], [scatter(None, "qa0", "qb0", "o0")])
    total = total + Last.total
    flight.send(total, "col", Last, "total")
    grads = jnp.concatenate([grads[:, :, 1:], Last.below], axis=2)
    one = grads[..., :cols_loc]
    two = grads[..., cols_loc:]
    flight.send(jnp.where(left, two, one), "col", Last, "image")
    count = pvals + 3
    tiny = TotalAndRows(None, count, list(range(bits)))
    agenda.tasks["t"] = tiny

    def begin_tiny(flight):
        tiny.value = jnp.concatenate([total + Last.total, sil0.astype(full)], axis=0)
        go("t")(flight)

    flight.fence([total], [begin_tiny])
    latent_grad = (jnp.where(left, one, two) + Last.image)[None]
    flight.fence([total], [go("t")])
    flight.fence([total], [go("t")])
    flight.fence([total])
    while any(task.path for task in agenda.tasks.values()):
        flight.fence([total], [go(name) for name, task in agenda.tasks.items() if task.path])
        flight.fence([total])
    dec_small = agenda.tasks["s"].value
    total = tiny.value[:count]
    dmod_all = tiny.value[count:]
    dmod_all = dmod_all.reshape(n_data, 7, width)
    enc_small = total
    enc_ada = jnp.dot(
        lax.dynamic_slice(dmod_all, (0, 6, me * own_rows), (n_data, 1, own_rows))[:, 0].T,
        dmod_all[:, :6].reshape(n_data, 6 * width),
        precision=highest,
        preferred_element_type=full,
    )
    enc_bada = jnp.sum(dmod_all[:, :6], axis=0)

    def own_lanes(value):
        return lax.dynamic_slice(value, (0, me * own_rows), (value.shape[0], own_rows))

    enc_patch = own_lanes(enc_small[: pvals + 1])
    dec_patch = own_lanes(dec_small[: pvals + 1])
    g_patch = jnp.stack([enc_patch[:pvals].T, dec_patch[:pvals].T])
    g_patch_b = jnp.stack([enc_patch[pvals], dec_patch[pvals]])
    bada = jnp.stack([enc_bada.reshape(-1), dec_small[pvals + 1 : pvals + 7].reshape(-1)])
    own_bada = 6 * own_rows
    g_bada = lax.dynamic_slice(bada, (0, me * own_bada), (2, own_bada))
    gains = jnp.stack([enc_small[pvals + 1 :], dec_small[pvals + 7 :]])
    gains = gains.reshape(2, 2, heads, head).sum(axis=2)
    def both(name):
        parts = [agenda.tasks[name + tag].value.astype(full) for tag in "01"]
        return jnp.stack(parts)

    for task in agenda.tasks.values():
        assert not task.path
    g_ada = jnp.concatenate([agenda.tasks["aa1"].value, agenda.tasks["ab1"].value], axis=1)
    g_ada_all = jnp.stack([enc_ada, g_ada.astype(full)])
    g_qkv = jnp.concatenate([both("qa"), both("qb")], axis=2)
    g_down = jnp.concatenate([both("da"), both("db")], axis=2)
    stacked = [g_qkv, both("o"), both("ga"), both("gb"), g_down]
    return (
        result,
        latent_grad,
        g_patch,
        g_patch_b,
        g_ada_all,
        g_bada,
        stacked[0],
        gains,
        stacked[1],
        stacked[2],
        stacked[3],
        stacked[4],
    )


def solution(mesh):
    tile = ("row", "col")
    every = ("dp", "row", "col")
    return jax.shard_map(
        per_device,
        mesh=mesh,
        in_specs=(
            P("dp", None, None, "row", "col"),
            P("dp"),
            P("dp", None),
            P(None, tile, None),
            P(None, tile),
            P(None, tile, None),
            P(None, tile),
            P(None, tile, None),
            P(),
            P(None, tile, None),
            P(None, tile, None),
            P(None, tile, None),
            P(None, tile, None),
            P("dp", None, "row", "col", None),
        ),
        out_specs=(
            P("dp", None, "row", "col", None),
            P("dp", None, None, "row", "col"),
            P(None, every, None),
            P(None, every),
            P(None, every, None),
            P(None, every),
            P(None, every, None),
            P(),
            P(None, every, None),
            P(None, every, None),
            P(None, every, None),
            P(None, every, None),
        ),
        check_vma=False,
    )
```
